32 devices in a mesh: wide: 16 (over z, y, core), narrow: 2 (over x).
Axes of the slice: x: 2, y: 2, z: 4, core: 2. Of those that a mesh axis runs over, the one named last changes fastest.
Arguments:
- hidden_in: bfloat16 [64, 512, 768], P(('wide', 'narrow')), may hold values from -6 to 6
- segment_ids: int32 [64, 512], P(('wide', 'narrow')), may hold values from 0 to 7, never falling along the last dimension, each value on 1 to 256 neighbouring positions
- cotangent: bfloat16 [64, 512, 768], P(('wide', 'narrow')), may hold values from -6 to 6
- attention_weights: float32 [4, 768, 768], P(None, 'wide'), may hold values from -1 to 1
- attention_momentum: float32 [4, 768, 768], P(None, 'wide'), may hold values from -32768 to 32768
- attention_average: float32 [4, 768, 768], P(None, 'wide'), may hold values from -0.21875 to 0.21875
- dense_weights: float32 [2, 768, 3072], P(None, 'wide'), may hold values from -0.21875 to 0.21875
- dense_momentum: float32 [2, 768, 3072], P(None, 'wide'), may hold values from -32768 to 32768
- dense_average: float32 [2, 768, 3072], P(None, 'wide'), may hold values from -0.21875 to 0.21875
- vector_params: float32 [12, 768], P(None, 'wide'), may hold values from -2 to 2
- vector_momentum: float32 [12, 768], P(None, 'wide'), may hold values from -32768 to 32768
- vector_average: float32 [12, 768], P(None, 'wide'), may hold values from -2 to 2
Outputs:
- block_output: bfloat16 [64, 512, 768], P(('wide', 'narrow'))
- grad_input: bfloat16 [64, 512, 768], P(('wide', 'narrow'))
- attention_momentum_new: float32 [4, 768, 768], P(None, 'wide')
- attention_weights_new: float32 [4, 768, 768], P(None, 'wide')
- attention_average_new: float32 [4, 768, 768], P(None, 'wide')
- dense_momentum_new: float32 [2, 768, 3072], P(None, 'wide')
- dense_weights_new: float32 [2, 768, 3072], P(None, 'wide')
- dense_average_new: float32 [2, 768, 3072], P(None, 'wide')
- vector_momentum_new: float32 [12, 768], P(None, 'wide')
- vector_params_new: float32 [12, 768], P(None, 'wide')
- vector_average_new: float32 [12, 768], P(None, 'wide')
The draws below stay inside these ranges and needn't reach their ends.
Inputs may be any that keep to these rules, and one draw needn't show every extreme that they name: `segment_ids`: ids never fall along a row; tokens with equal ids in a row form one document or the padding.
All inputs are finite; a program needn't handle non-finite values.
Results may differ from the reference program's by a relative error of at most 0.015.
The reference program's roundings to bfloat16 on the way count: a program that leaves them out, or rounds other values in their place, can miss the bound.
Values may be sent and summed in bfloat16 or wider, within the bound.
A program may use at most 192 MiB of HBM per device.

```python
import math
import jax
import jax.numpy as jnp
import numpy as np
from jax import lax

D = 768
HEAD_DIM = 64
FF = 3072
SEQ = 512
DOCS = 8
ROWS = 64
TOKENS = 32768
N_NARROW = 2


def grad_level():
    return math.sqrt(TOKENS) / N_NARROW


def draw_attention_weights(key, part):
    sample = jax.random.truncated_normal(key, -4.0, 4.0, (4, D, D), jnp.float32)
    factor = jnp.array([1.0, 1.0, 1.0, 4.0], jnp.float32).reshape(4, 1, 1)
    return sample * factor / math.sqrt(D)


def draw_attention_momentum(key, part):
    sample = jax.random.truncated_normal(key, -4.0, 4.0, (4, D, D), jnp.float32)
    return sample * (0.5 * grad_level())


def draw_dense_momentum(key, part):
    sample = jax.random.truncated_normal(key, -4.0, 4.0, (2, D, FF), jnp.float32)
    return sample * (0.5 * grad_level())


def vector_draw(key):
    sample = jax.random.truncated_normal(key, -4.0, 4.0, (8 + FF // D, D), jnp.float32)
    gain_marks = jnp.zeros((8 + FF // D, 1), jnp.float32).at[0].set(1.0).at[2].set(1.0)
    return gain_marks * (1.0 + 0.15 * sample) + (1.0 - gain_marks) * (0.3 * sample)


def draw_vector_params(key, part):
    return vector_draw(jax.random.fold_in(key, 11))


def draw_vector_average(key, part):
    return vector_draw(jax.random.fold_in(key, 23))


def draw_vector_momentum(key, part):
    sample = jax.random.truncated_normal(key, -4.0, 4.0, (8 + FF // D, D), jnp.float32)
    return sample * grad_level()


def steps_of(own_key, extent, shards, low, largest):
    level = 1.0
    for axis_at, shards_of in shards:
        draws = jax.random.uniform(jax.random.fold_in(jax.random.fold_in(own_key, 6), axis_at), (shards_of,), jnp.float32, low / len(shards), largest / len(shards))
        level = level * jnp.repeat(jnp.exp(draws), extent[axis_at] // shards_of).reshape((-1,) + (1,) * (len(extent) - 1 - axis_at))
    return level


def length_profile(amount, total, limit, skew):
    weights = [(1 << 20) // math.isqrt(rank ** skew) + 1 for rank in range(2, amount + 1)]
    surplus, counts = total - limit - (amount - 1), [1] * (amount - 1)
    while surplus > 0:
        free = [i for i in range(amount - 1) if counts[i] < limit]
        mass, budget = sum([weights[i] for i in free]), surplus
        for i in free:
            extra = min(limit - counts[i], max(1, budget * weights[i] // mass), surplus)
            counts[i] = counts[i] + extra
            surplus = surplus - extra
    return np.array([limit] + counts)


def uneven_parts(rng, number_of, total, most, slope):
    if number_of == 2:
        one = jax.random.randint(rng, (), max(1, total - most), min(most, total - 1) + 1)
        return jnp.stack([one, total - one])
    sizes = jnp.asarray(length_profile(number_of, total, most, slope), jnp.int32)
    twos = (number_of - 1) // 2
    giver, taker = sizes[1:1 + 2 * twos:2], sizes[2:2 + 2 * twos:2]
    margin = jnp.minimum(giver - 1, most - taker)
    moved = jax.random.randint(jax.random.fold_in(rng, 1), (twos,), 0, 1 << 20) % (margin + 1)
    sizes = sizes.at[1:1 + 2 * twos:2].set(giver - moved).at[2:2 + 2 * twos:2].set(taker + moved)
    return sizes[jax.random.permutation(jax.random.fold_in(rng, 2), number_of)]


def normal_values(stream_key, shape, scale, most, shards=(), dtype=jnp.bfloat16):
    level = steps_of(stream_key, shape, shards, -0.22, 0.18) if shards else 1.0
    drawn = jax.random.normal(stream_key, shape, jnp.float32) * scale * level
    return jnp.minimum(jnp.maximum(drawn, -most), most).astype(dtype)


def setup_inputs(seed: int = 0) -> dict:
    streams_of = jax.random.split(jax.random.key(seed), 13)
    return {
        "hidden_in": normal_values(streams_of[0], (ROWS, SEQ, D), 1.0, 6.0, ((0, 32),)),
        "segment_ids": jax.vmap(lambda own: jnp.searchsorted(jnp.cumsum(uneven_parts(own, DOCS, SEQ, SEQ // 2, 2)), jnp.arange(SEQ), side="right"))(jax.random.split(streams_of[1], ROWS)).reshape((ROWS, SEQ)).astype(jnp.int32),
        "cotangent": normal_values(streams_of[2], (ROWS, SEQ, D), 1.0, 6.0, ((0, 32),)),
        "attention_weights": draw_attention_weights(jax.random.fold_in(streams_of[12], 71), 0),
        "attention_momentum": draw_attention_momentum(jax.random.fold_in(streams_of[12], 71), 0),
        "attention_average": normal_values(streams_of[5], (4, D, D), D ** -0.5, 0.21875, ((1, 16),), jnp.float32),
        "dense_weights": normal_values(streams_of[6], (2, D, FF), D ** -0.5, 0.21875, ((1, 16),), jnp.float32),
        "dense_momentum": draw_dense_momentum(jax.random.fold_in(streams_of[12], 71), 0),
        "dense_average": normal_values(streams_of[8], (2, D, FF), D ** -0.5, 0.21875, ((1, 16),), jnp.float32),
        "vector_params": draw_vector_params(jax.random.fold_in(streams_of[12], 71), 0),
        "vector_momentum": draw_vector_momentum(jax.random.fold_in(streams_of[12], 71), 0),
        "vector_average": draw_vector_average(jax.random.fold_in(streams_of[12], 71), 0),
    }


epsilon = 1e-12
momentum_decay = 0.5
average_decay = 0.5
matrix_rate = 0.03
vector_rate = 0.3
score_scale = 0.125
masked_score = -1e+30

@jax.custom_vjp
def low(v):
    return lax.optimization_barrier(v.astype(jnp.bfloat16)).astype(jnp.float32)

@jax.custom_vjp
def low_back(v):
    return v

def low_keep(v):
    return (low(v), None)

def low_pass(kept, grad):
    return (grad,)

def back_keep(v):
    return (v, None)

def back_low(kept, grad):
    return (low(grad),)
low.defvjp(low_keep, low_pass)
low_back.defvjp(back_keep, back_low)

def matmul(left_side, right_side):
    return jnp.dot(left_side, right_side, precision=lax.Precision.HIGHEST, preferred_element_type=jnp.float32)

def layer_norm(hidden, gain, offset):
    center = hidden - lax.optimization_barrier(jnp.mean(hidden, -1, keepdims=True))
    variance = lax.optimization_barrier(jnp.mean(center * center, -1, keepdims=True))
    return center * lax.rsqrt(variance + epsilon) * gain + offset

def attend_row(operands):
    queries, key_rows, value_rows, segment = operands
    length = queries.shape[0]
    queries = queries.reshape(length, -1, HEAD_DIM)
    key_rows = key_rows.reshape(length, -1, HEAD_DIM)
    value_rows = value_rows.reshape(length, -1, HEAD_DIM)
    scores = jnp.einsum('qhd,khd->hqk', queries, key_rows, precision=lax.Precision.HIGHEST) * score_scale
    scores = low_back(scores)
    same_doc = segment[:, None] == segment[None, :]
    scores = jnp.where(same_doc[None], scores, masked_score)
    soft_weights = jax.nn.softmax(scores, axis=-1)
    context = jnp.einsum('hqk,khd->qhd', low(soft_weights), value_rows, precision=lax.Precision.HIGHEST)
    return context.reshape(length, -1)

def forward_group(tokens, attention, dense, vectors, segment):
    row_count, length, width = tokens.shape
    flat_in = tokens.reshape(-1, width)
    queries = low_back(low(matmul(flat_in, attention[0]) + vectors[4]))
    key_rows = low_back(low(matmul(flat_in, attention[1])))
    value_rows = low_back(low(matmul(flat_in, attention[2]) + vectors[5]))
    context = lax.map(jax.checkpoint(attend_row), (queries.reshape(row_count, length, width), key_rows.reshape(row_count, length, width), value_rows.reshape(row_count, length, width), segment))
    context = low_back(low(context.reshape(-1, width)))
    branch = low_back(matmul(context, attention[3]) + vectors[6])
    middle = layer_norm(flat_in + branch, vectors[0], vectors[1])
    inner_pre = low_back(matmul(low(middle), dense[0]) + vectors[8:].reshape(-1))
    active = low(jax.nn.gelu(inner_pre, approximate=False))
    second = low_back(matmul(active, dense[1].T) + vectors[7])
    return layer_norm(middle + second, vectors[2], vectors[3]).reshape(tokens.shape)

def advance(gradient, moment, weight, average, step_rate):
    moment_new = momentum_decay * moment + gradient
    weight_new = weight - step_rate * (gradient + momentum_decay * moment_new)
    average_new = average_decay * average + (1.0 - average_decay) * weight_new
    return (moment_new, weight_new, average_new)

def reference(hidden_in, segment_ids, cotangent, attention_weights, attention_momentum, attention_average, dense_weights, dense_momentum, dense_average, vector_params, vector_momentum, vector_average):
    attention_low = attention_weights.astype(jnp.bfloat16).astype(jnp.float32)
    dense_low = dense_weights.astype(jnp.bfloat16).astype(jnp.float32)
    vector_low = vector_params.astype(jnp.bfloat16).astype(jnp.float32)
    width = hidden_in.shape[-1]
    group_count = hidden_in.shape[0] // 8
    inputs = hidden_in.astype(jnp.float32).reshape(group_count, 8, SEQ, width)
    segments = segment_ids.reshape(group_count, 8, SEQ)
    upstreams = cotangent.astype(jnp.float32).reshape(group_count, 8, SEQ, width)

    def one_group(totals, member):
        tokens, segment, upstream = member

        def apply_block(token_vals, attention, dense, vectors):
            return forward_group(token_vals, attention, dense, vectors, segment)
        result, pull_back = jax.vjp(apply_block, tokens, attention_low, dense_low, vector_low)
        grad_tokens, grad_attention, grad_dense, grad_vector = pull_back(upstream)
        totals = (totals[0] + grad_attention, totals[1] + grad_dense, totals[2] + grad_vector)
        return (totals, (result.astype(jnp.bfloat16), grad_tokens.astype(jnp.bfloat16)))
    zero_init = (jnp.zeros_like(attention_low), jnp.zeros_like(dense_low), jnp.zeros_like(vector_low))
    grad_sums, (block_output, grad_input) = lax.scan(one_group, zero_init, (inputs, segments, upstreams))
    grad_scale = math.sqrt(TOKENS) / N_NARROW
    attention_new = advance(grad_sums[0] / N_NARROW, attention_momentum, attention_weights, attention_average, matrix_rate / grad_scale)
    dense_new = advance(grad_sums[1] / N_NARROW, dense_momentum, dense_weights, dense_average, matrix_rate / grad_scale)
    vector_new = advance(grad_sums[2] / N_NARROW, vector_momentum, vector_params, vector_average, vector_rate / grad_scale)
    return (block_output.reshape(hidden_in.shape), grad_input.reshape(hidden_in.shape), attention_new[0], attention_new[1], attention_new[2], dense_new[0], dense_new[1], dense_new[2], vector_new[0], vector_new[1], vector_new[2])
```

```python
import functools, math
import jax, jax.numpy as jnp
from jax import lax
from jax.sharding import PartitionSpec as P
from jax.experimental import pallas as pl
from jax.experimental.pallas import tpu as pltpu

HD = 64
LOG2E = 1.4426950408889634
SCALE2 = 0.125 * LOG2E
NEG = -1e30
EPS = 1e-12
momentum_decay = 0.5
average_decay = 0.5
matrix_rate = 0.03
vector_rate = 0.3
f32, bf16 = jnp.float32, jnp.bfloat16
BIG = 60 * 2**20

def dot(a, b):
    return lax.dot_general(a, b, (((1,), (0,)), ((), ())), preferred_element_type=f32)
def dot_nt(a, b):
    return lax.dot_general(a, b, (((1,), (1,)), ((), ())), preferred_element_type=f32)
def dot_tn(a, b):
    return lax.dot_general(a, b, (((0,), (0,)), ((), ())), preferred_element_type=f32)

def key_range(c, seq, blk):
    lo = max(0, c * blk - seq // 2 + 1) // blk * blk
    hi = min(seq, -(-((c + 1) * blk - 1 + seq // 2) // blk) * blk)
    return lo, hi

def fill_bias(seg_ref, bias_ref):
    segf = seg_ref[0].astype(f32)
    seq = segf.shape[1]
    rep = jnp.broadcast_to(segf, (128, seq)).T
    for j in range(seq // 128):
        bias_ref[:, j * 128:(j + 1) * 128] = jnp.where(rep == segf[:, j * 128:(j + 1) * 128], 0.0, NEG)

def fwd_kernel(blk, x_ref, seg_ref, w_ref, b_ref, qkv_ref, c_ref, lse_ref, bias_ref, lsea_ref):
    seq, width = x_ref.shape
    x = x_ref[...]
    for j in range(3):
        sl = slice(j * width, (j + 1) * width)
        qkv_ref[:, sl] = (dot(x, w_ref[:, sl]) + b_ref[:, sl]).astype(bf16)
    fill_bias(seg_ref, bias_ref)
    lane = lax.broadcasted_iota(jnp.int32, (blk, 128), 1)
    first = lane < HD
    ones = jnp.ones((seq, 128), bf16)
    def pair(p, _):
        col = pl.multiple_of(p * 128, 128)
        q2 = qkv_ref[:, pl.ds(col, 128)]
        k2 = qkv_ref[:, pl.ds(col + width, 128)]
        v2 = jnp.concatenate([qkv_ref[:, pl.ds(col + 2 * width, 128)], ones], 1)
        for c in range(seq // blk):
            lo, hi = key_range(c, seq, blk)
            rows = slice(c * blk, (c + 1) * blk)
            qc = q2[rows]
            outs = []
            la = lsea_ref[rows, :]
            for h in range(2):
                qm = jnp.where(first if h == 0 else ~first, qc, jnp.zeros_like(qc))
                s = dot_nt(qm, k2[lo:hi]) + bias_ref[rows, lo:hi]
                m = jnp.max(s, 1, keepdims=True)
                e = jnp.exp2((s - m) * SCALE2)
                o = dot(e.astype(bf16), v2[lo:hi])
                l = o[:, 128:]
                outs.append(o[:, :128] / l)
                la = jnp.where(lane == 2 * p + h, m * SCALE2 + jnp.log(l) * LOG2E, la)
            lsea_ref[rows, :] = la
            c_ref[rows, pl.ds(col, 128)] = jnp.where(first, outs[0], outs[1]).astype(bf16)
        return 0
    lax.fori_loop(0, width // 128, pair, 0)
    lse_ref[0] = lsea_ref[...].T[:lse_ref.shape[1]]

def attn_fwd(x, seg, w, b, blk=128):
    rows, seq = seg.shape
    width = x.shape[1]
    return pl.pallas_call(
        functools.partial(fwd_kernel, blk), grid=(rows,),
        out_shape=(jax.ShapeDtypeStruct((rows * seq, 3 * width), bf16), jax.ShapeDtypeStruct((rows * seq, width), bf16),
                   jax.ShapeDtypeStruct((rows, 16, seq), f32)),
        in_specs=[pl.BlockSpec((seq, width), lambda r: (r, 0)), pl.BlockSpec((1, 1, seq), lambda r: (r, 0, 0)),
                  pl.BlockSpec((width, 3 * width), lambda r: (0, 0)), pl.BlockSpec((1, 3 * width), lambda r: (0, 0))],
        out_specs=(pl.BlockSpec((seq, 3 * width), lambda r: (r, 0)), pl.BlockSpec((seq, width), lambda r: (r, 0)),
                   pl.BlockSpec((1, 16, seq), lambda r: (r, 0, 0))),
        scratch_shapes=[pltpu.VMEM((seq, seq), f32), pltpu.VMEM((seq, 128), f32)],
        compiler_params=pltpu.CompilerParams(vmem_limit_bytes=BIG),
        name="attn_fwd",
    )(x, seg.reshape(rows, 1, seq), w, b)

def bwd_kernel(blk, seg_ref, qkv_ref, dc_ref, lse_ref, delta_ref, dh1_ref, w_ref, x_ref, dqkv_ref, gin_ref, dw_ref, db_ref, bias_ref, ds_ref, acc_ref):
    r = pl.program_id(0)
    seq = dc_ref.shape[0]
    width = dc_ref.shape[1]
    fill_bias(seg_ref, bias_ref)
    ds_ref[...] = jnp.zeros_like(ds_ref)
    lane = lax.broadcasted_iota(jnp.int32, (blk, 128), 1)
    first = lane < HD
    lane_s = lax.broadcasted_iota(jnp.int32, (seq, 128), 1)
    def pair(p, _):
        col = pl.multiple_of(p * 128, 128)
        q2 = qkv_ref[:, pl.ds(col, 128)]
        k2 = qkv_ref[:, pl.ds(col + width, 128)]
        v2 = qkv_ref[:, pl.ds(col + 2 * width, 128)]
        dc2 = dc_ref[:, pl.ds(col, 128)]
        dqs = []
        for h in range(2):
            lse = lse_ref[0, pl.ds(2 * p + h, 1), :]
            dl = delta_ref[pl.ds(2 * p + h, 1), :]
            mine = first if h == 0 else ~first
            for c in range(seq // blk):
                lo, hi = key_range(c, seq, blk)
                rows = slice(c * blk, (c + 1) * blk)
                kc, vc = k2[rows], v2[rows]
                km = jnp.where(mine, kc, jnp.zeros_like(kc))
                vm = jnp.where(mine, vc, jnp.zeros_like(vc))
                st = dot_nt(km, q2[lo:hi])
                pt = jnp.exp2((st + bias_ref[rows, lo:hi]) * SCALE2 - lse[:, lo:hi])
                dp = dot_nt(vm, dc2[lo:hi])
                ds = (pt * (dp - dl[:, lo:hi])).astype(bf16)
                ds_ref[h, rows, lo:hi] = ds
                dv = dot(pt.astype(bf16), dc2[lo:hi])
                dk = dot(ds, q2[lo:hi]) * 0.125
                if h == 0:
                    dqkv_ref[rows, pl.ds(col + 2 * width, 128)] = dv.astype(bf16)
                    dqkv_ref[rows, pl.ds(col + width, 128)] = dk.astype(bf16)
                else:
                    ov = dqkv_ref[rows, pl.ds(col + 2 * width, 128)]
                    ok = dqkv_ref[rows, pl.ds(col + width, 128)]
                    dqkv_ref[rows, pl.ds(col + 2 * width, 128)] = jnp.where(first, ov, dv.astype(bf16))
                    dqkv_ref[rows, pl.ds(col + width, 128)] = jnp.where(first, ok, dk.astype(bf16))
            dqs.append(dot_tn(ds_ref[h], k2) * 0.125)
        dqkv_ref[:, pl.ds(col, 128)] = jnp.where(lane_s < HD, dqs[0], dqs[1]).astype(bf16)
        return 0
    lax.fori_loop(0, width // 128, pair, 0)
    dqkv = dqkv_ref[...]
    gin_ref[...] = (dh1_ref[...] + dot_nt(dqkv, w_ref[...])).astype(bf16)
    x = x_ref[...]
    for j in range(3):
        sl = slice(j * width, (j + 1) * width)
        d = dot_tn(x, dqkv[:, sl])
        s = jnp.sum(dqkv[:, sl].astype(f32), 0, keepdims=True)
        @pl.when(r == 0)
        def _():
            acc_ref[:, sl] = d
            db_ref[:, sl] = s
        @pl.when(r == pl.num_programs(0) - 1)
        def _():
            dw_ref[:, sl] = (acc_ref[:, sl] + d).astype(bf16)
            db_ref[:, sl] += s

def attn_bwd(seg, qkv, dc, lse, delta, dh1, w, x, blk=128):
    rows, seq = seg.shape
    width = dc.shape[1]
    assert rows == 2
    return pl.pallas_call(
        functools.partial(bwd_kernel, blk), grid=(rows,),
        out_shape=(jax.ShapeDtypeStruct((rows * seq, 3 * width), bf16), jax.ShapeDtypeStruct((rows * seq, width), bf16),
                   jax.ShapeDtypeStruct((width, 3 * width), bf16), jax.ShapeDtypeStruct((1, 3 * width), f32)),
        in_specs=[pl.BlockSpec((1, 1, seq), lambda r: (r, 0, 0)), pl.BlockSpec((seq, 3 * width), lambda r: (r, 0)),
                  pl.BlockSpec((seq, width), lambda r: (r, 0)), pl.BlockSpec((1, 16, seq), lambda r: (r, 0, 0)),
                  pl.BlockSpec((16, seq), lambda r: (0, r)), pl.BlockSpec((seq, width), lambda r: (r, 0)),
                  pl.BlockSpec((width, 3 * width), lambda r: (0, 0)), pl.BlockSpec((seq, width), lambda r: (r, 0))],
        out_specs=(pl.BlockSpec((seq, 3 * width), lambda r: (r, 0)), pl.BlockSpec((seq, width), lambda r: (r, 0)),
                   pl.BlockSpec((width, 3 * width), lambda r: (0, 0)), pl.BlockSpec((1, 3 * width), lambda r: (0, 0))),
        scratch_shapes=[pltpu.VMEM((seq, seq), f32), pltpu.VMEM((2, seq, seq), bf16), pltpu.VMEM((width, 3 * width), f32)],
        compiler_params=pltpu.CompilerParams(vmem_limit_bytes=BIG),
        name="attn_bwd",
    )(seg.reshape(rows, 1, seq), qkv, dc, lse, delta, dh1, w, x)

RSQRT_2PI = 1.0 / math.sqrt(2 * math.pi)
def gelu_parts(u):
    phi_cdf = 0.5 + 0.5 * lax.erf(u * math.sqrt(0.5))
    dens = jnp.exp2(u * u * (-0.5 * LOG2E)) * RSQRT_2PI
    return u * phi_cdf, phi_cdf + u * dens

def mid_kernel(chunk, x_ref, c_ref, e_ref, wo_ref, win_ref, wd_ref, v_ref, bin_ref,
               out_ref, y1_ref, g_ref, dz_ref, du_ref, da_ref, dc_ref, dh1_ref, delta_ref, dv_ref, dbin_ref, gp_ref):
    i = pl.program_id(0)
    blk, width = x_ref.shape
    ff = win_ref.shape[1]
    @pl.when(i == 0)
    def _():
        dv_ref[...] = jnp.zeros_like(dv_ref)
        dbin_ref[...] = jnp.zeros_like(dbin_ref)
    g1, s1, g2, s2, bo, bd = (v_ref[j:j + 1, :] for j in (0, 1, 2, 3, 6, 7))
    cb = c_ref[...]
    h1 = x_ref[...].astype(f32) + (dot(cb, wo_ref[...]) + bo)
    cen = h1 - jnp.mean(h1, 1, keepdims=True)
    r1 = lax.rsqrt(jnp.mean(cen * cen, 1, keepdims=True) + EPS)
    n1 = cen * r1
    y1 = n1 * g1 + s1
    y1l = y1.astype(bf16)
    y1_ref[...] = y1l
    z = jnp.zeros((blk, width), f32)
    for j in range(ff // chunk):
        sl = slice(j * chunk, (j + 1) * chunk)
        u = dot(y1l, win_ref[:, sl]) + bin_ref[:, sl]
        g, gp = gelu_parts(u)
        gl = g.astype(bf16)
        g_ref[:, sl] = gl
        gp_ref[:, sl] = gp
        z += dot_nt(gl, wd_ref[:, sl])
    h2 = y1 + (z + bd)
    cen = h2 - jnp.mean(h2, 1, keepdims=True)
    r2 = lax.rsqrt(jnp.mean(cen * cen, 1, keepdims=True) + EPS)
    n2 = cen * r2
    out_ref[...] = (n2 * g2 + s2).astype(bf16)
    e = e_ref[...].astype(f32)
    eg = e * g2
    dh2 = r2 * (eg - jnp.mean(eg, 1, keepdims=True) - n2 * jnp.mean(eg * n2, 1, keepdims=True))
    dz = dh2.astype(bf16)
    dz_ref[...] = dz
    dy1 = dh2
    for j in range(ff // chunk):
        sl = slice(j * chunk, (j + 1) * chunk)
        du = (dot(dz, wd_ref[:, sl]) * gp_ref[:, sl]).astype(bf16)
        du_ref[:, sl] = du
        dbin_ref[:, sl] += jnp.sum(du.astype(f32), 0, keepdims=True)
        dy1 += dot_nt(du, win_ref[:, sl])
    dn = dy1 * g1
    dh1 = r1 * (dn - jnp.mean(dn, 1, keepdims=True) - n1 * jnp.mean(dn * n1, 1, keepdims=True))
    dh1_ref[...] = dh1
    da = dh1.astype(bf16)
    da_ref[...] = da
    dc = dot_nt(da, wo_ref[...]).astype(bf16)
    dc_ref[...] = dc
    prod = dc.astype(f32) * cb.astype(f32)
    hi = prod.astype(bf16)
    lo = (prod - hi.astype(f32)).astype(bf16)
    sel = jnp.where(lax.broadcasted_iota(jnp.int32, (16, width), 0) == lax.broadcasted_iota(jnp.int32, (16, width), 1) // HD, 1.0, 0.0).astype(bf16)
    delta_ref[...] = dot_nt(sel, hi) + dot_nt(sel, lo)
    parts = [dy1 * n1, dy1, e * n2, e, da.astype(f32), dz.astype(f32)]
    for j, t in zip((0, 1, 2, 3, 6, 7), parts):
        dv_ref[j:j + 1, :] += jnp.sum(t, 0, keepdims=True)

def mid(x, c, e, wo, win, wd, vec, bin_, blk=256, chunk=768):
    n, width = x.shape
    ff = win.shape[1]
    tok = lambda w: pl.BlockSpec((blk, w), lambda i: (i, 0))
    full = lambda a: pl.BlockSpec(a.shape, lambda i: (0, 0), pipeline_mode=pl.Buffered(1))
    sh = jax.ShapeDtypeStruct
    return pl.pallas_call(
        functools.partial(mid_kernel, chunk), grid=(n // blk,),
        out_shape=(sh((n, width), bf16), sh((n, width), bf16), sh((n, ff), bf16), sh((n, width), bf16), sh((n, ff), bf16),
                   sh((n, width), bf16), sh((n, width), bf16), sh((n, width), f32), sh((16, n), f32), sh((8, width), f32), sh((1, ff), f32)),
        in_specs=[tok(width), tok(width), tok(width), full(wo), full(win), full(wd), full(vec), full(bin_)],
        out_specs=(tok(width), tok(width), tok(ff), tok(width), tok(ff), tok(width), tok(width), tok(width),
                   pl.BlockSpec((16, blk), lambda i: (0, i)), pl.BlockSpec((8, width), lambda i: (0, 0)), pl.BlockSpec((1, ff), lambda i: (0, 0))),
        scratch_shapes=[pltpu.VMEM((blk, ff), f32)],
        compiler_params=pltpu.CompilerParams(vmem_limit_bytes=BIG),
        name="middle",
    )(x, c, e, wo, win, wd, vec, bin_)

def wgrad_kernel(a_ref, b_ref, o_ref):
    o_ref[...] = dot_tn(a_ref[...], b_ref[...]).astype(bf16)

def wgrad(a, b, blk=768):
    n, m = a.shape
    k = b.shape[1]
    return pl.pallas_call(wgrad_kernel, grid=(k // blk,), out_shape=jax.ShapeDtypeStruct((m, k), bf16),
        in_specs=[pl.BlockSpec((n, m), lambda j: (0, 0)), pl.BlockSpec((n, blk), lambda j: (0, j))],
        out_specs=pl.BlockSpec((m, blk), lambda j: (0, j)),
        compiler_params=pltpu.CompilerParams(vmem_limit_bytes=BIG), name="wgrad")(a, b)


def pack_columns(attention, dense, vectors):
    count = vectors.shape[0]
    vector_cols = jnp.pad(vectors.T, ((0, 0), (0, 128 - count)))
    first = jnp.concatenate([attention[0], attention[1], attention[2], vector_cols], 1)
    second = jnp.concatenate([attention[3], dense[0], dense[1]], 1)
    return first, second


def advance(gradient, moment, weight, average, step_rate):
    moment_new = momentum_decay * moment + gradient
    weight_new = weight - step_rate * (gradient + momentum_decay * moment_new)
    average_new = average_decay * average + (1.0 - average_decay) * weight_new
    return (moment_new, weight_new, average_new)


def body(
    hidden_in,
    segment_ids,
    cotangent,
    attention_weights,
    attention_momentum,
    attention_average,
    dense_weights,
    dense_momentum,
    dense_average,
    vector_params,
    vector_momentum,
    vector_average,
):
    row_count, length, width = hidden_in.shape
    ff = dense_weights.shape[-1]
    vector_rows = vector_params.shape[0]
    x = hidden_in.reshape(-1, width)
    e = cotangent.reshape(-1, width)
    first, second = pack_columns(attention_weights, dense_weights, vector_params)
    first_full = lax.all_gather(first.astype(bf16), "wide", axis=0, tiled=True)
    second_full = lax.all_gather(second.astype(bf16), "wide", axis=0, tiled=True)
    vec = first_full[:, 3 * width : 3 * width + vector_rows].astype(f32).T
    bias_qkv = jnp.concatenate([vec[4:5], jnp.zeros((1, width), f32), vec[5:6]], 1)
    w_qkv = first_full[:, : 3 * width]
    wo, win, wd = (second_full[:, :width], second_full[:, width : width + ff], second_full[:, width + ff :])
    qkv, c, lse = attn_fwd(x, segment_ids, w_qkv, bias_qkv)
    out, y1, g, dz, du, da, dc, dh1, delta, dvec, dbin = mid(
        x, c, e, wo, win, wd, vec, vec[8:].reshape(1, ff)
    )
    grad_second = jnp.concatenate([wgrad(c, da), wgrad(y1, du), wgrad(dz, g)], 1)
    share_second = lax.psum_scatter(grad_second, "wide", scatter_dimension=0, tiled=True)
    dqkv, gin, dw, db = attn_bwd(segment_ids, qkv, dc, lse, delta, dh1, w_qkv, x)
    dvec = jnp.concatenate(
        [dvec[:4], db[:, :width], db[:, 2 * width :], dvec[6:8], dbin.reshape(-1, width)], 0
    )
    grad_first = jnp.concatenate(
        [dw, jnp.pad(dvec.T, ((0, 0), (0, 128 - vector_rows))).astype(bf16)], 1
    )
    share_first = lax.psum_scatter(grad_first, "wide", scatter_dimension=0, tiled=True)
    replicas = lax.axis_size("narrow")
    tokens_all = row_count * length * lax.axis_size("wide") * replicas
    grad_scale = math.sqrt(tokens_all) / replicas
    t1 = lax.psum(share_first, "narrow").astype(f32) / replicas
    t2 = lax.psum(share_second, "narrow").astype(f32) / replicas
    cut = lambda t, j: t[:, j * width : (j + 1) * width]
    attention_grad = jnp.stack([cut(t1, 0), cut(t1, 1), cut(t1, 2), cut(t2, 0)])
    dense_grad = jnp.stack([t2[:, width : width + ff], t2[:, width + ff :]])
    vector_grad = t1[:, 3 * width : 3 * width + vector_rows].T
    attention_new = advance(attention_grad, attention_momentum, attention_weights, attention_average, matrix_rate / grad_scale)
    dense_new = advance(dense_grad, dense_momentum, dense_weights, dense_average, matrix_rate / grad_scale)
    vector_new = advance(vector_grad, vector_momentum, vector_params, vector_average, vector_rate / grad_scale)
    return (out.reshape(hidden_in.shape), gin.reshape(hidden_in.shape)) + attention_new + dense_new + vector_new


def solution(mesh):
    token = P(("wide", "narrow"), None, None)
    matrix = P(None, "wide", None)
    vector = P(None, "wide")
    in_specs = (token, P(("wide", "narrow"), None), token) + (matrix,) * 6 + (vector,) * 3
    out_specs = (token, token) + (matrix,) * 6 + (vector,) * 3
    return jax.shard_map(body, mesh=mesh, in_specs=in_specs, out_specs=out_specs, check_vma=False)
```

```python
import functools, math
import jax, jax.numpy as jnp
from jax import lax
from jax.sharding import PartitionSpec as P
from jax.experimental import pallas as pl
from jax.experimental.pallas import tpu as pltpu

HD = 64
LOG2E = 1.4426950408889634
SCALE2 = 0.125 * LOG2E
NEG = -1e30
EPS = 1e-12
momentum_decay = 0.5
average_decay = 0.5
matrix_rate = 0.03
vector_rate = 0.3
f32, bf16 = jnp.float32, jnp.bfloat16
BIG = 60 * 2**20

def dot(a, b):
    return lax.dot_general(a, b, (((1,), (0,)), ((), ())), preferred_element_type=f32)
def dot_nt(a, b):
    return lax.dot_general(a, b, (((1,), (1,)), ((), ())), preferred_element_type=f32)
def dot_tn(a, b):
    return lax.dot_general(a, b, (((0,), (0,)), ((), ())), preferred_element_type=f32)

def key_range(c, seq, blk):
    lo = max(0, c * blk - seq // 2 + 1) // blk * blk
    hi = min(seq, -(-((c + 1) * blk - 1 + seq // 2) // blk) * blk)
    return lo, hi

def fill_bias(seg_ref, bias_ref):
    segf = seg_ref[0].astype(f32)
    seq = segf.shape[1]
    rep = jnp.broadcast_to(segf, (128, seq)).T
    for j in range(seq // 128):
        bias_ref[:, j * 128:(j + 1) * 128] = jnp.where(rep == segf[:, j * 128:(j + 1) * 128], 0.0, NEG)

def fwd_kernel(blk, x_ref, seg_ref, w_ref, b_ref, qkv_ref, c_ref, lse_ref, bias_ref, lsea_ref):
    seq, width = x_ref.shape
    x = x_ref[...]
    for j in range(3):
        sl = slice(j * width, (j + 1) * width)
        qkv_ref[:, sl] = (dot(x, w_ref[:, sl]) + b_ref[:, sl]).astype(bf16)
    fill_bias(seg_ref, bias_ref)
    lane = lax.broadcasted_iota(jnp.int32, (blk, 128), 1)
    first = lane < HD
    ones = jnp.ones((seq, 128), bf16)
    def pair(p, _):
        col = pl.multiple_of(p * 128, 128)
        q2 = qkv_ref[:, pl.ds(col, 128)]
        k2 = qkv_ref[:, pl.ds(col + width, 128)]
        v2 = jnp.concatenate([qkv_ref[:, pl.ds(col + 2 * width, 128)], ones], 1)
        for c in range(seq // blk):
            lo, hi = key_range(c, seq, blk)
            rows = slice(c * blk, (c + 1) * blk)
            qc = q2[rows]
            outs = []
            la = lsea_ref[rows, :]
            for h in range(2):
                qm = jnp.where(first if h == 0 else ~first, qc, jnp.zeros_like(qc))
                s = dot_nt(qm, k2[lo:hi]) + bias_ref[rows, lo:hi]
                m = jnp.max(s, 1, keepdims=True)
                e = jnp.exp2((s - m) * SCALE2)
                o = dot(e.astype(bf16), v2[lo:hi])
                l = o[:, 128:]
                outs.append(o[:, :128] / l)
                la = jnp.where(lane == 2 * p + h, m * SCALE2 + jnp.log(l) * LOG2E, la)
            lsea_ref[rows, :] = la
            c_ref[rows, pl.ds(col, 128)] = jnp.where(first, outs[0], outs[1]).astype(bf16)
        return 0
    lax.fori_loop(0, width // 128, pair, 0)
    lse_ref[0] = lsea_ref[...].T[:lse_ref.shape[1]]

def attn_fwd(x, seg, w, b, blk=128):
    rows, seq = seg.shape
    width = x.shape[1]
    return pl.pallas_call(
        functools.partial(fwd_kernel, blk), grid=(rows,),
        out_shape=(jax.ShapeDtypeStruct((rows * seq, 3 * width), bf16), jax.ShapeDtypeStruct((rows * seq, width), bf16),
                   jax.ShapeDtypeStruct((rows, 16, seq), f32)),
        in_specs=[pl.BlockSpec((seq, width), lambda r: (r, 0)), pl.BlockSpec((1, 1, seq), lambda r: (r, 0, 0)),
                  pl.BlockSpec((width, 3 * width), lambda r: (0, 0)), pl.BlockSpec((1, 3 * width), lambda r: (0, 0))],
        out_specs=(pl.BlockSpec((seq, 3 * width), lambda r: (r, 0)), pl.BlockSpec((seq, width), lambda r: (r, 0)),
                   pl.BlockSpec((1, 16, seq), lambda r: (r, 0, 0))),
        scratch_shapes=[pltpu.VMEM((seq, seq), f32), pltpu.VMEM((seq, 128), f32)],
        compiler_params=pltpu.CompilerParams(vmem_limit_bytes=BIG),
        name="attn_fwd",
    )(x, seg.reshape(rows, 1, seq), w, b)

def bwd_kernel(blk, seg_ref, qkv_ref, dc_ref, lse_ref, delta_ref, dh1_ref, w_ref, x_ref, dqkv_ref, gin_ref, dw_ref, db_ref, bias_ref, ds_ref, acc_ref):
    r = pl.program_id(0)
    seq = dc_ref.shape[0]
    width = dc_ref.shape[1]
    fill_bias(seg_ref, bias_ref)
    ds_ref[...] = jnp.zeros_like(ds_ref)
    lane = lax.broadcasted_iota(jnp.int32, (blk, 128), 1)
    first = lane < HD
    lane_s = lax.broadcasted_iota(jnp.int32, (seq, 128), 1)
    def pair(p, _):
        col = pl.multiple_of(p * 128, 128)
        q2 = qkv_ref[:, pl.ds(col, 128)]
        k2 = qkv_ref[:, pl.ds(col + width, 128)]
        v2 = qkv_ref[:, pl.ds(col + 2 * width, 128)]
        dc2 = dc_ref[:, pl.ds(col, 128)]
        dqs = []
        for h in range(2):
            lse = lse_ref[0, pl.ds(2 * p + h, 1), :]
            dl = delta_ref[pl.ds(2 * p + h, 1), :]
            mine = first if h == 0 else ~first
            for c in range(seq // blk):
                lo, hi = key_range(c, seq, blk)
                rows = slice(c * blk, (c + 1) * blk)
                kc, vc = k2[rows], v2[rows]
                km = jnp.where(mine, kc, jnp.zeros_like(kc))
                vm = jnp.where(mine, vc, jnp.zeros_like(vc))
                st = dot_nt(km, q2[lo:hi])
                pt = jnp.exp2((st + bias_ref[rows, lo:hi]) * SCALE2 - lse[:, lo:hi])
                dp = dot_nt(vm, dc2[lo:hi])
                ds = (pt * (dp - dl[:, lo:hi])).astype(bf16)
                ds_ref[h, rows, lo:hi] = ds
                dv = dot(pt.astype(bf16), dc2[lo:hi])
                dk = dot(ds, q2[lo:hi]) * 0.125
                if h == 0:
                    dqkv_ref[rows, pl.ds(col + 2 * width, 128)] = dv.astype(bf16)
                    dqkv_ref[rows, pl.ds(col + width, 128)] = dk.astype(bf16)
                else:
                    ov = dqkv_ref[rows, pl.ds(col + 2 * width, 128)]
                    ok = dqkv_ref[rows, pl.ds(col + width, 128)]
                    dqkv_ref[rows, pl.ds(col + 2 * width, 128)] = jnp.where(first, ov, dv.astype(bf16))
                    dqkv_ref[rows, pl.ds(col + width, 128)] = jnp.where(first, ok, dk.astype(bf16))
            dqs.append(dot_tn(ds_ref[h], k2) * 0.125)
        dqkv_ref[:, pl.ds(col, 128)] = jnp.where(lane_s < HD, dqs[0], dqs[1]).astype(bf16)
        return 0
    lax.fori_loop(0, width // 128, pair, 0)
    dqkv = dqkv_ref[...]
    gin_ref[...] = (dh1_ref[...] + dot_nt(dqkv, w_ref[...])).astype(bf16)
    x = x_ref[...]
    for j in range(3):
        sl = slice(j * width, (j + 1) * width)
        d = dot_tn(x, dqkv[:, sl])
        s = jnp.sum(dqkv[:, sl].astype(f32), 0, keepdims=True)
        @pl.when(r == 0)
        def _():
            acc_ref[:, sl] = d
            db_ref[:, sl] = s
        @pl.when(r == pl.num_programs(0) - 1)
        def _():
            dw_ref[:, sl] = (acc_ref[:, sl] + d).astype(bf16)
            db_ref[:, sl] += s

def attn_bwd(seg, qkv, dc, lse, delta, dh1, w, x, blk=128):
    rows, seq = seg.shape
    width = dc.shape[1]
    assert rows == 2
    return pl.pallas_call(
        functools.partial(bwd_kernel, blk), grid=(rows,),
        out_shape=(jax.ShapeDtypeStruct((rows * seq, 3 * width), bf16), jax.ShapeDtypeStruct((rows * seq, width), bf16),
                   jax.ShapeDtypeStruct((width, 3 * width), bf16), jax.ShapeDtypeStruct((1, 3 * width), f32)),
        in_specs=[pl.BlockSpec((1, 1, seq), lambda r: (r, 0, 0)), pl.BlockSpec((seq, 3 * width), lambda r: (r, 0)),
                  pl.BlockSpec((seq, width), lambda r: (r, 0)), pl.BlockSpec((1, 16, seq), lambda r: (r, 0, 0)),
                  pl.BlockSpec((16, seq), lambda r: (0, r)), pl.BlockSpec((seq, width), lambda r: (r, 0)),
                  pl.BlockSpec((width, 3 * width), lambda r: (0, 0)), pl.BlockSpec((seq, width), lambda r: (r, 0))],
        out_specs=(pl.BlockSpec((seq, 3 * width), lambda r: (r, 0)), pl.BlockSpec((seq, width), lambda r: (r, 0)),
                   pl.BlockSpec((width, 3 * width), lambda r: (0, 0)), pl.BlockSpec((1, 3 * width), lambda r: (0, 0))),
        scratch_shapes=[pltpu.VMEM((seq, seq), f32), pltpu.VMEM((2, seq, seq), bf16), pltpu.VMEM((width, 3 * width), f32)],
        compiler_params=pltpu.CompilerParams(vmem_limit_bytes=BIG),
        name="attn_bwd",
    )(seg.reshape(rows, 1, seq), qkv, dc, lse, delta, dh1, w, x)

RSQRT_2PI = 1.0 / math.sqrt(2 * math.pi)
def gelu_parts(u):
    phi_cdf = 0.5 + 0.5 * lax.erf(u * math.sqrt(0.5))
    dens = jnp.exp2(u * u * (-0.5 * LOG2E)) * RSQRT_2PI
    return u * phi_cdf, phi_cdf + u * dens

def mid_kernel(chunk, x_ref, c_ref, e_ref, wo_ref, win_ref, wd_ref, v_ref, bin_ref,
               out_ref, y1_ref, g_ref, dz_ref, du_ref, da_ref, dc_ref, dh1_ref, delta_ref, dv_ref, dbin_ref, gp_ref):
    i = pl.program_id(0)
    blk, width = x_ref.shape
    ff = win_ref.shape[1]
    @pl.when(i == 0)
    def _():
        dv_ref[...] = jnp.zeros_like(dv_ref)
        dbin_ref[...] = jnp.zeros_like(dbin_ref)
    g1, s1, g2, s2, bo, bd = (v_ref[j:j + 1, :] for j in (0, 1, 2, 3, 6, 7))
    cb = c_ref[...]
    h1 = x_ref[...].astype(f32) + (dot(cb, wo_ref[...]) + bo)
    cen = h1 - jnp.mean(h1, 1, keepdims=True)
    r1 = lax.rsqrt(jnp.mean(cen * cen, 1, keepdims=True) + EPS)
    n1 = cen * r1
    y1 = n1 * g1 + s1
    y1l = y1.astype(bf16)
    y1_ref[...] = y1l
    z = jnp.zeros((blk, width), f32)
    for j in range(ff // chunk):
        sl = slice(j * chunk, (j + 1) * chunk)
        u = dot(y1l, win_ref[:, sl]) + bin_ref[:, sl]
        g, gp = gelu_parts(u)
        gl = g.astype(bf16)
        g_ref[:, sl] = gl
        gp_ref[:, sl] = gp
        z += dot_nt(gl, wd_ref[:, sl])
    h2 = y1 + (z + bd)
    cen = h2 - jnp.mean(h2, 1, keepdims=True)
    r2 = lax.rsqrt(jnp.mean(cen * cen, 1, keepdims=True) + EPS)
    n2 = cen * r2
    out_ref[...] = (n2 * g2 + s2).astype(bf16)
    e = e_ref[...].astype(f32)
    eg = e * g2
    dh2 = r2 * (eg - jnp.mean(eg, 1, keepdims=True) - n2 * jnp.mean(eg * n2, 1, keepdims=True))
    dz = dh2.astype(bf16)
    dz_ref[...] = dz
    dy1 = dh2
    for j in range(ff // chunk):
        sl = slice(j * chunk, (j + 1) * chunk)
        du = (dot(dz, wd_ref[:, sl]) * gp_ref[:, sl]).astype(bf16)
        du_ref[:, sl] = du
        dbin_ref[:, sl] += jnp.sum(du.astype(f32), 0, keepdims=True)
        dy1 += dot_nt(du, win_ref[:, sl])
    dn = dy1 * g1
    dh1 = r1 * (dn - jnp.mean(dn, 1, keepdims=True) - n1 * jnp.mean(dn * n1, 1, keepdims=True))
    dh1_ref[...] = dh1
    da = dh1.astype(bf16)
    da_ref[...] = da
    dc = dot_nt(da, wo_ref[...]).astype(bf16)
    dc_ref[...] = dc
    prod = dc.astype(f32) * cb.astype(f32)
    hi = prod.astype(bf16)
    lo = (prod - hi.astype(f32)).astype(bf16)
    sel = jnp.where(lax.broadcasted_iota(jnp.int32, (16, width), 0) == lax.broadcasted_iota(jnp.int32, (16, width), 1) // HD, 1.0, 0.0).astype(bf16)
    delta_ref[...] = dot_nt(sel, hi) + dot_nt(sel, lo)
    parts = [dy1 * n1, dy1, e * n2, e, da.astype(f32), dz.astype(f32)]
    for j, t in zip((0, 1, 2, 3, 6, 7), parts):
        dv_ref[j:j + 1, :] += jnp.sum(t, 0, keepdims=True)

def mid(x, c, e, wo, win, wd, vec, bin_, blk=256, chunk=768):
    n, width = x.shape
    ff = win.shape[1]
    tok = lambda w: pl.BlockSpec((blk, w), lambda i: (i, 0))
    full = lambda a: pl.BlockSpec(a.shape, lambda i: (0, 0), pipeline_mode=pl.Buffered(1))
    sh = jax.ShapeDtypeStruct
    return pl.pallas_call(
        functools.partial(mid_kernel, chunk), grid=(n // blk,),
        out_shape=(sh((n, width), bf16), sh((n, width), bf16), sh((n, ff), bf16), sh((n, width), bf16), sh((n, ff), bf16),
                   sh((n, width), bf16), sh((n, width), bf16), sh((n, width), f32), sh((16, n), f32), sh((8, width), f32), sh((1, ff), f32)),
        in_specs=[tok(width), tok(width), tok(width), full(wo), full(win), full(wd), full(vec), full(bin_)],
        out_specs=(tok(width), tok(width), tok(ff), tok(width), tok(ff), tok(width), tok(width), tok(width),
                   pl.BlockSpec((16, blk), lambda i: (0, i)), pl.BlockSpec((8, width), lambda i: (0, 0)), pl.BlockSpec((1, ff), lambda i: (0, 0))),
        scratch_shapes=[pltpu.VMEM((blk, ff), f32)],
        compiler_params=pltpu.CompilerParams(vmem_limit_bytes=BIG),
        name="middle",
    )(x, c, e, wo, win, wd, vec, bin_)

def wgrad_kernel(a_ref, b_ref, o_ref):
    o_ref[...] = dot_tn(a_ref[...], b_ref[...]).astype(bf16)

def wgrad(a, b, blk=768):
    n, m = a.shape
    k = b.shape[1]
    return pl.pallas_call(wgrad_kernel, grid=(k // blk,), out_shape=jax.ShapeDtypeStruct((m, k), bf16),
        in_specs=[pl.BlockSpec((n, m), lambda j: (0, 0)), pl.BlockSpec((n, blk), lambda j: (0, j))],
        out_specs=pl.BlockSpec((m, blk), lambda j: (0, j)),
        compiler_params=pltpu.CompilerParams(vmem_limit_bytes=BIG), name="wgrad")(a, b)


MESH = pl.DeviceIdType.MESH
LANES = 128
PIECE = 3 * LANES
LAG = 2
AHEAD = 8


class Place:
    def __init__(self):
        self.w = lax.axis_index("wide")
        self.x = lax.axis_index("narrow")
        self.core = lax.rem(self.w, 2)
        self.y = lax.rem(self.w // 2, 2)
        self.z = self.w // 4

    def at(self, z=None, y=None, core=None):
        z, y, core = (mine if v is None else v for v, mine in ((z, self.z), (y, self.y), (core, self.core)))
        return (4 * z + 2 * y + core, self.x)

    def z_peer(self, k):
        return lax.rem(self.z + k, 4)

    def greet(self):
        barrier = pltpu.get_barrier_semaphore()
        peers = [self.at(z=self.z_peer(k)) for k in (1, 2, 3)]
        peers += [self.at(y=1 - self.y), self.at(core=1 - self.core), (self.w, 1 - self.x)]
        for peer in peers:
            pl.semaphore_signal(barrier, inc=1, device_id=peer, device_id_type=MESH)
        pl.semaphore_wait(barrier, len(peers))


def remote(src, dst, send, recv, device):
    return pltpu.make_async_remote_copy(src_ref=src, dst_ref=dst, send_sem=send, recv_sem=recv, device_id=device, device_id_type=MESH)


def window(col, size):
    return pl.ds(pl.multiple_of(col, LANES), size)


class Gather:
    def __init__(self, place, shard, full, sems):
        self.p, self.shard, self.full = place, shard, full
        self.zs, self.zr, self.ys, self.yr, self.xs, self.xr, self.cs, self.cr = sems

    def own(self, i, col, vec):
        return window(col, LANES) if vec else window(col + self.p.x * LANES, 2 * LANES)

    def split(self, col, x):
        return window(col + 2 * LANES * x, LANES)

    def z_copy(self, i, col, vec, k):
        p = self.p
        cols = self.own(i, col, vec)
        return remote(self.shard.at[:, cols], self.full.at[p.z, p.y, p.core, :, cols], self.zs.at[i, k], self.zr.at[i, p.z], p.at(z=p.z_peer(k)))

    def z_arrival(self, i, col, vec, k):
        p = self.p
        cols = self.own(i, col, vec)
        src = p.z_peer(k)
        return remote(self.shard.at[:, cols], self.full.at[src, p.y, p.core, :, cols], self.zs.at[i, k], self.zr.at[i, src], p.at(z=src))

    def y_copy(self, i, col, vec, incoming):
        p = self.p
        part = self.full.at[:, 1 - p.y if incoming else p.y, p.core, :, self.own(i, col, vec)]
        return remote(part, part, self.ys.at[i], self.yr.at[i], p.at(y=1 - p.y))

    def x_copy(self, i, col, incoming):
        p = self.p
        part = self.full.at[:, :, p.core, :, self.split(col, 1 - p.x if incoming else p.x)]
        return remote(part, part, self.xs.at[i], self.xr.at[i], (p.w, 1 - p.x))

    def core_copy(self, i, col, vec, incoming):
        p = self.p
        part = self.full.at[:, :, 1 - p.core if incoming else p.core, :, window(col, LANES if vec else PIECE)]
        return remote(part, part, self.cs.at[i], self.cr.at[i], p.at(core=1 - p.core))

    def z_start(self, i, col, vec=False):
        for k in (2, 1, 3):
            self.z_copy(i, col, vec, k).start()

    def y_step(self, i, col, vec=False):
        for k in (1, 2, 3):
            self.z_arrival(i, col, vec, k).wait_recv()
        self.y_copy(i, col, vec, False).start()

    def x_step(self, i, col, vec=False):
        self.y_copy(i, col, vec, True).wait_recv()
        if not vec:
            self.x_copy(i, col, False).start()

    def core_step(self, i, col, vec=False):
        if not vec:
            self.x_copy(i, col, True).wait_recv()
        self.core_copy(i, col, vec, False).start()

    def arrive(self, i, col, vec=False):
        self.core_copy(i, col, vec, True).wait_recv()

    def sent(self, i, col, vec=False):
        for k in (1, 2, 3):
            self.z_copy(i, col, vec, k).wait_send()
        self.y_copy(i, col, vec, False).wait_send()
        if not vec:
            self.x_copy(i, col, False).wait_send()
        self.core_copy(i, col, vec, False).wait_send()


def gather_sems(pieces):
    dma = pltpu.SemaphoreType.DMA
    return [dma((pieces, 4)), dma((pieces, 4))] + [dma((pieces,))] * 6


def gather_kernel(shard, full, own_sem, *sems):
    place = Place()
    total = shard.shape[1] // PIECE
    vec_col = total * PIECE
    g = Gather(place, shard, full, sems)

    def keep(i, col, vec=False):
        cols = g.own(i, col, vec)
        return pltpu.make_async_copy(shard.at[:, cols], full.at[place.z, place.y, place.core, :, cols], own_sem.at[i])

    lax.fori_loop(0, total, lambda i, _: (keep(i, i * PIECE).start(), 0)[1], 0)
    keep(total, vec_col, True).start()
    place.greet()
    g.z_start(total, vec_col, True)

    def each(step):
        lax.fori_loop(0, total, lambda i, _: (step(i, i * PIECE), 0)[1], 0)

    each(g.z_start)
    lax.fori_loop(0, total, lambda i, _: (keep(i, i * PIECE).wait(), 0)[1], 0)
    keep(total, vec_col, True).wait()
    g.y_step(total, vec_col, True)

    def turn(i, _):
        def at(lag, step):
            @pl.when((i >= lag) & (i < total + lag))
            def _():
                step(i - lag, (i - lag) * PIECE)

        at(0, g.y_step)
        at(LAG, g.x_step)
        at(2 * LAG, g.core_step)
        return 0

    lax.fori_loop(0, total + 2 * LAG, turn, 0)
    g.x_step(total, vec_col, True)
    g.core_step(total, vec_col, True)
    each(g.arrive)
    g.arrive(total, vec_col, True)
    each(g.sent)
    g.sent(total, vec_col, True)


def gather_all(shard):
    rows, cols = shard.shape
    total = cols // PIECE
    assert cols == total * PIECE + LANES
    full = pl.pallas_call(
        gather_kernel,
        out_shape=jax.ShapeDtypeStruct((4, 2, 2, rows, cols), bf16),
        in_specs=[pl.BlockSpec(memory_space=pl.ANY)],
        out_specs=pl.BlockSpec(memory_space=pl.ANY),
        scratch_shapes=[pltpu.SemaphoreType.DMA((total + 1,))] + gather_sems(total + 1),
        compiler_params=pltpu.CompilerParams(collective_id=0, has_side_effects=True),
        name="gather",
    )(shard)
    return full.reshape(16 * rows, cols)


class Reduce:
    def __init__(self, place, part, own, fromc, fromx, fromy, fromz, fromp, done, sems):
        self.p, self.part, self.own = place, part, own
        self.fromc, self.fromx, self.fromy, self.fromz, self.fromp, self.done = fromc, fromx, fromy, fromz, fromp, done
        self.ls, self.cs, self.cr, self.xs, self.xr, self.ys, self.yr, self.zs, self.zr, self.ps, self.pr = sems

    def local(self, i, col):
        return pltpu.make_async_copy(self.part.at[:, :, self.p.core, :, window(col, PIECE)], self.own.at[i], self.ls.at[i])

    def core_copy(self, i, col):
        p = self.p
        return remote(self.part.at[:, :, 1 - p.core, :, window(col, PIECE)], self.fromc.at[i], self.cs.at[i], self.cr.at[i], p.at(core=1 - p.core))

    def lanes(self, x):
        return window(2 * LANES * x, LANES)

    def mine(self):
        return window(self.p.x * LANES, 2 * LANES)

    def x_copy(self, i):
        p = self.p
        return remote(self.own.at[i, :, :, :, self.lanes(1 - p.x)], self.fromx.at[i], self.xs.at[i], self.xr.at[i], (p.w, 1 - p.x))

    def y_copy(self, i):
        p = self.p
        return remote(self.own.at[i, :, 1 - p.y, :, self.mine()], self.fromy.at[i], self.ys.at[i], self.yr.at[i], p.at(y=1 - p.y))

    def z_copy(self, i, k):
        p = self.p
        to = p.z_peer(k)
        return remote(self.own.at[i, to, p.y, :, self.mine()], self.fromz.at[i, p.z], self.zs.at[i, k], self.zr.at[i, p.z], p.at(z=to))

    def z_arrival(self, i, k):
        p = self.p
        src = p.z_peer(k)
        return remote(self.own.at[i, p.z, p.y, :, self.mine()], self.fromz.at[i, src], self.zs.at[i, k], self.zr.at[i, src], p.at(z=src))

    def p_copy(self, i):
        p = self.p
        return remote(self.done.at[i], self.fromp.at[i], self.ps.at[i], self.pr.at[i], (p.w, 1 - p.x))

    def start(self, i, col):
        self.local(i, col).start()
        self.core_copy(i, col).start()

    def x_step(self, i, col):
        self.local(i, col).wait()
        self.core_copy(i, col).wait_recv()
        for z in range(4):
            self.own[i, z] = self.own[i, z] + self.fromc[i, z]
        self.x_copy(i).start()

    def y_step(self, i):
        p = self.p
        self.x_copy(i).wait_recv()
        cols = self.lanes(p.x)
        for y in range(2):
            self.own[i, :, y, :, cols] = self.own[i, :, y, :, cols] + self.fromx[i, :, y]
        self.y_copy(i).start()

    def z_step(self, i):
        p = self.p
        self.y_copy(i).wait_recv()
        self.own[i, :, p.y, :, self.mine()] = self.own[i, :, p.y, :, self.mine()] + self.fromy[i]
        for k in (2, 1, 3):
            self.z_copy(i, k).start()

    def p_step(self, i):
        p = self.p
        total = self.own[i, p.z, p.y, :, self.mine()].astype(f32)
        for k in (1, 2, 3):
            self.z_arrival(i, k).wait_recv()
            total += self.fromz[i, p.z_peer(k)].astype(f32)
        self.done[i] = total.astype(bf16)
        self.p_copy(i).start()

    def finish(self, i):
        p = self.p
        self.p_copy(i).wait_recv()
        a, b = self.done[i].astype(f32), self.fromp[i].astype(f32)
        low, high = jnp.where(p.x == 0, a, b), jnp.where(p.x == 0, b, a)
        both = low[:, LANES:] + high[:, :LANES]
        return jnp.concatenate([low[:, :LANES], both, high[:, LANES:]], 1)

    def sent(self, i, col):
        self.core_copy(i, col).wait_send()
        self.x_copy(i).wait_send()
        self.y_copy(i).wait_send()
        for k in (1, 2, 3):
            self.z_copy(i, k).wait_send()
        self.p_copy(i).wait_send()


def reduce_scratch(pieces, rows):
    dma = pltpu.SemaphoreType.DMA
    v = lambda *s: pltpu.VMEM((pieces,) + s, bf16)
    bufs = [v(4, 2, rows, PIECE), v(4, 2, rows, PIECE), v(4, 2, rows, LANES), v(4, rows, 2 * LANES), v(4, rows, 2 * LANES), v(rows, 2 * LANES), v(rows, 2 * LANES)]
    return bufs + [dma((pieces,))] * 7 + [dma((pieces, 4))] * 2 + [dma((pieces,))] * 2


def reduce_kernel(part, out, own, fromc, fromx, fromy, fromz, fromp, done, *sems):
    place = Place()
    total = part.shape[-1] // PIECE
    place.greet()
    r = Reduce(place, part, own, fromc, fromx, fromy, fromz, fromp, done, sems)
    lax.fori_loop(0, min(AHEAD, total), lambda i, _: (r.start(i, i * PIECE), 0)[1], 0)

    def turn(i, _):
        def at(lag, step):
            @pl.when((i >= lag) & (i < total + lag))
            def _():
                step(i - lag)

        @pl.when(i + AHEAD < total)
        def _():
            r.start(i + AHEAD, (i + AHEAD) * PIECE)

        at(0, lambda j: r.x_step(j, j * PIECE))
        at(LAG, r.y_step)
        at(2 * LAG, r.z_step)
        at(3 * LAG, r.p_step)

        def last(j):
            out[j] = r.finish(j)

        at(4 * LAG, last)
        return 0

    lax.fori_loop(0, total + 4 * LAG, turn, 0)
    lax.fori_loop(0, total, lambda i, _: (r.sent(i, i * PIECE), 0)[1], 0)


def reduce_all(part):
    rows16, cols = part.shape
    rows = rows16 // 16
    total = cols // PIECE
    assert cols == total * PIECE
    out = pl.pallas_call(
        reduce_kernel,
        out_shape=jax.ShapeDtypeStruct((total, rows, PIECE), f32),
        in_specs=[pl.BlockSpec(memory_space=pl.ANY)],
        out_specs=pl.BlockSpec(memory_space=pltpu.VMEM),
        scratch_shapes=reduce_scratch(total, rows),
        compiler_params=pltpu.CompilerParams(collective_id=1, has_side_effects=True, vmem_limit_bytes=BIG),
        name="reduce",
    )(part.reshape(4, 2, 2, rows, cols))
    return out


def pack_columns(attention, dense, vectors):
    count = vectors.shape[0]
    vector_cols = jnp.pad(vectors.T, ((0, 0), (0, 128 - count)))
    first = jnp.concatenate([attention[0], attention[1], attention[2], vector_cols], 1)
    second = jnp.concatenate([attention[3], dense[0], dense[1]], 1)
    return first, second


def advance(gradient, moment, weight, average, step_rate):
    moment_new = momentum_decay * moment + gradient
    weight_new = weight - step_rate * (gradient + momentum_decay * moment_new)
    average_new = average_decay * average + (1.0 - average_decay) * weight_new
    return (moment_new, weight_new, average_new)


def body(
    hidden_in,
    segment_ids,
    cotangent,
    attention_weights,
    attention_momentum,
    attention_average,
    dense_weights,
    dense_momentum,
    dense_average,
    vector_params,
    vector_momentum,
    vector_average,
):
    row_count, length, width = hidden_in.shape
    ff = dense_weights.shape[-1]
    vector_rows = vector_params.shape[0]
    x = hidden_in.reshape(-1, width)
    e = cotangent.reshape(-1, width)
    first, second = pack_columns(attention_weights, dense_weights, vector_params)
    ours = lax.axis_size("wide") == 16 and lax.axis_size("narrow") == 2
    if ours:
        cols = first.shape[1] - LANES
        shard = jnp.concatenate([first[:, :cols], second, first[:, cols:]], 1).astype(bf16)
        full = gather_all(shard)
        first_full = jnp.concatenate([full[:, :cols], full[:, -LANES:]], 1)
        second_full = full[:, cols:-LANES]
    else:
        first_full = lax.all_gather(first.astype(bf16), "wide", axis=0, tiled=True)
        second_full = lax.all_gather(second.astype(bf16), "wide", axis=0, tiled=True)
    vec = first_full[:, 3 * width : 3 * width + vector_rows].astype(f32).T
    bias_qkv = jnp.concatenate([vec[4:5], jnp.zeros((1, width), f32), vec[5:6]], 1)
    w_qkv = first_full[:, : 3 * width]
    wo, win, wd = (second_full[:, :width], second_full[:, width : width + ff], second_full[:, width + ff :])
    qkv, c, lse = attn_fwd(x, segment_ids, w_qkv, bias_qkv)
    out, y1, g, dz, du, da, dc, dh1, delta, dvec, dbin = mid(
        x, c, e, wo, win, wd, vec, vec[8:].reshape(1, ff)
    )
    grad_second = jnp.concatenate([wgrad(c, da), wgrad(y1, du), wgrad(dz, g)], 1)
    dqkv, gin, dw, db = attn_bwd(segment_ids, qkv, dc, lse, delta, dh1, w_qkv, x)
    dvec = jnp.concatenate(
        [dvec[:4], db[:, :width], db[:, 2 * width :], dvec[6:8], dbin.reshape(-1, width)], 0
    )
    replicas = lax.axis_size("narrow")
    tokens_all = row_count * length * lax.axis_size("wide") * replicas
    grad_scale = math.sqrt(tokens_all) / replicas
    if ours:
        vec_cols = jnp.pad(dvec.T, ((0, 0), (0, PIECE - vector_rows))).astype(bf16)
        share = reduce_all(jnp.concatenate([dw, vec_cols, grad_second], 1))
        share = jnp.swapaxes(share, 0, 1).reshape(share.shape[1], -1) / replicas
        t1, t2 = share[:, : 3 * width + PIECE], share[:, 3 * width + PIECE :]
    else:
        vec_cols = jnp.pad(dvec.T, ((0, 0), (0, LANES - vector_rows))).astype(bf16)
        share_first = lax.psum_scatter(jnp.concatenate([dw, vec_cols], 1), "wide", scatter_dimension=0, tiled=True)
        share_second = lax.psum_scatter(grad_second, "wide", scatter_dimension=0, tiled=True)
        t1 = lax.psum(share_first, "narrow").astype(f32) / replicas
        t2 = lax.psum(share_second, "narrow").astype(f32) / replicas
    cut = lambda t, j: t[:, j * width : (j + 1) * width]
    attention_grad = jnp.stack([cut(t1, 0), cut(t1, 1), cut(t1, 2), cut(t2, 0)])
    dense_grad = jnp.stack([t2[:, width : width + ff], t2[:, width + ff :]])
    vector_grad = t1[:, 3 * width : 3 * width + vector_rows].T
    attention_new = advance(attention_grad, attention_momentum, attention_weights, attention_average, matrix_rate / grad_scale)
    dense_new = advance(dense_grad, dense_momentum, dense_weights, dense_average, matrix_rate / grad_scale)
    vector_new = advance(vector_grad, vector_momentum, vector_params, vector_average, vector_rate / grad_scale)
    return (out.reshape(hidden_in.shape), gin.reshape(hidden_in.shape)) + attention_new + dense_new + vector_new


def solution(mesh):
    token = P(("wide", "narrow"), None, None)
    matrix = P(None, "wide", None)
    vector = P(None, "wide")
    in_specs = (token, P(("wide", "narrow"), None), token) + (matrix,) * 6 + (vector,) * 3
    out_specs = (token, token) + (matrix,) * 6 + (vector,) * 3
    return jax.shard_map(body, mesh=mesh, in_specs=in_specs, out_specs=out_specs, check_vma=False)
```

```python
import functools, math
import jax, jax.numpy as jnp
from jax import lax
from jax.sharding import PartitionSpec as P
from jax.experimental import pallas as pl
from jax.experimental.pallas import tpu as pltpu

HD = 64
LOG2E = 1.4426950408889634
SCALE2 = 0.125 * LOG2E
NEG = -1e30
EPS = 1e-12
momentum_decay = 0.5
average_decay = 0.5
matrix_rate = 0.03
vector_rate = 0.3
f32, bf16 = jnp.float32, jnp.bfloat16
BIG = 60 * 2**20

def dot(a, b):
    return lax.dot_general(a, b, (((1,), (0,)), ((), ())), preferred_element_type=f32)
def dot_nt(a, b):
    return lax.dot_general(a, b, (((1,), (1,)), ((), ())), preferred_element_type=f32)
def dot_tn(a, b):
    return lax.dot_general(a, b, (((0,), (0,)), ((), ())), preferred_element_type=f32)

def key_range(c, seq, blk):
    lo = max(0, c * blk - seq // 2 + 1) // blk * blk
    hi = min(seq, -(-((c + 1) * blk - 1 + seq // 2) // blk) * blk)
    return lo, hi

def fill_bias(seg_ref, bias_ref):
    segf = seg_ref[0].astype(f32)
    seq = segf.shape[1]
    rep = jnp.broadcast_to(segf, (128, seq)).T
    for j in range(seq // 128):
        bias_ref[:, j * 128:(j + 1) * 128] = jnp.where(rep == segf[:, j * 128:(j + 1) * 128], 0.0, NEG)

def fwd_kernel(blk, x_ref, seg_ref, w_ref, b_ref, qkv_ref, c_ref, lse_ref, bias_ref, lsea_ref):
    seq, width = x_ref.shape
    x = x_ref[...]
    for j in range(3):
        sl = slice(j * width, (j + 1) * width)
        qkv_ref[:, sl] = (dot(x, w_ref[:, sl]) + b_ref[:, sl]).astype(bf16)
    fill_bias(seg_ref, bias_ref)
    lane = lax.broadcasted_iota(jnp.int32, (blk, 128), 1)
    first = lane < HD
    ones = jnp.ones((seq, 128), bf16)
    def pair(p, _):
        col = pl.multiple_of(p * 128, 128)
        q2 = qkv_ref[:, pl.ds(col, 128)]
        k2 = qkv_ref[:, pl.ds(col + width, 128)]
        v2 = jnp.concatenate([qkv_ref[:, pl.ds(col + 2 * width, 128)], ones], 1)
        for c in range(seq // blk):
            lo, hi = key_range(c, seq, blk)
            rows = slice(c * blk, (c + 1) * blk)
            qc = q2[rows]
            outs = []
            la = lsea_ref[rows, :]
            for h in range(2):
                qm = jnp.where(first if h == 0 else ~first, qc, jnp.zeros_like(qc))
                s = dot_nt(qm, k2[lo:hi]) + bias_ref[rows, lo:hi]
                m = jnp.max(s, 1, keepdims=True)
                e = jnp.exp2((s - m) * SCALE2)
                o = dot(e.astype(bf16), v2[lo:hi])
                l = o[:, 128:]
                outs.append(o[:, :128] / l)
                la = jnp.where(lane == 2 * p + h, m * SCALE2 + jnp.log(l) * LOG2E, la)
            lsea_ref[rows, :] = la
            c_ref[rows, pl.ds(col, 128)] = jnp.where(first, outs[0], outs[1]).astype(bf16)
        return 0
    lax.fori_loop(0, width // 128, pair, 0)
    lse_ref[0] = lsea_ref[...].T[:lse_ref.shape[1]]

def attn_fwd(x, seg, w, b, blk=128):
    rows, seq = seg.shape
    width = x.shape[1]
    return pl.pallas_call(
        functools.partial(fwd_kernel, blk), grid=(rows,),
        out_shape=(jax.ShapeDtypeStruct((rows * seq, 3 * width), bf16), jax.ShapeDtypeStruct((rows * seq, width), bf16),
                   jax.ShapeDtypeStruct((rows, 16, seq), f32)),
        in_specs=[pl.BlockSpec((seq, width), lambda r: (r, 0)), pl.BlockSpec((1, 1, seq), lambda r: (r, 0, 0)),
                  pl.BlockSpec((width, 3 * width), lambda r: (0, 0)), pl.BlockSpec((1, 3 * width), lambda r: (0, 0))],
        out_specs=(pl.BlockSpec((seq, 3 * width), lambda r: (r, 0)), pl.BlockSpec((seq, width), lambda r: (r, 0)),
                   pl.BlockSpec((1, 16, seq), lambda r: (r, 0, 0))),
        scratch_shapes=[pltpu.VMEM((seq, seq), f32), pltpu.VMEM((seq, 128), f32)],
        compiler_params=pltpu.CompilerParams(vmem_limit_bytes=BIG),
        name="attn_fwd",
    )(x, seg.reshape(rows, 1, seq), w, b)

def bwd_kernel(blk, seg_ref, qkv_ref, dc_ref, lse_ref, delta_ref, dh1_ref, w_ref, x_ref, dqkv_ref, gin_ref, dw_ref, db_ref, bias_ref, ds_ref, acc_ref):
    r = pl.program_id(0)
    seq = dc_ref.shape[0]
    width = dc_ref.shape[1]
    fill_bias(seg_ref, bias_ref)
    ds_ref[...] = jnp.zeros_like(ds_ref)
    lane = lax.broadcasted_iota(jnp.int32, (blk, 128), 1)
    first = lane < HD
    lane_s = lax.broadcasted_iota(jnp.int32, (seq, 128), 1)
    def pair(p, _):
        col = pl.multiple_of(p * 128, 128)
        q2 = qkv_ref[:, pl.ds(col, 128)]
        k2 = qkv_ref[:, pl.ds(col + width, 128)]
        v2 = qkv_ref[:, pl.ds(col + 2 * width, 128)]
        dc2 = dc_ref[:, pl.ds(col, 128)]
        dqs = []
        for h in range(2):
            lse = lse_ref[0, pl.ds(2 * p + h, 1), :]
            dl = delta_ref[pl.ds(2 * p + h, 1), :]
            mine = first if h == 0 else ~first
            for c in range(seq // blk):
                lo, hi = key_range(c, seq, blk)
                rows = slice(c * blk, (c + 1) * blk)
                kc, vc = k2[rows], v2[rows]
                km = jnp.where(mine, kc, jnp.zeros_like(kc))
                vm = jnp.where(mine, vc, jnp.zeros_like(vc))
                st = dot_nt(km, q2[lo:hi])
                pt = jnp.exp2((st + bias_ref[rows, lo:hi]) * SCALE2 - lse[:, lo:hi])
                dp = dot_nt(vm, dc2[lo:hi])
                ds = (pt * (dp - dl[:, lo:hi])).astype(bf16)
                ds_ref[h, rows, lo:hi] = ds
                dv = dot(pt.astype(bf16), dc2[lo:hi])
                dk = dot(ds, q2[lo:hi]) * 0.125
                if h == 0:
                    dqkv_ref[rows, pl.ds(col + 2 * width, 128)] = dv.astype(bf16)
                    dqkv_ref[rows, pl.ds(col + width, 128)] = dk.astype(bf16)
                else:
                    ov = dqkv_ref[rows, pl.ds(col + 2 * width, 128)]
                    ok = dqkv_ref[rows, pl.ds(col + width, 128)]
                    dqkv_ref[rows, pl.ds(col + 2 * width, 128)] = jnp.where(first, ov, dv.astype(bf16))
                    dqkv_ref[rows, pl.ds(col + width, 128)] = jnp.where(first, ok, dk.astype(bf16))
            dqs.append(dot_tn(ds_ref[h], k2) * 0.125)
        dqkv_ref[:, pl.ds(col, 128)] = jnp.where(lane_s < HD, dqs[0], dqs[1]).astype(bf16)
        return 0
    lax.fori_loop(0, width // 128, pair, 0)
    dqkv = dqkv_ref[...]
    gin_ref[...] = (dh1_ref[...] + dot_nt(dqkv, w_ref[...])).astype(bf16)
    x = x_ref[...]
    for j in range(3):
        sl = slice(j * width, (j + 1) * width)
        d = dot_tn(x, dqkv[:, sl])
        s = jnp.sum(dqkv[:, sl].astype(f32), 0, keepdims=True)
        @pl.when(r == 0)
        def _():
            acc_ref[:, sl] = d
            db_ref[:, sl] = s
        @pl.when(r == pl.num_programs(0) - 1)
        def _():
            dw_ref[:, sl] = (acc_ref[:, sl] + d).astype(bf16)
            db_ref[:, sl] += s

def attn_bwd(seg, qkv, dc, lse, delta, dh1, w, x, blk=128):
    rows, seq = seg.shape
    width = dc.shape[1]
    assert rows == 2
    return pl.pallas_call(
        functools.partial(bwd_kernel, blk), grid=(rows,),
        out_shape=(jax.ShapeDtypeStruct((rows * seq, 3 * width), bf16), jax.ShapeDtypeStruct((rows * seq, width), bf16),
                   jax.ShapeDtypeStruct((width, 3 * width), bf16), jax.ShapeDtypeStruct((1, 3 * width), f32)),
        in_specs=[pl.BlockSpec((1, 1, seq), lambda r: (r, 0, 0)), pl.BlockSpec((seq, 3 * width), lambda r: (r, 0)),
                  pl.BlockSpec((seq, width), lambda r: (r, 0)), pl.BlockSpec((1, 16, seq), lambda r: (r, 0, 0)),
                  pl.BlockSpec((16, seq), lambda r: (0, r)), pl.BlockSpec((seq, width), lambda r: (r, 0)),
                  pl.BlockSpec((width, 3 * width), lambda r: (0, 0)), pl.BlockSpec((seq, width), lambda r: (r, 0))],
        out_specs=(pl.BlockSpec((seq, 3 * width), lambda r: (r, 0)), pl.BlockSpec((seq, width), lambda r: (r, 0)),
                   pl.BlockSpec((width, 3 * width), lambda r: (0, 0)), pl.BlockSpec((1, 3 * width), lambda r: (0, 0))),
        scratch_shapes=[pltpu.VMEM((seq, seq), f32), pltpu.VMEM((2, seq, seq), bf16), pltpu.VMEM((width, 3 * width), f32)],
        compiler_params=pltpu.CompilerParams(vmem_limit_bytes=BIG),
        name="attn_bwd",
    )(seg.reshape(rows, 1, seq), qkv, dc, lse, delta, dh1, w, x)

RSQRT_2PI = 1.0 / math.sqrt(2 * math.pi)
def gelu_parts(u):
    phi_cdf = 0.5 + 0.5 * lax.erf(u * math.sqrt(0.5))
    dens = jnp.exp2(u * u * (-0.5 * LOG2E)) * RSQRT_2PI
    return u * phi_cdf, phi_cdf + u * dens

def mid_kernel(chunk, x_ref, c_ref, e_ref, wo_ref, win_ref, wd_ref, v_ref, bin_ref,
               out_ref, y1_ref, g_ref, dz_ref, du_ref, da_ref, dc_ref, dh1_ref, delta_ref, dv_ref, dbin_ref, gp_ref):
    i = pl.program_id(0)
    blk, width = x_ref.shape
    ff = win_ref.shape[1]
    @pl.when(i == 0)
    def _():
        dv_ref[...] = jnp.zeros_like(dv_ref)
        dbin_ref[...] = jnp.zeros_like(dbin_ref)
    g1, s1, g2, s2, bo, bd = (v_ref[j:j + 1, :] for j in (0, 1, 2, 3, 6, 7))
    cb = c_ref[...]
    h1 = x_ref[...].astype(f32) + (dot(cb, wo_ref[...]) + bo)
    cen = h1 - jnp.mean(h1, 1, keepdims=True)
    r1 = lax.rsqrt(jnp.mean(cen * cen, 1, keepdims=True) + EPS)
    n1 = cen * r1
    y1 = n1 * g1 + s1
    y1l = y1.astype(bf16)
    y1_ref[...] = y1l
    z = jnp.zeros((blk, width), f32)
    for j in range(ff // chunk):
        sl = slice(j * chunk, (j + 1) * chunk)
        u = dot(y1l, win_ref[:, sl]) + bin_ref[:, sl]
        g, gp = gelu_parts(u)
        gl = g.astype(bf16)
        g_ref[:, sl] = gl
        gp_ref[:, sl] = gp
        z += dot_nt(gl, wd_ref[:, sl])
    h2 = y1 + (z + bd)
    cen = h2 - jnp.mean(h2, 1, keepdims=True)
    r2 = lax.rsqrt(jnp.mean(cen * cen, 1, keepdims=True) + EPS)
    n2 = cen * r2
    out_ref[...] = (n2 * g2 + s2).astype(bf16)
    e = e_ref[...].astype(f32)
    eg = e * g2
    dh2 = r2 * (eg - jnp.mean(eg, 1, keepdims=True) - n2 * jnp.mean(eg * n2, 1, keepdims=True))
    dz = dh2.astype(bf16)
    dz_ref[...] = dz
    dy1 = dh2
    for j in range(ff // chunk):
        sl = slice(j * chunk, (j + 1) * chunk)
        du = (dot(dz, wd_ref[:, sl]) * gp_ref[:, sl]).astype(bf16)
        du_ref[:, sl] = du
        dbin_ref[:, sl] += jnp.sum(du.astype(f32), 0, keepdims=True)
        dy1 += dot_nt(du, win_ref[:, sl])
    dn = dy1 * g1
    dh1 = r1 * (dn - jnp.mean(dn, 1, keepdims=True) - n1 * jnp.mean(dn * n1, 1, keepdims=True))
    dh1_ref[...] = dh1
    da = dh1.astype(bf16)
    da_ref[...] = da
    dc = dot_nt(da, wo_ref[...]).astype(bf16)
    dc_ref[...] = dc
    prod = dc.astype(f32) * cb.astype(f32)
    hi = prod.astype(bf16)
    lo = (prod - hi.astype(f32)).astype(bf16)
    sel = jnp.where(lax.broadcasted_iota(jnp.int32, (16, width), 0) == lax.broadcasted_iota(jnp.int32, (16, width), 1) // HD, 1.0, 0.0).astype(bf16)
    delta_ref[...] = dot_nt(sel, hi) + dot_nt(sel, lo)
    parts = [dy1 * n1, dy1, e * n2, e, da.astype(f32), dz.astype(f32)]
    for j, t in zip((0, 1, 2, 3, 6, 7), parts):
        dv_ref[j:j + 1, :] += jnp.sum(t, 0, keepdims=True)

def mid(x, c, e, wo, win, wd, vec, bin_, blk=256, chunk=768):
    n, width = x.shape
    ff = win.shape[1]
    tok = lambda w: pl.BlockSpec((blk, w), lambda i: (i, 0))
    full = lambda a: pl.BlockSpec(a.shape, lambda i: (0, 0), pipeline_mode=pl.Buffered(1))
    sh = jax.ShapeDtypeStruct
    return pl.pallas_call(
        functools.partial(mid_kernel, chunk), grid=(n // blk,),
        out_shape=(sh((n, width), bf16), sh((n, width), bf16), sh((n, ff), bf16), sh((n, width), bf16), sh((n, ff), bf16),
                   sh((n, width), bf16), sh((n, width), bf16), sh((n, width), f32), sh((16, n), f32), sh((8, width), f32), sh((1, ff), f32)),
        in_specs=[tok(width), tok(width), tok(width), full(wo), full(win), full(wd), full(vec), full(bin_)],
        out_specs=(tok(width), tok(width), tok(ff), tok(width), tok(ff), tok(width), tok(width), tok(width),
                   pl.BlockSpec((16, blk), lambda i: (0, i)), pl.BlockSpec((8, width), lambda i: (0, 0)), pl.BlockSpec((1, ff), lambda i: (0, 0))),
        scratch_shapes=[pltpu.VMEM((blk, ff), f32)],
        compiler_params=pltpu.CompilerParams(vmem_limit_bytes=BIG),
        name="middle",
    )(x, c, e, wo, win, wd, vec, bin_)

def wgrad_kernel(a_ref, b_ref, o_ref):
    o_ref[...] = dot_tn(a_ref[...], b_ref[...]).astype(bf16)

def wgrad(a, b, blk=768):
    n, m = a.shape
    k = b.shape[1]
    return pl.pallas_call(wgrad_kernel, grid=(k // blk,), out_shape=jax.ShapeDtypeStruct((m, k), bf16),
        in_specs=[pl.BlockSpec((n, m), lambda j: (0, 0)), pl.BlockSpec((n, blk), lambda j: (0, j))],
        out_specs=pl.BlockSpec((m, blk), lambda j: (0, j)),
        compiler_params=pltpu.CompilerParams(vmem_limit_bytes=BIG), name="wgrad")(a, b)


LANES = 128
PIECE = 3 * LANES
LAG = 2
AHEAD = 3
MESH = pl.DeviceIdType.MESH


class Place:
    def __init__(self):
        self.w = lax.axis_index("wide")
        self.x = lax.axis_index("narrow")
        self.core = lax.rem(self.w, 2)
        self.y = lax.rem(self.w // 2, 2)
        self.b = lax.rem(self.w // 4, 2)
        self.a = self.w // 8

    def over(self, name):
        if name == "x":
            return (self.w, 1 - self.x)
        step = {"a": 8, "b": 4, "y": 2, "core": 1}[name]
        return (self.w + step * (1 - 2 * getattr(self, name)), self.x)

    def greet(self):
        barrier = pltpu.get_barrier_semaphore()
        names = ("a", "b", "y", "x", "core")
        for name in names:
            pl.semaphore_signal(barrier, inc=1, device_id=self.over(name), device_id_type=MESH)
        pl.semaphore_wait(barrier, len(names))


def remote(src, dst, send, recv, device):
    return pltpu.make_async_remote_copy(src_ref=src, dst_ref=dst, send_sem=send, recv_sem=recv, device_id=device, device_id_type=MESH)


def when(condition, step):
    @pl.when(condition)
    def _():
        step()


def loop(count, step):
    lax.fori_loop(0, count, lambda i, _: (step(i), 0)[1], 0)


class Gather:
    def __init__(self, place, shard, full, sems, pieces):
        self.p, self.shard, self.full, self.pieces = place, shard, full, pieces
        self.sems = {name: (sems[2 * k], sems[2 * k + 1]) for k, name in enumerate(("a", "b", "y", "x", "core"))}
        self.kept = sems[10]
        self.own = pl.ds(place.x, 2)

    def mine(self, i, a):
        return self.full.at[i, self.own, a, self.p.b, self.p.y, self.p.core]

    def keep(self, i):
        return pltpu.make_async_copy(self.shard.at[i, self.own], self.mine(i, self.p.a), self.kept.at[i])

    def copy(self, name, i, incoming=False):
        p, f = self.p, self.full
        at = {n: (1 - getattr(p, n) if incoming and n == name else getattr(p, n)) for n in ("a", "b", "y", "x", "core")}
        every = slice(None)
        if name == "a":
            dst = self.mine(i, at["a"])
            src = self.shard.at[i, self.own]
        else:
            if name == "b":
                dst = f.at[i, self.own, :, at["b"], p.y, p.core]
            elif name == "y":
                dst = f.at[i, self.own, :, :, at["y"], p.core]
            elif name == "x":
                dst = f.at[i, 2 * at["x"], :, :, :, p.core]
            else:
                dst = f.at[i, :, :, :, :, at["core"]]
            src = dst
        send, recv = self.sems[name]
        return remote(src, dst, send.at[i], recv.at[i], p.over(name))

    def start(self, i):
        self.keep(i).start()
        self.copy("a", i).start()

    def b_step(self, i):
        self.keep(i).wait()
        self.copy("a", i, True).wait_recv()
        self.copy("b", i).start()

    def y_step(self, i):
        self.copy("b", i, True).wait_recv()
        self.copy("y", i).start()

    def x_step(self, i):
        self.copy("y", i, True).wait_recv()
        self.copy("x", i).start()

    def core_step(self, i):
        self.copy("x", i, True).wait_recv()
        self.copy("core", i).start()

    def arrive(self, i):
        self.copy("core", i, True).wait_recv()

    def turn(self, t):
        for k in range(2):
            ahead = AHEAD + 2 * t + k
            when(ahead < self.pieces, lambda ahead=ahead: self.start(ahead))
        for lag, step in enumerate((self.b_step, self.y_step, self.x_step, self.core_step)):
            lag = lag * LAG
            when((t >= lag) & (t < self.pieces + lag), lambda lag=lag, step=step: step(t - lag))

    def sent(self, i):
        for name in ("a", "b", "y", "x", "core"):
            self.copy(name, i).wait_send()


class GatherVector:
    def __init__(self, place, shard, full, sems):
        self.p, self.shard, self.full = place, shard, full
        self.sems = {name: (sems[2 * k], sems[2 * k + 1]) for k, name in enumerate(("a", "b", "y", "core"))}
        self.kept = sems[8]

    def keep(self):
        p = self.p
        return pltpu.make_async_copy(self.shard, self.full.at[p.a, p.b, p.y, p.core], self.kept)

    def copy(self, name, incoming=False):
        p = self.p
        at = {n: (1 - getattr(p, n) if incoming and n == name else getattr(p, n)) for n in ("a", "b", "y", "core")}
        every = slice(None)
        first = ("a", "b", "y", "core").index(name)
        dst = self.full.at[tuple(at[n] if n == name or n == "core" or k > first else every for k, n in enumerate(("a", "b", "y", "core")))]
        src = self.shard if name == "a" else dst
        send, recv = self.sems[name]
        return remote(src, dst, send, recv, p.over(name))

    def start(self):
        self.keep().start()
        self.copy("a").start()

    def step(self, name, then):
        if name == "a":
            self.keep().wait()
        self.copy(name, True).wait_recv()
        self.copy(then).start()

    def arrive(self):
        self.copy("core", True).wait_recv()

    def sent(self):
        for name in ("a", "b", "y", "core"):
            self.copy(name).wait_send()


def tile(ref, i, t):
    rows = 16 * ref.shape[-2]
    return ref[i, t].reshape(rows, LANES)


def columns(ref, *pieces):
    return jnp.concatenate([tile(ref, i, t) for i in pieces for t in range(3)], 1)


def doc_bias(seg_row, bias_ref, r):
    segf = seg_row.astype(f32)
    seq = segf.shape[1]
    rep = jnp.broadcast_to(segf, (LANES, seq)).T
    for j in range(seq // LANES):
        sl = slice(j * LANES, (j + 1) * LANES)
        bias_ref[r, :, sl] = jnp.where(rep == segf[:, sl], 0.0, NEG)


def stage_kernel(heads, x_hbm, seg_ref, e_hbm, aw_hbm, dw_hbm, vp_ref,
                 qkv_o, c_o, lse_o, wq_o, out_o, y1_o, g_o, dz_o, du_o, da_o, dc_o, dh1_o, delta_o, dv_o, dbin_o,
                 full, vfull, shard, vshard, square, xb, eb, cb, n1b, y1b, acc, gp, gb, dzb, bias, lsea, vrow, binr, r1b,
                 in_sem, out_sem, *sems):
    place = Place()
    rows, _, seq = seg_ref.shape
    tokens, width = x_hbm.shape
    pairs = heads // 2
    pieces = shard.shape[0]
    chunks = gb.shape[0]
    own_rows = aw_hbm.shape[1]
    blk = 256
    g = Gather(place, shard, full, sems[:11], pieces)
    gv = GatherVector(place, vshard, vfull, sems[11:])

    loads = [pltpu.make_async_copy(aw_hbm.at[k], gp.at[0, pl.ds(k * own_rows, own_rows)], in_sem.at[k]) for k in range(4)]
    for k in range(2):
        for j in range(chunks):
            loads.append(pltpu.make_async_copy(
                dw_hbm.at[k, :, pl.ds(j * width, width)], gp.at[1 + k, pl.ds(j * own_rows, own_rows)], in_sem.at[4 + k * chunks + j]))
    n = len(loads)
    x_load = pltpu.make_async_copy(x_hbm, xb, in_sem.at[n])
    e_load = pltpu.make_async_copy(e_hbm, eb, in_sem.at[n + 1])
    for c in loads:
        c.start()
    x_load.start()
    e_load.start()
    square[...] = jnp.zeros_like(square)
    lsea[...] = jnp.zeros_like(lsea)
    square[: vp_ref.shape[0], :own_rows] = vp_ref[...]
    vshard[...] = square[...].T[:own_rows].astype(bf16)

    def own_tile(k, j, t):
        return gp[k, j * own_rows : (j + 1) * own_rows, t * LANES : (t + 1) * LANES].astype(bf16)

    for c in loads[:3]:
        c.wait()
    for p in range(pairs):
        for t in range(3):
            shard[p, t] = own_tile(0, t, p)
    place.greet()
    gv.start()
    for i in range(AHEAD):
        g.start(i)
    for c in loads[3:]:
        c.wait()
    for t in range(6):
        shard[pairs + t // 3, t % 3] = own_tile(0, 3, t)
        for j in range(chunks):
            for k in range(2):
                shard[pairs + 2 + 4 * j + 2 * k + t // 3, t % 3] = own_tile(1 + k, j, t)
    for r in range(rows):
        doc_bias(seg_ref[r], bias, r)
    gv.step("a", "b")
    fill = 3 * LAG + 1
    for t in range(fill):
        g.turn(t)
        if t == LAG // 2:
            gv.step("b", "y")
        if t == 2 * LAG:
            gv.step("y", "core")
    gv.arrive()
    vec = vfull[...].reshape(16 * own_rows, LANES).astype(f32).T
    vrow[...] = vec[: vrow.shape[0]]
    for j in range(chunks):
        binr[j] = vrow[8 + j : 9 + j, :]
    x_load.wait()

    first = lax.broadcasted_iota(jnp.int32, (LANES, LANES), 1) < HD
    lane = lax.broadcasted_iota(jnp.int32, (LANES, LANES), 1)
    ones = jnp.ones((seq, LANES), bf16)

    def qkv_at(p):
        return gb.at[p // 2, :, pl.ds(pl.multiple_of(lax.rem(p, 2) * PIECE, LANES), PIECE)]

    def qkv_out(p):
        return pltpu.make_async_copy(qkv_at(p), qkv_o.at[p], out_sem.at[p])

    def pair(p):
        g.arrive(p)
        head = pl.ds(pl.multiple_of(p * LANES, LANES), LANES)
        w = columns(full, p)
        b = jnp.concatenate([vrow[4:5, head], jnp.zeros((1, LANES), f32), vrow[5:6, head]], 1)
        col = pl.multiple_of(lax.rem(p, 2) * PIECE, LANES)
        gb[p // 2, :, pl.ds(col, PIECE)] = (dot(xb[...], w) + b).astype(bf16)
        qkv_out(p).start()

        def row(r):
            tok = pl.ds(pl.multiple_of(r * seq, seq), seq)
            q2 = gb[p // 2, tok, pl.ds(col, LANES)]
            k2 = gb[p // 2, tok, pl.ds(col + LANES, LANES)]
            v2 = jnp.concatenate([gb[p // 2, tok, pl.ds(col + 2 * LANES, LANES)], ones], 1)
            for c in range(seq // LANES):
                lo, hi = key_range(c, seq, LANES)
                cut = slice(c * LANES, (c + 1) * LANES)
                outs = []
                la = lsea[r, cut, :]
                for h in range(2):
                    qm = jnp.where(first if h == 0 else ~first, q2[cut], jnp.zeros_like(q2[cut]))
                    s = dot_nt(qm, k2[lo:hi]) + bias[r, cut, lo:hi]
                    m = jnp.max(s, 1, keepdims=True)
                    o = dot(jnp.exp2((s - m) * SCALE2).astype(bf16), v2[lo:hi])
                    l = o[:, LANES:]
                    outs.append(o[:, :LANES] / l)
                    la = jnp.where(lane == 2 * p + h, m * SCALE2 + jnp.log(l) * LOG2E, la)
                lsea[r, cut, :] = la
                cb[pl.ds(pl.multiple_of(r * seq + c * LANES, LANES), LANES), head] = jnp.where(first, outs[0], outs[1]).astype(bf16)
            g.turn(fill + 2 * p + r)

        loop(rows, row)

    loop(pairs, pair)
    done = fill + 2 * pairs
    for r in range(rows):
        lse_o[r] = lsea[r].T[: lse_o.shape[1]]
    c_out = pltpu.make_async_copy(cb, c_o, out_sem.at[pairs])
    c_out.start()
    wq_out = pltpu.make_async_copy(full.at[pl.ds(0, pairs)], wq_o, out_sem.at[pairs + 1])
    wq_out.start()
    g1, s1, g2, s2, bo, bd = (vrow[j : j + 1, :] for j in (0, 1, 2, 3, 6, 7))

    def block(i):
        return pl.ds(pl.multiple_of(i * blk, blk), blk)

    g.arrive(pairs)
    g.arrive(pairs + 1)

    def norm_one(i):
        at = block(i)
        h1 = xb[at, :].astype(f32) + (dot(cb[at, :], columns(full, pairs, pairs + 1)) + bo)
        cen = h1 - jnp.mean(h1, 1, keepdims=True)
        r1 = lax.rsqrt(jnp.mean(cen * cen, 1, keepdims=True) + EPS)
        n1 = cen * r1
        y1 = n1 * g1 + s1
        n1b[at, :] = n1
        r1b[at, :] = r1
        y1b[at, :] = y1.astype(bf16)
        acc[at, :] = y1 + bd
        when(lax.rem(i, 2) == 1, lambda: g.turn(done + i // 2))

    loop(tokens // blk, norm_one)
    done += 2
    y1_out = pltpu.make_async_copy(y1b, y1_o, out_sem.at[pairs + 2])
    y1_out.start()
    loop(pairs, lambda p: qkv_out(p).wait())

    def up(j):
        return columns(full, pairs + 2 + 4 * j, pairs + 3 + 4 * j)

    def down(j):
        return columns(full, pairs + 4 + 4 * j, pairs + 5 + 4 * j)

    def g_out(j):
        return pltpu.make_async_copy(gb.at[j], g_o.at[j], out_sem.at[pairs + 3 + j])

    def ff_chunk(j):
        for t in range(4):
            g.arrive(pairs + 2 + 4 * j + t)

        def ff_block(i):
            at = block(i)
            u = dot(y1b[at, :], up(j)) + binr[j]
            act, slope = gelu_parts(u)
            gl = act.astype(bf16)
            gb[j, at, :] = gl
            gp[j, at, :] = slope
            acc[at, :] += dot_nt(gl, down(j))
            when(i < 3, lambda: g.turn(done + 3 * j + i))

        loop(tokens // blk, ff_block)
        g_out(j).start()

    loop(chunks, ff_chunk)
    e_load.wait()
    dv_o[...] = jnp.zeros_like(dv_o)
    dbin_o[...] = jnp.zeros_like(dbin_o)

    def colsum(t):
        return jnp.sum(t, 0, keepdims=True)

    def norm_two(i):
        at = block(i)
        h2 = acc[at, :]
        cen = h2 - jnp.mean(h2, 1, keepdims=True)
        r2 = lax.rsqrt(jnp.mean(cen * cen, 1, keepdims=True) + EPS)
        n2 = cen * r2
        xb[at, :] = (n2 * g2 + s2).astype(bf16)
        e = eb[at, :].astype(f32)
        eg = e * g2
        dh2 = r2 * (eg - jnp.mean(eg, 1, keepdims=True) - n2 * jnp.mean(eg * n2, 1, keepdims=True))
        dz = dh2.astype(bf16)
        dzb[at, :] = dz
        acc[at, :] = dh2
        dv_o[2:3, :] += colsum(e * n2)
        dv_o[3:4, :] += colsum(e)
        dv_o[7:8, :] += colsum(dz.astype(f32))

    loop(tokens // blk, norm_two)
    out_out = pltpu.make_async_copy(xb, out_o, out_sem.at[pairs + 3 + chunks])
    dz_out = pltpu.make_async_copy(dzb, dz_o, out_sem.at[pairs + 4 + chunks])
    out_out.start()
    dz_out.start()

    def du_out(j):
        return pltpu.make_async_copy(gb.at[j], du_o.at[j], out_sem.at[pairs + 5 + chunks + j])

    def back_chunk(j):
        g_out(j).wait()

        def back_block(i):
            at = block(i)
            du = (dot(dzb[at, :], down(j)) * gp[j, at, :]).astype(bf16)
            gb[j, at, :] = du
            dbin_o[j] += colsum(du.astype(f32))
            acc[at, :] += dot_nt(du, up(j))

        loop(tokens // blk, back_block)
        du_out(j).start()

    loop(chunks, back_chunk)
    c_out.wait()
    y1_out.wait()
    sel_shape = (delta_o.shape[0], width)
    sel = jnp.where(lax.broadcasted_iota(jnp.int32, sel_shape, 0) == lax.broadcasted_iota(jnp.int32, sel_shape, 1) // HD, 1.0, 0.0).astype(bf16)

    def norm_one_back(i):
        at = block(i)
        dy1 = acc[at, :]
        n1 = n1b[at, :]
        dn = dy1 * g1
        dh1 = r1b[at, :] * (dn - jnp.mean(dn, 1, keepdims=True) - n1 * jnp.mean(dn * n1, 1, keepdims=True))
        acc[at, :] = dh1
        da = dh1.astype(bf16)
        eb[at, :] = da
        dc = dot_nt(da, columns(full, pairs, pairs + 1)).astype(bf16)
        y1b[at, :] = dc
        prod = dc.astype(f32) * cb[at, :].astype(f32)
        hi = prod.astype(bf16)
        lo = (prod - hi.astype(f32)).astype(bf16)
        delta_o[:, at] = dot_nt(sel, hi) + dot_nt(sel, lo)
        dv_o[0:1, :] += colsum(dy1 * n1)
        dv_o[1:2, :] += colsum(dy1)
        dv_o[6:7, :] += colsum(da.astype(f32))

    loop(tokens // blk, norm_one_back)
    base = pairs + 5 + 2 * chunks
    last = [pltpu.make_async_copy(s, d, out_sem.at[base + k]) for k, (s, d) in enumerate(((acc, dh1_o), (eb, da_o), (y1b, dc_o)))]
    for c in last:
        c.start()
    gv.sent()
    loop(pieces, g.sent)
    wq_out.wait()
    out_out.wait()
    dz_out.wait()
    loop(chunks, lambda j: du_out(j).wait())
    for c in last:
        c.wait()


def stage(x, seg, e, aw, dw, vp):
    rows, seq = seg.shape
    tokens, width = x.shape
    own_rows, ff = dw.shape[1:]
    heads, chunks = width // HD, ff // width
    pairs = heads // 2
    pieces = pairs + 2 + 4 * chunks
    sh = jax.ShapeDtypeStruct
    dma = pltpu.SemaphoreType.DMA
    v = pltpu.VMEM
    hbm = pl.BlockSpec(memory_space=pl.ANY)
    vmem = pl.BlockSpec(memory_space=pltpu.VMEM)
    tok = sh((tokens, width), bf16)
    wide = sh((chunks, tokens, width), bf16)
    block = (2, 2, 2, 2, own_rows, LANES)
    scratch = [
        v((pieces, 3) + block, bf16), v(block, bf16), v((pieces, 3, own_rows, LANES), bf16), v((own_rows, LANES), bf16),
        v((LANES, LANES), f32), v((tokens, width), bf16), v((tokens, width), bf16), v((tokens, width), bf16),
        v((tokens, width), f32), v((tokens, width), bf16), v((tokens, width), f32), v((chunks, tokens, width), f32),
        v((chunks, tokens, width), bf16), v((tokens, width), bf16), v((rows, seq, seq), f32), v((rows, seq, LANES), f32),
        v((16, width), f32), v((chunks, 1, width), f32), v((tokens, 1), f32),
        dma((6 + 2 * chunks,)), dma((pairs + 8 + 2 * chunks,)),
    ] + [dma((pieces,))] * 11 + [dma(())] * 9
    return pl.pallas_call(
        functools.partial(stage_kernel, heads),
        out_shape=(sh((pairs, tokens, PIECE), bf16), tok, sh((rows, 16, seq), f32), sh((pairs, 3) + block, bf16), tok, tok, wide,
                   tok, wide, tok, tok, sh((tokens, width), f32), sh((16, tokens), f32), sh((8, width), f32), sh((chunks, 1, width), f32)),
        in_specs=[hbm, vmem, hbm, hbm, hbm, vmem],
        out_specs=(hbm, hbm, vmem, hbm, hbm, hbm, hbm, hbm, hbm, hbm, hbm, hbm, vmem, vmem, vmem),
        scratch_shapes=scratch,
        compiler_params=pltpu.CompilerParams(collective_id=0, has_side_effects=True, vmem_limit_bytes=BIG),
        name="stage",
    )(x, seg.reshape(rows, 1, seq), e, aw, dw, vp)


class Reduce:
    names = ("core", "x", "y", "b", "a", "p")

    def __init__(self, place, part, froms, done, sems, pieces):
        self.p, self.part, self.done, self.pieces = place, part, done, pieces
        self.froms = dict(zip(self.names, froms))
        self.sems = {name: (sems[2 * k], sems[2 * k + 1]) for k, name in enumerate(self.names)}
        self.own = pl.ds(place.x, 2)

    def copy(self, name, i):
        p, f = self.p, self.part
        if name == "core":
            src = f.at[i, :, :, :, :, 1 - p.core]
        elif name == "x":
            src = f.at[i, 2 * (1 - p.x), :, :, :, p.core]
        elif name == "y":
            src = f.at[i, self.own, :, :, 1 - p.y, p.core]
        elif name == "b":
            src = f.at[i, self.own, :, 1 - p.b, p.y, p.core]
        elif name == "a":
            src = f.at[i, self.own, 1 - p.a, p.b, p.y, p.core]
        else:
            src = self.done.at[i]
        send, recv = self.sems[name]
        return remote(src, self.froms[name].at[i], send.at[i], recv.at[i], p.over("x" if name == "p" else name))

    def start(self, i):
        self.copy("core", i).start()

    def x_step(self, i):
        p, f = self.p, self.part
        self.copy("core", i).wait_recv()
        for t in range(3):
            f[i, t, :, :, :, p.core] = f[i, t, :, :, :, p.core] + self.froms["core"][i, t]
        self.copy("x", i).start()

    def y_step(self, i):
        p, f = self.p, self.part
        self.copy("x", i).wait_recv()
        f[i, 2 * p.x, :, :, :, p.core] = f[i, 2 * p.x, :, :, :, p.core] + self.froms["x"][i]
        self.copy("y", i).start()

    def b_step(self, i):
        p, f = self.p, self.part
        self.copy("y", i).wait_recv()
        f[i, self.own, :, :, p.y, p.core] = f[i, self.own, :, :, p.y, p.core] + self.froms["y"][i]
        self.copy("b", i).start()

    def a_step(self, i):
        p, f = self.p, self.part
        self.copy("b", i).wait_recv()
        f[i, self.own, :, p.b, p.y, p.core] = f[i, self.own, :, p.b, p.y, p.core] + self.froms["b"][i]
        self.copy("a", i).start()

    def p_step(self, i):
        p, f = self.p, self.part
        self.copy("a", i).wait_recv()
        total = f[i, self.own, p.a, p.b, p.y, p.core].astype(f32) + self.froms["a"][i].astype(f32)
        self.done[i] = total.astype(bf16)
        self.copy("p", i).start()

    def finish(self, i):
        self.copy("p", i).wait_recv()
        a, b = self.done[i].astype(f32), self.froms["p"][i].astype(f32)
        first = self.p.x == 0
        low, high = jnp.where(first, a, b), jnp.where(first, b, a)
        return jnp.concatenate([low[0], low[1] + high[0], high[1]], 1)

    def turn(self, t, consume):
        steps = (self.x_step, self.y_step, self.b_step, self.a_step, self.p_step, consume)
        for lag, step in enumerate(steps):
            lag = lag * LAG
            when((t >= lag) & (t < self.pieces + lag), lambda lag=lag, step=step: step(t - lag))

    def sent(self, i):
        for name in self.names:
            self.copy(name, i).wait_send()


def back_kernel(heads, rates, x_hbm, c_hbm, y1_hbm, dz_hbm, da_hbm, g_hbm, du_hbm, qkv_hbm, dc_hbm, dh1_hbm, wq_hbm,
                seg_ref, lse_ref, delta_ref, dv_ref, dbin_ref, am, aw, aa, dm, dw, da_, vm, vw, va,
                gin_o, am_o, aw_o, aa_o, dm_o, dw_o, da_o, vm_o, vw_o, va_o,
                part, fromc, fromx, fromy, fromb, froma, fromp, done, stg, ch, lhs, qb, dqb, wq, bias, dsb, hb, sa, sd, vrow,
                ld, sem_in, sem_out, *sems):
    place = Place()
    rows, _, seq = seg_ref.shape
    tokens, width = x_hbm.shape
    pairs = heads // 2
    chunks = g_hbm.shape[0]
    own_rows = sa.shape[2]
    pieces = part.shape[0]
    half = tokens // 2
    r_ = Reduce(place, part, (fromc, fromx, fromy, fromb, froma, fromp), done, sems, pieces)
    matrix_rate_, vector_rate_, replicas = rates

    def load(src, dst, k):
        return pltpu.make_async_copy(src, dst, ld.at[k])

    state_in = [pltpu.make_async_copy(s, d, sem_in.at[k]) for k, (s, d) in enumerate(
        [(am, sa.at[0]), (aw, sa.at[1]), (aa, sa.at[2]), (dm, sd.at[0]), (dw, sd.at[1]), (da_, sd.at[2])])]
    wq_in = pltpu.make_async_copy(wq_hbm, wq, sem_in.at[6])
    items = [g_hbm.at[j] for j in range(chunks)] + [du_hbm.at[j] for j in range(chunks)] + [da_hbm]
    lefts = [dz_hbm, y1_hbm, c_hbm, x_hbm, dc_hbm]
    left_in = [load(s, stg, k) for k, s in enumerate(lefts)]
    item_in = [load(s, ch.at[k % 2], 5 + k) for k, s in enumerate(items)]
    left_in[0].start()
    item_in[0].start()
    item_in[1].start()
    place.greet()
    for c in state_in:
        c.start()
    wq_in.start()
    for r in range(rows):
        doc_bias(seg_ref[r], bias, r)

    def advance_to(grad, ref, index, rate):
        grad = grad / replicas
        moment = momentum_decay * ref[(0,) + index] + grad
        weight = ref[(1,) + index] - rate * (grad + momentum_decay * moment)
        ref[(0,) + index] = moment
        ref[(1,) + index] = weight
        ref[(2,) + index] = average_decay * ref[(2,) + index] + (1.0 - average_decay) * weight

    ff_pieces = 4 * chunks

    def consume(i):
        grad = r_.finish(i)

        def dense():
            per = 2 * chunks
            which = 1 - i // per
            cols = pl.ds(pl.multiple_of(lax.rem(i, per) * PIECE, LANES), PIECE)
            advance_to(grad, sd, (which, slice(None), cols), matrix_rate_)

        def output():
            cols = pl.ds(pl.multiple_of((i - ff_pieces) * PIECE, LANES), PIECE)
            advance_to(grad, sa, (3, slice(None), cols), matrix_rate_)

        def projections():
            cols = pl.ds(pl.multiple_of((i - ff_pieces - 2) * LANES, LANES), LANES)
            for k in range(3):
                advance_to(grad[:, k * LANES : (k + 1) * LANES], sa, (k, slice(None), cols), matrix_rate_)

        def vectors():
            vrow[:own_rows, :LANES] = grad[:, :LANES]
            vec = vrow[:, :LANES].T[: vm.shape[0], :own_rows] / replicas
            moment = momentum_decay * vm[...] + vec
            weight = vw[...] - vector_rate_ * (vec + momentum_decay * moment)
            vm_o[...] = moment
            vw_o[...] = weight
            va_o[...] = average_decay * va[...] + (1.0 - average_decay) * weight

        when(i < ff_pieces, dense)
        when((i >= ff_pieces) & (i < ff_pieces + 2), output)
        when((i >= ff_pieces + 2) & (i < pieces - 1), projections)
        when(i == pieces - 1, vectors)

    def transpose_left(k):
        left_in[k].wait()
        for j in range(tokens // 256):
            lhs[:, j * 256 : (j + 1) * 256] = stg[j * 256 : (j + 1) * 256, :].T
        left_in[k + 1].start()

    n_half = width // 2

    for k in range(len(items)):
        if k % chunks == 0:
            transpose_left(k // chunks)
        item_in[k].wait()

        def product(a, k=k):
            d = dot(lhs[pl.ds(pl.multiple_of(a * n_half, LANES), n_half), :], ch[k % 2])
            for t in range(6):
                part[2 * k + t // 3, t % 3, a] = d[:, t * LANES : (t + 1) * LANES].astype(bf16).reshape(2, 2, 2, own_rows, LANES)

        loop(2, product)
        r_.start(2 * k)
        r_.start(2 * k + 1)
        if k + 2 < len(items):
            item_in[k + 2].start()
        if k == 1:
            for c in state_in:
                c.wait()
        if k >= 1:
            r_.turn(k - 1, consume)
    t0 = len(items) - 1
    transpose_left(3)
    q_in = lambda p: pltpu.make_async_copy(qkv_hbm.at[p], qb.at[lax.rem(p, 2)], sem_in.at[7 + p])
    q_in(0).start()
    q_in(1).start()
    left_in[4].wait()
    wq_in.wait()
    vrow[...] = jnp.zeros_like(vrow)
    vrow[:8, :] = dv_ref[...]
    for j in range(chunks):
        vrow[8 + j : 9 + j, :] = dbin_ref[j]
    dsb[...] = jnp.zeros_like(dsb)
    first = lax.broadcasted_iota(jnp.int32, (LANES, LANES), 1) < HD
    first_seq = lax.broadcasted_iota(jnp.int32, (seq, LANES), 1) < HD

    def pair(p):
        head = pl.ds(pl.multiple_of(p * LANES, LANES), LANES)
        slot = lax.rem(p, 2)
        q_in(p).wait()

        def row(r):
            tok = pl.ds(pl.multiple_of(r * seq, seq), seq)
            q2 = qb[slot, tok, :LANES]
            k2 = qb[slot, tok, LANES : 2 * LANES]
            v2 = qb[slot, tok, 2 * LANES :]
            dc2 = stg[tok, head]
            dqs = []
            for h in range(2):
                lse = lse_ref[r, pl.ds(2 * p + h, 1), :]
                dl = delta_ref[pl.ds(2 * p + h, 1), tok]
                own = first if h == 0 else ~first
                for c in range(seq // LANES):
                    lo, hi = key_range(c, seq, LANES)
                    cut = slice(c * LANES, (c + 1) * LANES)
                    km = jnp.where(own, k2[cut], jnp.zeros_like(k2[cut]))
                    vm_ = jnp.where(own, v2[cut], jnp.zeros_like(v2[cut]))
                    pt = jnp.exp2((dot_nt(km, q2[lo:hi]) + bias[r, cut, lo:hi]) * SCALE2 - lse[:, lo:hi])
                    ds = (pt * (dot_nt(vm_, dc2[lo:hi]) - dl[:, lo:hi])).astype(bf16)
                    dsb[h, cut, lo:hi] = ds
                    dv = dot(pt.astype(bf16), dc2[lo:hi]).astype(bf16)
                    dk = (dot(ds, q2[lo:hi]) * 0.125).astype(bf16)
                    at = pl.ds(pl.multiple_of(r * seq + c * LANES, LANES), LANES)
                    if h == 1:
                        dv = jnp.where(first, dqb[p, at, 2 * LANES :], dv)
                        dk = jnp.where(first, dqb[p, at, LANES : 2 * LANES], dk)
                    dqb[p, at, 2 * LANES :] = dv
                    dqb[p, at, LANES : 2 * LANES] = dk
                dqs.append(dot_tn(dsb[h], k2) * 0.125)
            dqb[p, tok, :LANES] = jnp.where(first_seq, dqs[0], dqs[1]).astype(bf16)
            when(t0 + 3 * p + r <= ff_pieces + 2 + p - 1, lambda: r_.turn(t0 + 3 * p + r, consume))

        loop(rows, row)
        when(p + 2 < pairs, lambda: q_in(p + 2).start())
        piece = ff_pieces + 2 + p

        def product(a):
            d = dot(lhs[pl.ds(pl.multiple_of(a * n_half, LANES), n_half), :], dqb[p])
            for t in range(3):
                part[piece, t, a] = d[:, t * LANES : (t + 1) * LANES].astype(bf16).reshape(2, 2, 2, own_rows, LANES)

        loop(2, product)
        r_.start(piece)
        sums = jnp.sum(dqb[p].astype(f32), 0, keepdims=True)
        vrow[4:5, head] = sums[:, :LANES]
        vrow[5:6, head] = sums[:, 2 * LANES :]
        when(t0 + 3 * p + 2 <= piece, lambda: r_.turn(t0 + 3 * p + 2, consume))

    loop(pairs, pair)
    return_turn = t0 + 3 * pairs
    left_out = [t for p in range(pairs) for t, last in ((t0 + 3 * p, ff_pieces + 1 + p), (t0 + 3 * p + 1, ff_pieces + 1 + p), (t0 + 3 * p + 2, ff_pieces + 2 + p)) if t > last]
    cols = vrow[...].T.astype(bf16)
    part[pieces - 1, 0] = cols.reshape(2, 2, 2, 2, own_rows, LANES)
    part[pieces - 1, 1] = jnp.zeros_like(part[pieces - 1, 1])
    part[pieces - 1, 2] = jnp.zeros_like(part[pieces - 1, 2])
    r_.start(pieces - 1)
    vrow[...] = jnp.zeros_like(vrow)
    for t in left_out:
        r_.turn(t, consume)
    h_in = lambda i: pltpu.make_async_copy(dh1_hbm.at[pl.ds(pl.multiple_of(i * 256, 256), 256)], hb.at[lax.rem(i, 2)], sem_in.at[7 + pairs + i])
    h_in(0).start()
    h_in(1).start()
    blocks = tokens // 256
    gin = stg

    def gin_block(i):
        at = pl.ds(pl.multiple_of(i * 256, 256), 256)
        h_in(i).wait()
        d = jnp.concatenate([dqb[p, at, :] for p in range(pairs)], 1)
        w = jnp.concatenate([tile(wq, p, t) for p in range(pairs) for t in range(3)], 1)
        gin[at, :] = (hb[lax.rem(i, 2)] + dot_nt(d, w)).astype(bf16)
        when(i + 2 < blocks, lambda: h_in(i + 2).start())
        r_.turn(return_turn + i, consume)

    loop(blocks, gin_block)
    gin_out = pltpu.make_async_copy(gin, gin_o, sem_out.at[6])
    gin_out.start()
    rest = pieces + 5 * LAG - (return_turn + blocks)
    loop(rest, lambda i: r_.turn(return_turn + blocks + i, consume))
    outs = [pltpu.make_async_copy(s, d, sem_out.at[k]) for k, (s, d) in enumerate(
        [(sa.at[0], am_o), (sa.at[1], aw_o), (sa.at[2], aa_o), (sd.at[0], dm_o), (sd.at[1], dw_o), (sd.at[2], da_o)])]
    for c in outs:
        c.start()
    loop(pieces, r_.sent)
    gin_out.wait()
    for c in outs:
        c.wait()


def back(rates, x, c, y1, dz, da, g, du, qkv, dc, dh1, wq, seg, lse, delta, dv, dbin, states):
    rows, seq = seg.shape
    tokens, width = x.shape
    chunks = g.shape[0]
    own_rows = states[0].shape[1]
    heads = width // HD
    pairs = heads // 2
    pieces = 4 * chunks + 2 + pairs + 1
    sh = jax.ShapeDtypeStruct
    dma = pltpu.SemaphoreType.DMA
    v = pltpu.VMEM
    hbm = pl.BlockSpec(memory_space=pl.ANY)
    vmem = pl.BlockSpec(memory_space=pltpu.VMEM)
    tail = (own_rows, LANES)
    scratch = [
        v((pieces, 3, 2, 2, 2, 2) + tail, bf16), v((pieces, 3, 2, 2, 2) + tail, bf16), v((pieces, 2, 2, 2) + tail, bf16),
        v((pieces, 2, 2, 2) + tail, bf16), v((pieces, 2, 2) + tail, bf16), v((pieces, 2) + tail, bf16), v((pieces, 2) + tail, bf16),
        v((pieces, 2) + tail, bf16), v((tokens, width), bf16), v((2, tokens, width), bf16), v((width, tokens), bf16),
        v((2, tokens, PIECE), bf16), v((pairs, tokens, PIECE), bf16), v(wq.shape, bf16), v((rows, seq, seq), f32),
        v((2, seq, seq), bf16), v((2, 256, width), f32), v((3,) + states[0].shape, f32), v((3,) + states[3].shape, f32),
        v((LANES, width), f32),
        dma((5 + 2 * chunks + 1,)), dma((7 + pairs + tokens // 256,)), dma((7,))] + [dma((pieces,))] * 12
    return pl.pallas_call(
        functools.partial(back_kernel, heads, rates),
        out_shape=(sh((tokens, width), bf16),) + tuple(sh(s.shape, f32) for s in states),
        in_specs=[hbm] * 11 + [vmem] * 5 + [hbm] * 6 + [vmem] * 3,
        out_specs=(hbm,) * 7 + (vmem,) * 3,
        scratch_shapes=scratch,
        compiler_params=pltpu.CompilerParams(collective_id=1, has_side_effects=True, vmem_limit_bytes=62 * 2**20),
        name="back",
    )(x, c, y1, dz, da, g, du, qkv, dc, dh1, wq, seg.reshape(rows, 1, seq), lse, delta, dv, dbin, *states)


def pack_columns(attention, dense, vectors):
    count = vectors.shape[0]
    vector_cols = jnp.pad(vectors.T, ((0, 0), (0, 128 - count)))
    first = jnp.concatenate([attention[0], attention[1], attention[2], vector_cols], 1)
    second = jnp.concatenate([attention[3], dense[0], dense[1]], 1)
    return first, second


def advance(gradient, moment, weight, average, step_rate):
    moment_new = momentum_decay * moment + gradient
    weight_new = weight - step_rate * (gradient + momentum_decay * moment_new)
    average_new = average_decay * average + (1.0 - average_decay) * weight_new
    return (moment_new, weight_new, average_new)


def plain_body(
    hidden_in,
    segment_ids,
    cotangent,
    attention_weights,
    attention_momentum,
    attention_average,
    dense_weights,
    dense_momentum,
    dense_average,
    vector_params,
    vector_momentum,
    vector_average,
):
    row_count, length, width = hidden_in.shape
    ff = dense_weights.shape[-1]
    vector_rows = vector_params.shape[0]
    x = hidden_in.reshape(-1, width)
    e = cotangent.reshape(-1, width)
    first, second = pack_columns(attention_weights, dense_weights, vector_params)
    first_full = lax.all_gather(first.astype(bf16), "wide", axis=0, tiled=True)
    second_full = lax.all_gather(second.astype(bf16), "wide", axis=0, tiled=True)
    vec = first_full[:, 3 * width : 3 * width + vector_rows].astype(f32).T
    bias_qkv = jnp.concatenate([vec[4:5], jnp.zeros((1, width), f32), vec[5:6]], 1)
    w_qkv = first_full[:, : 3 * width]
    wo, win, wd = (second_full[:, :width], second_full[:, width : width + ff], second_full[:, width + ff :])
    qkv, c, lse = attn_fwd(x, segment_ids, w_qkv, bias_qkv)
    out, y1, g, dz, du, da, dc, dh1, delta, dvec, dbin = mid(
        x, c, e, wo, win, wd, vec, vec[8:].reshape(1, ff)
    )
    grad_second = jnp.concatenate([wgrad(c, da), wgrad(y1, du), wgrad(dz, g)], 1)
    share_second = lax.psum_scatter(grad_second, "wide", scatter_dimension=0, tiled=True)
    dqkv, gin, dw, db = attn_bwd(segment_ids, qkv, dc, lse, delta, dh1, w_qkv, x)
    dvec = jnp.concatenate(
        [dvec[:4], db[:, :width], db[:, 2 * width :], dvec[6:8], dbin.reshape(-1, width)], 0
    )
    grad_first = jnp.concatenate(
        [dw, jnp.pad(dvec.T, ((0, 0), (0, 128 - vector_rows))).astype(bf16)], 1
    )
    share_first = lax.psum_scatter(grad_first, "wide", scatter_dimension=0, tiled=True)
    replicas = lax.axis_size("narrow")
    tokens_all = row_count * length * lax.axis_size("wide") * replicas
    grad_scale = math.sqrt(tokens_all) / replicas
    t1 = lax.psum(share_first, "narrow").astype(f32) / replicas
    t2 = lax.psum(share_second, "narrow").astype(f32) / replicas
    cut = lambda t, j: t[:, j * width : (j + 1) * width]
    attention_grad = jnp.stack([cut(t1, 0), cut(t1, 1), cut(t1, 2), cut(t2, 0)])
    dense_grad = jnp.stack([t2[:, width : width + ff], t2[:, width + ff :]])
    vector_grad = t1[:, 3 * width : 3 * width + vector_rows].T
    attention_new = advance(attention_grad, attention_momentum, attention_weights, attention_average, matrix_rate / grad_scale)
    dense_new = advance(dense_grad, dense_momentum, dense_weights, dense_average, matrix_rate / grad_scale)
    vector_new = advance(vector_grad, vector_momentum, vector_params, vector_average, vector_rate / grad_scale)
    return (out.reshape(hidden_in.shape), gin.reshape(hidden_in.shape)) + attention_new + dense_new + vector_new


def body(
    hidden_in,
    segment_ids,
    cotangent,
    attention_weights,
    attention_momentum,
    attention_average,
    dense_weights,
    dense_momentum,
    dense_average,
    vector_params,
    vector_momentum,
    vector_average,
):
    row_count, length, width = hidden_in.shape
    x = hidden_in.reshape(-1, width)
    e = cotangent.reshape(-1, width)
    replicas = lax.axis_size("narrow")
    tokens_all = row_count * length * lax.axis_size("wide") * replicas
    grad_scale = math.sqrt(tokens_all) / replicas
    rates = (matrix_rate / grad_scale, vector_rate / grad_scale, replicas)
    qkv, c, lse, wq, out, y1, g, dz, du, da, dc, dh1, delta, dv, dbin = stage(
        x, segment_ids, e, attention_weights, dense_weights, vector_params
    )
    states = (
        attention_momentum, attention_weights, attention_average,
        dense_momentum, dense_weights, dense_average,
        vector_momentum, vector_params, vector_average,
    )
    news = back(rates, x, c, y1, dz, da, g, du, qkv, dc, dh1, wq, segment_ids, lse, delta, dv, dbin, states)
    return (out.reshape(hidden_in.shape), news[0].reshape(hidden_in.shape)) + tuple(news[1:])


def solution(mesh):
    token = P(("wide", "narrow"), None, None)
    matrix = P(None, "wide", None)
    vector = P(None, "wide")
    in_specs = (token, P(("wide", "narrow"), None), token) + (matrix,) * 6 + (vector,) * 3
    out_specs = (token, token) + (matrix,) * 6 + (vector,) * 3
    ours = mesh.shape["wide"] == 16 and mesh.shape["narrow"] == 2
    return jax.shard_map(body if ours else plain_body, mesh=mesh, in_specs=in_specs, out_specs=out_specs, check_vma=False)
```

```python
import functools, math
import jax, jax.numpy as jnp
from jax import lax
from jax.sharding import PartitionSpec as P
from jax.experimental import pallas as pl
from jax.experimental.pallas import tpu as pltpu

HD = 64
LOG2E = 1.4426950408889634
SCALE2 = 0.125 * LOG2E
NEG = -1e30
EPS = 1e-12
momentum_decay = 0.5
average_decay = 0.5
matrix_rate = 0.03
vector_rate = 0.3
f32, bf16 = jnp.float32, jnp.bfloat16
BIG = 60 * 2**20

def dot(a, b):
    return lax.dot_general(a, b, (((1,), (0,)), ((), ())), preferred_element_type=f32)
def dot_nt(a, b):
    return lax.dot_general(a, b, (((1,), (1,)), ((), ())), preferred_element_type=f32)
def dot_tn(a, b):
    return lax.dot_general(a, b, (((0,), (0,)), ((), ())), preferred_element_type=f32)

def key_range(c, seq, blk):
    lo = max(0, c * blk - seq // 2 + 1) // blk * blk
    hi = min(seq, -(-((c + 1) * blk - 1 + seq // 2) // blk) * blk)
    return lo, hi

def fill_bias(seg_ref, bias_ref):
    segf = seg_ref[0].astype(f32)
    seq = segf.shape[1]
    rep = jnp.broadcast_to(segf, (128, seq)).T
    for j in range(seq // 128):
        bias_ref[:, j * 128:(j + 1) * 128] = jnp.where(rep == segf[:, j * 128:(j + 1) * 128], 0.0, NEG)

def fwd_kernel(blk, x_ref, seg_ref, w_ref, b_ref, qkv_ref, c_ref, lse_ref, bias_ref, lsea_ref):
    seq, width = x_ref.shape
    x = x_ref[...]
    for j in range(3):
        sl = slice(j * width, (j + 1) * width)
        qkv_ref[:, sl] = (dot(x, w_ref[:, sl]) + b_ref[:, sl]).astype(bf16)
    fill_bias(seg_ref, bias_ref)
    lane = lax.broadcasted_iota(jnp.int32, (blk, 128), 1)
    first = lane < HD
    ones = jnp.ones((seq, 128), bf16)
    def pair(p, _):
        col = pl.multiple_of(p * 128, 128)
        q2 = qkv_ref[:, pl.ds(col, 128)]
        k2 = qkv_ref[:, pl.ds(col + width, 128)]
        v2 = jnp.concatenate([qkv_ref[:, pl.ds(col + 2 * width, 128)], ones], 1)
        for c in range(seq // blk):
            lo, hi = key_range(c, seq, blk)
            rows = slice(c * blk, (c + 1) * blk)
            qc = q2[rows]
            outs = []
            la = lsea_ref[rows, :]
            for h in range(2):
                qm = jnp.where(first if h == 0 else ~first, qc, jnp.zeros_like(qc))
                s = dot_nt(qm, k2[lo:hi]) + bias_ref[rows, lo:hi]
                m = jnp.max(s, 1, keepdims=True)
                e = jnp.exp2((s - m) * SCALE2)
                o = dot(e.astype(bf16), v2[lo:hi])
                l = o[:, 128:]
                outs.append(o[:, :128] / l)
                la = jnp.where(lane == 2 * p + h, m * SCALE2 + jnp.log(l) * LOG2E, la)
            lsea_ref[rows, :] = la
            c_ref[rows, pl.ds(col, 128)] = jnp.where(first, outs[0], outs[1]).astype(bf16)
        return 0
    lax.fori_loop(0, width // 128, pair, 0)
    lse_ref[0] = lsea_ref[...].T[:lse_ref.shape[1]]

def attn_fwd(x, seg, w, b, blk=128):
    rows, seq = seg.shape
    width = x.shape[1]
    return pl.pallas_call(
        functools.partial(fwd_kernel, blk), grid=(rows,),
        out_shape=(jax.ShapeDtypeStruct((rows * seq, 3 * width), bf16), jax.ShapeDtypeStruct((rows * seq, width), bf16),
                   jax.ShapeDtypeStruct((rows, 16, seq), f32)),
        in_specs=[pl.BlockSpec((seq, width), lambda r: (r, 0)), pl.BlockSpec((1, 1, seq), lambda r: (r, 0, 0)),
                  pl.BlockSpec((width, 3 * width), lambda r: (0, 0)), pl.BlockSpec((1, 3 * width), lambda r: (0, 0))],
        out_specs=(pl.BlockSpec((seq, 3 * width), lambda r: (r, 0)), pl.BlockSpec((seq, width), lambda r: (r, 0)),
                   pl.BlockSpec((1, 16, seq), lambda r: (r, 0, 0))),
        scratch_shapes=[pltpu.VMEM((seq, seq), f32), pltpu.VMEM((seq, 128), f32)],
        compiler_params=pltpu.CompilerParams(vmem_limit_bytes=BIG),
        name="attn_fwd",
    )(x, seg.reshape(rows, 1, seq), w, b)

def bwd_kernel(blk, seg_ref, qkv_ref, dc_ref, lse_ref, delta_ref, dh1_ref, w_ref, x_ref, dqkv_ref, gin_ref, dw_ref, db_ref, bias_ref, ds_ref, acc_ref):
    r = pl.program_id(0)
    seq = dc_ref.shape[0]
    width = dc_ref.shape[1]
    fill_bias(seg_ref, bias_ref)
    ds_ref[...] = jnp.zeros_like(ds_ref)
    lane = lax.broadcasted_iota(jnp.int32, (blk, 128), 1)
    first = lane < HD
    lane_s = lax.broadcasted_iota(jnp.int32, (seq, 128), 1)
    def pair(p, _):
        col = pl.multiple_of(p * 128, 128)
        q2 = qkv_ref[:, pl.ds(col, 128)]
        k2 = qkv_ref[:, pl.ds(col + width, 128)]
        v2 = qkv_ref[:, pl.ds(col + 2 * width, 128)]
        dc2 = dc_ref[:, pl.ds(col, 128)]
        dqs = []
        for h in range(2):
            lse = lse_ref[0, pl.ds(2 * p + h, 1), :]
            dl = delta_ref[pl.ds(2 * p + h, 1), :]
            mine = first if h == 0 else ~first
            for c in range(seq // blk):
                lo, hi = key_range(c, seq, blk)
                rows = slice(c * blk, (c + 1) * blk)
                kc, vc = k2[rows], v2[rows]
                km = jnp.where(mine, kc, jnp.zeros_like(kc))
                vm = jnp.where(mine, vc, jnp.zeros_like(vc))
                st = dot_nt(km, q2[lo:hi])
                pt = jnp.exp2((st + bias_ref[rows, lo:hi]) * SCALE2 - lse[:, lo:hi])
                dp = dot_nt(vm, dc2[lo:hi])
                ds = (pt * (dp - dl[:, lo:hi])).astype(bf16)
                ds_ref[h, rows, lo:hi] = ds
                dv = dot(pt.astype(bf16), dc2[lo:hi])
                dk = dot(ds, q2[lo:hi]) * 0.125
                if h == 0:
                    dqkv_ref[rows, pl.ds(col + 2 * width, 128)] = dv.astype(bf16)
                    dqkv_ref[rows, pl.ds(col + width, 128)] = dk.astype(bf16)
                else:
                    ov = dqkv_ref[rows, pl.ds(col + 2 * width, 128)]
                    ok = dqkv_ref[rows, pl.ds(col + width, 128)]
                    dqkv_ref[rows, pl.ds(col + 2 * width, 128)] = jnp.where(first, ov, dv.astype(bf16))
                    dqkv_ref[rows, pl.ds(col + width, 128)] = jnp.where(first, ok, dk.astype(bf16))
            dqs.append(dot_tn(ds_ref[h], k2) * 0.125)
        dqkv_ref[:, pl.ds(col, 128)] = jnp.where(lane_s < HD, dqs[0], dqs[1]).astype(bf16)
        return 0
    lax.fori_loop(0, width // 128, pair, 0)
    dqkv = dqkv_ref[...]
    gin_ref[...] = (dh1_ref[...] + dot_nt(dqkv, w_ref[...])).astype(bf16)
    x = x_ref[...]
    for j in range(3):
        sl = slice(j * width, (j + 1) * width)
        d = dot_tn(x, dqkv[:, sl])
        s = jnp.sum(dqkv[:, sl].astype(f32), 0, keepdims=True)
        @pl.when(r == 0)
        def _():
            acc_ref[:, sl] = d
            db_ref[:, sl] = s
        @pl.when(r == pl.num_programs(0) - 1)
        def _():
            dw_ref[:, sl] = (acc_ref[:, sl] + d).astype(bf16)
            db_ref[:, sl] += s

def attn_bwd(seg, qkv, dc, lse, delta, dh1, w, x, blk=128):
    rows, seq = seg.shape
    width = dc.shape[1]
    assert rows == 2
    return pl.pallas_call(
        functools.partial(bwd_kernel, blk), grid=(rows,),
        out_shape=(jax.ShapeDtypeStruct((rows * seq, 3 * width), bf16), jax.ShapeDtypeStruct((rows * seq, width), bf16),
                   jax.ShapeDtypeStruct((width, 3 * width), bf16), jax.ShapeDtypeStruct((1, 3 * width), f32)),
        in_specs=[pl.BlockSpec((1, 1, seq), lambda r: (r, 0, 0)), pl.BlockSpec((seq, 3 * width), lambda r: (r, 0)),
                  pl.BlockSpec((seq, width), lambda r: (r, 0)), pl.BlockSpec((1, 16, seq), lambda r: (r, 0, 0)),
                  pl.BlockSpec((16, seq), lambda r: (0, r)), pl.BlockSpec((seq, width), lambda r: (r, 0)),
                  pl.BlockSpec((width, 3 * width), lambda r: (0, 0)), pl.BlockSpec((seq, width), lambda r: (r, 0))],
        out_specs=(pl.BlockSpec((seq, 3 * width), lambda r: (r, 0)), pl.BlockSpec((seq, width), lambda r: (r, 0)),
                   pl.BlockSpec((width, 3 * width), lambda r: (0, 0)), pl.BlockSpec((1, 3 * width), lambda r: (0, 0))),
        scratch_shapes=[pltpu.VMEM((seq, seq), f32), pltpu.VMEM((2, seq, seq), bf16), pltpu.VMEM((width, 3 * width), f32)],
        compiler_params=pltpu.CompilerParams(vmem_limit_bytes=BIG),
        name="attn_bwd",
    )(seg.reshape(rows, 1, seq), qkv, dc, lse, delta, dh1, w, x)

RSQRT_2PI = 1.0 / math.sqrt(2 * math.pi)
def gelu_parts(u):
    phi_cdf = 0.5 + 0.5 * lax.erf(u * math.sqrt(0.5))
    dens = jnp.exp2(u * u * (-0.5 * LOG2E)) * RSQRT_2PI
    return u * phi_cdf, phi_cdf + u * dens

def mid_kernel(chunk, x_ref, c_ref, e_ref, wo_ref, win_ref, wd_ref, v_ref, bin_ref,
               out_ref, y1_ref, g_ref, dz_ref, du_ref, da_ref, dc_ref, dh1_ref, delta_ref, dv_ref, dbin_ref, gp_ref):
    i = pl.program_id(0)
    blk, width = x_ref.shape
    ff = win_ref.shape[1]
    @pl.when(i == 0)
    def _():
        dv_ref[...] = jnp.zeros_like(dv_ref)
        dbin_ref[...] = jnp.zeros_like(dbin_ref)
    g1, s1, g2, s2, bo, bd = (v_ref[j:j + 1, :] for j in (0, 1, 2, 3, 6, 7))
    cb = c_ref[...]
    h1 = x_ref[...].astype(f32) + (dot(cb, wo_ref[...]) + bo)
    cen = h1 - jnp.mean(h1, 1, keepdims=True)
    r1 = lax.rsqrt(jnp.mean(cen * cen, 1, keepdims=True) + EPS)
    n1 = cen * r1
    y1 = n1 * g1 + s1
    y1l = y1.astype(bf16)
    y1_ref[...] = y1l
    z = jnp.zeros((blk, width), f32)
    for j in range(ff // chunk):
        sl = slice(j * chunk, (j + 1) * chunk)
        u = dot(y1l, win_ref[:, sl]) + bin_ref[:, sl]
        g, gp = gelu_parts(u)
        gl = g.astype(bf16)
        g_ref[:, sl] = gl
        gp_ref[:, sl] = gp
        z += dot_nt(gl, wd_ref[:, sl])
    h2 = y1 + (z + bd)
    cen = h2 - jnp.mean(h2, 1, keepdims=True)
    r2 = lax.rsqrt(jnp.mean(cen * cen, 1, keepdims=True) + EPS)
    n2 = cen * r2
    out_ref[...] = (n2 * g2 + s2).astype(bf16)
    e = e_ref[...].astype(f32)
    eg = e * g2
    dh2 = r2 * (eg - jnp.mean(eg, 1, keepdims=True) - n2 * jnp.mean(eg * n2, 1, keepdims=True))
    dz = dh2.astype(bf16)
    dz_ref[...] = dz
    dy1 = dh2
    for j in range(ff // chunk):
        sl = slice(j * chunk, (j + 1) * chunk)
        du = (dot(dz, wd_ref[:, sl]) * gp_ref[:, sl]).astype(bf16)
        du_ref[:, sl] = du
        dbin_ref[:, sl] += jnp.sum(du.astype(f32), 0, keepdims=True)
        dy1 += dot_nt(du, win_ref[:, sl])
    dn = dy1 * g1
    dh1 = r1 * (dn - jnp.mean(dn, 1, keepdims=True) - n1 * jnp.mean(dn * n1, 1, keepdims=True))
    dh1_ref[...] = dh1
    da = dh1.astype(bf16)
    da_ref[...] = da
    dc = dot_nt(da, wo_ref[...]).astype(bf16)
    dc_ref[...] = dc
    prod = dc.astype(f32) * cb.astype(f32)
    hi = prod.astype(bf16)
    lo = (prod - hi.astype(f32)).astype(bf16)
    sel = jnp.where(lax.broadcasted_iota(jnp.int32, (16, width), 0) == lax.broadcasted_iota(jnp.int32, (16, width), 1) // HD, 1.0, 0.0).astype(bf16)
    delta_ref[...] = dot_nt(sel, hi) + dot_nt(sel, lo)
    parts = [dy1 * n1, dy1, e * n2, e, da.astype(f32), dz.astype(f32)]
    for j, t in zip((0, 1, 2, 3, 6, 7), parts):
        dv_ref[j:j + 1, :] += jnp.sum(t, 0, keepdims=True)

def mid(x, c, e, wo, win, wd, vec, bin_, blk=256, chunk=768):
    n, width = x.shape
    ff = win.shape[1]
    tok = lambda w: pl.BlockSpec((blk, w), lambda i: (i, 0))
    full = lambda a: pl.BlockSpec(a.shape, lambda i: (0, 0), pipeline_mode=pl.Buffered(1))
    sh = jax.ShapeDtypeStruct
    return pl.pallas_call(
        functools.partial(mid_kernel, chunk), grid=(n // blk,),
        out_shape=(sh((n, width), bf16), sh((n, width), bf16), sh((n, ff), bf16), sh((n, width), bf16), sh((n, ff), bf16),
                   sh((n, width), bf16), sh((n, width), bf16), sh((n, width), f32), sh((16, n), f32), sh((8, width), f32), sh((1, ff), f32)),
        in_specs=[tok(width), tok(width), tok(width), full(wo), full(win), full(wd), full(vec), full(bin_)],
        out_specs=(tok(width), tok(width), tok(ff), tok(width), tok(ff), tok(width), tok(width), tok(width),
                   pl.BlockSpec((16, blk), lambda i: (0, i)), pl.BlockSpec((8, width), lambda i: (0, 0)), pl.BlockSpec((1, ff), lambda i: (0, 0))),
        scratch_shapes=[pltpu.VMEM((blk, ff), f32)],
        compiler_params=pltpu.CompilerParams(vmem_limit_bytes=BIG),
        name="middle",
    )(x, c, e, wo, win, wd, vec, bin_)

def wgrad_kernel(a_ref, b_ref, o_ref):
    o_ref[...] = dot_tn(a_ref[...], b_ref[...]).astype(bf16)

def wgrad(a, b, blk=768):
    n, m = a.shape
    k = b.shape[1]
    return pl.pallas_call(wgrad_kernel, grid=(k // blk,), out_shape=jax.ShapeDtypeStruct((m, k), bf16),
        in_specs=[pl.BlockSpec((n, m), lambda j: (0, 0)), pl.BlockSpec((n, blk), lambda j: (0, j))],
        out_specs=pl.BlockSpec((m, blk), lambda j: (0, j)),
        compiler_params=pltpu.CompilerParams(vmem_limit_bytes=BIG), name="wgrad")(a, b)


LANES = 128
PIECE = 3 * LANES
LAG = 2
AHEAD = 3
MESH = pl.DeviceIdType.MESH


class Place:
    def __init__(self):
        self.w = lax.axis_index("wide")
        self.x = lax.axis_index("narrow")
        self.core = lax.rem(self.w, 2)
        self.y = lax.rem(self.w // 2, 2)
        self.b = lax.rem(self.w // 4, 2)
        self.a = self.w // 8

    def over(self, name):
        if name == "x":
            return (self.w, 1 - self.x)
        step = {"a": 8, "b": 4, "y": 2, "core": 1}[name]
        return (self.w + step * (1 - 2 * getattr(self, name)), self.x)

    def greet(self):
        barrier = pltpu.get_barrier_semaphore()
        names = ("a", "b", "y", "x", "core")
        for name in names:
            pl.semaphore_signal(barrier, inc=1, device_id=self.over(name), device_id_type=MESH)
        pl.semaphore_wait(barrier, len(names))


def remote(src, dst, send, recv, device):
    return pltpu.make_async_remote_copy(src_ref=src, dst_ref=dst, send_sem=send, recv_sem=recv, device_id=device, device_id_type=MESH)


def when(condition, step):
    @pl.when(condition)
    def _():
        step()


def loop(count, step):
    lax.fori_loop(0, count, lambda i, _: (step(i), 0)[1], 0)


class Gather:
    def __init__(self, place, shard, full, sems, pieces):
        self.p, self.shard, self.full, self.pieces = place, shard, full, pieces
        self.sems = {name: (sems[2 * k], sems[2 * k + 1]) for k, name in enumerate(("a", "b", "y", "x", "core"))}
        self.kept = sems[10]
        self.own = pl.ds(place.x, 2)

    def mine(self, i, a):
        return self.full.at[i, self.own, a, self.p.b, self.p.y, self.p.core]

    def keep(self, i):
        return pltpu.make_async_copy(self.shard.at[i, self.own], self.mine(i, self.p.a), self.kept.at[i])

    def copy(self, name, i, incoming=False):
        p, f = self.p, self.full
        at = {n: (1 - getattr(p, n) if incoming and n == name else getattr(p, n)) for n in ("a", "b", "y", "x", "core")}
        every = slice(None)
        if name == "a":
            dst = self.mine(i, at["a"])
            src = self.shard.at[i, self.own]
        else:
            if name == "b":
                dst = f.at[i, self.own, :, at["b"], p.y, p.core]
            elif name == "y":
                dst = f.at[i, self.own, :, :, at["y"], p.core]
            elif name == "x":
                dst = f.at[i, 2 * at["x"], :, :, :, p.core]
            else:
                dst = f.at[i, :, :, :, :, at["core"]]
            src = dst
        send, recv = self.sems[name]
        return remote(src, dst, send.at[i], recv.at[i], p.over(name))

    def start(self, i):
        self.keep(i).start()
        self.copy("a", i).start()

    def b_step(self, i):
        self.keep(i).wait()
        self.copy("a", i, True).wait_recv()
        self.copy("b", i).start()

    def y_step(self, i):
        self.copy("b", i, True).wait_recv()
        self.copy("y", i).start()

    def x_step(self, i):
        self.copy("y", i, True).wait_recv()
        self.copy("x", i).start()

    def core_step(self, i):
        self.copy("x", i, True).wait_recv()
        self.copy("core", i).start()

    def arrive(self, i):
        self.copy("core", i, True).wait_recv()

    def turn(self, t):
        for k in range(2):
            ahead = AHEAD + 2 * t + k
            when(ahead < self.pieces, lambda ahead=ahead: self.start(ahead))
        for lag, step in enumerate((self.b_step, self.y_step, self.x_step, self.core_step)):
            lag = lag * LAG
            when((t >= lag) & (t < self.pieces + lag), lambda lag=lag, step=step: step(t - lag))

    def sent(self, i):
        for name in ("a", "b", "y", "x", "core"):
            self.copy(name, i).wait_send()


class GatherVector:
    def __init__(self, place, shard, full, sems):
        self.p, self.shard, self.full = place, shard, full
        self.sems = {name: (sems[2 * k], sems[2 * k + 1]) for k, name in enumerate(("a", "b", "y", "core"))}
        self.kept = sems[8]

    def keep(self):
        p = self.p
        return pltpu.make_async_copy(self.shard, self.full.at[p.a, p.b, p.y, p.core], self.kept)

    def copy(self, name, incoming=False):
        p = self.p
        at = {n: (1 - getattr(p, n) if incoming and n == name else getattr(p, n)) for n in ("a", "b", "y", "core")}
        every = slice(None)
        first = ("a", "b", "y", "core").index(name)
        dst = self.full.at[tuple(at[n] if n == name or n == "core" or k > first else every for k, n in enumerate(("a", "b", "y", "core")))]
        src = self.shard if name == "a" else dst
        send, recv = self.sems[name]
        return remote(src, dst, send, recv, p.over(name))

    def start(self):
        self.keep().start()
        self.copy("a").start()

    def step(self, name, then):
        if name == "a":
            self.keep().wait()
        self.copy(name, True).wait_recv()
        self.copy(then).start()

    def arrive(self):
        self.copy("core", True).wait_recv()

    def sent(self):
        for name in ("a", "b", "y", "core"):
            self.copy(name).wait_send()


def tile(ref, i, t):
    rows = 16 * ref.shape[-2]
    return ref[i, t].reshape(rows, LANES)


def columns(ref, *pieces):
    return jnp.concatenate([tile(ref, i, t) for i in pieces for t in range(3)], 1)


def doc_bias(seg_row, bias_ref, r):
    segf = seg_row.astype(f32)
    seq = segf.shape[1]
    rep = jnp.broadcast_to(segf, (LANES, seq)).T
    for j in range(seq // LANES):
        sl = slice(j * LANES, (j + 1) * LANES)
        bias_ref[r, :, sl] = jnp.where(rep == segf[:, sl], 0.0, NEG)


def stage_kernel(heads, x_hbm, seg_ref, e_hbm, aw_hbm, dw_hbm, vp_ref,
                 qkv_o, c_o, lse_o, w_o, out_o, y1_o, g_o, gp_o, dz_o, dh2_o, n1_o, r1_o, dv_o, vrow,
                 full, vfull, shard, vshard, square, xb, eb, cb, n1b, y1b, acc, gp, gb, dzb, bias, lsea, binr, r1b,
                 in_sem, out_sem, w_sem, *sems):
    place = Place()
    rows, _, seq = seg_ref.shape
    tokens, width = x_hbm.shape
    pairs = heads // 2
    pieces = shard.shape[0]
    chunks = gb.shape[0]
    own_rows = aw_hbm.shape[1]
    blk = 256
    big = 512
    g = Gather(place, shard, full, sems[:11], pieces)
    gv = GatherVector(place, vshard, vfull, sems[11:])

    loads = [pltpu.make_async_copy(aw_hbm.at[k], gp.at[0, pl.ds(k * own_rows, own_rows)], in_sem.at[k]) for k in range(4)]
    for k in range(2):
        for j in range(chunks):
            loads.append(pltpu.make_async_copy(
                dw_hbm.at[k, :, pl.ds(j * width, width)], gp.at[1 + k, pl.ds(j * own_rows, own_rows)], in_sem.at[4 + k * chunks + j]))
    n = len(loads)
    x_load = pltpu.make_async_copy(x_hbm, xb, in_sem.at[n])
    e_load = pltpu.make_async_copy(e_hbm, eb, in_sem.at[n + 1])
    for c in loads:
        c.start()
    x_load.start()
    e_load.start()
    square[...] = jnp.zeros_like(square)
    lsea[...] = jnp.zeros_like(lsea)
    square[: vp_ref.shape[0], :own_rows] = vp_ref[...]
    vshard[...] = square[...].T[:own_rows].astype(bf16)

    def own_tile(k, j, t):
        return gp[k, j * own_rows : (j + 1) * own_rows, t * LANES : (t + 1) * LANES].astype(bf16)

    for c in loads[:3]:
        c.wait()
    for p in range(pairs):
        for t in range(3):
            shard[p, t] = own_tile(0, t, p)
    place.greet()
    gv.start()
    for i in range(AHEAD):
        g.start(i)
    for c in loads[3:]:
        c.wait()
    for t in range(6):
        shard[pairs + t // 3, t % 3] = own_tile(0, 3, t)
        for j in range(chunks):
            for k in range(2):
                shard[pairs + 2 + 4 * j + 2 * k + t // 3, t % 3] = own_tile(1 + k, j, t)
    for r in range(rows):
        doc_bias(seg_ref[r], bias, r)
    gv.step("a", "b")
    fill = 3 * LAG + 1
    for t in range(fill):
        g.turn(t)
        if t == LAG // 2:
            gv.step("b", "y")
        if t == 2 * LAG:
            gv.step("y", "core")
    gv.arrive()
    vec = vfull[...].reshape(16 * own_rows, LANES).astype(f32).T
    vrow[...] = vec[: vrow.shape[0]]
    for j in range(chunks):
        binr[j] = vrow[8 + j : 9 + j, :]
    x_load.wait()

    first = lax.broadcasted_iota(jnp.int32, (LANES, LANES), 1) < HD
    lane = lax.broadcasted_iota(jnp.int32, (LANES, LANES), 1)
    ones = jnp.ones((seq, LANES), bf16)

    def qkv_at(p):
        return gb.at[p // 2, :, pl.ds(pl.multiple_of(lax.rem(p, 2) * PIECE, LANES), PIECE)]

    def qkv_out(p):
        return pltpu.make_async_copy(qkv_at(p), qkv_o.at[p], out_sem.at[p])

    def w_out(i):
        return pltpu.make_async_copy(full.at[i], w_o.at[i], w_sem.at[i])

    def pair(p):
        g.arrive(p)
        w_out(p).start()
        head = pl.ds(pl.multiple_of(p * LANES, LANES), LANES)
        w = columns(full, p)
        b = jnp.concatenate([vrow[4:5, head], jnp.zeros((1, LANES), f32), vrow[5:6, head]], 1)
        col = pl.multiple_of(lax.rem(p, 2) * PIECE, LANES)
        gb[p // 2, :, pl.ds(col, PIECE)] = (dot(xb[...], w) + b).astype(bf16)
        qkv_out(p).start()

        def row(r):
            tok = pl.ds(pl.multiple_of(r * seq, seq), seq)
            q2 = gb[p // 2, tok, pl.ds(col, LANES)]
            k2 = gb[p // 2, tok, pl.ds(col + LANES, LANES)]
            v2 = jnp.concatenate([gb[p // 2, tok, pl.ds(col + 2 * LANES, LANES)], ones], 1)
            for c in range(seq // LANES):
                lo, hi = key_range(c, seq, LANES)
                cut = slice(c * LANES, (c + 1) * LANES)
                outs = []
                la = lsea[r, cut, :]
                for h in range(2):
                    qm = jnp.where(first if h == 0 else ~first, q2[cut], jnp.zeros_like(q2[cut]))
                    s = dot_nt(qm, k2[lo:hi]) + bias[r, cut, lo:hi]
                    m = jnp.max(s, 1, keepdims=True)
                    o = dot(jnp.exp2((s - m) * SCALE2).astype(bf16), v2[lo:hi])
                    l = o[:, LANES:]
                    outs.append(o[:, :LANES] / l)
                    la = jnp.where(lane == 2 * p + h, m * SCALE2 + jnp.log(l) * LOG2E, la)
                lsea[r, cut, :] = la
                cb[pl.ds(pl.multiple_of(r * seq + c * LANES, LANES), LANES), head] = jnp.where(first, outs[0], outs[1]).astype(bf16)
            g.turn(fill + 2 * p + r)

        loop(rows, row)

    loop(pairs, pair)
    done = fill + 2 * pairs
    for r in range(rows):
        lse_o[r] = lsea[r].T[: lse_o.shape[1]]
    c_out = pltpu.make_async_copy(cb, c_o, out_sem.at[pairs])
    c_out.start()
    g1, s1, g2, s2, bo, bd = (vrow[j : j + 1, :] for j in (0, 1, 2, 3, 6, 7))

    def block(i):
        return pl.ds(pl.multiple_of(i * blk, blk), blk)

    for i in (pairs, pairs + 1):
        g.arrive(i)
        w_out(i).start()

    def norm_one(i):
        at = block(i)
        h1 = xb[at, :].astype(f32) + (dot(cb[at, :], columns(full, pairs, pairs + 1)) + bo)
        cen = h1 - jnp.mean(h1, 1, keepdims=True)
        r1 = lax.rsqrt(jnp.mean(cen * cen, 1, keepdims=True) + EPS)
        n1 = cen * r1
        y1 = n1 * g1 + s1
        n1b[at, :] = n1
        r1b[at, :] = jnp.broadcast_to(r1, (blk, LANES))
        y1b[at, :] = y1.astype(bf16)
        acc[at, :] = y1 + bd
        when(lax.rem(i, 2) == 1, lambda: g.turn(done + i // 2))

    loop(tokens // blk, norm_one)
    done += 2
    y1_out = pltpu.make_async_copy(y1b, y1_o, out_sem.at[pairs + 2])
    y1_out.start()
    n1_out = pltpu.make_async_copy(n1b, n1_o, out_sem.at[pairs + 1])
    n1_out.start()
    r1_out = pltpu.make_async_copy(r1b, r1_o, out_sem.at[pairs + 5 + chunks])
    r1_out.start()
    loop(pairs, lambda p: qkv_out(p).wait())

    def up(j):
        return columns(full, pairs + 2 + 4 * j, pairs + 3 + 4 * j)

    def down(j):
        return columns(full, pairs + 4 + 4 * j, pairs + 5 + 4 * j)

    def g_out(j):
        return pltpu.make_async_copy(gb.at[j], g_o.at[j], out_sem.at[pairs + 7 + j])

    def gp_out(j):
        return pltpu.make_async_copy(gp.at[j], gp_o.at[j], out_sem.at[pairs + 7 + chunks + j])

    def ff_chunk(j):
        for t in range(4):
            g.arrive(pairs + 2 + 4 * j + t)
            w_out(pairs + 2 + 4 * j + t).start()

        def ff_block(i):
            at = pl.ds(pl.multiple_of(i * big, big), big)
            u = dot(y1b[at, :], up(j)) + binr[j]
            act, slope = gelu_parts(u)
            gl = act.astype(bf16)
            gb[j, at, :] = gl
            gp[j, at, :] = slope
            acc[at, :] += dot_nt(gl, down(j))
            g.turn(done + 3 * j + i)

        loop(tokens // big, ff_block)
        g.turn(done + 3 * j + 2)
        g_out(j).start()
        gp_out(j).start()

    loop(chunks, ff_chunk)
    e_load.wait()
    dv_o[...] = jnp.zeros_like(dv_o)

    def colsum(t):
        return jnp.sum(t, 0, keepdims=True)

    def norm_two(i):
        at = block(i)
        h2 = acc[at, :]
        cen = h2 - jnp.mean(h2, 1, keepdims=True)
        r2 = lax.rsqrt(jnp.mean(cen * cen, 1, keepdims=True) + EPS)
        n2 = cen * r2
        xb[at, :] = (n2 * g2 + s2).astype(bf16)
        e = eb[at, :].astype(f32)
        eg = e * g2
        dh2 = r2 * (eg - jnp.mean(eg, 1, keepdims=True) - n2 * jnp.mean(eg * n2, 1, keepdims=True))
        dz = dh2.astype(bf16)
        dzb[at, :] = dz
        acc[at, :] = dh2
        dv_o[2:3, :] += colsum(e * n2)
        dv_o[3:4, :] += colsum(e)
        dv_o[7:8, :] += colsum(dz.astype(f32))

    loop(tokens // blk, norm_two)
    last = [pltpu.make_async_copy(s, d, out_sem.at[pairs + k]) for k, (s, d) in ((3, (xb, out_o)), (4, (dzb, dz_o)), (6, (acc, dh2_o)))]
    for c in last:
        c.start()
    gv.sent()
    loop(pieces, g.sent)
    loop(pieces, lambda i: w_out(i).wait())
    for c in [c_out, y1_out, n1_out, r1_out] + last:
        c.wait()
    loop(chunks, lambda j: g_out(j).wait())
    loop(chunks, lambda j: gp_out(j).wait())


def stage(x, seg, e, aw, dw, vp):
    rows, seq = seg.shape
    tokens, width = x.shape
    own_rows, ff = dw.shape[1:]
    heads, chunks = width // HD, ff // width
    pairs = heads // 2
    pieces = pairs + 2 + 4 * chunks
    sh = jax.ShapeDtypeStruct
    dma = pltpu.SemaphoreType.DMA
    v = pltpu.VMEM
    hbm = pl.BlockSpec(memory_space=pl.ANY)
    vmem = pl.BlockSpec(memory_space=pltpu.VMEM)
    tok = sh((tokens, width), bf16)
    wide = sh((chunks, tokens, width), bf16)
    long = sh((tokens, width), f32)
    block = (2, 2, 2, 2, own_rows, LANES)
    scratch = [
        v((pieces, 3) + block, bf16), v(block, bf16), v((pieces, 3, own_rows, LANES), bf16), v((own_rows, LANES), bf16),
        v((LANES, LANES), f32), v((tokens, width), bf16), v((tokens, width), bf16), v((tokens, width), bf16),
        v((tokens, width), f32), v((tokens, width), bf16), v((tokens, width), f32), v((chunks, tokens, width), f32),
        v((chunks, tokens, width), bf16), v((tokens, width), bf16), v((rows, seq, seq), f32), v((rows, seq, LANES), f32),
        v((chunks, 1, width), f32), v((tokens, LANES), f32),
        dma((6 + 2 * chunks,)), dma((pairs + 7 + 2 * chunks,)), dma((pieces,)),
    ] + [dma((pieces,))] * 11 + [dma(())] * 9
    return pl.pallas_call(
        functools.partial(stage_kernel, heads),
        out_shape=(sh((pairs, tokens, PIECE), bf16), tok, sh((rows, 16, seq), f32), sh((pieces, 3) + block, bf16), tok, tok, wide,
                   sh((chunks, tokens, width), f32), tok, long, long, sh((tokens, LANES), f32), sh((8, width), f32), sh((16, width), f32)),
        in_specs=[hbm, vmem, hbm, hbm, hbm, vmem],
        out_specs=(hbm, hbm, vmem) + (hbm,) * 9 + (vmem, vmem),
        scratch_shapes=scratch,
        compiler_params=pltpu.CompilerParams(collective_id=0, has_side_effects=True, vmem_limit_bytes=BIG),
        name="stage",
    )(x, seg.reshape(rows, 1, seq), e, aw, dw, vp)


class Reduce:
    names = ("core", "x", "y", "b", "a", "p")

    def __init__(self, place, part, froms, done, out, sems, pieces):
        self.p, self.part, self.done, self.out, self.pieces = place, part, done, out, pieces
        self.froms = dict(zip(self.names, froms))
        self.sems = {name: (sems[2 * k], sems[2 * k + 1]) for k, name in enumerate(self.names)}
        self.own = pl.ds(place.x, 2)

    def copy(self, name, i):
        p, f = self.p, self.part
        if name == "core":
            src = f.at[i, :, :, :, :, 1 - p.core]
        elif name == "x":
            src = f.at[i, 2 * (1 - p.x), :, :, :, p.core]
        elif name == "y":
            src = f.at[i, self.own, :, :, 1 - p.y, p.core]
        elif name == "b":
            src = f.at[i, self.own, :, 1 - p.b, p.y, p.core]
        elif name == "a":
            src = f.at[i, self.own, 1 - p.a, p.b, p.y, p.core]
        else:
            src = self.done.at[i]
        send, recv = self.sems[name]
        return remote(src, self.froms[name].at[i], send.at[i], recv.at[i], p.over("x" if name == "p" else name))

    def start(self, i):
        self.copy("core", i).start()

    def x_step(self, i):
        p, f = self.p, self.part
        self.copy("core", i).wait_recv()
        for t in range(3):
            f[i, t, :, :, :, p.core] = f[i, t, :, :, :, p.core] + self.froms["core"][i, t]
        self.copy("x", i).start()

    def y_step(self, i):
        p, f = self.p, self.part
        self.copy("x", i).wait_recv()
        f[i, 2 * p.x, :, :, :, p.core] = f[i, 2 * p.x, :, :, :, p.core] + self.froms["x"][i]
        self.copy("y", i).start()

    def b_step(self, i):
        p, f = self.p, self.part
        self.copy("y", i).wait_recv()
        f[i, self.own, :, :, p.y, p.core] = f[i, self.own, :, :, p.y, p.core] + self.froms["y"][i]
        self.copy("b", i).start()

    def a_step(self, i):
        p, f = self.p, self.part
        self.copy("b", i).wait_recv()
        f[i, self.own, :, p.b, p.y, p.core] = f[i, self.own, :, p.b, p.y, p.core] + self.froms["b"][i]
        self.copy("a", i).start()

    def p_step(self, i):
        p, f = self.p, self.part
        self.copy("a", i).wait_recv()
        total = f[i, self.own, p.a, p.b, p.y, p.core].astype(f32) + self.froms["a"][i].astype(f32)
        self.done[i] = total.astype(bf16)
        self.copy("p", i).start()

    def finish(self, i):
        self.copy("p", i).wait_recv()
        a, b = self.done[i].astype(f32), self.froms["p"][i].astype(f32)
        first = self.p.x == 0
        low, high = jnp.where(first, a, b), jnp.where(first, b, a)
        self.out[i] = jnp.concatenate([low[0], low[1] + high[0], high[1]], 1)

    def turn(self, t):
        steps = (self.x_step, self.y_step, self.b_step, self.a_step, self.p_step, self.finish)
        for lag, step in enumerate(steps):
            lag = lag * LAG
            when((t >= lag) & (t < self.pieces + lag), lambda lag=lag, step=step: step(t - lag))

    def sent(self, i):
        for name in self.names:
            self.copy(name, i).wait_send()


def back_kernel(heads, x_hbm, c_hbm, y1_hbm, dz_hbm, dh2_hbm, n1_hbm, r1_hbm, g_hbm, gp_hbm, qkv_hbm, w_hbm,
                seg_ref, lse_ref, dv_ref, vec_ref, gin_o, sum_o,
                part, fromc, fromx, fromy, fromb, froma, fromp, done, pool, wpool, gpool, acc, cb, dab, dcb, r1b, dsb, delta, vrow,
                ld, out_sem, *sems):
    place = Place()
    rows, _, seq = seg_ref.shape
    tokens, width = x_hbm.shape
    pairs = heads // 2
    chunks = g_hbm.shape[0]
    own_rows = part.shape[-2]
    pieces = part.shape[0]
    big = 512
    r_ = Reduce(place, part, (fromc, fromx, fromy, fromb, froma, fromp), done, sum_o, sems, pieces)
    ff_pieces = 4 * chunks
    first_ff = pairs + 2
    du, dz, y1 = pool.at[2], pool.at[3], pool.at[4]
    x = y1

    def load(k, src, dst):
        return pltpu.make_async_copy(src, dst, ld.at[k])

    g_in = [load(j, g_hbm.at[j], pool.at[j % 2]) for j in range(chunks)]
    gp_in = [load(chunks + j, gp_hbm.at[j], gpool.at[j % 2]) for j in range(chunks)]
    w_in = [load(2 * chunks + j, w_hbm.at[pl.ds(first_ff + 4 * j, 4)], wpool.at[pl.ds(4 * (j % 2), 4)]) for j in range(chunks)]
    base = 3 * chunks
    dz_in, y1_in, acc_in, c_in, r1_in = (load(base + k, s, d) for k, (s, d) in enumerate(
        ((dz_hbm, dz), (y1_hbm, y1), (dh2_hbm, acc), (c_hbm, cb), (r1_hbm, r1b))))
    base += 5
    n1_in = load(base, n1_hbm, gpool.at[1])
    wo_in = load(base + 1, w_hbm.at[pl.ds(pairs, 2)], wpool.at[pl.ds(6, 2)])
    wq_in = load(base + 2, w_hbm.at[pl.ds(0, pairs)], wpool.at[pl.ds(0, pairs)])
    x_in = load(base + 3, x_hbm, x)
    base += 4

    def q_in(p):
        return load(base + p, qkv_hbm.at[p], pool.at[3, :, pl.ds(pl.multiple_of(lax.rem(p, 2) * PIECE, LANES), PIECE)])

    for c in (dz_in, g_in[0], gp_in[0], w_in[0], y1_in, acc_in, g_in[1], gp_in[1], w_in[1], c_in, r1_in):
        c.start()
    place.greet()
    vrow[...] = jnp.zeros_like(vrow)
    vrow[:8, :] = dv_ref[...]

    def colsum(t):
        return jnp.sum(t, 0, keepdims=True)

    half = width // 2

    def weight_grad(left, right, piece, count):
        def product(a):
            d = dot_tn(left[:, pl.ds(pl.multiple_of(a * half, LANES), half)], right)
            for t in range(3 * count):
                part[piece + t // 3, t % 3, a] = d[:, t * LANES : (t + 1) * LANES].astype(bf16).reshape(2, 2, 2, own_rows, LANES)

        loop(2, product)
        for k in range(count):
            r_.start(piece + k)

    dz_in.wait()
    for j in range(chunks):
        s = j % 2
        g_in[j].wait()
        weight_grad(dz, pool[s], 4 * j, 2)
        r_.turn(2 * j)
        gp_in[j].wait()
        w_in[j].wait()
        if j == 0:
            y1_in.wait()
            acc_in.wait()

        def block(i, j=j, s=s):
            at = pl.ds(pl.multiple_of(i * big, big), big)
            d = (dot(dz[at, :], columns(wpool, 4 * s + 2, 4 * s + 3)) * gpool[s, at, :]).astype(bf16)
            du[at, :] = d
            acc[at, :] += dot_nt(d, columns(wpool, 4 * s, 4 * s + 1))
            vrow[8 + j : 9 + j, :] += colsum(d.astype(f32))

        loop(tokens // big, block)
        if j + 2 < chunks:
            g_in[j + 2].start()
            gp_in[j + 2].start()
            w_in[j + 2].start()
        weight_grad(y1, du[...], 4 * j + 2, 2)
        r_.turn(2 * j + 1)
    n1_in.start()
    wo_in.start()
    x_in.start()
    q_in(0).start()
    q_in(1).start()
    for r in range(rows):
        segf = seg_ref[r].astype(f32)
        rep = jnp.broadcast_to(segf, (LANES, seq)).T
        for k in range(seq // LANES):
            sl = slice(k * LANES, (k + 1) * LANES)
            gpool[0, r * seq : (r + 1) * seq, sl] = jnp.where(rep == segf[:, sl], 0.0, NEG)
    dsb[...] = jnp.zeros_like(dsb)
    c_in.wait()
    r1_in.wait()
    n1_in.wait()
    wo_in.wait()
    g1 = vec_ref[0:1, :]
    sel_shape = (delta.shape[0], width)
    sel = jnp.where(lax.broadcasted_iota(jnp.int32, sel_shape, 0) == lax.broadcasted_iota(jnp.int32, sel_shape, 1) // HD, 1.0, 0.0).astype(bf16)

    def norm_one_back(i):
        at = pl.ds(pl.multiple_of(i * 256, 256), 256)
        dy1 = acc[at, :]
        n1 = gpool[1, at, :]
        dn = dy1 * g1
        r1 = r1b[at, :1]
        dh1 = r1 * (dn - jnp.mean(dn, 1, keepdims=True) - n1 * jnp.mean(dn * n1, 1, keepdims=True))
        acc[at, :] = dh1
        da = dh1.astype(bf16)
        dab[at, :] = da
        dc = dot_nt(da, columns(wpool, 6, 7)).astype(bf16)
        dcb[at, :] = dc
        prod = dc.astype(f32) * cb[at, :].astype(f32)
        hi = prod.astype(bf16)
        lo = (prod - hi.astype(f32)).astype(bf16)
        delta[:, at] = dot_nt(sel, hi) + dot_nt(sel, lo)
        vrow[0:1, :] += colsum(dy1 * n1)
        vrow[1:2, :] += colsum(dy1)
        vrow[6:7, :] += colsum(da.astype(f32))

    loop(tokens // 256, norm_one_back)
    wq_in.start()
    r_.turn(2 * chunks)
    weight_grad(cb, dab[...], ff_pieces, 2)
    r_.turn(2 * chunks + 1)
    t0 = 2 * chunks + 2
    x_in.wait()
    first = lax.broadcasted_iota(jnp.int32, (LANES, LANES), 1) < HD
    first_seq = lax.broadcasted_iota(jnp.int32, (seq, LANES), 1) < HD

    def pair(p):
        head = pl.ds(pl.multiple_of(p * LANES, LANES), LANES)
        col = pl.multiple_of(lax.rem(p, 2) * PIECE, LANES)
        to = p // 2
        q_in(p).wait()

        def row(r):
            tok = pl.ds(pl.multiple_of(r * seq, seq), seq)
            q2 = pool[3, tok, pl.ds(col, LANES)]
            k2 = pool[3, tok, pl.ds(col + LANES, LANES)]
            v2 = pool[3, tok, pl.ds(col + 2 * LANES, LANES)]
            dc2 = dcb[tok, head]
            dqs = []
            for h in range(2):
                lse = lse_ref[r, pl.ds(2 * p + h, 1), :]
                dl = delta[pl.ds(2 * p + h, 1), tok]
                own = first if h == 0 else ~first
                for c in range(seq // LANES):
                    lo, hi = key_range(c, seq, LANES)
                    cut = slice(c * LANES, (c + 1) * LANES)
                    at = pl.ds(pl.multiple_of(r * seq + c * LANES, LANES), LANES)
                    km = jnp.where(own, k2[cut], jnp.zeros_like(k2[cut]))
                    vm_ = jnp.where(own, v2[cut], jnp.zeros_like(v2[cut]))
                    pt = jnp.exp2((dot_nt(km, q2[lo:hi]) + gpool[0, at, lo:hi]) * SCALE2 - lse[:, lo:hi])
                    ds = (pt * (dot_nt(vm_, dc2[lo:hi]) - dl[:, lo:hi])).astype(bf16)
                    dsb[h, cut, lo:hi] = ds
                    dv = dot(pt.astype(bf16), dc2[lo:hi]).astype(bf16)
                    dk = (dot(ds, q2[lo:hi]) * 0.125).astype(bf16)
                    if h == 1:
                        dv = jnp.where(first, pool[to, at, pl.ds(col + 2 * LANES, LANES)], dv)
                        dk = jnp.where(first, pool[to, at, pl.ds(col + LANES, LANES)], dk)
                    pool[to, at, pl.ds(col + 2 * LANES, LANES)] = dv
                    pool[to, at, pl.ds(col + LANES, LANES)] = dk
                dqs.append(dot_tn(dsb[h], k2) * 0.125)
            pool[to, tok, pl.ds(col, LANES)] = jnp.where(first_seq, dqs[0], dqs[1]).astype(bf16)
            when(r == 0, lambda: r_.turn(t0 + 2 * p))

        loop(rows, row)
        when(p + 2 < pairs, lambda: q_in(p + 2).start())
        d = pool[to, :, pl.ds(col, PIECE)]
        weight_grad(x, d, ff_pieces + 2 + p, 1)
        sums = colsum(d.astype(f32))
        vrow[4:5, head] = sums[:, :LANES]
        vrow[5:6, head] = sums[:, 2 * LANES :]
        r_.turn(t0 + 2 * p + 1)

    loop(pairs, pair)
    t0 += 2 * pairs
    cols = vrow[...].T.astype(bf16)
    part[pieces - 1, 0] = cols.reshape(2, 2, 2, 2, own_rows, LANES)
    part[pieces - 1, 1] = jnp.zeros_like(part[pieces - 1, 1])
    part[pieces - 1, 2] = jnp.zeros_like(part[pieces - 1, 2])
    r_.start(pieces - 1)
    left = pieces - t0
    loop(left, lambda i: r_.turn(t0 + i))
    t0 += left
    wq_in.wait()
    blocks = tokens // 256

    def gin_block(i):
        at = pl.ds(pl.multiple_of(i * 256, 256), 256)
        d = jnp.concatenate([pool[k, at, :] for k in range(pairs // 2)], 1)
        dcb[at, :] = (acc[at, :] + dot_nt(d, columns(wpool, *range(pairs)))).astype(bf16)
        r_.turn(t0 + i)

    loop(blocks, gin_block)
    gin_out = pltpu.make_async_copy(dcb, gin_o, out_sem)
    gin_out.start()
    loop(5 * LAG - blocks, lambda i: r_.turn(t0 + blocks + i))
    loop(pieces, r_.sent)
    gin_out.wait()


def back(x, c, y1, dz, dh2, n1, r1, g, gp, qkv, w, seg, lse, dv, vec):
    rows, seq = seg.shape
    tokens, width = x.shape
    chunks = g.shape[0]
    own_rows = w.shape[-2]
    heads = width // HD
    pairs = heads // 2
    pieces = 4 * chunks + 2 + pairs + 1
    sh = jax.ShapeDtypeStruct
    dma = pltpu.SemaphoreType.DMA
    v = pltpu.VMEM
    hbm = pl.BlockSpec(memory_space=pl.ANY)
    vmem = pl.BlockSpec(memory_space=pltpu.VMEM)
    tail = (own_rows, LANES)
    tok = v((tokens, width), bf16)
    scratch = [
        v((pieces, 3, 2, 2, 2, 2) + tail, bf16), v((pieces, 3, 2, 2, 2) + tail, bf16), v((pieces, 2, 2, 2) + tail, bf16),
        v((pieces, 2, 2, 2) + tail, bf16), v((pieces, 2, 2) + tail, bf16), v((pieces, 2) + tail, bf16), v((pieces, 2) + tail, bf16),
        v((pieces, 2) + tail, bf16), v((5, tokens, width), bf16), v((8,) + w.shape[1:], bf16), v((2, tokens, width), f32),
        v((tokens, width), f32), tok, tok, tok, v((tokens, LANES), f32), v((2, seq, seq), bf16), v((16, tokens), f32),
        v((LANES, width), f32),
        dma((3 * chunks + 9 + pairs,)), dma(())] + [dma((pieces,))] * 12
    return pl.pallas_call(
        functools.partial(back_kernel, heads),
        out_shape=(sh((tokens, width), bf16), sh((pieces, own_rows, PIECE), f32)),
        in_specs=[hbm] * 11 + [vmem] * 4,
        out_specs=(hbm, vmem),
        scratch_shapes=scratch,
        compiler_params=pltpu.CompilerParams(collective_id=1, has_side_effects=True, vmem_limit_bytes=63 * 2**20),
        name="back",
    )(x, c, y1, dz, dh2, n1, r1, g, gp, qkv, w, seg.reshape(rows, 1, seq), lse, dv, vec)


def update_kernel(rates, sum_ref, gin_ref, out_ref, am, aw, aa, dm, dw, da, vm, vw, va,
                  gin_o, out_o, am_o, aw_o, aa_o, dm_o, dw_o, da_o, vm_o, vw_o, va_o, square):
    matrix, vector, replicas = rates
    j = pl.program_id(0)
    gin_o[...] = gin_ref[...]
    out_o[...] = out_ref[...]

    def advance_to(grad, rate, ins, outs, index):
        grad = grad / replicas
        moment = momentum_decay * ins[0][index] + grad
        weight = ins[1][index] - rate * (grad + momentum_decay * moment)
        outs[0][index] = moment
        outs[1][index] = weight
        outs[2][index] = average_decay * ins[2][index] + (1.0 - average_decay) * weight

    for k in range(4):
        cols = slice(k % 2 * PIECE, (k % 2 + 1) * PIECE)
        advance_to(sum_ref[4 * j + k], matrix, (dm, dw, da), (dm_o, dw_o, da_o), (1 - k // 2, slice(None), cols))
    last = pl.num_programs(0) - 1
    ff_pieces = sum_ref.shape[0] - 3 - am_o.shape[2] // LANES
    pairs = am_o.shape[2] // LANES

    @pl.when(j < last)
    def _():
        for p in range(pairs):
            cols = slice(p * LANES, (p + 1) * LANES)
            grad = sum_ref[ff_pieces + 2 + p, :, pl.ds(pl.multiple_of(j * LANES, LANES), LANES)]
            advance_to(grad, matrix, (am, aw, aa), (am_o, aw_o, aa_o), (0, slice(None), cols))

    @pl.when(j == last)
    def _():
        for k in range(2):
            cols = slice(k * PIECE, (k + 1) * PIECE)
            advance_to(sum_ref[ff_pieces + k], matrix, (am, aw, aa), (am_o, aw_o, aa_o), (0, slice(None), cols))
        rows, own = vm.shape
        square[...] = jnp.zeros_like(square)
        square[:own, :] = sum_ref[ff_pieces + pairs + 2, :, :LANES]
        every = (slice(None), slice(None))
        advance_to(square[...].T[:rows, :own], vector, (vm, vw, va), (vm_o, vw_o, va_o), every)


def update(rates, sums, gin, out, states):
    am, dm, vm = states[0], states[3], states[6]
    pieces, own_rows, _ = sums.shape
    tokens, width = gin.shape
    steps = am.shape[0]
    chunks = dm.shape[2] // width
    assert steps == chunks == 4
    tok = pl.BlockSpec((tokens // steps, width), lambda j: (j, 0))
    att = pl.BlockSpec((1, own_rows, width), lambda j: (j, 0, 0))
    den = pl.BlockSpec((2, own_rows, width), lambda j: (0, 0, j))
    vec = pl.BlockSpec(vm.shape, lambda j: (0, 0))
    sh = jax.ShapeDtypeStruct
    return pl.pallas_call(
        functools.partial(update_kernel, rates), grid=(steps,),
        out_shape=(sh(gin.shape, bf16), sh(out.shape, bf16)) + tuple(sh(s.shape, f32) for s in states),
        in_specs=[pl.BlockSpec(sums.shape, lambda j: (0, 0, 0)), tok, tok] + [att] * 3 + [den] * 3 + [vec] * 3,
        out_specs=(tok, tok) + (att,) * 3 + (den,) * 3 + (vec,) * 3,
        scratch_shapes=[pltpu.VMEM((LANES, LANES), f32)],
        name="update",
    )(sums, gin, out, *states)


def pack_columns(attention, dense, vectors):
    count = vectors.shape[0]
    vector_cols = jnp.pad(vectors.T, ((0, 0), (0, 128 - count)))
    first = jnp.concatenate([attention[0], attention[1], attention[2], vector_cols], 1)
    second = jnp.concatenate([attention[3], dense[0], dense[1]], 1)
    return first, second


def advance(gradient, moment, weight, average, step_rate):
    moment_new = momentum_decay * moment + gradient
    weight_new = weight - step_rate * (gradient + momentum_decay * moment_new)
    average_new = average_decay * average + (1.0 - average_decay) * weight_new
    return (moment_new, weight_new, average_new)


def plain_body(
    hidden_in,
    segment_ids,
    cotangent,
    attention_weights,
    attention_momentum,
    attention_average,
    dense_weights,
    dense_momentum,
    dense_average,
    vector_params,
    vector_momentum,
    vector_average,
):
    row_count, length, width = hidden_in.shape
    ff = dense_weights.shape[-1]
    vector_rows = vector_params.shape[0]
    x = hidden_in.reshape(-1, width)
    e = cotangent.reshape(-1, width)
    first, second = pack_columns(attention_weights, dense_weights, vector_params)
    first_full = lax.all_gather(first.astype(bf16), "wide", axis=0, tiled=True)
    second_full = lax.all_gather(second.astype(bf16), "wide", axis=0, tiled=True)
    vec = first_full[:, 3 * width : 3 * width + vector_rows].astype(f32).T
    bias_qkv = jnp.concatenate([vec[4:5], jnp.zeros((1, width), f32), vec[5:6]], 1)
    w_qkv = first_full[:, : 3 * width]
    wo, win, wd = (second_full[:, :width], second_full[:, width : width + ff], second_full[:, width + ff :])
    qkv, c, lse = attn_fwd(x, segment_ids, w_qkv, bias_qkv)
    out, y1, g, dz, du, da, dc, dh1, delta, dvec, dbin = mid(
        x, c, e, wo, win, wd, vec, vec[8:].reshape(1, ff)
    )
    grad_second = jnp.concatenate([wgrad(c, da), wgrad(y1, du), wgrad(dz, g)], 1)
    share_second = lax.psum_scatter(grad_second, "wide", scatter_dimension=0, tiled=True)
    dqkv, gin, dw, db = attn_bwd(segment_ids, qkv, dc, lse, delta, dh1, w_qkv, x)
    dvec = jnp.concatenate(
        [dvec[:4], db[:, :width], db[:, 2 * width :], dvec[6:8], dbin.reshape(-1, width)], 0
    )
    grad_first = jnp.concatenate(
        [dw, jnp.pad(dvec.T, ((0, 0), (0, 128 - vector_rows))).astype(bf16)], 1
    )
    share_first = lax.psum_scatter(grad_first, "wide", scatter_dimension=0, tiled=True)
    replicas = lax.axis_size("narrow")
    tokens_all = row_count * length * lax.axis_size("wide") * replicas
    grad_scale = math.sqrt(tokens_all) / replicas
    t1 = lax.psum(share_first, "narrow").astype(f32) / replicas
    t2 = lax.psum(share_second, "narrow").astype(f32) / replicas
    cut = lambda t, j: t[:, j * width : (j + 1) * width]
    attention_grad = jnp.stack([cut(t1, 0), cut(t1, 1), cut(t1, 2), cut(t2, 0)])
    dense_grad = jnp.stack([t2[:, width : width + ff], t2[:, width + ff :]])
    vector_grad = t1[:, 3 * width : 3 * width + vector_rows].T
    attention_new = advance(attention_grad, attention_momentum, attention_weights, attention_average, matrix_rate / grad_scale)
    dense_new = advance(dense_grad, dense_momentum, dense_weights, dense_average, matrix_rate / grad_scale)
    vector_new = advance(vector_grad, vector_momentum, vector_params, vector_average, vector_rate / grad_scale)
    return (out.reshape(hidden_in.shape), gin.reshape(hidden_in.shape)) + attention_new + dense_new + vector_new


def body(
    hidden_in,
    segment_ids,
    cotangent,
    attention_weights,
    attention_momentum,
    attention_average,
    dense_weights,
    dense_momentum,
    dense_average,
    vector_params,
    vector_momentum,
    vector_average,
):
    row_count, length, width = hidden_in.shape
    x = hidden_in.reshape(-1, width)
    e = cotangent.reshape(-1, width)
    replicas = lax.axis_size("narrow")
    tokens_all = row_count * length * lax.axis_size("wide") * replicas
    grad_scale = math.sqrt(tokens_all) / replicas
    rates = (matrix_rate / grad_scale, vector_rate / grad_scale, replicas)
    qkv, c, lse, w, out, y1, g, gp, dz, dh2, n1, r1, dv, vec = stage(
        x, segment_ids, e, attention_weights, dense_weights, vector_params
    )
    states = (
        attention_momentum, attention_weights, attention_average,
        dense_momentum, dense_weights, dense_average,
        vector_momentum, vector_params, vector_average,
    )
    gin, sums = back(x, c, y1, dz, dh2, n1, r1, g, gp, qkv, w, segment_ids, lse, dv, vec)
    news = update(rates, sums, gin, out, states)
    return (news[1].reshape(hidden_in.shape), news[0].reshape(hidden_in.shape)) + tuple(news[2:])


def solution(mesh):
    token = P(("wide", "narrow"), None, None)
    matrix = P(None, "wide", None)
    vector = P(None, "wide")
    in_specs = (token, P(("wide", "narrow"), None), token) + (matrix,) * 6 + (vector,) * 3
    out_specs = (token, token) + (matrix,) * 6 + (vector,) * 3
    ours = mesh.shape["wide"] == 16 and mesh.shape["narrow"] == 2
    return jax.shard_map(body if ours else plain_body, mesh=mesh, in_specs=in_specs, out_specs=out_specs, check_vma=False)
```

```python
import functools, math
import jax, jax.numpy as jnp
from jax import lax
from jax.sharding import PartitionSpec as P
from jax.experimental import pallas as pl
from jax.experimental.pallas import tpu as pltpu

HD = 64
LOG2E = 1.4426950408889634
SCALE2 = 0.125 * LOG2E
NEG = -1e30
EPS = 1e-12
momentum_decay = 0.5
average_decay = 0.5
matrix_rate = 0.03
vector_rate = 0.3
f32, bf16 = jnp.float32, jnp.bfloat16
BIG = 60 * 2**20

def dot(a, b):
    return lax.dot_general(a, b, (((1,), (0,)), ((), ())), preferred_element_type=f32)
def dot_nt(a, b):
    return lax.dot_general(a, b, (((1,), (1,)), ((), ())), preferred_element_type=f32)
def dot_tn(a, b):
    return lax.dot_general(a, b, (((0,), (0,)), ((), ())), preferred_element_type=f32)

def key_range(c, seq, blk):
    lo = max(0, c * blk - seq // 2 + 1) // blk * blk
    hi = min(seq, -(-((c + 1) * blk - 1 + seq // 2) // blk) * blk)
    return lo, hi

def fill_bias(seg_ref, bias_ref):
    segf = seg_ref[0].astype(f32)
    seq = segf.shape[1]
    rep = jnp.broadcast_to(segf, (128, seq)).T
    for j in range(seq // 128):
        bias_ref[:, j * 128:(j + 1) * 128] = jnp.where(rep == segf[:, j * 128:(j + 1) * 128], 0.0, NEG)

def fwd_kernel(blk, x_ref, seg_ref, w_ref, b_ref, qkv_ref, c_ref, lse_ref, bias_ref, lsea_ref):
    seq, width = x_ref.shape
    x = x_ref[...]
    for j in range(3):
        sl = slice(j * width, (j + 1) * width)
        qkv_ref[:, sl] = (dot(x, w_ref[:, sl]) + b_ref[:, sl]).astype(bf16)
    fill_bias(seg_ref, bias_ref)
    lane = lax.broadcasted_iota(jnp.int32, (blk, 128), 1)
    first = lane < HD
    ones = jnp.ones((seq, 128), bf16)
    def pair(p, _):
        col = pl.multiple_of(p * 128, 128)
        q2 = qkv_ref[:, pl.ds(col, 128)]
        k2 = qkv_ref[:, pl.ds(col + width, 128)]
        v2 = jnp.concatenate([qkv_ref[:, pl.ds(col + 2 * width, 128)], ones], 1)
        for c in range(seq // blk):
            lo, hi = key_range(c, seq, blk)
            rows = slice(c * blk, (c + 1) * blk)
            qc = q2[rows]
            outs = []
            la = lsea_ref[rows, :]
            for h in range(2):
                qm = jnp.where(first if h == 0 else ~first, qc, jnp.zeros_like(qc))
                s = dot_nt(qm, k2[lo:hi]) + bias_ref[rows, lo:hi]
                m = jnp.max(s, 1, keepdims=True)
                e = jnp.exp2((s - m) * SCALE2)
                o = dot(e.astype(bf16), v2[lo:hi])
                l = o[:, 128:]
                outs.append(o[:, :128] / l)
                la = jnp.where(lane == 2 * p + h, m * SCALE2 + jnp.log(l) * LOG2E, la)
            lsea_ref[rows, :] = la
            c_ref[rows, pl.ds(col, 128)] = jnp.where(first, outs[0], outs[1]).astype(bf16)
        return 0
    lax.fori_loop(0, width // 128, pair, 0)
    lse_ref[0] = lsea_ref[...].T[:lse_ref.shape[1]]

def attn_fwd(x, seg, w, b, blk=128):
    rows, seq = seg.shape
    width = x.shape[1]
    return pl.pallas_call(
        functools.partial(fwd_kernel, blk), grid=(rows,),
        out_shape=(jax.ShapeDtypeStruct((rows * seq, 3 * width), bf16), jax.ShapeDtypeStruct((rows * seq, width), bf16),
                   jax.ShapeDtypeStruct((rows, 16, seq), f32)),
        in_specs=[pl.BlockSpec((seq, width), lambda r: (r, 0)), pl.BlockSpec((1, 1, seq), lambda r: (r, 0, 0)),
                  pl.BlockSpec((width, 3 * width), lambda r: (0, 0)), pl.BlockSpec((1, 3 * width), lambda r: (0, 0))],
        out_specs=(pl.BlockSpec((seq, 3 * width), lambda r: (r, 0)), pl.BlockSpec((seq, width), lambda r: (r, 0)),
                   pl.BlockSpec((1, 16, seq), lambda r: (r, 0, 0))),
        scratch_shapes=[pltpu.VMEM((seq, seq), f32), pltpu.VMEM((seq, 128), f32)],
        compiler_params=pltpu.CompilerParams(vmem_limit_bytes=BIG),
        name="attn_fwd",
    )(x, seg.reshape(rows, 1, seq), w, b)

def bwd_kernel(blk, seg_ref, qkv_ref, dc_ref, lse_ref, delta_ref, dh1_ref, w_ref, x_ref, dqkv_ref, gin_ref, dw_ref, db_ref, bias_ref, ds_ref, acc_ref):
    r = pl.program_id(0)
    seq = dc_ref.shape[0]
    width = dc_ref.shape[1]
    fill_bias(seg_ref, bias_ref)
    ds_ref[...] = jnp.zeros_like(ds_ref)
    lane = lax.broadcasted_iota(jnp.int32, (blk, 128), 1)
    first = lane < HD
    lane_s = lax.broadcasted_iota(jnp.int32, (seq, 128), 1)
    def pair(p, _):
        col = pl.multiple_of(p * 128, 128)
        q2 = qkv_ref[:, pl.ds(col, 128)]
        k2 = qkv_ref[:, pl.ds(col + width, 128)]
        v2 = qkv_ref[:, pl.ds(col + 2 * width, 128)]
        dc2 = dc_ref[:, pl.ds(col, 128)]
        dqs = []
        for h in range(2):
            lse = lse_ref[0, pl.ds(2 * p + h, 1), :]
            dl = delta_ref[pl.ds(2 * p + h, 1), :]
            mine = first if h == 0 else ~first
            for c in range(seq // blk):
                lo, hi = key_range(c, seq, blk)
                rows = slice(c * blk, (c + 1) * blk)
                kc, vc = k2[rows], v2[rows]
                km = jnp.where(mine, kc, jnp.zeros_like(kc))
                vm = jnp.where(mine, vc, jnp.zeros_like(vc))
                st = dot_nt(km, q2[lo:hi])
                pt = jnp.exp2((st + bias_ref[rows, lo:hi]) * SCALE2 - lse[:, lo:hi])
                dp = dot_nt(vm, dc2[lo:hi])
                ds = (pt * (dp - dl[:, lo:hi])).astype(bf16)
                ds_ref[h, rows, lo:hi] = ds
                dv = dot(pt.astype(bf16), dc2[lo:hi])
                dk = dot(ds, q2[lo:hi]) * 0.125
                if h == 0:
                    dqkv_ref[rows, pl.ds(col + 2 * width, 128)] = dv.astype(bf16)
                    dqkv_ref[rows, pl.ds(col + width, 128)] = dk.astype(bf16)
                else:
                    ov = dqkv_ref[rows, pl.ds(col + 2 * width, 128)]
                    ok = dqkv_ref[rows, pl.ds(col + width, 128)]
                    dqkv_ref[rows, pl.ds(col + 2 * width, 128)] = jnp.where(first, ov, dv.astype(bf16))
                    dqkv_ref[rows, pl.ds(col + width, 128)] = jnp.where(first, ok, dk.astype(bf16))
            dqs.append(dot_tn(ds_ref[h], k2) * 0.125)
        dqkv_ref[:, pl.ds(col, 128)] = jnp.where(lane_s < HD, dqs[0], dqs[1]).astype(bf16)
        return 0
    lax.fori_loop(0, width // 128, pair, 0)
    dqkv = dqkv_ref[...]
    gin_ref[...] = (dh1_ref[...] + dot_nt(dqkv, w_ref[...])).astype(bf16)
    x = x_ref[...]
    for j in range(3):
        sl = slice(j * width, (j + 1) * width)
        d = dot_tn(x, dqkv[:, sl])
        s = jnp.sum(dqkv[:, sl].astype(f32), 0, keepdims=True)
        @pl.when(r == 0)
        def _():
            acc_ref[:, sl] = d
            db_ref[:, sl] = s
        @pl.when(r == pl.num_programs(0) - 1)
        def _():
            dw_ref[:, sl] = (acc_ref[:, sl] + d).astype(bf16)
            db_ref[:, sl] += s

def attn_bwd(seg, qkv, dc, lse, delta, dh1, w, x, blk=128):
    rows, seq = seg.shape
    width = dc.shape[1]
    assert rows == 2
    return pl.pallas_call(
        functools.partial(bwd_kernel, blk), grid=(rows,),
        out_shape=(jax.ShapeDtypeStruct((rows * seq, 3 * width), bf16), jax.ShapeDtypeStruct((rows * seq, width), bf16),
                   jax.ShapeDtypeStruct((width, 3 * width), bf16), jax.ShapeDtypeStruct((1, 3 * width), f32)),
        in_specs=[pl.BlockSpec((1, 1, seq), lambda r: (r, 0, 0)), pl.BlockSpec((seq, 3 * width), lambda r: (r, 0)),
                  pl.BlockSpec((seq, width), lambda r: (r, 0)), pl.BlockSpec((1, 16, seq), lambda r: (r, 0, 0)),
                  pl.BlockSpec((16, seq), lambda r: (0, r)), pl.BlockSpec((seq, width), lambda r: (r, 0)),
                  pl.BlockSpec((width, 3 * width), lambda r: (0, 0)), pl.BlockSpec((seq, width), lambda r: (r, 0))],
        out_specs=(pl.BlockSpec((seq, 3 * width), lambda r: (r, 0)), pl.BlockSpec((seq, width), lambda r: (r, 0)),
                   pl.BlockSpec((width, 3 * width), lambda r: (0, 0)), pl.BlockSpec((1, 3 * width), lambda r: (0, 0))),
        scratch_shapes=[pltpu.VMEM((seq, seq), f32), pltpu.VMEM((2, seq, seq), bf16), pltpu.VMEM((width, 3 * width), f32)],
        compiler_params=pltpu.CompilerParams(vmem_limit_bytes=BIG),
        name="attn_bwd",
    )(seg.reshape(rows, 1, seq), qkv, dc, lse, delta, dh1, w, x)

RSQRT_2PI = 1.0 / math.sqrt(2 * math.pi)
def gelu_parts(u):
    phi_cdf = 0.5 + 0.5 * lax.erf(u * math.sqrt(0.5))
    dens = jnp.exp2(u * u * (-0.5 * LOG2E)) * RSQRT_2PI
    return u * phi_cdf, phi_cdf + u * dens

def mid_kernel(chunk, x_ref, c_ref, e_ref, wo_ref, win_ref, wd_ref, v_ref, bin_ref,
               out_ref, y1_ref, g_ref, dz_ref, du_ref, da_ref, dc_ref, dh1_ref, delta_ref, dv_ref, dbin_ref, gp_ref):
    i = pl.program_id(0)
    blk, width = x_ref.shape
    ff = win_ref.shape[1]
    @pl.when(i == 0)
    def _():
        dv_ref[...] = jnp.zeros_like(dv_ref)
        dbin_ref[...] = jnp.zeros_like(dbin_ref)
    g1, s1, g2, s2, bo, bd = (v_ref[j:j + 1, :] for j in (0, 1, 2, 3, 6, 7))
    cb = c_ref[...]
    h1 = x_ref[...].astype(f32) + (dot(cb, wo_ref[...]) + bo)
    cen = h1 - jnp.mean(h1, 1, keepdims=True)
    r1 = lax.rsqrt(jnp.mean(cen * cen, 1, keepdims=True) + EPS)
    n1 = cen * r1
    y1 = n1 * g1 + s1
    y1l = y1.astype(bf16)
    y1_ref[...] = y1l
    z = jnp.zeros((blk, width), f32)
    for j in range(ff // chunk):
        sl = slice(j * chunk, (j + 1) * chunk)
        u = dot(y1l, win_ref[:, sl]) + bin_ref[:, sl]
        g, gp = gelu_parts(u)
        gl = g.astype(bf16)
        g_ref[:, sl] = gl
        gp_ref[:, sl] = gp
        z += dot_nt(gl, wd_ref[:, sl])
    h2 = y1 + (z + bd)
    cen = h2 - jnp.mean(h2, 1, keepdims=True)
    r2 = lax.rsqrt(jnp.mean(cen * cen, 1, keepdims=True) + EPS)
    n2 = cen * r2
    out_ref[...] = (n2 * g2 + s2).astype(bf16)
    e = e_ref[...].astype(f32)
    eg = e * g2
    dh2 = r2 * (eg - jnp.mean(eg, 1, keepdims=True) - n2 * jnp.mean(eg * n2, 1, keepdims=True))
    dz = dh2.astype(bf16)
    dz_ref[...] = dz
    dy1 = dh2
    for j in range(ff // chunk):
        sl = slice(j * chunk, (j + 1) * chunk)
        du = (dot(dz, wd_ref[:, sl]) * gp_ref[:, sl]).astype(bf16)
        du_ref[:, sl] = du
        dbin_ref[:, sl] += jnp.sum(du.astype(f32), 0, keepdims=True)
        dy1 += dot_nt(du, win_ref[:, sl])
    dn = dy1 * g1
    dh1 = r1 * (dn - jnp.mean(dn, 1, keepdims=True) - n1 * jnp.mean(dn * n1, 1, keepdims=True))
    dh1_ref[...] = dh1
    da = dh1.astype(bf16)
    da_ref[...] = da
    dc = dot_nt(da, wo_ref[...]).astype(bf16)
    dc_ref[...] = dc
    prod = dc.astype(f32) * cb.astype(f32)
    hi = prod.astype(bf16)
    lo = (prod - hi.astype(f32)).astype(bf16)
    sel = jnp.where(lax.broadcasted_iota(jnp.int32, (16, width), 0) == lax.broadcasted_iota(jnp.int32, (16, width), 1) // HD, 1.0, 0.0).astype(bf16)
    delta_ref[...] = dot_nt(sel, hi) + dot_nt(sel, lo)
    parts = [dy1 * n1, dy1, e * n2, e, da.astype(f32), dz.astype(f32)]
    for j, t in zip((0, 1, 2, 3, 6, 7), parts):
        dv_ref[j:j + 1, :] += jnp.sum(t, 0, keepdims=True)

def mid(x, c, e, wo, win, wd, vec, bin_, blk=256, chunk=768):
    n, width = x.shape
    ff = win.shape[1]
    tok = lambda w: pl.BlockSpec((blk, w), lambda i: (i, 0))
    full = lambda a: pl.BlockSpec(a.shape, lambda i: (0, 0), pipeline_mode=pl.Buffered(1))
    sh = jax.ShapeDtypeStruct
    return pl.pallas_call(
        functools.partial(mid_kernel, chunk), grid=(n // blk,),
        out_shape=(sh((n, width), bf16), sh((n, width), bf16), sh((n, ff), bf16), sh((n, width), bf16), sh((n, ff), bf16),
                   sh((n, width), bf16), sh((n, width), bf16), sh((n, width), f32), sh((16, n), f32), sh((8, width), f32), sh((1, ff), f32)),
        in_specs=[tok(width), tok(width), tok(width), full(wo), full(win), full(wd), full(vec), full(bin_)],
        out_specs=(tok(width), tok(width), tok(ff), tok(width), tok(ff), tok(width), tok(width), tok(width),
                   pl.BlockSpec((16, blk), lambda i: (0, i)), pl.BlockSpec((8, width), lambda i: (0, 0)), pl.BlockSpec((1, ff), lambda i: (0, 0))),
        scratch_shapes=[pltpu.VMEM((blk, ff), f32)],
        compiler_params=pltpu.CompilerParams(vmem_limit_bytes=BIG),
        name="middle",
    )(x, c, e, wo, win, wd, vec, bin_)

def wgrad_kernel(a_ref, b_ref, o_ref):
    o_ref[...] = dot_tn(a_ref[...], b_ref[...]).astype(bf16)

def wgrad(a, b, blk=768):
    n, m = a.shape
    k = b.shape[1]
    return pl.pallas_call(wgrad_kernel, grid=(k // blk,), out_shape=jax.ShapeDtypeStruct((m, k), bf16),
        in_specs=[pl.BlockSpec((n, m), lambda j: (0, 0)), pl.BlockSpec((n, blk), lambda j: (0, j))],
        out_specs=pl.BlockSpec((m, blk), lambda j: (0, j)),
        compiler_params=pltpu.CompilerParams(vmem_limit_bytes=BIG), name="wgrad")(a, b)


LANES = 128
PIECE = 3 * LANES
GATHER_LAGS = (0, 2, 4, 6)
REDUCE_LAGS = (0, 2, 4, 6, 8)
AHEAD = 3
MESH = pl.DeviceIdType.MESH


class Place:
    def __init__(self):
        self.w = lax.axis_index("wide")
        self.x = lax.axis_index("narrow")
        self.core = lax.rem(self.w, 2)
        self.y = lax.rem(self.w // 2, 2)
        self.b = lax.rem(self.w // 4, 2)
        self.a = self.w // 8
        self.z = self.w // 4

    def z_peer(self, k):
        return lax.rem(self.z + k, 4)

    def over(self, name):
        if name == "x":
            return (self.w, 1 - self.x)
        if name in (1, 2, 3):
            return (4 * self.z_peer(name) + lax.rem(self.w, 4), self.x)
        step = {"a": 8, "b": 4, "y": 2, "core": 1}[name]
        return (self.w + step * (1 - 2 * getattr(self, name)), self.x)

    near = ("a", "b", "y", "x", "core")
    reduce_peers = (1, 2, 3, "y", "x", "core")

    def greet(self, names):
        for name in names:
            pl.semaphore_signal(pltpu.get_barrier_semaphore(), inc=1, device_id=self.over(name), device_id_type=MESH)

    def met(self, names):
        pl.semaphore_wait(pltpu.get_barrier_semaphore(), len(names))


def remote(src, dst, send, recv, device):
    return pltpu.make_async_remote_copy(src_ref=src, dst_ref=dst, send_sem=send, recv_sem=recv, device_id=device, device_id_type=MESH)


def when(condition, step):
    @pl.when(condition)
    def _():
        step()


def loop(count, step):
    lax.fori_loop(0, count, lambda i, _: (step(i), 0)[1], 0)


class Gather:
    def __init__(self, place, shard, full, sems, pieces):
        self.p, self.shard, self.full, self.pieces = place, shard, full, pieces
        self.sems = {name: (sems[2 * k], sems[2 * k + 1]) for k, name in enumerate(("a", "b", "y", "x", "core"))}
        self.kept = sems[10]
        self.own = pl.ds(place.x, 2)

    def mine(self, i, a):
        return self.full.at[i, self.own, a, self.p.b, self.p.y, self.p.core]

    def keep(self, i):
        return pltpu.make_async_copy(self.shard.at[i, self.own], self.mine(i, self.p.a), self.kept.at[i])

    def copy(self, name, i, incoming=False):
        p, f = self.p, self.full
        at = {n: (1 - getattr(p, n) if incoming and n == name else getattr(p, n)) for n in ("a", "b", "y", "x", "core")}
        every = slice(None)
        if name == "a":
            dst = self.mine(i, at["a"])
            src = self.shard.at[i, self.own]
        else:
            if name == "b":
                dst = f.at[i, self.own, :, at["b"], p.y, p.core]
            elif name == "y":
                dst = f.at[i, self.own, :, :, at["y"], p.core]
            elif name == "x":
                dst = f.at[i, 2 * at["x"], :, :, :, p.core]
            else:
                dst = f.at[i, :, :, :, :, at["core"]]
            src = dst
        send, recv = self.sems[name]
        return remote(src, dst, send.at[i], recv.at[i], p.over(name))

    def start(self, i):
        self.keep(i).start()
        self.copy("a", i).start()

    def b_step(self, i):
        self.keep(i).wait()
        self.copy("a", i, True).wait_recv()
        self.copy("b", i).start()

    def y_step(self, i):
        self.copy("b", i, True).wait_recv()
        self.copy("y", i).start()

    def x_step(self, i):
        self.copy("y", i, True).wait_recv()
        self.copy("x", i).start()

    def core_step(self, i):
        self.copy("x", i, True).wait_recv()
        self.copy("core", i).start()

    def arrive(self, i):
        self.copy("core", i, True).wait_recv()

    def turn(self, t):
        for k in range(2):
            ahead = AHEAD + 2 * t + k
            when(ahead < self.pieces, lambda ahead=ahead: self.start(ahead))
        for lag, step in zip(GATHER_LAGS, (self.b_step, self.y_step, self.x_step, self.core_step)):
            when((t >= lag) & (t < self.pieces + lag), lambda lag=lag, step=step: step(t - lag))

    def sent(self, i):
        for name in ("a", "b", "y", "x", "core"):
            self.copy(name, i).wait_send()


class GatherVector:
    def __init__(self, place, shard, full, sems):
        self.p, self.shard, self.full = place, shard, full
        self.sems = {name: (sems[2 * k], sems[2 * k + 1]) for k, name in enumerate(("a", "b", "y", "core"))}
        self.kept = sems[8]

    def keep(self):
        p = self.p
        return pltpu.make_async_copy(self.shard, self.full.at[p.a, p.b, p.y, p.core], self.kept)

    def copy(self, name, incoming=False):
        p = self.p
        at = {n: (1 - getattr(p, n) if incoming and n == name else getattr(p, n)) for n in ("a", "b", "y", "core")}
        every = slice(None)
        first = ("a", "b", "y", "core").index(name)
        dst = self.full.at[tuple(at[n] if n == name or n == "core" or k > first else every for k, n in enumerate(("a", "b", "y", "core")))]
        src = self.shard if name == "a" else dst
        send, recv = self.sems[name]
        return remote(src, dst, send, recv, p.over(name))

    def start(self):
        self.keep().start()
        self.copy("a").start()

    def step(self, name, then):
        if name == "a":
            self.keep().wait()
        self.copy(name, True).wait_recv()
        self.copy(then).start()

    def arrive(self):
        self.copy("core", True).wait_recv()

    def sent(self):
        for name in ("a", "b", "y", "core"):
            self.copy(name).wait_send()


def tile(ref, i, t):
    rows = 16 * ref.shape[-2]
    return ref[i, t].reshape(rows, LANES)


def columns(ref, *pieces):
    return jnp.concatenate([tile(ref, i, t) for i in pieces for t in range(3)], 1)


def doc_bias(seg_row, bias_ref, r):
    segf = seg_row.astype(f32)
    seq = segf.shape[1]
    rep = jnp.broadcast_to(segf, (LANES, seq)).T
    for j in range(seq // LANES):
        sl = slice(j * LANES, (j + 1) * LANES)
        bias_ref[r, :, sl] = jnp.where(rep == segf[:, sl], 0.0, NEG)


def stage_kernel(heads, x_hbm, seg_ref, e_hbm, aw_hbm, dw_hbm, vp_ref,
                 qkv_o, c_o, lse_o, w_o, out_o, y1_o, g_o, gp_o, dz_o, dh2_o, n1_o, r1_o, dv_o, vrow,
                 full, vfull, shard, vshard, square, xb, eb, cb, n1b, y1b, acc, gp, gb, dzb, bias, lsea, binr, r1b,
                 in_sem, out_sem, w_sem, *sems):
    place = Place()
    rows, seq = seg_ref.shape
    tokens, width = x_hbm.shape
    pairs = heads // 2
    pieces = shard.shape[0]
    chunks = gb.shape[0]
    own_rows = aw_hbm.shape[1]
    blk = 256
    big = 512
    g = Gather(place, shard, full, sems[:11], pieces)
    gv = GatherVector(place, vshard, vfull, sems[11:])

    loads = [pltpu.make_async_copy(aw_hbm.at[k], gp.at[0, pl.ds(k * own_rows, own_rows)], in_sem.at[k]) for k in range(4)]
    for k in range(2):
        for j in range(chunks):
            loads.append(pltpu.make_async_copy(
                dw_hbm.at[k, :, pl.ds(j * width, width)], gp.at[1 + k, pl.ds(j * own_rows, own_rows)], in_sem.at[4 + k * chunks + j]))
    n = len(loads)
    x_load = pltpu.make_async_copy(x_hbm, xb, in_sem.at[n])
    e_load = pltpu.make_async_copy(e_hbm, eb, in_sem.at[n + 1])
    for c in loads:
        c.start()
    place.greet(place.near)
    x_load.start()
    e_load.start()
    square[...] = jnp.zeros_like(square)
    lsea[...] = jnp.zeros_like(lsea)
    square[: vp_ref.shape[0], :own_rows] = vp_ref[...]
    vshard[...] = square[...].T[:own_rows].astype(bf16)

    def own_tile(k, j, t):
        return gp[k, j * own_rows : (j + 1) * own_rows, t * LANES : (t + 1) * LANES].astype(bf16)

    for c in loads[:3]:
        c.wait()
    for p in range(pairs):
        for t in range(3):
            shard[p, t] = own_tile(0, t, p)
    place.met(place.near)
    gv.start()
    for i in range(AHEAD):
        g.start(i)
    for c in loads[3:]:
        c.wait()
    for t in range(6):
        shard[pairs + t // 3, t % 3] = own_tile(0, 3, t)
        for j in range(chunks):
            for k in range(2):
                shard[pairs + 2 + 4 * j + 2 * k + t // 3, t % 3] = own_tile(1 + k, j, t)
    for r in range(rows):
        doc_bias(seg_ref[r : r + 1, :], bias, r)
    gv.step("a", "b")
    fill = GATHER_LAGS[-1] + 1
    for t in range(fill):
        g.turn(t)
        if t == 1:
            gv.step("b", "y")
        if t == 4:
            gv.step("y", "core")
    gv.arrive()
    vec = vfull[...].reshape(16 * own_rows, LANES).astype(f32).T
    vrow[...] = vec[: vrow.shape[0]]
    for j in range(chunks):
        binr[j] = vrow[8 + j : 9 + j, :]
    x_load.wait()

    first = lax.broadcasted_iota(jnp.int32, (LANES, LANES), 1) < HD
    lane = lax.broadcasted_iota(jnp.int32, (LANES, LANES), 1)
    ones = jnp.ones((seq, LANES), bf16)

    def qkv_at(p):
        return gb.at[p // 2, :, pl.ds(pl.multiple_of(lax.rem(p, 2) * PIECE, LANES), PIECE)]

    def qkv_out(p):
        return pltpu.make_async_copy(qkv_at(p), qkv_o.at[p], out_sem.at[p])

    def w_out(i):
        return pltpu.make_async_copy(full.at[i], w_o.at[i], w_sem.at[i])

    def pair(p):
        g.arrive(p)
        w_out(p).start()
        head = pl.ds(pl.multiple_of(p * LANES, LANES), LANES)
        w = columns(full, p)
        b = jnp.concatenate([vrow[4:5, head], jnp.zeros((1, LANES), f32), vrow[5:6, head]], 1)
        col = pl.multiple_of(lax.rem(p, 2) * PIECE, LANES)
        gb[p // 2, :, pl.ds(col, PIECE)] = (dot(xb[...], w) + b).astype(bf16)
        qkv_out(p).start()

        def row(r):
            tok = pl.ds(pl.multiple_of(r * seq, seq), seq)
            q2 = gb[p // 2, tok, pl.ds(col, LANES)]
            k2 = gb[p // 2, tok, pl.ds(col + LANES, LANES)]
            v2 = jnp.concatenate([gb[p // 2, tok, pl.ds(col + 2 * LANES, LANES)], ones], 1)
            for c in range(seq // LANES):
                lo, hi = key_range(c, seq, LANES)
                cut = slice(c * LANES, (c + 1) * LANES)
                outs = []
                la = lsea[r, cut, :]
                for h in range(2):
                    qm = jnp.where(first if h == 0 else ~first, q2[cut], jnp.zeros_like(q2[cut]))
                    s = dot_nt(qm, k2[lo:hi]) + bias[r, cut, lo:hi]
                    m = jnp.max(s, 1, keepdims=True)
                    o = dot(jnp.exp2((s - m) * SCALE2).astype(bf16), v2[lo:hi])
                    l = o[:, LANES:]
                    outs.append(o[:, :LANES] / l)
                    la = jnp.where(lane == 2 * p + h, m * SCALE2 + jnp.log(l) * LOG2E, la)
                lsea[r, cut, :] = la
                cb[pl.ds(pl.multiple_of(r * seq + c * LANES, LANES), LANES), head] = jnp.where(first, outs[0], outs[1]).astype(bf16)
            g.turn(fill + 2 * p + r)

        loop(rows, row)

    loop(pairs, pair)
    done = fill + 2 * pairs
    for r in range(rows):
        lse_o[r] = lsea[r].T[: lse_o.shape[1]]
    c_out = pltpu.make_async_copy(cb, c_o, out_sem.at[pairs])
    c_out.start()
    g1, s1, g2, s2, bo, bd = (vrow[j : j + 1, :] for j in (0, 1, 2, 3, 6, 7))

    def block(i):
        return pl.ds(pl.multiple_of(i * blk, blk), blk)

    for i in (pairs, pairs + 1):
        g.arrive(i)
        w_out(i).start()

    def norm_one(i):
        at = block(i)
        h1 = xb[at, :].astype(f32) + (dot(cb[at, :], columns(full, pairs, pairs + 1)) + bo)
        cen = h1 - jnp.mean(h1, 1, keepdims=True)
        r1 = lax.rsqrt(jnp.mean(cen * cen, 1, keepdims=True) + EPS)
        n1 = cen * r1
        y1 = n1 * g1 + s1
        n1b[at, :] = n1
        r1b[at, :] = jnp.broadcast_to(r1, (blk, LANES))
        y1b[at, :] = y1.astype(bf16)
        acc[at, :] = y1 + bd
        when(lax.rem(i, 2) == 1, lambda: g.turn(done + i // 2))

    loop(tokens // blk, norm_one)
    done += 2
    y1_out = pltpu.make_async_copy(y1b, y1_o, out_sem.at[pairs + 2])
    y1_out.start()
    n1_out = pltpu.make_async_copy(n1b, n1_o, out_sem.at[pairs + 1])
    n1_out.start()
    r1_out = pltpu.make_async_copy(r1b, r1_o, out_sem.at[pairs + 5 + chunks])
    r1_out.start()
    loop(pairs, lambda p: qkv_out(p).wait())

    def up(j):
        return columns(full, pairs + 2 + 4 * j, pairs + 3 + 4 * j)

    def down(j):
        return columns(full, pairs + 4 + 4 * j, pairs + 5 + 4 * j)

    def g_out(j):
        return pltpu.make_async_copy(gb.at[j], g_o.at[j], out_sem.at[pairs + 7 + j])

    def gp_out(j):
        return pltpu.make_async_copy(gp.at[j], gp_o.at[j], out_sem.at[pairs + 7 + chunks + j])

    def ff_chunk(j):
        def ready(k):
            for t in (k, k + 1):
                g.arrive(pairs + 2 + 4 * j + t)
                w_out(pairs + 2 + 4 * j + t).start()

        def up_block(i):
            at = pl.ds(pl.multiple_of(i * big, big), big)
            act, slope = gelu_parts(dot(y1b[at, :], up(j)) + binr[j])
            gb[j, at, :] = act.astype(bf16)
            gp[j, at, :] = slope
            g.turn(done + 4 * j + i)

        def down_block(i):
            at = pl.ds(pl.multiple_of(i * big, big), big)
            acc[at, :] += dot_nt(gb[j, at, :], down(j))
            g.turn(done + 4 * j + 2 + i)

        ready(0)
        loop(tokens // big, up_block)
        g_out(j).start()
        gp_out(j).start()
        ready(2)
        loop(tokens // big, down_block)

    loop(chunks, ff_chunk)
    e_load.wait()
    dv_o[...] = jnp.zeros_like(dv_o)

    def colsum(t):
        return jnp.sum(t, 0, keepdims=True)

    def norm_two(i):
        at = block(i)
        h2 = acc[at, :]
        cen = h2 - jnp.mean(h2, 1, keepdims=True)
        r2 = lax.rsqrt(jnp.mean(cen * cen, 1, keepdims=True) + EPS)
        n2 = cen * r2
        xb[at, :] = (n2 * g2 + s2).astype(bf16)
        e = eb[at, :].astype(f32)
        eg = e * g2
        dh2 = r2 * (eg - jnp.mean(eg, 1, keepdims=True) - n2 * jnp.mean(eg * n2, 1, keepdims=True))
        dz = dh2.astype(bf16)
        dzb[at, :] = dz
        acc[at, :] = dh2
        dv_o[2:3, :] += colsum(e * n2)
        dv_o[3:4, :] += colsum(e)
        dv_o[7:8, :] += colsum(dz.astype(f32))

    loop(tokens // blk, norm_two)
    last = [pltpu.make_async_copy(s, d, out_sem.at[pairs + k]) for k, (s, d) in ((3, (xb, out_o)), (4, (dzb, dz_o)), (6, (acc, dh2_o)))]
    for c in last:
        c.start()
    gv.sent()
    loop(pieces, g.sent)
    loop(pieces, lambda i: w_out(i).wait())
    for c in [c_out, y1_out, n1_out, r1_out] + last:
        c.wait()
    loop(chunks, lambda j: g_out(j).wait())
    loop(chunks, lambda j: gp_out(j).wait())


def stage(x, seg, e, aw, dw, vp):
    rows, seq = seg.shape
    tokens, width = x.shape
    own_rows, ff = dw.shape[1:]
    heads, chunks = width // HD, ff // width
    pairs = heads // 2
    pieces = pairs + 2 + 4 * chunks
    sh = jax.ShapeDtypeStruct
    dma = pltpu.SemaphoreType.DMA
    v = pltpu.VMEM
    hbm = pl.BlockSpec(memory_space=pl.ANY)
    vmem = pl.BlockSpec(memory_space=pltpu.VMEM)
    tok = sh((tokens, width), bf16)
    wide = sh((chunks, tokens, width), bf16)
    long = sh((tokens, width), f32)
    block = (2, 2, 2, 2, own_rows, LANES)
    scratch = [
        v((pieces, 3) + block, bf16), v(block, bf16), v((pieces, 3, own_rows, LANES), bf16), v((own_rows, LANES), bf16),
        v((LANES, LANES), f32), v((tokens, width), bf16), v((tokens, width), bf16), v((tokens, width), bf16),
        v((tokens, width), f32), v((tokens, width), bf16), v((tokens, width), f32), v((chunks, tokens, width), f32),
        v((chunks, tokens, width), bf16), v((tokens, width), bf16), v((rows, seq, seq), f32), v((rows, seq, LANES), f32),
        v((chunks, 1, width), f32), v((tokens, LANES), f32),
        dma((6 + 2 * chunks,)), dma((pairs + 7 + 2 * chunks,)), dma((pieces,)),
    ] + [dma((pieces,))] * 11 + [dma(())] * 9
    return pl.pallas_call(
        functools.partial(stage_kernel, heads),
        out_shape=(sh((pairs, tokens, PIECE), bf16), tok, sh((rows, 16, seq), f32), sh((pieces, 3) + block, bf16), tok, tok, wide,
                   sh((chunks, tokens, width), f32), tok, long, long, sh((tokens, LANES), f32), sh((8, width), f32), sh((16, width), f32)),
        in_specs=[hbm, vmem, hbm, hbm, hbm, vmem],
        out_specs=(hbm, hbm, vmem) + (hbm,) * 9 + (vmem, vmem),
        scratch_shapes=scratch,
        compiler_params=pltpu.CompilerParams(collective_id=0, has_side_effects=True, vmem_limit_bytes=BIG),
        name="stage",
    )(x, seg, e, aw, dw, vp)


class Reduce:
    def __init__(self, place, part, froms, done, out, sems, pieces, tiles=3):
        self.p, self.part, self.done, self.out, self.pieces, self.whole = place, part, done, out, pieces, tiles == 1
        self.names = ("core", "y", "p") if self.whole else ("core", "y", "p", "x")
        self.froms = dict(zip(("core", "y", "p", "z", "x"), froms))
        self.zs, self.zr = sems[:2]
        self.sems = {name: (sems[2 + 2 * k], sems[3 + 2 * k]) for k, name in enumerate(self.names)}
        self.own = pl.ds(0, 1) if self.whole else pl.ds(place.x, 2)

    def copy(self, name, i):
        p, f = self.p, self.part
        if name == "core":
            src = f.at[i, :, :, :, 1 - p.core]
        elif name == "x":
            src = f.at[i, 2 * (1 - p.x), :, :, p.core]
        elif name == "y":
            src = f.at[i, self.own, :, 1 - p.y, p.core]
        else:
            src = self.done.at[i]
        send, recv = self.sems[name]
        return remote(src, self.froms[name].at[i], send.at[i], recv.at[i], p.over("x" if name == "p" else name))

    def z_copy(self, i, k, incoming=False):
        p = self.p
        peer = p.z_peer(k)
        came = peer if incoming else p.z
        return remote(self.part.at[i, self.own, peer, p.y, p.core], self.froms["z"].at[i, came], self.zs.at[i, k], self.zr.at[i, came], p.over(k))

    def start(self, i):
        self.copy("core", i).start()

    def x_step(self, i):
        p, f = self.p, self.part
        self.copy("core", i).wait_recv()
        for t in range(1 if self.whole else 3):
            f[i, t, :, :, p.core] = f[i, t, :, :, p.core] + self.froms["core"][i, t]
        self.copy("y" if self.whole else "x", i).start()

    def y_step(self, i):
        p, f = self.p, self.part
        self.copy("x", i).wait_recv()
        f[i, 2 * p.x, :, :, p.core] = f[i, 2 * p.x, :, :, p.core] + self.froms["x"][i]
        self.copy("y", i).start()

    def z_step(self, i):
        p, f = self.p, self.part
        self.copy("y", i).wait_recv()
        f[i, self.own, :, p.y, p.core] = f[i, self.own, :, p.y, p.core] + self.froms["y"][i]
        for k in (2, 1, 3):
            self.z_copy(i, k).start()

    def p_step(self, i):
        p, f = self.p, self.part
        total = f[i, self.own, p.z, p.y, p.core].astype(f32)
        for k in (1, 2, 3):
            self.z_copy(i, k, True).wait_recv()
            total += self.froms["z"][i, p.z_peer(k)].astype(f32)
        self.done[i] = total.astype(bf16)
        self.copy("p", i).start()

    def finish(self, i):
        self.copy("p", i).wait_recv()
        a, b = self.done[i].astype(f32), self.froms["p"][i].astype(f32)
        if self.whole:
            self.out[i] = a[0] + b[0]
            return
        first = self.p.x == 0
        low, high = jnp.where(first, a, b), jnp.where(first, b, a)
        self.out[i] = jnp.concatenate([low[0], low[1] + high[0], high[1]], 1)

    def turn(self, t):
        for lag, step in zip(REDUCE_LAGS, (self.x_step, self.y_step, self.z_step, self.p_step, self.finish)):
            when((t >= lag) & (t < self.pieces + lag), lambda lag=lag, step=step: step(t - lag))

    def sent(self, i):
        for name in self.names:
            self.copy(name, i).wait_send()
        for k in (1, 2, 3):
            self.z_copy(i, k).wait_send()


def back_kernel(heads, x_hbm, c_hbm, y1_hbm, dz_hbm, dh2_hbm, n1_hbm, r1_hbm, g_hbm, gp_hbm, qkv_hbm, w_hbm,
                seg_ref, lse_ref, dv_ref, vec_ref, gin_o, sum_o, vsum_o,
                part, fromc, fromy, fromp, fromz, fromx, done, vpart, vfromc, vfromy, vfromp, vfromz, vdone, pool, wpool, gpool, acc, cb, dab, dcb, r1b, delta, vrow,
                ld, out_sem, *sems):
    place = Place()
    rows, seq = seg_ref.shape
    tokens, width = x_hbm.shape
    pairs = heads // 2
    chunks = g_hbm.shape[0]
    own_rows = part.shape[-2]
    pieces = part.shape[0]
    big = 512
    r_ = Reduce(place, part, (fromc, fromy, fromp, fromz, fromx), done, sum_o, sems[:10], pieces)
    rv = Reduce(place, vpart, (vfromc, vfromy, vfromp, vfromz), vdone, vsum_o, sems[10:], 1, 1)
    ff_pieces = 4 * chunks
    first_ff = pairs + 2
    du, dz, y1 = pool.at[2], pool.at[3], pool.at[4]
    x = y1

    def load(k, src, dst):
        return pltpu.make_async_copy(src, dst, ld.at[k])

    g_in = [load(j, g_hbm.at[j], pool.at[j % 2]) for j in range(chunks)]
    gp_in = [load(chunks + j, gp_hbm.at[j], gpool.at[j % 2]) for j in range(chunks)]
    w_in = [load(2 * chunks + j, w_hbm.at[pl.ds(first_ff + 4 * j, 4)], wpool.at[pl.ds(4 * (j % 2), 4)]) for j in range(chunks)]
    base = 3 * chunks
    dz_in, y1_in, acc_in, c_in, r1_in = (load(base + k, s, d) for k, (s, d) in enumerate(
        ((dz_hbm, dz), (y1_hbm, y1), (dh2_hbm, acc), (c_hbm, cb), (r1_hbm, r1b))))
    base += 5
    n1_in = load(base, n1_hbm, gpool.at[0])
    wo_in = load(base + 1, w_hbm.at[pl.ds(pairs, 2)], wpool.at[pl.ds(0, 2)])
    wq_in = load(base + 2, w_hbm.at[pl.ds(0, pairs)], wpool.at[pl.ds(2, pairs)])
    x_in = load(base + 3, x_hbm, x)
    base += 4

    def q_in(p):
        return load(base + p, qkv_hbm.at[p], pool.at[3, :, pl.ds(pl.multiple_of(lax.rem(p, 2) * PIECE, LANES), PIECE)])

    for c in (dz_in, g_in[0]):
        c.start()
    place.greet(place.reduce_peers)
    place.met(place.reduce_peers)
    vrow[...] = jnp.zeros_like(vrow)
    vrow[:8, :] = dv_ref[...]

    def colsum(t):
        return jnp.sum(t, 0, keepdims=True)

    half = width // 2

    def weight_grad(left, right, piece, count):
        def product(a):
            d = dot_tn(left[:, pl.ds(pl.multiple_of(a * half, LANES), half)], right)
            for t in range(3 * count):
                part[piece + t // 3, t % 3, pl.ds(2 * a, 2)] = d[:, t * LANES : (t + 1) * LANES].astype(bf16).reshape(2, 2, 2, own_rows, LANES)

        loop(2, product)
        for k in range(count):
            r_.start(piece + k)

    dz_in.wait()
    for j in range(chunks):
        s = j % 2
        g_in[j].wait()
        if j == 0:
            for c in (gp_in[0], w_in[0], acc_in, y1_in, g_in[1], gp_in[1], w_in[1], c_in, r1_in):
                c.start()
        weight_grad(dz, pool[s], 4 * j, 2)
        r_.turn(3 * j)
        gp_in[j].wait()
        w_in[j].wait()
        if j == 0:
            y1_in.wait()
            acc_in.wait()

        def block(i, j=j, s=s):
            at = pl.ds(pl.multiple_of(i * big, big), big)
            d = (dot(dz[at, :], columns(wpool, 4 * s + 2, 4 * s + 3)) * gpool[s, at, :]).astype(bf16)
            du[at, :] = d
            acc[at, :] += dot_nt(d, columns(wpool, 4 * s, 4 * s + 1))
            vrow[8 + j : 9 + j, :] += colsum(d.astype(f32))

        loop(tokens // big, block)
        r_.turn(3 * j + 1)
        if j + 2 < chunks:
            g_in[j + 2].start()
            gp_in[j + 2].start()
            w_in[j + 2].start()
        if j == chunks - 2:
            n1_in.start()
            wo_in.start()
        weight_grad(y1, du[...], 4 * j + 2, 2)
        r_.turn(3 * j + 2)
    wq_in.start()
    x_in.start()
    q_in(0).start()
    q_in(1).start()
    for r in range(rows):
        segf = seg_ref[r : r + 1, :].astype(f32)
        rep = jnp.broadcast_to(segf, (LANES, seq)).T
        for k in range(seq // LANES):
            sl = slice(k * LANES, (k + 1) * LANES)
            gpool[1, r * seq : (r + 1) * seq, sl] = jnp.where(rep == segf[:, sl], 0.0, NEG)
    c_in.wait()
    r1_in.wait()
    n1_in.wait()
    wo_in.wait()
    g1 = vec_ref[0:1, :]
    sel_shape = (delta.shape[0], width)
    sel = jnp.where(lax.broadcasted_iota(jnp.int32, sel_shape, 0) == lax.broadcasted_iota(jnp.int32, sel_shape, 1) // HD, 1.0, 0.0).astype(bf16)

    def norm_one_back(i):
        at = pl.ds(pl.multiple_of(i * 256, 256), 256)
        dy1 = acc[at, :]
        n1 = gpool[0, at, :]
        dn = dy1 * g1
        r1 = r1b[at, :1]
        dh1 = r1 * (dn - jnp.mean(dn, 1, keepdims=True) - n1 * jnp.mean(dn * n1, 1, keepdims=True))
        acc[at, :] = dh1
        da = dh1.astype(bf16)
        dab[at, :] = da
        dc = dot_nt(da, columns(wpool, 0, 1)).astype(bf16)
        dcb[at, :] = dc
        prod = dc.astype(f32) * cb[at, :].astype(f32)
        hi = prod.astype(bf16)
        lo = (prod - hi.astype(f32)).astype(bf16)
        delta[:, at] = dot_nt(sel, hi) + dot_nt(sel, lo)
        vrow[0:1, :] += colsum(dy1 * n1)
        vrow[1:2, :] += colsum(dy1)
        vrow[6:7, :] += colsum(da.astype(f32))

    loop(tokens // 256, norm_one_back)
    r_.turn(3 * chunks)
    weight_grad(cb, dab[...], ff_pieces, 2)
    r_.turn(3 * chunks + 1)
    t0 = 3 * chunks + 2
    twice = ff_pieces + 2 - t0
    x_in.wait()
    first_seq = lax.broadcasted_iota(jnp.int32, (seq, LANES), 1) < HD

    def pair(p):
        head = pl.ds(pl.multiple_of(p * LANES, LANES), LANES)
        col = pl.multiple_of(lax.rem(p, 2) * PIECE, LANES)
        to = p // 2
        q_in(p).wait()

        def row(r):
            tok = pl.ds(pl.multiple_of(r * seq, seq), seq)
            q2 = pool[3, tok, pl.ds(col, LANES)]
            k2 = pool[3, tok, pl.ds(col + LANES, LANES)]
            v2 = pool[3, tok, pl.ds(col + 2 * LANES, LANES)]
            dc2 = dcb[tok, head]
            zero = jnp.zeros_like(k2)
            near = gpool[1, tok, :seq]
            grads = []
            for h in range(2):
                lse = lse_ref[r, pl.ds(2 * p + h, 1), :]
                dl = delta[pl.ds(2 * p + h, 1), tok]
                own = first_seq if h == 0 else ~first_seq
                pt = jnp.exp2((dot_nt(jnp.where(own, k2, zero), q2) + near) * SCALE2 - lse)
                ds = (pt * (dot_nt(jnp.where(own, v2, zero), dc2) - dl)).astype(bf16)
                dv = dot(pt.astype(bf16), dc2)
                grads.append((dot_tn(ds, k2) * 0.125, dot(ds, q2) * 0.125, dv))
            for k, (a, b) in enumerate(zip(*grads)):
                pool[to, tok, pl.ds(col + k * LANES, LANES)] = jnp.where(first_seq, a, b).astype(bf16)
            when((r == 0) & (p < twice), lambda: r_.turn(t0 + 2 * p))

        loop(rows, row)
        when(p + 2 < pairs, lambda: q_in(p + 2).start())
        d = pool[to, :, pl.ds(col, PIECE)]
        weight_grad(x, d, ff_pieces + 2 + p, 1)
        sums = colsum(d.astype(f32))
        vrow[4:5, head] = sums[:, :LANES]
        vrow[5:6, head] = sums[:, 2 * LANES :]
        r_.turn(t0 + p + jnp.minimum(p + 1, twice))

    loop(pairs, pair)
    t0 += pairs + twice
    vpart[0, 0] = vrow[...].T.astype(bf16).reshape(4, 2, 2, own_rows, LANES)
    rv.start(0)
    left = pieces - t0
    loop(left, lambda i: r_.turn(t0 + i))
    t0 += left
    wq_in.wait()
    blocks = tokens // 256

    def gin_block(i):
        at = pl.ds(pl.multiple_of(i * 256, 256), 256)
        d = jnp.concatenate([pool[k, at, :] for k in range(pairs // 2)], 1)
        dcb[at, :] = (acc[at, :] + dot_nt(d, columns(wpool, *range(2, 2 + pairs)))).astype(bf16)
        r_.turn(t0 + i)
        for k, step in ((0, rv.x_step), (2, rv.z_step)):
            when(i == k, lambda step=step: step(0))

    loop(blocks, gin_block)
    gin_out = pltpu.make_async_copy(dcb, gin_o, out_sem)
    gin_out.start()
    rv.p_step(0)
    loop(REDUCE_LAGS[-1] - blocks, lambda i: r_.turn(t0 + blocks + i))
    rv.finish(0)
    loop(pieces, r_.sent)
    rv.sent(0)
    gin_out.wait()


def back(x, c, y1, dz, dh2, n1, r1, g, gp, qkv, w, seg, lse, dv, vec):
    rows, seq = seg.shape
    tokens, width = x.shape
    chunks = g.shape[0]
    own_rows = w.shape[-2]
    heads = width // HD
    pairs = heads // 2
    pieces = 4 * chunks + 2 + pairs
    sh = jax.ShapeDtypeStruct
    dma = pltpu.SemaphoreType.DMA
    v = pltpu.VMEM
    hbm = pl.BlockSpec(memory_space=pl.ANY)
    vmem = pl.BlockSpec(memory_space=pltpu.VMEM)
    tail = (own_rows, LANES)
    tok = v((tokens, width), bf16)
    scratch = [
        v((pieces, 3, 4, 2, 2) + tail, bf16), v((pieces, 3, 4, 2) + tail, bf16), v((pieces, 2, 4) + tail, bf16), v((pieces, 2) + tail, bf16),
        v((pieces, 4, 2) + tail, bf16), v((pieces, 4, 2) + tail, bf16), v((pieces, 2) + tail, bf16),
        v((1, 1, 4, 2, 2) + tail, bf16), v((1, 1, 4, 2) + tail, bf16), v((1, 1, 4) + tail, bf16), v((1, 1) + tail, bf16),
        v((1, 4, 1) + tail, bf16), v((1, 1) + tail, bf16), v((5, tokens, width), bf16), v((8,) + w.shape[1:], bf16), v((2, tokens, width), f32),
        v((tokens, width), f32), tok, tok, tok, v((tokens, LANES), f32), v((16, tokens), f32),
        v((LANES, width), f32),
        dma((3 * chunks + 9 + pairs,)), dma(())] + [dma((pieces, 4))] * 2 + [dma((pieces,))] * 8 + [dma((1, 4))] * 2 + [dma((1,))] * 6
    return pl.pallas_call(
        functools.partial(back_kernel, heads),
        out_shape=(sh((tokens, width), bf16), sh((pieces, own_rows, PIECE), f32), sh((1, own_rows, LANES), f32)),
        in_specs=[hbm] * 11 + [vmem] * 4,
        out_specs=(hbm, vmem, vmem),
        scratch_shapes=scratch,
        compiler_params=pltpu.CompilerParams(collective_id=1, has_side_effects=True, vmem_limit_bytes=63 * 2**20),
        name="back",
    )(x, c, y1, dz, dh2, n1, r1, g, gp, qkv, w, seg, lse, dv, vec)


def update_kernel(rates, sum_ref, vsum_ref, gin_hbm, out_hbm, am, aw, aa, dm, dw, da, vm, vw, va,
                  gin_o, out_o, am_o, aw_o, aa_o, dm_o, dw_o, da_o, vm_o, vw_o, va_o, square, tok, att, den, ld, st):
    matrix, vector, replicas = rates
    moves = [(dm, den.at[0], dm_o), (dw, den.at[1], dw_o), (da, den.at[2], da_o), (am, att.at[0], am_o), (aw, att.at[1], aw_o),
             (aa, att.at[2], aa_o), (gin_hbm, tok.at[0], gin_o), (out_hbm, tok.at[1], out_o)]
    loads = [pltpu.make_async_copy(s, d, ld.at[k]) for k, (s, d, _) in enumerate(moves)]
    stores = [pltpu.make_async_copy(d, o, st.at[k]) for k, (_, d, o) in enumerate(moves)]
    for c in loads:
        c.start()

    def advance(grad, rate, moment, weight, average):
        grad = grad / replicas
        moment = momentum_decay * moment + grad
        weight = weight - rate * (grad + momentum_decay * moment)
        return moment, weight, average_decay * average + (1.0 - average_decay) * weight

    def advance_in(grad, ref, index):
        news = advance(grad, matrix, *(ref[(k,) + index] for k in range(3)))
        for k in range(3):
            ref[(k,) + index] = news[k]

    rows, own = vm.shape
    square[...] = jnp.zeros_like(square)
    square[:own, :] = vsum_ref[0]
    vm_o[...], vw_o[...], va_o[...] = advance(square[...].T[:rows, :own], vector, vm[...], vw[...], va[...])
    every = slice(None)
    pairs = att.shape[3] // LANES
    ff_pieces = sum_ref.shape[0] - 2 - pairs
    for c in loads[:3]:
        c.wait()
    for i in range(ff_pieces):
        col = i // 4 * 2 * PIECE + i % 2 * PIECE
        advance_in(sum_ref[i], den, (1 - i % 4 // 2, every, slice(col, col + PIECE)))
    for c in stores[:3]:
        c.start()
    for c in loads[3:6]:
        c.wait()
    for i in range(2):
        advance_in(sum_ref[ff_pieces + i], att, (3, every, slice(i * PIECE, (i + 1) * PIECE)))
    for p in range(pairs):
        for k in range(3):
            advance_in(sum_ref[ff_pieces + 2 + p, :, k * LANES : (k + 1) * LANES], att, (k, every, slice(p * LANES, (p + 1) * LANES)))
    for c in loads[6:]:
        c.wait()
    for c in stores[3:]:
        c.start()
    for c in stores:
        c.wait()


def update(rates, sums, vsums, gin, out, states):
    am, dm = states[0], states[3]
    sh = jax.ShapeDtypeStruct
    v = pltpu.VMEM
    hbm = pl.BlockSpec(memory_space=pl.ANY)
    vmem = pl.BlockSpec(memory_space=pltpu.VMEM)
    places = [hbm] * 8 + [vmem] * 3
    return pl.pallas_call(
        functools.partial(update_kernel, rates),
        out_shape=(sh(gin.shape, bf16), sh(out.shape, bf16)) + tuple(sh(s.shape, f32) for s in states),
        in_specs=[vmem, vmem] + places,
        out_specs=tuple(places),
        scratch_shapes=[v((LANES, LANES), f32), v((2,) + gin.shape, bf16), v((3,) + am.shape, f32), v((3,) + dm.shape, f32),
                        pltpu.SemaphoreType.DMA((8,)), pltpu.SemaphoreType.DMA((8,))],
        compiler_params=pltpu.CompilerParams(vmem_limit_bytes=BIG),
        name="update",
    )(sums, vsums, gin, out, *states)


def pack_columns(attention, dense, vectors):
    count = vectors.shape[0]
    vector_cols = jnp.pad(vectors.T, ((0, 0), (0, 128 - count)))
    first = jnp.concatenate([attention[0], attention[1], attention[2], vector_cols], 1)
    second = jnp.concatenate([attention[3], dense[0], dense[1]], 1)
    return first, second


def advance(gradient, moment, weight, average, step_rate):
    moment_new = momentum_decay * moment + gradient
    weight_new = weight - step_rate * (gradient + momentum_decay * moment_new)
    average_new = average_decay * average + (1.0 - average_decay) * weight_new
    return (moment_new, weight_new, average_new)


def plain_body(
    hidden_in,
    segment_ids,
    cotangent,
    attention_weights,
    attention_momentum,
    attention_average,
    dense_weights,
    dense_momentum,
    dense_average,
    vector_params,
    vector_momentum,
    vector_average,
):
    row_count, length, width = hidden_in.shape
    ff = dense_weights.shape[-1]
    vector_rows = vector_params.shape[0]
    x = hidden_in.reshape(-1, width)
    e = cotangent.reshape(-1, width)
    first, second = pack_columns(attention_weights, dense_weights, vector_params)
    first_full = lax.all_gather(first.astype(bf16), "wide", axis=0, tiled=True)
    second_full = lax.all_gather(second.astype(bf16), "wide", axis=0, tiled=True)
    vec = first_full[:, 3 * width : 3 * width + vector_rows].astype(f32).T
    bias_qkv = jnp.concatenate([vec[4:5], jnp.zeros((1, width), f32), vec[5:6]], 1)
    w_qkv = first_full[:, : 3 * width]
    wo, win, wd = (second_full[:, :width], second_full[:, width : width + ff], second_full[:, width + ff :])
    qkv, c, lse = attn_fwd(x, segment_ids, w_qkv, bias_qkv)
    out, y1, g, dz, du, da, dc, dh1, delta, dvec, dbin = mid(
        x, c, e, wo, win, wd, vec, vec[8:].reshape(1, ff)
    )
    grad_second = jnp.concatenate([wgrad(c, da), wgrad(y1, du), wgrad(dz, g)], 1)
    share_second = lax.psum_scatter(grad_second, "wide", scatter_dimension=0, tiled=True)
    dqkv, gin, dw, db = attn_bwd(segment_ids, qkv, dc, lse, delta, dh1, w_qkv, x)
    dvec = jnp.concatenate(
        [dvec[:4], db[:, :width], db[:, 2 * width :], dvec[6:8], dbin.reshape(-1, width)], 0
    )
    grad_first = jnp.concatenate(
        [dw, jnp.pad(dvec.T, ((0, 0), (0, 128 - vector_rows))).astype(bf16)], 1
    )
    share_first = lax.psum_scatter(grad_first, "wide", scatter_dimension=0, tiled=True)
    replicas = lax.axis_size("narrow")
    tokens_all = row_count * length * lax.axis_size("wide") * replicas
    grad_scale = math.sqrt(tokens_all) / replicas
    t1 = lax.psum(share_first, "narrow").astype(f32) / replicas
    t2 = lax.psum(share_second, "narrow").astype(f32) / replicas
    cut = lambda t, j: t[:, j * width : (j + 1) * width]
    attention_grad = jnp.stack([cut(t1, 0), cut(t1, 1), cut(t1, 2), cut(t2, 0)])
    dense_grad = jnp.stack([t2[:, width : width + ff], t2[:, width + ff :]])
    vector_grad = t1[:, 3 * width : 3 * width + vector_rows].T
    attention_new = advance(attention_grad, attention_momentum, attention_weights, attention_average, matrix_rate / grad_scale)
    dense_new = advance(dense_grad, dense_momentum, dense_weights, dense_average, matrix_rate / grad_scale)
    vector_new = advance(vector_grad, vector_momentum, vector_params, vector_average, vector_rate / grad_scale)
    return (out.reshape(hidden_in.shape), gin.reshape(hidden_in.shape)) + attention_new + dense_new + vector_new


def body(
    hidden_in,
    segment_ids,
    cotangent,
    attention_weights,
    attention_momentum,
    attention_average,
    dense_weights,
    dense_momentum,
    dense_average,
    vector_params,
    vector_momentum,
    vector_average,
):
    row_count, length, width = hidden_in.shape
    x = hidden_in.reshape(-1, width)
    e = cotangent.reshape(-1, width)
    replicas = lax.axis_size("narrow")
    tokens_all = row_count * length * lax.axis_size("wide") * replicas
    grad_scale = math.sqrt(tokens_all) / replicas
    rates = (matrix_rate / grad_scale, vector_rate / grad_scale, replicas)
    qkv, c, lse, w, out, y1, g, gp, dz, dh2, n1, r1, dv, vec = stage(
        x, segment_ids, e, attention_weights, dense_weights, vector_params
    )
    states = (
        attention_momentum, attention_weights, attention_average,
        dense_momentum, dense_weights, dense_average,
        vector_momentum, vector_params, vector_average,
    )
    gin, sums, vsums = back(x, c, y1, dz, dh2, n1, r1, g, gp, qkv, w, segment_ids, lse, dv, vec)
    news = update(rates, sums, vsums, gin, out, states)
    return (news[1].reshape(hidden_in.shape), news[0].reshape(hidden_in.shape)) + tuple(news[2:])


def solution(mesh):
    token = P(("wide", "narrow"), None, None)
    matrix = P(None, "wide", None)
    vector = P(None, "wide")
    in_specs = (token, P(("wide", "narrow"), None), token) + (matrix,) * 6 + (vector,) * 3
    out_specs = (token, token) + (matrix,) * 6 + (vector,) * 3
    ours = mesh.shape["wide"] == 16 and mesh.shape["narrow"] == 2
    return jax.shard_map(body if ours else plain_body, mesh=mesh, in_specs=in_specs, out_specs=out_specs, check_vma=False)
```

```python
import functools, math
import jax, jax.numpy as jnp
from jax import lax
from jax.sharding import PartitionSpec as P
from jax.experimental import pallas as pl
from jax.experimental.pallas import tpu as pltpu

HD = 64
LOG2E = 1.4426950408889634
SCALE2 = 0.125 * LOG2E
NEG = -1e30
EPS = 1e-12
momentum_decay = 0.5
average_decay = 0.5
matrix_rate = 0.03
vector_rate = 0.3
f32, bf16 = jnp.float32, jnp.bfloat16
BIG = 60 * 2**20

def dot(a, b):
    return lax.dot_general(a, b, (((1,), (0,)), ((), ())), preferred_element_type=f32)
def dot_nt(a, b):
    return lax.dot_general(a, b, (((1,), (1,)), ((), ())), preferred_element_type=f32)
def dot_tn(a, b):
    return lax.dot_general(a, b, (((0,), (0,)), ((), ())), preferred_element_type=f32)

def key_range(c, seq, blk):
    lo = max(0, c * blk - seq // 2 + 1) // blk * blk
    hi = min(seq, -(-((c + 1) * blk - 1 + seq // 2) // blk) * blk)
    return lo, hi

def fill_bias(seg_ref, bias_ref):
    segf = seg_ref[0].astype(f32)
    seq = segf.shape[1]
    rep = jnp.broadcast_to(segf, (128, seq)).T
    for j in range(seq // 128):
        bias_ref[:, j * 128:(j + 1) * 128] = jnp.where(rep == segf[:, j * 128:(j + 1) * 128], 0.0, NEG)

def fwd_kernel(blk, x_ref, seg_ref, w_ref, b_ref, qkv_ref, c_ref, lse_ref, bias_ref, lsea_ref):
    seq, width = x_ref.shape
    x = x_ref[...]
    for j in range(3):
        sl = slice(j * width, (j + 1) * width)
        qkv_ref[:, sl] = (dot(x, w_ref[:, sl]) + b_ref[:, sl]).astype(bf16)
    fill_bias(seg_ref, bias_ref)
    lane = lax.broadcasted_iota(jnp.int32, (blk, 128), 1)
    first = lane < HD
    ones = jnp.ones((seq, 128), bf16)
    def pair(p, _):
        col = pl.multiple_of(p * 128, 128)
        q2 = qkv_ref[:, pl.ds(col, 128)]
        k2 = qkv_ref[:, pl.ds(col + width, 128)]
        v2 = jnp.concatenate([qkv_ref[:, pl.ds(col + 2 * width, 128)], ones], 1)
        for c in range(seq // blk):
            lo, hi = key_range(c, seq, blk)
            rows = slice(c * blk, (c + 1) * blk)
            qc = q2[rows]
            outs = []
            la = lsea_ref[rows, :]
            for h in range(2):
                qm = jnp.where(first if h == 0 else ~first, qc, jnp.zeros_like(qc))
                s = dot_nt(qm, k2[lo:hi]) + bias_ref[rows, lo:hi]
                m = jnp.max(s, 1, keepdims=True)
                e = jnp.exp2((s - m) * SCALE2)
                o = dot(e.astype(bf16), v2[lo:hi])
                l = o[:, 128:]
                outs.append(o[:, :128] / l)
                la = jnp.where(lane == 2 * p + h, m * SCALE2 + jnp.log(l) * LOG2E, la)
            lsea_ref[rows, :] = la
            c_ref[rows, pl.ds(col, 128)] = jnp.where(first, outs[0], outs[1]).astype(bf16)
        return 0
    lax.fori_loop(0, width // 128, pair, 0)
    lse_ref[0] = lsea_ref[...].T[:lse_ref.shape[1]]

def attn_fwd(x, seg, w, b, blk=128):
    rows, seq = seg.shape
    width = x.shape[1]
    return pl.pallas_call(
        functools.partial(fwd_kernel, blk), grid=(rows,),
        out_shape=(jax.ShapeDtypeStruct((rows * seq, 3 * width), bf16), jax.ShapeDtypeStruct((rows * seq, width), bf16),
                   jax.ShapeDtypeStruct((rows, 16, seq), f32)),
        in_specs=[pl.BlockSpec((seq, width), lambda r: (r, 0)), pl.BlockSpec((1, 1, seq), lambda r: (r, 0, 0)),
                  pl.BlockSpec((width, 3 * width), lambda r: (0, 0)), pl.BlockSpec((1, 3 * width), lambda r: (0, 0))],
        out_specs=(pl.BlockSpec((seq, 3 * width), lambda r: (r, 0)), pl.BlockSpec((seq, width), lambda r: (r, 0)),
                   pl.BlockSpec((1, 16, seq), lambda r: (r, 0, 0))),
        scratch_shapes=[pltpu.VMEM((seq, seq), f32), pltpu.VMEM((seq, 128), f32)],
        compiler_params=pltpu.CompilerParams(vmem_limit_bytes=BIG),
        name="attn_fwd",
    )(x, seg.reshape(rows, 1, seq), w, b)

def bwd_kernel(blk, seg_ref, qkv_ref, dc_ref, lse_ref, delta_ref, dh1_ref, w_ref, x_ref, dqkv_ref, gin_ref, dw_ref, db_ref, bias_ref, ds_ref, acc_ref):
    r = pl.program_id(0)
    seq = dc_ref.shape[0]
    width = dc_ref.shape[1]
    fill_bias(seg_ref, bias_ref)
    ds_ref[...] = jnp.zeros_like(ds_ref)
    lane = lax.broadcasted_iota(jnp.int32, (blk, 128), 1)
    first = lane < HD
    lane_s = lax.broadcasted_iota(jnp.int32, (seq, 128), 1)
    def pair(p, _):
        col = pl.multiple_of(p * 128, 128)
        q2 = qkv_ref[:, pl.ds(col, 128)]
        k2 = qkv_ref[:, pl.ds(col + width, 128)]
        v2 = qkv_ref[:, pl.ds(col + 2 * width, 128)]
        dc2 = dc_ref[:, pl.ds(col, 128)]
        dqs = []
        for h in range(2):
            lse = lse_ref[0, pl.ds(2 * p + h, 1), :]
            dl = delta_ref[pl.ds(2 * p + h, 1), :]
            mine = first if h == 0 else ~first
            for c in range(seq // blk):
                lo, hi = key_range(c, seq, blk)
                rows = slice(c * blk, (c + 1) * blk)
                kc, vc = k2[rows], v2[rows]
                km = jnp.where(mine, kc, jnp.zeros_like(kc))
                vm = jnp.where(mine, vc, jnp.zeros_like(vc))
                st = dot_nt(km, q2[lo:hi])
                pt = jnp.exp2((st + bias_ref[rows, lo:hi]) * SCALE2 - lse[:, lo:hi])
                dp = dot_nt(vm, dc2[lo:hi])
                ds = (pt * (dp - dl[:, lo:hi])).astype(bf16)
                ds_ref[h, rows, lo:hi] = ds
                dv = dot(pt.astype(bf16), dc2[lo:hi])
                dk = dot(ds, q2[lo:hi]) * 0.125
                if h == 0:
                    dqkv_ref[rows, pl.ds(col + 2 * width, 128)] = dv.astype(bf16)
                    dqkv_ref[rows, pl.ds(col + width, 128)] = dk.astype(bf16)
                else:
                    ov = dqkv_ref[rows, pl.ds(col + 2 * width, 128)]
                    ok = dqkv_ref[rows, pl.ds(col + width, 128)]
                    dqkv_ref[rows, pl.ds(col + 2 * width, 128)] = jnp.where(first, ov, dv.astype(bf16))
                    dqkv_ref[rows, pl.ds(col + width, 128)] = jnp.where(first, ok, dk.astype(bf16))
            dqs.append(dot_tn(ds_ref[h], k2) * 0.125)
        dqkv_ref[:, pl.ds(col, 128)] = jnp.where(lane_s < HD, dqs[0], dqs[1]).astype(bf16)
        return 0
    lax.fori_loop(0, width // 128, pair, 0)
    dqkv = dqkv_ref[...]
    gin_ref[...] = (dh1_ref[...] + dot_nt(dqkv, w_ref[...])).astype(bf16)
    x = x_ref[...]
    for j in range(3):
        sl = slice(j * width, (j + 1) * width)
        d = dot_tn(x, dqkv[:, sl])
        s = jnp.sum(dqkv[:, sl].astype(f32), 0, keepdims=True)
        @pl.when(r == 0)
        def _():
            acc_ref[:, sl] = d
            db_ref[:, sl] = s
        @pl.when(r == pl.num_programs(0) - 1)
        def _():
            dw_ref[:, sl] = (acc_ref[:, sl] + d).astype(bf16)
            db_ref[:, sl] += s

def attn_bwd(seg, qkv, dc, lse, delta, dh1, w, x, blk=128):
    rows, seq = seg.shape
    width = dc.shape[1]
    assert rows == 2
    return pl.pallas_call(
        functools.partial(bwd_kernel, blk), grid=(rows,),
        out_shape=(jax.ShapeDtypeStruct((rows * seq, 3 * width), bf16), jax.ShapeDtypeStruct((rows * seq, width), bf16),
                   jax.ShapeDtypeStruct((width, 3 * width), bf16), jax.ShapeDtypeStruct((1, 3 * width), f32)),
        in_specs=[pl.BlockSpec((1, 1, seq), lambda r: (r, 0, 0)), pl.BlockSpec((seq, 3 * width), lambda r: (r, 0)),
                  pl.BlockSpec((seq, width), lambda r: (r, 0)), pl.BlockSpec((1, 16, seq), lambda r: (r, 0, 0)),
                  pl.BlockSpec((16, seq), lambda r: (0, r)), pl.BlockSpec((seq, width), lambda r: (r, 0)),
                  pl.BlockSpec((width, 3 * width), lambda r: (0, 0)), pl.BlockSpec((seq, width), lambda r: (r, 0))],
        out_specs=(pl.BlockSpec((seq, 3 * width), lambda r: (r, 0)), pl.BlockSpec((seq, width), lambda r: (r, 0)),
                   pl.BlockSpec((width, 3 * width), lambda r: (0, 0)), pl.BlockSpec((1, 3 * width), lambda r: (0, 0))),
        scratch_shapes=[pltpu.VMEM((seq, seq), f32), pltpu.VMEM((2, seq, seq), bf16), pltpu.VMEM((width, 3 * width), f32)],
        compiler_params=pltpu.CompilerParams(vmem_limit_bytes=BIG),
        name="attn_bwd",
    )(seg.reshape(rows, 1, seq), qkv, dc, lse, delta, dh1, w, x)

RSQRT_2PI = 1.0 / math.sqrt(2 * math.pi)
def gelu_parts(u):
    phi_cdf = 0.5 + 0.5 * lax.erf(u * math.sqrt(0.5))
    dens = jnp.exp2(u * u * (-0.5 * LOG2E)) * RSQRT_2PI
    return u * phi_cdf, phi_cdf + u * dens

def mid_kernel(chunk, x_ref, c_ref, e_ref, wo_ref, win_ref, wd_ref, v_ref, bin_ref,
               out_ref, y1_ref, g_ref, dz_ref, du_ref, da_ref, dc_ref, dh1_ref, delta_ref, dv_ref, dbin_ref, gp_ref):
    i = pl.program_id(0)
    blk, width = x_ref.shape
    ff = win_ref.shape[1]
    @pl.when(i == 0)
    def _():
        dv_ref[...] = jnp.zeros_like(dv_ref)
        dbin_ref[...] = jnp.zeros_like(dbin_ref)
    g1, s1, g2, s2, bo, bd = (v_ref[j:j + 1, :] for j in (0, 1, 2, 3, 6, 7))
    cb = c_ref[...]
    h1 = x_ref[...].astype(f32) + (dot(cb, wo_ref[...]) + bo)
    cen = h1 - jnp.mean(h1, 1, keepdims=True)
    r1 = lax.rsqrt(jnp.mean(cen * cen, 1, keepdims=True) + EPS)
    n1 = cen * r1
    y1 = n1 * g1 + s1
    y1l = y1.astype(bf16)
    y1_ref[...] = y1l
    z = jnp.zeros((blk, width), f32)
    for j in range(ff // chunk):
        sl = slice(j * chunk, (j + 1) * chunk)
        u = dot(y1l, win_ref[:, sl]) + bin_ref[:, sl]
        g, gp = gelu_parts(u)
        gl = g.astype(bf16)
        g_ref[:, sl] = gl
        gp_ref[:, sl] = gp
        z += dot_nt(gl, wd_ref[:, sl])
    h2 = y1 + (z + bd)
    cen = h2 - jnp.mean(h2, 1, keepdims=True)
    r2 = lax.rsqrt(jnp.mean(cen * cen, 1, keepdims=True) + EPS)
    n2 = cen * r2
    out_ref[...] = (n2 * g2 + s2).astype(bf16)
    e = e_ref[...].astype(f32)
    eg = e * g2
    dh2 = r2 * (eg - jnp.mean(eg, 1, keepdims=True) - n2 * jnp.mean(eg * n2, 1, keepdims=True))
    dz = dh2.astype(bf16)
    dz_ref[...] = dz
    dy1 = dh2
    for j in range(ff // chunk):
        sl = slice(j * chunk, (j + 1) * chunk)
        du = (dot(dz, wd_ref[:, sl]) * gp_ref[:, sl]).astype(bf16)
        du_ref[:, sl] = du
        dbin_ref[:, sl] += jnp.sum(du.astype(f32), 0, keepdims=True)
        dy1 += dot_nt(du, win_ref[:, sl])
    dn = dy1 * g1
    dh1 = r1 * (dn - jnp.mean(dn, 1, keepdims=True) - n1 * jnp.mean(dn * n1, 1, keepdims=True))
    dh1_ref[...] = dh1
    da = dh1.astype(bf16)
    da_ref[...] = da
    dc = dot_nt(da, wo_ref[...]).astype(bf16)
    dc_ref[...] = dc
    prod = dc.astype(f32) * cb.astype(f32)
    hi = prod.astype(bf16)
    lo = (prod - hi.astype(f32)).astype(bf16)
    sel = jnp.where(lax.broadcasted_iota(jnp.int32, (16, width), 0) == lax.broadcasted_iota(jnp.int32, (16, width), 1) // HD, 1.0, 0.0).astype(bf16)
    delta_ref[...] = dot_nt(sel, hi) + dot_nt(sel, lo)
    parts = [dy1 * n1, dy1, e * n2, e, da.astype(f32), dz.astype(f32)]
    for j, t in zip((0, 1, 2, 3, 6, 7), parts):
        dv_ref[j:j + 1, :] += jnp.sum(t, 0, keepdims=True)

def mid(x, c, e, wo, win, wd, vec, bin_, blk=256, chunk=768):
    n, width = x.shape
    ff = win.shape[1]
    tok = lambda w: pl.BlockSpec((blk, w), lambda i: (i, 0))
    full = lambda a: pl.BlockSpec(a.shape, lambda i: (0, 0), pipeline_mode=pl.Buffered(1))
    sh = jax.ShapeDtypeStruct
    return pl.pallas_call(
        functools.partial(mid_kernel, chunk), grid=(n // blk,),
        out_shape=(sh((n, width), bf16), sh((n, width), bf16), sh((n, ff), bf16), sh((n, width), bf16), sh((n, ff), bf16),
                   sh((n, width), bf16), sh((n, width), bf16), sh((n, width), f32), sh((16, n), f32), sh((8, width), f32), sh((1, ff), f32)),
        in_specs=[tok(width), tok(width), tok(width), full(wo), full(win), full(wd), full(vec), full(bin_)],
        out_specs=(tok(width), tok(width), tok(ff), tok(width), tok(ff), tok(width), tok(width), tok(width),
                   pl.BlockSpec((16, blk), lambda i: (0, i)), pl.BlockSpec((8, width), lambda i: (0, 0)), pl.BlockSpec((1, ff), lambda i: (0, 0))),
        scratch_shapes=[pltpu.VMEM((blk, ff), f32)],
        compiler_params=pltpu.CompilerParams(vmem_limit_bytes=BIG),
        name="middle",
    )(x, c, e, wo, win, wd, vec, bin_)

def wgrad_kernel(a_ref, b_ref, o_ref):
    o_ref[...] = dot_tn(a_ref[...], b_ref[...]).astype(bf16)

def wgrad(a, b, blk=768):
    n, m = a.shape
    k = b.shape[1]
    return pl.pallas_call(wgrad_kernel, grid=(k // blk,), out_shape=jax.ShapeDtypeStruct((m, k), bf16),
        in_specs=[pl.BlockSpec((n, m), lambda j: (0, 0)), pl.BlockSpec((n, blk), lambda j: (0, j))],
        out_specs=pl.BlockSpec((m, blk), lambda j: (0, j)),
        compiler_params=pltpu.CompilerParams(vmem_limit_bytes=BIG), name="wgrad")(a, b)


LANES = 128
PIECE = 3 * LANES
GATHER_LAGS = (0, 2, 4, 6)
REDUCE_LAGS = (0, 2, 4, 6, 8)
AHEAD = 3
MESH = pl.DeviceIdType.MESH


class Place:
    def __init__(self):
        self.w = lax.axis_index("wide")
        self.x = lax.axis_index("narrow")
        self.core = lax.rem(self.w, 2)
        self.y = lax.rem(self.w // 2, 2)
        self.b = lax.rem(self.w // 4, 2)
        self.a = self.w // 8
        self.z = self.w // 4

    def z_peer(self, k):
        return lax.rem(self.z + k, 4)

    def over(self, name):
        if name == "x":
            return (self.w, 1 - self.x)
        if name in (1, 2, 3):
            return (4 * self.z_peer(name) + lax.rem(self.w, 4), self.x)
        step = {"a": 8, "b": 4, "y": 2, "core": 1}[name]
        return (self.w + step * (1 - 2 * getattr(self, name)), self.x)

    near = ("a", "b", "y", "x", "core")
    reduce_peers = (1, 2, 3, "y", "x", "core")

    def greet(self, names):
        for name in names:
            pl.semaphore_signal(pltpu.get_barrier_semaphore(), inc=1, device_id=self.over(name), device_id_type=MESH)

    def met(self, names):
        pl.semaphore_wait(pltpu.get_barrier_semaphore(), len(names))


def remote(src, dst, send, recv, device):
    return pltpu.make_async_remote_copy(src_ref=src, dst_ref=dst, send_sem=send, recv_sem=recv, device_id=device, device_id_type=MESH)


def when(condition, step):
    @pl.when(condition)
    def _():
        step()


def loop(count, step):
    lax.fori_loop(0, count, lambda i, _: (step(i), 0)[1], 0)


class Gather:
    def __init__(self, place, shard, full, sems, pieces):
        self.p, self.shard, self.full, self.pieces = place, shard, full, pieces
        self.sems = {name: (sems[2 * k], sems[2 * k + 1]) for k, name in enumerate(("a", "b", "y", "x", "core"))}
        self.kept = sems[10]
        self.own = pl.ds(place.x, 2)

    def mine(self, i, a):
        return self.full.at[i, self.own, a, self.p.b, self.p.y, self.p.core]

    def keep(self, i):
        return pltpu.make_async_copy(self.shard.at[i, self.own], self.mine(i, self.p.a), self.kept.at[i])

    def copy(self, name, i, incoming=False):
        p, f = self.p, self.full
        at = {n: (1 - getattr(p, n) if incoming and n == name else getattr(p, n)) for n in ("a", "b", "y", "x", "core")}
        every = slice(None)
        if name == "a":
            dst = self.mine(i, at["a"])
            src = self.shard.at[i, self.own]
        else:
            if name == "b":
                dst = f.at[i, self.own, :, at["b"], p.y, p.core]
            elif name == "y":
                dst = f.at[i, self.own, :, :, at["y"], p.core]
            elif name == "x":
                dst = f.at[i, 2 * at["x"], :, :, :, p.core]
            else:
                dst = f.at[i, :, :, :, :, at["core"]]
            src = dst
        send, recv = self.sems[name]
        return remote(src, dst, send.at[i], recv.at[i], p.over(name))

    def start(self, i):
        self.keep(i).start()
        self.copy("a", i).start()

    def b_step(self, i):
        self.keep(i).wait()
        self.copy("a", i, True).wait_recv()
        self.copy("b", i).start()

    def y_step(self, i):
        self.copy("b", i, True).wait_recv()
        self.copy("y", i).start()

    def x_step(self, i):
        self.copy("y", i, True).wait_recv()
        self.copy("x", i).start()

    def core_step(self, i):
        self.copy("x", i, True).wait_recv()
        self.copy("core", i).start()

    def arrive(self, i):
        self.copy("core", i, True).wait_recv()

    def turn(self, t):
        for k in range(2):
            ahead = AHEAD + 2 * t + k
            when(ahead < self.pieces, lambda ahead=ahead: self.start(ahead))
        for lag, step in zip(GATHER_LAGS, (self.b_step, self.y_step, self.x_step, self.core_step)):
            when((t >= lag) & (t < self.pieces + lag), lambda lag=lag, step=step: step(t - lag))

    def sent(self, i):
        for name in ("a", "b", "y", "x", "core"):
            self.copy(name, i).wait_send()


class GatherVector:
    def __init__(self, place, shard, full, sems):
        self.p, self.shard, self.full = place, shard, full
        self.sems = {name: (sems[2 * k], sems[2 * k + 1]) for k, name in enumerate(("a", "b", "y", "core"))}
        self.kept = sems[8]

    def keep(self):
        p = self.p
        return pltpu.make_async_copy(self.shard, self.full.at[p.a, p.b, p.y, p.core], self.kept)

    def copy(self, name, incoming=False):
        p = self.p
        at = {n: (1 - getattr(p, n) if incoming and n == name else getattr(p, n)) for n in ("a", "b", "y", "core")}
        every = slice(None)
        first = ("a", "b", "y", "core").index(name)
        dst = self.full.at[tuple(at[n] if n == name or n == "core" or k > first else every for k, n in enumerate(("a", "b", "y", "core")))]
        src = self.shard if name == "a" else dst
        send, recv = self.sems[name]
        return remote(src, dst, send, recv, p.over(name))

    def start(self):
        self.keep().start()
        self.copy("a").start()

    def step(self, name, then):
        if name == "a":
            self.keep().wait()
        self.copy(name, True).wait_recv()
        self.copy(then).start()

    def arrive(self):
        self.copy("core", True).wait_recv()

    def sent(self):
        for name in ("a", "b", "y", "core"):
            self.copy(name).wait_send()


def tile(ref, i, t):
    rows = 16 * ref.shape[-2]
    return ref[i, t].reshape(rows, LANES)


def columns(ref, *pieces):
    return jnp.concatenate([tile(ref, i, t) for i in pieces for t in range(3)], 1)


def doc_bias(seg_row, bias_ref, r):
    segf = seg_row.astype(f32)
    seq = segf.shape[1]
    rep = jnp.broadcast_to(segf, (LANES, seq)).T
    for j in range(seq // LANES):
        sl = slice(j * LANES, (j + 1) * LANES)
        bias_ref[r, :, sl] = jnp.where(rep == segf[:, sl], 0.0, NEG)


def stage_kernel(heads, x_hbm, seg_ref, e_hbm, aw_hbm, dw_hbm, vp_ref,
                 qkv_o, c_o, lse_o, w_o, out_o, y1_o, g_o, gp_o, dz_o, dh2_o, n1_o, r1_o, dv_o, vrow,
                 full, vfull, shard, vshard, square, xb, eb, cb, n1b, y1b, acc, gp, gb, dzb, bias, lsea, binr, r1b,
                 in_sem, out_sem, w_sem, two_sem, *sems):
    place = Place()
    rows, seq = seg_ref.shape
    tokens, width = x_hbm.shape
    pairs = heads // 2
    pieces = shard.shape[0]
    chunks = gb.shape[0]
    own_rows = aw_hbm.shape[1]
    blk = 256
    big = 512
    g = Gather(place, shard, full, sems[:11], pieces)
    gv = GatherVector(place, vshard, vfull, sems[11:])

    loads = [pltpu.make_async_copy(aw_hbm.at[k], gp.at[0, pl.ds(k * own_rows, own_rows)], in_sem.at[k]) for k in range(4)]
    for k in range(2):
        for j in range(chunks):
            loads.append(pltpu.make_async_copy(
                dw_hbm.at[k, :, pl.ds(j * width, width)], gp.at[1 + k, pl.ds(j * own_rows, own_rows)], in_sem.at[4 + k * chunks + j]))
    n = len(loads)
    x_load = pltpu.make_async_copy(x_hbm, xb, in_sem.at[n])
    e_load = pltpu.make_async_copy(e_hbm, eb, in_sem.at[n + 1])
    for c in loads:
        c.start()
    place.greet(place.near)
    x_load.start()
    e_load.start()
    square[...] = jnp.zeros_like(square)
    lsea[...] = jnp.zeros_like(lsea)
    square[: vp_ref.shape[0], :own_rows] = vp_ref[...]
    vshard[...] = square[...].T[:own_rows].astype(bf16)

    def own_tile(k, j, t):
        return gp[k, j * own_rows : (j + 1) * own_rows, t * LANES : (t + 1) * LANES].astype(bf16)

    for c in loads[:3]:
        c.wait()
    for p in range(pairs):
        for t in range(3):
            shard[p, t] = own_tile(0, t, p)
    place.met(place.near)
    gv.start()
    for i in range(AHEAD):
        g.start(i)
    for c in loads[3:]:
        c.wait()
    for t in range(6):
        shard[pairs + t // 3, t % 3] = own_tile(0, 3, t)
        for j in range(chunks):
            for k in range(2):
                shard[pairs + 2 + 4 * j + 2 * k + t // 3, t % 3] = own_tile(1 + k, j, t)
    for r in range(rows):
        doc_bias(seg_ref[r : r + 1, :], bias, r)
    gv.step("a", "b")
    fill = GATHER_LAGS[-1] + 1
    for t in range(fill):
        g.turn(t)
        if t == 1:
            gv.step("b", "y")
        if t == 4:
            gv.step("y", "core")
    gv.arrive()
    vec = vfull[...].reshape(16 * own_rows, LANES).astype(f32).T
    vrow[...] = vec[: vrow.shape[0]]
    for j in range(chunks):
        binr[j] = vrow[8 + j : 9 + j, :]
    x_load.wait()

    first = lax.broadcasted_iota(jnp.int32, (LANES, LANES), 1) < HD
    lane = lax.broadcasted_iota(jnp.int32, (LANES, LANES), 1)
    ones = jnp.ones((seq, LANES), bf16)

    def qkv_at(p):
        return gb.at[p // 2, :, pl.ds(pl.multiple_of(lax.rem(p, 2) * PIECE, LANES), PIECE)]

    def qkv_out(p):
        return pltpu.make_async_copy(qkv_at(p), qkv_o.at[p], out_sem.at[p])

    def w_out(i):
        return pltpu.make_async_copy(full.at[i], w_o.at[i], w_sem.at[i])

    def pair(p):
        g.arrive(p)
        w_out(p).start()
        head = pl.ds(pl.multiple_of(p * LANES, LANES), LANES)
        w = columns(full, p)
        b = jnp.concatenate([vrow[4:5, head], jnp.zeros((1, LANES), f32), vrow[5:6, head]], 1)
        col = pl.multiple_of(lax.rem(p, 2) * PIECE, LANES)
        gb[p // 2, :, pl.ds(col, PIECE)] = (dot(xb[...], w) + b).astype(bf16)
        qkv_out(p).start()

        def row(r):
            tok = pl.ds(pl.multiple_of(r * seq, seq), seq)
            q2 = gb[p // 2, tok, pl.ds(col, LANES)]
            k2 = gb[p // 2, tok, pl.ds(col + LANES, LANES)]
            v2 = jnp.concatenate([gb[p // 2, tok, pl.ds(col + 2 * LANES, LANES)], ones], 1)
            for c in range(seq // LANES):
                lo, hi = key_range(c, seq, LANES)
                cut = slice(c * LANES, (c + 1) * LANES)
                outs = []
                la = lsea[r, cut, :]
                for h in range(2):
                    qm = jnp.where(first if h == 0 else ~first, q2[cut], jnp.zeros_like(q2[cut]))
                    s = dot_nt(qm, k2[lo:hi]) + bias[r, cut, lo:hi]
                    m = jnp.max(s, 1, keepdims=True)
                    o = dot(jnp.exp2((s - m) * SCALE2).astype(bf16), v2[lo:hi])
                    l = o[:, LANES:]
                    outs.append(o[:, :LANES] / l)
                    la = jnp.where(lane == 2 * p + h, m * SCALE2 + jnp.log(l) * LOG2E, la)
                lsea[r, cut, :] = la
                cb[pl.ds(pl.multiple_of(r * seq + c * LANES, LANES), LANES), head] = jnp.where(first, outs[0], outs[1]).astype(bf16)
            g.turn(fill + 2 * p + r)

        loop(rows, row)

    loop(pairs, pair)
    done = fill + 2 * pairs
    for r in range(rows):
        lse_o[r] = lsea[r].T[: lse_o.shape[1]]
    c_out = pltpu.make_async_copy(cb, c_o, out_sem.at[pairs])
    c_out.start()
    g1, s1, g2, s2, bo, bd = (vrow[j : j + 1, :] for j in (0, 1, 2, 3, 6, 7))

    def block(i):
        return pl.ds(pl.multiple_of(i * blk, blk), blk)

    for i in (pairs, pairs + 1):
        g.arrive(i)
        w_out(i).start()

    def norm_one(i):
        at = block(i)
        h1 = xb[at, :].astype(f32) + (dot(cb[at, :], columns(full, pairs, pairs + 1)) + bo)
        cen = h1 - jnp.mean(h1, 1, keepdims=True)
        r1 = lax.rsqrt(jnp.mean(cen * cen, 1, keepdims=True) + EPS)
        n1 = cen * r1
        y1 = n1 * g1 + s1
        n1b[at, :] = n1
        r1b[at, :] = jnp.broadcast_to(r1, (blk, LANES))
        y1b[at, :] = y1.astype(bf16)
        acc[at, :] = y1 + bd
        when(lax.rem(i, 2) == 1, lambda: g.turn(done + i // 2))

    loop(tokens // blk, norm_one)
    done += 2
    y1_out = pltpu.make_async_copy(y1b, y1_o, out_sem.at[pairs + 2])
    y1_out.start()
    n1_out = pltpu.make_async_copy(n1b, n1_o, out_sem.at[pairs + 1])
    n1_out.start()
    r1_out = pltpu.make_async_copy(r1b, r1_o, out_sem.at[pairs + 5 + chunks])
    r1_out.start()
    loop(pairs, lambda p: qkv_out(p).wait())

    def up(j):
        return columns(full, pairs + 2 + 4 * j, pairs + 3 + 4 * j)

    def down(j):
        return columns(full, pairs + 4 + 4 * j, pairs + 5 + 4 * j)

    def g_out(j):
        return pltpu.make_async_copy(gb.at[j], g_o.at[j], out_sem.at[pairs + 7 + j])

    def gp_out(j):
        return pltpu.make_async_copy(gp.at[j], gp_o.at[j], out_sem.at[pairs + 7 + chunks + j])

    def ff_chunk(j):
        def ready(k):
            for t in (k, k + 1):
                g.arrive(pairs + 2 + 4 * j + t)
                w_out(pairs + 2 + 4 * j + t).start()

        def up_block(i):
            at = pl.ds(pl.multiple_of(i * big, big), big)
            act, slope = gelu_parts(dot(y1b[at, :], up(j)) + binr[j])
            gb[j, at, :] = act.astype(bf16)
            gp[j, at, :] = slope
            g.turn(done + 4 * j + i)

        def down_block(i):
            at = pl.ds(pl.multiple_of(i * big, big), big)
            acc[at, :] += dot_nt(gb[j, at, :], down(j))
            g.turn(done + 4 * j + 2 + i)

        ready(0)
        loop(tokens // big, up_block)
        g_out(j).start()
        gp_out(j).start()
        ready(2)
        loop(tokens // big, down_block)

    loop(chunks, ff_chunk)
    e_load.wait()
    dv_o[...] = jnp.zeros_like(dv_o)

    def colsum(t):
        return jnp.sum(t, 0, keepdims=True)

    def norm_two(i):
        at = block(i)
        h2 = acc[at, :]
        cen = h2 - jnp.mean(h2, 1, keepdims=True)
        r2 = lax.rsqrt(jnp.mean(cen * cen, 1, keepdims=True) + EPS)
        n2 = cen * r2
        xb[at, :] = (n2 * g2 + s2).astype(bf16)
        e = eb[at, :].astype(f32)
        eg = e * g2
        dh2 = r2 * (eg - jnp.mean(eg, 1, keepdims=True) - n2 * jnp.mean(eg * n2, 1, keepdims=True))
        dz = dh2.astype(bf16)
        dzb[at, :] = dz
        acc[at, :] = dh2
        dv_o[2:3, :] += colsum(e * n2)
        dv_o[3:4, :] += colsum(e)
        dv_o[7:8, :] += colsum(dz.astype(f32))

    def norm_two_out(i):
        at = block(i)
        pairs_of = ((xb, out_o), (dzb, dz_o), (acc, dh2_o))
        return [pltpu.make_async_copy(src.at[at], dst.at[at], two_sem.at[k, i]) for k, (src, dst) in enumerate(pairs_of)]

    def norm_two_step(i):
        norm_two(i)
        for c in norm_two_out(i):
            c.start()

    loop(tokens // blk, norm_two_step)
    gv.sent()
    loop(pieces, g.sent)
    loop(pieces, lambda i: w_out(i).wait())
    for c in [c_out, y1_out, n1_out, r1_out]:
        c.wait()
    for i in range(tokens // blk):
        for c in norm_two_out(i):
            c.wait()
    loop(chunks, lambda j: g_out(j).wait())
    loop(chunks, lambda j: gp_out(j).wait())


def stage(x, seg, e, aw, dw, vp):
    rows, seq = seg.shape
    tokens, width = x.shape
    own_rows, ff = dw.shape[1:]
    heads, chunks = width // HD, ff // width
    pairs = heads // 2
    pieces = pairs + 2 + 4 * chunks
    sh = jax.ShapeDtypeStruct
    dma = pltpu.SemaphoreType.DMA
    v = pltpu.VMEM
    hbm = pl.BlockSpec(memory_space=pl.ANY)
    vmem = pl.BlockSpec(memory_space=pltpu.VMEM)
    tok = sh((tokens, width), bf16)
    wide = sh((chunks, tokens, width), bf16)
    long = sh((tokens, width), f32)
    block = (2, 2, 2, 2, own_rows, LANES)
    scratch = [
        v((pieces, 3) + block, bf16), v(block, bf16), v((pieces, 3, own_rows, LANES), bf16), v((own_rows, LANES), bf16),
        v((LANES, LANES), f32), v((tokens, width), bf16), v((tokens, width), bf16), v((tokens, width), bf16),
        v((tokens, width), f32), v((tokens, width), bf16), v((tokens, width), f32), v((chunks, tokens, width), f32),
        v((chunks, tokens, width), bf16), v((tokens, width), bf16), v((rows, seq, seq), f32), v((rows, seq, LANES), f32),
        v((chunks, 1, width), f32), v((tokens, LANES), f32),
        dma((6 + 2 * chunks,)), dma((pairs + 7 + 2 * chunks,)), dma((pieces,)), dma((3, tokens // 256)),
    ] + [dma((pieces,))] * 11 + [dma(())] * 9
    return pl.pallas_call(
        functools.partial(stage_kernel, heads),
        out_shape=(sh((pairs, tokens, PIECE), bf16), tok, sh((rows, 16, seq), f32), sh((pieces, 3) + block, bf16), tok, tok, wide,
                   sh((chunks, tokens, width), f32), tok, long, long, sh((tokens, LANES), f32), sh((8, width), f32), sh((16, width), f32)),
        in_specs=[hbm, vmem, hbm, hbm, hbm, vmem],
        out_specs=(hbm, hbm, vmem) + (hbm,) * 9 + (vmem, vmem),
        scratch_shapes=scratch,
        compiler_params=pltpu.CompilerParams(collective_id=0, has_side_effects=True, vmem_limit_bytes=BIG),
        name="stage",
    )(x, seg, e, aw, dw, vp)


class Reduce:
    def __init__(self, place, part, froms, done, out, sems, pieces, tiles=3):
        self.p, self.part, self.done, self.out, self.pieces, self.whole = place, part, done, out, pieces, tiles == 1
        self.names = ("core", "y", "p") if self.whole else ("core", "y", "p", "x", "early_y", "late_x")
        self.froms = dict(zip(("core", "y", "p", "z", "x", "early_y"), froms))
        self.zs, self.zr = sems[:2]
        self.sems = {name: (sems[2 + 2 * k], sems[3 + 2 * k]) for k, name in enumerate(self.names)}
        self.own = pl.ds(0, 1) if self.whole else pl.ds(place.x, 2)
        self.most = slice(None) if self.whole else pl.ds(0, 3)

    def copy(self, name, i):
        p, f, landing = self.p, self.part, self.froms
        if name == "core":
            src, dst = f.at[i, :, :, :, 1 - p.core], landing[name].at[i]
        elif name == "x":
            src, dst = f.at[i, 2 * (1 - p.x), self.most, :, p.core], landing[name].at[i, self.most]
        elif name == "late_x":
            src, dst = f.at[i, 2 * (1 - p.x), 3, p.y, p.core], landing["x"].at[i, 3, 0]
        elif name == "y":
            src, dst = f.at[i, self.own, self.most, 1 - p.y, p.core], landing[name].at[i, :, self.most]
        elif name == "early_y":
            src, dst = f.at[i, :, 3, 1 - p.y, p.core], landing[name].at[i]
        else:
            src, dst = self.done.at[i], landing[name].at[i]
        send, recv = self.sems[name]
        axis = {"p": "x", "early_y": "y", "late_x": "x"}.get(name, name)
        return remote(src, dst, send.at[i], recv.at[i], p.over(axis))

    def z_copy(self, i, k, incoming=False):
        p = self.p
        peer = p.z_peer(k)
        came = peer if incoming else p.z
        return remote(self.part.at[i, self.own, peer, p.y, p.core], self.froms["z"].at[i, came], self.zs.at[i, k], self.zr.at[i, came], p.over(k))

    def start(self, i):
        self.copy("core", i).start()

    def add(self, at, term):
        self.part[at] = self.part[at] + term

    def x_step(self, i):
        p = self.p
        self.copy("core", i).wait_recv()
        for t in range(1 if self.whole else 3):
            self.add((i, t, slice(None), slice(None), p.core), self.froms["core"][i, t])
        for name in ("y",) if self.whole else ("x", "early_y"):
            self.copy(name, i).start()

    def y_step(self, i):
        p = self.p
        self.copy("early_y", i).wait_recv()
        self.add((i, slice(None), 3, p.y, p.core), self.froms["early_y"][i])
        self.copy("late_x", i).start()
        self.copy("x", i).wait_recv()
        self.add((i, 2 * p.x, self.most, slice(None), p.core), self.froms["x"][i, :3])
        self.copy("y", i).start()

    def z_step(self, i):
        p = self.p
        self.copy("y", i).wait_recv()
        self.add((i, self.own, self.most, p.y, p.core), self.froms["y"][i, :, self.most])
        if not self.whole:
            self.copy("late_x", i).wait_recv()
            self.add((i, 2 * p.x, 3, p.y, p.core), self.froms["x"][i, 3, 0])
        for k in (2, 1, 3):
            self.z_copy(i, k).start()

    def p_step(self, i):
        p, f = self.p, self.part
        total = f[i, self.own, p.z, p.y, p.core].astype(f32)
        for k in (1, 2, 3):
            self.z_copy(i, k, True).wait_recv()
            total += self.froms["z"][i, p.z_peer(k)].astype(f32)
        self.done[i] = total.astype(bf16)
        self.copy("p", i).start()

    def finish(self, i):
        self.copy("p", i).wait_recv()
        a, b = self.done[i].astype(f32), self.froms["p"][i].astype(f32)
        if self.whole:
            self.out[i] = a[0] + b[0]
            return
        first = self.p.x == 0
        low, high = jnp.where(first, a, b), jnp.where(first, b, a)
        self.out[i] = jnp.concatenate([low[0], low[1] + high[0], high[1]], 1)

    def turn(self, t):
        for lag, step in zip(REDUCE_LAGS, (self.x_step, self.y_step, self.z_step, self.p_step, self.finish)):
            when((t >= lag) & (t < self.pieces + lag), lambda lag=lag, step=step: step(t - lag))

    def sent(self, i):
        for name in self.names:
            self.copy(name, i).wait_send()
        for k in (1, 2, 3):
            self.z_copy(i, k).wait_send()


def back_kernel(heads, x_hbm, c_hbm, y1_hbm, dz_hbm, dh2_hbm, n1_hbm, r1_hbm, g_hbm, gp_hbm, qkv_hbm, w_hbm,
                seg_ref, lse_ref, dv_ref, vec_ref, gin_o, sum_o, vsum_o,
                part, fromc, fromy, fromp, fromz, fromx, frome, done, vpart, vfromc, vfromy, vfromp, vfromz, vdone, pool, wpool, gpool, acc, cb, dab, dcb, r1b, delta, vrow,
                ld, out_sem, *sems):
    place = Place()
    rows, seq = seg_ref.shape
    tokens, width = x_hbm.shape
    pairs = heads // 2
    chunks = g_hbm.shape[0]
    own_rows = part.shape[-2]
    pieces = part.shape[0]
    big = 512
    r_ = Reduce(place, part, (fromc, fromy, fromp, fromz, fromx, frome), done, sum_o, sems[:14], pieces)
    rv = Reduce(place, vpart, (vfromc, vfromy, vfromp, vfromz), vdone, vsum_o, sems[14:], vpart.shape[0], 1)
    ff_pieces = 4 * chunks
    first_ff = pairs + 2
    du, dz, y1 = pool.at[2], pool.at[3], pool.at[4]
    x = y1

    def load(k, src, dst):
        return pltpu.make_async_copy(src, dst, ld.at[k])

    g_in = [load(j, g_hbm.at[j], pool.at[j % 2]) for j in range(chunks)]
    gp_in = [load(chunks + j, gp_hbm.at[j], gpool.at[j % 2]) for j in range(chunks)]
    w_in = [load(2 * chunks + j, w_hbm.at[pl.ds(first_ff + 4 * j, 4)], wpool.at[pl.ds(4 * (j % 2), 4)]) for j in range(chunks)]
    base = 3 * chunks
    dz_in, y1_in, acc_in, c_in, r1_in = (load(base + k, s, d) for k, (s, d) in enumerate(
        ((dz_hbm, dz), (y1_hbm, y1), (dh2_hbm, acc), (c_hbm, cb), (r1_hbm, r1b))))
    base += 5
    n1_in = load(base, n1_hbm, gpool.at[0])
    wo_in = load(base + 1, w_hbm.at[pl.ds(pairs, 2)], wpool.at[pl.ds(0, 2)])
    wq_in = load(base + 2, w_hbm.at[pl.ds(0, pairs)], wpool.at[pl.ds(2, pairs)])
    x_in = load(base + 3, x_hbm, x)
    base += 4

    def q_in(p):
        return load(base + p, qkv_hbm.at[p], pool.at[3, :, pl.ds(pl.multiple_of(lax.rem(p, 2) * PIECE, LANES), PIECE)])

    for c in (dz_in, g_in[0]):
        c.start()
    place.greet(place.reduce_peers)
    place.met(place.reduce_peers)
    vrow[...] = jnp.zeros_like(vrow)
    vrow[:8, :] = dv_ref[...]

    def colsum(t):
        return jnp.sum(t, 0, keepdims=True)

    half = width // 2

    def weight_grad(left, right, piece, count):
        def product(a):
            d = dot_tn(left[:, pl.ds(pl.multiple_of(a * half, LANES), half)], right)
            for t in range(3 * count):
                part[piece + t // 3, t % 3, pl.ds(2 * a, 2)] = d[:, t * LANES : (t + 1) * LANES].astype(bf16).reshape(2, 2, 2, own_rows, LANES)

        loop(2, product)
        for k in range(count):
            r_.start(piece + k)

    dz_in.wait()
    for j in range(chunks):
        s = j % 2
        g_in[j].wait()
        if j == 0:
            for c in (gp_in[0], w_in[0], acc_in, y1_in, g_in[1], gp_in[1], w_in[1], c_in, r1_in):
                c.start()
        weight_grad(dz, pool[s], 4 * j, 2)
        r_.turn(3 * j)
        gp_in[j].wait()
        w_in[j].wait()
        if j == 0:
            y1_in.wait()
            acc_in.wait()

        def block(i, j=j, s=s):
            at = pl.ds(pl.multiple_of(i * big, big), big)
            d = (dot(dz[at, :], columns(wpool, 4 * s + 2, 4 * s + 3)) * gpool[s, at, :]).astype(bf16)
            du[at, :] = d
            acc[at, :] += dot_nt(d, columns(wpool, 4 * s, 4 * s + 1))
            vrow[8 + j : 9 + j, :] += colsum(d.astype(f32))

        loop(tokens // big, block)
        r_.turn(3 * j + 1)
        if j + 2 < chunks:
            g_in[j + 2].start()
            gp_in[j + 2].start()
            w_in[j + 2].start()
        if j == chunks - 2:
            n1_in.start()
            wo_in.start()
        weight_grad(y1, du[...], 4 * j + 2, 2)
        r_.turn(3 * j + 2)
    wq_in.start()
    x_in.start()
    q_in(0).start()
    q_in(1).start()
    for r in range(rows):
        segf = seg_ref[r : r + 1, :].astype(f32)
        rep = jnp.broadcast_to(segf, (LANES, seq)).T
        for k in range(seq // LANES):
            sl = slice(k * LANES, (k + 1) * LANES)
            gpool[1, r * seq : (r + 1) * seq, sl] = jnp.where(rep == segf[:, sl], 0.0, NEG)
    c_in.wait()
    r1_in.wait()
    n1_in.wait()
    wo_in.wait()
    g1 = vec_ref[0:1, :]
    sel_shape = (delta.shape[0], width)
    sel = jnp.where(lax.broadcasted_iota(jnp.int32, sel_shape, 0) == lax.broadcasted_iota(jnp.int32, sel_shape, 1) // HD, 1.0, 0.0).astype(bf16)

    def norm_one_back(i):
        at = pl.ds(pl.multiple_of(i * 256, 256), 256)
        dy1 = acc[at, :]
        n1 = gpool[0, at, :]
        dn = dy1 * g1
        r1 = r1b[at, :1]
        dh1 = r1 * (dn - jnp.mean(dn, 1, keepdims=True) - n1 * jnp.mean(dn * n1, 1, keepdims=True))
        acc[at, :] = dh1
        da = dh1.astype(bf16)
        dab[at, :] = da
        dc = dot_nt(da, columns(wpool, 0, 1)).astype(bf16)
        dcb[at, :] = dc
        prod = dc.astype(f32) * cb[at, :].astype(f32)
        hi = prod.astype(bf16)
        lo = (prod - hi.astype(f32)).astype(bf16)
        delta[:, at] = dot_nt(sel, hi) + dot_nt(sel, lo)
        vrow[0:1, :] += colsum(dy1 * n1)
        vrow[1:2, :] += colsum(dy1)
        vrow[6:7, :] += colsum(da.astype(f32))

    loop(tokens // 256, norm_one_back)
    r_.turn(3 * chunks)
    weight_grad(cb, dab[...], ff_pieces, 2)
    r_.turn(3 * chunks + 1)
    t0 = 3 * chunks + 2
    twice = ff_pieces + 2 - t0
    x_in.wait()
    first_seq = lax.broadcasted_iota(jnp.int32, (seq, LANES), 1) < HD

    def pair(p, last=False):
        head = pl.ds(pl.multiple_of(p * LANES, LANES), LANES)
        col = pl.multiple_of(lax.rem(p, 2) * PIECE, LANES)
        to = p // 2
        q_in(p).wait()

        def row(r):
            tok = pl.ds(pl.multiple_of(r * seq, seq), seq)
            q2 = pool[3, tok, pl.ds(col, LANES)]
            k2 = pool[3, tok, pl.ds(col + LANES, LANES)]
            v2 = pool[3, tok, pl.ds(col + 2 * LANES, LANES)]
            dc2 = dcb[tok, head]
            zero = jnp.zeros_like(k2)
            near = gpool[1, tok, :seq]
            grads = []
            for h in range(2):
                lse = lse_ref[r, pl.ds(2 * p + h, 1), :]
                dl = delta[pl.ds(2 * p + h, 1), tok]
                own = first_seq if h == 0 else ~first_seq
                pt = jnp.exp2((dot_nt(jnp.where(own, k2, zero), q2) + near) * SCALE2 - lse)
                ds = (pt * (dot_nt(jnp.where(own, v2, zero), dc2) - dl)).astype(bf16)
                dv = dot(pt.astype(bf16), dc2)
                grads.append((dot_tn(ds, k2) * 0.125, dot(ds, q2) * 0.125, dv))
            for k, (a, b) in enumerate(zip(*grads)):
                pool[to, tok, pl.ds(col + k * LANES, LANES)] = jnp.where(first_seq, a, b).astype(bf16)
            if last:
                r_.turn(t0 + p + twice + r)
            else:
                when((r == 0) & (p < twice), lambda: r_.turn(t0 + 2 * p))

        loop(rows, row)
        if not last:
            when(p + 2 < pairs, lambda: q_in(p + 2).start())
        d = pool[to, :, pl.ds(col, PIECE)]
        sums = colsum(d.astype(f32))
        vrow[4:5, head] = sums[:, :LANES]
        vrow[5:6, head] = sums[:, 2 * LANES :]
        if last:
            def product(a):
                w = dot_tn(x[:, pl.ds(pl.multiple_of(a * half, LANES), half)], d)
                for t in range(3):
                    vpart[t, 0, pl.ds(2 * a, 2)] = w[:, t * LANES : (t + 1) * LANES].astype(bf16).reshape(2, 2, 2, own_rows, LANES)

            loop(2, product)
            for t in range(3):
                rv.start(t)
            vpart[3, 0] = vrow[...].T.astype(bf16).reshape(4, 2, 2, own_rows, LANES)
            rv.start(3)
        else:
            weight_grad(x, d, ff_pieces + 2 + p, 1)
            r_.turn(t0 + p + jnp.minimum(p + 1, twice))

    loop(pairs - 1, pair)
    pair(pairs - 1, True)
    t0 += pairs - 1 + twice + rows
    singles = vpart.shape[0]
    wq_in.wait()
    blocks = tokens // 256

    def gin_block(i):
        at = pl.ds(pl.multiple_of(i * 256, 256), 256)
        d = jnp.concatenate([pool[k, at, :] for k in range(pairs // 2)], 1)
        dcb[at, :] = (acc[at, :] + dot_nt(d, columns(wpool, *range(2, 2 + pairs)))).astype(bf16)
        when(i == 0, lambda: loop(singles, rv.x_step))
        when(i < 2, lambda: r_.turn(t0 + i))
        when(i == 2, lambda: loop(singles, rv.z_step))
        when(i == 3, lambda: r_.turn(t0 + 2))

    loop(blocks, gin_block)
    gin_out = pltpu.make_async_copy(dcb, gin_o, out_sem)
    gin_out.start()
    t0 += 3
    rest = pieces + REDUCE_LAGS[-1] - t0

    def rest_turn(i):
        r_.turn(t0 + i)
        when(i == 0, lambda: loop(singles, rv.p_step))

    loop(rest, rest_turn)
    loop(singles, rv.finish)
    loop(pieces, r_.sent)
    loop(singles, rv.sent)
    gin_out.wait()


def back(x, c, y1, dz, dh2, n1, r1, g, gp, qkv, w, seg, lse, dv, vec):
    rows, seq = seg.shape
    tokens, width = x.shape
    chunks = g.shape[0]
    own_rows = w.shape[-2]
    heads = width // HD
    pairs = heads // 2
    pieces = 4 * chunks + 2 + pairs - 1
    sh = jax.ShapeDtypeStruct
    dma = pltpu.SemaphoreType.DMA
    v = pltpu.VMEM
    hbm = pl.BlockSpec(memory_space=pl.ANY)
    vmem = pl.BlockSpec(memory_space=pltpu.VMEM)
    tail = (own_rows, LANES)
    tok = v((tokens, width), bf16)
    scratch = [
        v((pieces, 3, 4, 2, 2) + tail, bf16), v((pieces, 3, 4, 2) + tail, bf16), v((pieces, 2, 4) + tail, bf16), v((pieces, 2) + tail, bf16),
        v((pieces, 4, 2) + tail, bf16), v((pieces, 4, 2) + tail, bf16), v((pieces, 3) + tail, bf16), v((pieces, 2) + tail, bf16),
        v((4, 1, 4, 2, 2) + tail, bf16), v((4, 1, 4, 2) + tail, bf16), v((4, 1, 4) + tail, bf16), v((4, 1) + tail, bf16),
        v((4, 4, 1) + tail, bf16), v((4, 1) + tail, bf16), v((5, tokens, width), bf16), v((8,) + w.shape[1:], bf16), v((2, tokens, width), f32),
        v((tokens, width), f32), tok, tok, tok, v((tokens, LANES), f32), v((16, tokens), f32),
        v((LANES, width), f32),
        dma((3 * chunks + 9 + pairs,)), dma(())] + [dma((pieces, 4))] * 2 + [dma((pieces,))] * 12 + [dma((4, 4))] * 2 + [dma((4,))] * 6
    return pl.pallas_call(
        functools.partial(back_kernel, heads),
        out_shape=(sh((tokens, width), bf16), sh((pieces, own_rows, PIECE), f32), sh((4, own_rows, LANES), f32)),
        in_specs=[hbm] * 11 + [vmem] * 4,
        out_specs=(hbm, vmem, vmem),
        scratch_shapes=scratch,
        compiler_params=pltpu.CompilerParams(collective_id=1, has_side_effects=True, vmem_limit_bytes=63 * 2**20),
        name="back",
    )(x, c, y1, dz, dh2, n1, r1, g, gp, qkv, w, seg, lse, dv, vec)


def update_kernel(rates, sum_ref, vsum_ref, gin_hbm, out_hbm, am, aw, aa, dm, dw, da, vm, vw, va,
                  gin_o, out_o, am_o, aw_o, aa_o, dm_o, dw_o, da_o, vm_o, vw_o, va_o, square, tok, att, den, ld, st):
    matrix, vector, replicas = rates
    moves = [(dm, den.at[0], dm_o), (dw, den.at[1], dw_o), (da, den.at[2], da_o), (am, att.at[0], am_o), (aw, att.at[1], aw_o),
             (aa, att.at[2], aa_o), (gin_hbm, tok.at[0], gin_o), (out_hbm, tok.at[1], out_o)]
    loads = [pltpu.make_async_copy(s, d, ld.at[k]) for k, (s, d, _) in enumerate(moves)]
    stores = [pltpu.make_async_copy(d, o, st.at[k]) for k, (_, d, o) in enumerate(moves)]
    for c in loads:
        c.start()

    def advance(grad, rate, moment, weight, average):
        grad = grad / replicas
        moment = momentum_decay * moment + grad
        weight = weight - rate * (grad + momentum_decay * moment)
        return moment, weight, average_decay * average + (1.0 - average_decay) * weight

    def advance_in(grad, ref, index):
        news = advance(grad, matrix, *(ref[(k,) + index] for k in range(3)))
        for k in range(3):
            ref[(k,) + index] = news[k]

    rows, own = vm.shape
    square[...] = jnp.zeros_like(square)
    square[:own, :] = vsum_ref[3]
    vm_o[...], vw_o[...], va_o[...] = advance(square[...].T[:rows, :own], vector, vm[...], vw[...], va[...])
    every = slice(None)
    pairs = att.shape[3] // LANES
    ff_pieces = sum_ref.shape[0] - 1 - pairs
    for c in loads[:3]:
        c.wait()
    for i in range(ff_pieces):
        col = i // 4 * 2 * PIECE + i % 2 * PIECE
        advance_in(sum_ref[i], den, (1 - i % 4 // 2, every, slice(col, col + PIECE)))
    for c in stores[:3]:
        c.start()
    for c in loads[3:6]:
        c.wait()
    for i in range(2):
        advance_in(sum_ref[ff_pieces + i], att, (3, every, slice(i * PIECE, (i + 1) * PIECE)))
    for p in range(pairs):
        for k in range(3):
            grad = vsum_ref[k] if p == pairs - 1 else sum_ref[ff_pieces + 2 + p, :, k * LANES : (k + 1) * LANES]
            advance_in(grad, att, (k, every, slice(p * LANES, (p + 1) * LANES)))
    for c in loads[6:]:
        c.wait()
    for c in stores[3:]:
        c.start()
    for c in stores:
        c.wait()


def update(rates, sums, vsums, gin, out, states):
    am, dm = states[0], states[3]
    sh = jax.ShapeDtypeStruct
    v = pltpu.VMEM
    hbm = pl.BlockSpec(memory_space=pl.ANY)
    vmem = pl.BlockSpec(memory_space=pltpu.VMEM)
    places = [hbm] * 8 + [vmem] * 3
    return pl.pallas_call(
        functools.partial(update_kernel, rates),
        out_shape=(sh(gin.shape, bf16), sh(out.shape, bf16)) + tuple(sh(s.shape, f32) for s in states),
        in_specs=[vmem, vmem] + places,
        out_specs=tuple(places),
        scratch_shapes=[v((LANES, LANES), f32), v((2,) + gin.shape, bf16), v((3,) + am.shape, f32), v((3,) + dm.shape, f32),
                        pltpu.SemaphoreType.DMA((8,)), pltpu.SemaphoreType.DMA((8,))],
        compiler_params=pltpu.CompilerParams(vmem_limit_bytes=BIG),
        name="update",
    )(sums, vsums, gin, out, *states)


def pack_columns(attention, dense, vectors):
    count = vectors.shape[0]
    vector_cols = jnp.pad(vectors.T, ((0, 0), (0, 128 - count)))
    first = jnp.concatenate([attention[0], attention[1], attention[2], vector_cols], 1)
    second = jnp.concatenate([attention[3], dense[0], dense[1]], 1)
    return first, second


def advance(gradient, moment, weight, average, step_rate):
    moment_new = momentum_decay * moment + gradient
    weight_new = weight - step_rate * (gradient + momentum_decay * moment_new)
    average_new = average_decay * average + (1.0 - average_decay) * weight_new
    return (moment_new, weight_new, average_new)


def plain_body(
    hidden_in,
    segment_ids,
    cotangent,
    attention_weights,
    attention_momentum,
    attention_average,
    dense_weights,
    dense_momentum,
    dense_average,
    vector_params,
    vector_momentum,
    vector_average,
):
    row_count, length, width = hidden_in.shape
    ff = dense_weights.shape[-1]
    vector_rows = vector_params.shape[0]
    x = hidden_in.reshape(-1, width)
    e = cotangent.reshape(-1, width)
    first, second = pack_columns(attention_weights, dense_weights, vector_params)
    first_full = lax.all_gather(first.astype(bf16), "wide", axis=0, tiled=True)
    second_full = lax.all_gather(second.astype(bf16), "wide", axis=0, tiled=True)
    vec = first_full[:, 3 * width : 3 * width + vector_rows].astype(f32).T
    bias_qkv = jnp.concatenate([vec[4:5], jnp.zeros((1, width), f32), vec[5:6]], 1)
    w_qkv = first_full[:, : 3 * width]
    wo, win, wd = (second_full[:, :width], second_full[:, width : width + ff], second_full[:, width + ff :])
    qkv, c, lse = attn_fwd(x, segment_ids, w_qkv, bias_qkv)
    out, y1, g, dz, du, da, dc, dh1, delta, dvec, dbin = mid(
        x, c, e, wo, win, wd, vec, vec[8:].reshape(1, ff)
    )
    grad_second = jnp.concatenate([wgrad(c, da), wgrad(y1, du), wgrad(dz, g)], 1)
    share_second = lax.psum_scatter(grad_second, "wide", scatter_dimension=0, tiled=True)
    dqkv, gin, dw, db = attn_bwd(segment_ids, qkv, dc, lse, delta, dh1, w_qkv, x)
    dvec = jnp.concatenate(
        [dvec[:4], db[:, :width], db[:, 2 * width :], dvec[6:8], dbin.reshape(-1, width)], 0
    )
    grad_first = jnp.concatenate(
        [dw, jnp.pad(dvec.T, ((0, 0), (0, 128 - vector_rows))).astype(bf16)], 1
    )
    share_first = lax.psum_scatter(grad_first, "wide", scatter_dimension=0, tiled=True)
    replicas = lax.axis_size("narrow")
    tokens_all = row_count * length * lax.axis_size("wide") * replicas
    grad_scale = math.sqrt(tokens_all) / replicas
    t1 = lax.psum(share_first, "narrow").astype(f32) / replicas
    t2 = lax.psum(share_second, "narrow").astype(f32) / replicas
    cut = lambda t, j: t[:, j * width : (j + 1) * width]
    attention_grad = jnp.stack([cut(t1, 0), cut(t1, 1), cut(t1, 2), cut(t2, 0)])
    dense_grad = jnp.stack([t2[:, width : width + ff], t2[:, width + ff :]])
    vector_grad = t1[:, 3 * width : 3 * width + vector_rows].T
    attention_new = advance(attention_grad, attention_momentum, attention_weights, attention_average, matrix_rate / grad_scale)
    dense_new = advance(dense_grad, dense_momentum, dense_weights, dense_average, matrix_rate / grad_scale)
    vector_new = advance(vector_grad, vector_momentum, vector_params, vector_average, vector_rate / grad_scale)
    return (out.reshape(hidden_in.shape), gin.reshape(hidden_in.shape)) + attention_new + dense_new + vector_new


def body(
    hidden_in,
    segment_ids,
    cotangent,
    attention_weights,
    attention_momentum,
    attention_average,
    dense_weights,
    dense_momentum,
    dense_average,
    vector_params,
    vector_momentum,
    vector_average,
):
    row_count, length, width = hidden_in.shape
    x = hidden_in.reshape(-1, width)
    e = cotangent.reshape(-1, width)
    replicas = lax.axis_size("narrow")
    tokens_all = row_count * length * lax.axis_size("wide") * replicas
    grad_scale = math.sqrt(tokens_all) / replicas
    rates = (matrix_rate / grad_scale, vector_rate / grad_scale, replicas)
    qkv, c, lse, w, out, y1, g, gp, dz, dh2, n1, r1, dv, vec = stage(
        x, segment_ids, e, attention_weights, dense_weights, vector_params
    )
    states = (
        attention_momentum, attention_weights, attention_average,
        dense_momentum, dense_weights, dense_average,
        vector_momentum, vector_params, vector_average,
    )
    gin, sums, vsums = back(x, c, y1, dz, dh2, n1, r1, g, gp, qkv, w, segment_ids, lse, dv, vec)
    news = update(rates, sums, vsums, gin, out, states)
    return (news[1].reshape(hidden_in.shape), news[0].reshape(hidden_in.shape)) + tuple(news[2:])


def solution(mesh):
    token = P(("wide", "narrow"), None, None)
    matrix = P(None, "wide", None)
    vector = P(None, "wide")
    in_specs = (token, P(("wide", "narrow"), None), token) + (matrix,) * 6 + (vector,) * 3
    out_specs = (token, token) + (matrix,) * 6 + (vector,) * 3
    ours = mesh.shape["wide"] == 16 and mesh.shape["narrow"] == 2
    return jax.shard_map(body if ours else plain_body, mesh=mesh, in_specs=in_specs, out_specs=out_specs, check_vma=False)
```

```python
import functools, math
import jax, jax.numpy as jnp
from jax import lax
from jax.sharding import PartitionSpec as P
from jax.experimental import pallas as pl
from jax.experimental.pallas import tpu as pltpu

HD = 64
LOG2E = 1.4426950408889634
SCALE2 = 0.125 * LOG2E
NEG = -1e30
EPS = 1e-12
momentum_decay = 0.5
average_decay = 0.5
matrix_rate = 0.03
vector_rate = 0.3
f32, bf16 = jnp.float32, jnp.bfloat16
BIG = 60 * 2**20

def dot(a, b):
    return lax.dot_general(a, b, (((1,), (0,)), ((), ())), preferred_element_type=f32)
def dot_nt(a, b):
    return lax.dot_general(a, b, (((1,), (1,)), ((), ())), preferred_element_type=f32)
def dot_tn(a, b):
    return lax.dot_general(a, b, (((0,), (0,)), ((), ())), preferred_element_type=f32)

def key_range(c, seq, blk):
    lo = max(0, c * blk - seq // 2 + 1) // blk * blk
    hi = min(seq, -(-((c + 1) * blk - 1 + seq // 2) // blk) * blk)
    return lo, hi

def fill_bias(seg_ref, bias_ref):
    segf = seg_ref[0].astype(f32)
    seq = segf.shape[1]
    rep = jnp.broadcast_to(segf, (128, seq)).T
    for j in range(seq // 128):
        bias_ref[:, j * 128:(j + 1) * 128] = jnp.where(rep == segf[:, j * 128:(j + 1) * 128], 0.0, NEG)

def fwd_kernel(blk, x_ref, seg_ref, w_ref, b_ref, qkv_ref, c_ref, lse_ref, bias_ref, lsea_ref):
    seq, width = x_ref.shape
    x = x_ref[...]
    for j in range(3):
        sl = slice(j * width, (j + 1) * width)
        qkv_ref[:, sl] = (dot(x, w_ref[:, sl]) + b_ref[:, sl]).astype(bf16)
    fill_bias(seg_ref, bias_ref)
    lane = lax.broadcasted_iota(jnp.int32, (blk, 128), 1)
    first = lane < HD
    ones = jnp.ones((seq, 128), bf16)
    def pair(p, _):
        col = pl.multiple_of(p * 128, 128)
        q2 = qkv_ref[:, pl.ds(col, 128)]
        k2 = qkv_ref[:, pl.ds(col + width, 128)]
        v2 = jnp.concatenate([qkv_ref[:, pl.ds(col + 2 * width, 128)], ones], 1)
        for c in range(seq // blk):
            lo, hi = key_range(c, seq, blk)
            rows = slice(c * blk, (c + 1) * blk)
            qc = q2[rows]
            outs = []
            la = lsea_ref[rows, :]
            for h in range(2):
                qm = jnp.where(first if h == 0 else ~first, qc, jnp.zeros_like(qc))
                s = dot_nt(qm, k2[lo:hi]) + bias_ref[rows, lo:hi]
                m = jnp.max(s, 1, keepdims=True)
                e = jnp.exp2((s - m) * SCALE2)
                o = dot(e.astype(bf16), v2[lo:hi])
                l = o[:, 128:]
                outs.append(o[:, :128] / l)
                la = jnp.where(lane == 2 * p + h, m * SCALE2 + jnp.log(l) * LOG2E, la)
            lsea_ref[rows, :] = la
            c_ref[rows, pl.ds(col, 128)] = jnp.where(first, outs[0], outs[1]).astype(bf16)
        return 0
    lax.fori_loop(0, width // 128, pair, 0)
    lse_ref[0] = lsea_ref[...].T[:lse_ref.shape[1]]

def attn_fwd(x, seg, w, b, blk=128):
    rows, seq = seg.shape
    width = x.shape[1]
    return pl.pallas_call(
        functools.partial(fwd_kernel, blk), grid=(rows,),
        out_shape=(jax.ShapeDtypeStruct((rows * seq, 3 * width), bf16), jax.ShapeDtypeStruct((rows * seq, width), bf16),
                   jax.ShapeDtypeStruct((rows, 16, seq), f32)),
        in_specs=[pl.BlockSpec((seq, width), lambda r: (r, 0)), pl.BlockSpec((1, 1, seq), lambda r: (r, 0, 0)),
                  pl.BlockSpec((width, 3 * width), lambda r: (0, 0)), pl.BlockSpec((1, 3 * width), lambda r: (0, 0))],
        out_specs=(pl.BlockSpec((seq, 3 * width), lambda r: (r, 0)), pl.BlockSpec((seq, width), lambda r: (r, 0)),
                   pl.BlockSpec((1, 16, seq), lambda r: (r, 0, 0))),
        scratch_shapes=[pltpu.VMEM((seq, seq), f32), pltpu.VMEM((seq, 128), f32)],
        compiler_params=pltpu.CompilerParams(vmem_limit_bytes=BIG),
        name="attn_fwd",
    )(x, seg.reshape(rows, 1, seq), w, b)

def bwd_kernel(blk, seg_ref, qkv_ref, dc_ref, lse_ref, delta_ref, dh1_ref, w_ref, x_ref, dqkv_ref, gin_ref, dw_ref, db_ref, bias_ref, ds_ref, acc_ref):
    r = pl.program_id(0)
    seq = dc_ref.shape[0]
    width = dc_ref.shape[1]
    fill_bias(seg_ref, bias_ref)
    ds_ref[...] = jnp.zeros_like(ds_ref)
    lane = lax.broadcasted_iota(jnp.int32, (blk, 128), 1)
    first = lane < HD
    lane_s = lax.broadcasted_iota(jnp.int32, (seq, 128), 1)
    def pair(p, _):
        col = pl.multiple_of(p * 128, 128)
        q2 = qkv_ref[:, pl.ds(col, 128)]
        k2 = qkv_ref[:, pl.ds(col + width, 128)]
        v2 = qkv_ref[:, pl.ds(col + 2 * width, 128)]
        dc2 = dc_ref[:, pl.ds(col, 128)]
        dqs = []
        for h in range(2):
            lse = lse_ref[0, pl.ds(2 * p + h, 1), :]
            dl = delta_ref[pl.ds(2 * p + h, 1), :]
            mine = first if h == 0 else ~first
            for c in range(seq // blk):
                lo, hi = key_range(c, seq, blk)
                rows = slice(c * blk, (c + 1) * blk)
                kc, vc = k2[rows], v2[rows]
                km = jnp.where(mine, kc, jnp.zeros_like(kc))
                vm = jnp.where(mine, vc, jnp.zeros_like(vc))
                st = dot_nt(km, q2[lo:hi])
                pt = jnp.exp2((st + bias_ref[rows, lo:hi]) * SCALE2 - lse[:, lo:hi])
                dp = dot_nt(vm, dc2[lo:hi])
                ds = (pt * (dp - dl[:, lo:hi])).astype(bf16)
                ds_ref[h, rows, lo:hi] = ds
                dv = dot(pt.astype(bf16), dc2[lo:hi])
                dk = dot(ds, q2[lo:hi]) * 0.125
                if h == 0:
                    dqkv_ref[rows, pl.ds(col + 2 * width, 128)] = dv.astype(bf16)
                    dqkv_ref[rows, pl.ds(col + width, 128)] = dk.astype(bf16)
                else:
                    ov = dqkv_ref[rows, pl.ds(col + 2 * width, 128)]
                    ok = dqkv_ref[rows, pl.ds(col + width, 128)]
                    dqkv_ref[rows, pl.ds(col + 2 * width, 128)] = jnp.where(first, ov, dv.astype(bf16))
                    dqkv_ref[rows, pl.ds(col + width, 128)] = jnp.where(first, ok, dk.astype(bf16))
            dqs.append(dot_tn(ds_ref[h], k2) * 0.125)
        dqkv_ref[:, pl.ds(col, 128)] = jnp.where(lane_s < HD, dqs[0], dqs[1]).astype(bf16)
        return 0
    lax.fori_loop(0, width // 128, pair, 0)
    dqkv = dqkv_ref[...]
    gin_ref[...] = (dh1_ref[...] + dot_nt(dqkv, w_ref[...])).astype(bf16)
    x = x_ref[...]
    for j in range(3):
        sl = slice(j * width, (j + 1) * width)
        d = dot_tn(x, dqkv[:, sl])
        s = jnp.sum(dqkv[:, sl].astype(f32), 0, keepdims=True)
        @pl.when(r == 0)
        def _():
            acc_ref[:, sl] = d
            db_ref[:, sl] = s
        @pl.when(r == pl.num_programs(0) - 1)
        def _():
            dw_ref[:, sl] = (acc_ref[:, sl] + d).astype(bf16)
            db_ref[:, sl] += s

def attn_bwd(seg, qkv, dc, lse, delta, dh1, w, x, blk=128):
    rows, seq = seg.shape
    width = dc.shape[1]
    assert rows == 2
    return pl.pallas_call(
        functools.partial(bwd_kernel, blk), grid=(rows,),
        out_shape=(jax.ShapeDtypeStruct((rows * seq, 3 * width), bf16), jax.ShapeDtypeStruct((rows * seq, width), bf16),
                   jax.ShapeDtypeStruct((width, 3 * width), bf16), jax.ShapeDtypeStruct((1, 3 * width), f32)),
        in_specs=[pl.BlockSpec((1, 1, seq), lambda r: (r, 0, 0)), pl.BlockSpec((seq, 3 * width), lambda r: (r, 0)),
                  pl.BlockSpec((seq, width), lambda r: (r, 0)), pl.BlockSpec((1, 16, seq), lambda r: (r, 0, 0)),
                  pl.BlockSpec((16, seq), lambda r: (0, r)), pl.BlockSpec((seq, width), lambda r: (r, 0)),
                  pl.BlockSpec((width, 3 * width), lambda r: (0, 0)), pl.BlockSpec((seq, width), lambda r: (r, 0))],
        out_specs=(pl.BlockSpec((seq, 3 * width), lambda r: (r, 0)), pl.BlockSpec((seq, width), lambda r: (r, 0)),
                   pl.BlockSpec((width, 3 * width), lambda r: (0, 0)), pl.BlockSpec((1, 3 * width), lambda r: (0, 0))),
        scratch_shapes=[pltpu.VMEM((seq, seq), f32), pltpu.VMEM((2, seq, seq), bf16), pltpu.VMEM((width, 3 * width), f32)],
        compiler_params=pltpu.CompilerParams(vmem_limit_bytes=BIG),
        name="attn_bwd",
    )(seg.reshape(rows, 1, seq), qkv, dc, lse, delta, dh1, w, x)

RSQRT_2PI = 1.0 / math.sqrt(2 * math.pi)
def gelu_parts(u):
    phi_cdf = 0.5 + 0.5 * lax.erf(u * math.sqrt(0.5))
    dens = jnp.exp2(u * u * (-0.5 * LOG2E)) * RSQRT_2PI
    return u * phi_cdf, phi_cdf + u * dens

def mid_kernel(chunk, x_ref, c_ref, e_ref, wo_ref, win_ref, wd_ref, v_ref, bin_ref,
               out_ref, y1_ref, g_ref, dz_ref, du_ref, da_ref, dc_ref, dh1_ref, delta_ref, dv_ref, dbin_ref, gp_ref):
    i = pl.program_id(0)
    blk, width = x_ref.shape
    ff = win_ref.shape[1]
    @pl.when(i == 0)
    def _():
        dv_ref[...] = jnp.zeros_like(dv_ref)
        dbin_ref[...] = jnp.zeros_like(dbin_ref)
    g1, s1, g2, s2, bo, bd = (v_ref[j:j + 1, :] for j in (0, 1, 2, 3, 6, 7))
    cb = c_ref[...]
    h1 = x_ref[...].astype(f32) + (dot(cb, wo_ref[...]) + bo)
    cen = h1 - jnp.mean(h1, 1, keepdims=True)
    r1 = lax.rsqrt(jnp.mean(cen * cen, 1, keepdims=True) + EPS)
    n1 = cen * r1
    y1 = n1 * g1 + s1
    y1l = y1.astype(bf16)
    y1_ref[...] = y1l
    z = jnp.zeros((blk, width), f32)
    for j in range(ff // chunk):
        sl = slice(j * chunk, (j + 1) * chunk)
        u = dot(y1l, win_ref[:, sl]) + bin_ref[:, sl]
        g, gp = gelu_parts(u)
        gl = g.astype(bf16)
        g_ref[:, sl] = gl
        gp_ref[:, sl] = gp
        z += dot_nt(gl, wd_ref[:, sl])
    h2 = y1 + (z + bd)
    cen = h2 - jnp.mean(h2, 1, keepdims=True)
    r2 = lax.rsqrt(jnp.mean(cen * cen, 1, keepdims=True) + EPS)
    n2 = cen * r2
    out_ref[...] = (n2 * g2 + s2).astype(bf16)
    e = e_ref[...].astype(f32)
    eg = e * g2
    dh2 = r2 * (eg - jnp.mean(eg, 1, keepdims=True) - n2 * jnp.mean(eg * n2, 1, keepdims=True))
    dz = dh2.astype(bf16)
    dz_ref[...] = dz
    dy1 = dh2
    for j in range(ff // chunk):
        sl = slice(j * chunk, (j + 1) * chunk)
        du = (dot(dz, wd_ref[:, sl]) * gp_ref[:, sl]).astype(bf16)
        du_ref[:, sl] = du
        dbin_ref[:, sl] += jnp.sum(du.astype(f32), 0, keepdims=True)
        dy1 += dot_nt(du, win_ref[:, sl])
    dn = dy1 * g1
    dh1 = r1 * (dn - jnp.mean(dn, 1, keepdims=True) - n1 * jnp.mean(dn * n1, 1, keepdims=True))
    dh1_ref[...] = dh1
    da = dh1.astype(bf16)
    da_ref[...] = da
    dc = dot_nt(da, wo_ref[...]).astype(bf16)
    dc_ref[...] = dc
    prod = dc.astype(f32) * cb.astype(f32)
    hi = prod.astype(bf16)
    lo = (prod - hi.astype(f32)).astype(bf16)
    sel = jnp.where(lax.broadcasted_iota(jnp.int32, (16, width), 0) == lax.broadcasted_iota(jnp.int32, (16, width), 1) // HD, 1.0, 0.0).astype(bf16)
    delta_ref[...] = dot_nt(sel, hi) + dot_nt(sel, lo)
    parts = [dy1 * n1, dy1, e * n2, e, da.astype(f32), dz.astype(f32)]
    for j, t in zip((0, 1, 2, 3, 6, 7), parts):
        dv_ref[j:j + 1, :] += jnp.sum(t, 0, keepdims=True)

def mid(x, c, e, wo, win, wd, vec, bin_, blk=256, chunk=768):
    n, width = x.shape
    ff = win.shape[1]
    tok = lambda w: pl.BlockSpec((blk, w), lambda i: (i, 0))
    full = lambda a: pl.BlockSpec(a.shape, lambda i: (0, 0), pipeline_mode=pl.Buffered(1))
    sh = jax.ShapeDtypeStruct
    return pl.pallas_call(
        functools.partial(mid_kernel, chunk), grid=(n // blk,),
        out_shape=(sh((n, width), bf16), sh((n, width), bf16), sh((n, ff), bf16), sh((n, width), bf16), sh((n, ff), bf16),
                   sh((n, width), bf16), sh((n, width), bf16), sh((n, width), f32), sh((16, n), f32), sh((8, width), f32), sh((1, ff), f32)),
        in_specs=[tok(width), tok(width), tok(width), full(wo), full(win), full(wd), full(vec), full(bin_)],
        out_specs=(tok(width), tok(width), tok(ff), tok(width), tok(ff), tok(width), tok(width), tok(width),
                   pl.BlockSpec((16, blk), lambda i: (0, i)), pl.BlockSpec((8, width), lambda i: (0, 0)), pl.BlockSpec((1, ff), lambda i: (0, 0))),
        scratch_shapes=[pltpu.VMEM((blk, ff), f32)],
        compiler_params=pltpu.CompilerParams(vmem_limit_bytes=BIG),
        name="middle",
    )(x, c, e, wo, win, wd, vec, bin_)

def wgrad_kernel(a_ref, b_ref, o_ref):
    o_ref[...] = dot_tn(a_ref[...], b_ref[...]).astype(bf16)

def wgrad(a, b, blk=768):
    n, m = a.shape
    k = b.shape[1]
    return pl.pallas_call(wgrad_kernel, grid=(k // blk,), out_shape=jax.ShapeDtypeStruct((m, k), bf16),
        in_specs=[pl.BlockSpec((n, m), lambda j: (0, 0)), pl.BlockSpec((n, blk), lambda j: (0, j))],
        out_specs=pl.BlockSpec((m, blk), lambda j: (0, j)),
        compiler_params=pltpu.CompilerParams(vmem_limit_bytes=BIG), name="wgrad")(a, b)


LANES = 128
PIECE = 3 * LANES
GATHER_LAGS = (0, 2, 4, 6)
REDUCE_LAGS = (2, 4, 6, 8)
AHEAD = 3
MESH = pl.DeviceIdType.MESH


class Place:
    def __init__(self):
        self.w = lax.axis_index("wide")
        self.x = lax.axis_index("narrow")
        self.core = lax.rem(self.w, 2)
        self.y = lax.rem(self.w // 2, 2)
        self.b = lax.rem(self.w // 4, 2)
        self.a = self.w // 8
        self.z = self.w // 4

    def z_peer(self, k):
        return lax.rem(self.z + k, 4)

    def over(self, name):
        if name == "x":
            return (self.w, 1 - self.x)
        if name in (1, 2, 3):
            return (4 * self.z_peer(name) + lax.rem(self.w, 4), self.x)
        step = {"a": 8, "b": 4, "y": 2, "core": 1}[name]
        return (self.w + step * (1 - 2 * getattr(self, name)), self.x)

    near = ("a", "b", "y", "x", "core")
    reduce_peers = (1, 2, 3, "y", "x", "core")

    def greet(self, names):
        for name in names:
            pl.semaphore_signal(pltpu.get_barrier_semaphore(), inc=1, device_id=self.over(name), device_id_type=MESH)

    def met(self, names):
        pl.semaphore_wait(pltpu.get_barrier_semaphore(), len(names))


def remote(src, dst, send, recv, device):
    return pltpu.make_async_remote_copy(src_ref=src, dst_ref=dst, send_sem=send, recv_sem=recv, device_id=device, device_id_type=MESH)


def when(condition, step):
    @pl.when(condition)
    def _():
        step()


def loop(count, step):
    lax.fori_loop(0, count, lambda i, _: (step(i), 0)[1], 0)


class Gather:
    def __init__(self, place, shard, full, sems, pieces):
        self.p, self.shard, self.full, self.pieces = place, shard, full, pieces
        self.sems = {name: (sems[2 * k], sems[2 * k + 1]) for k, name in enumerate(("a", "b", "y", "x", "core"))}
        self.kept = sems[10]
        self.own = pl.ds(place.x, 2)

    def mine(self, i, a):
        return self.full.at[i, self.own, a, self.p.b, self.p.y, self.p.core]

    def keep(self, i):
        return pltpu.make_async_copy(self.shard.at[i, self.own], self.mine(i, self.p.a), self.kept.at[i])

    def copy(self, name, i, incoming=False):
        p, f = self.p, self.full
        at = {n: (1 - getattr(p, n) if incoming and n == name else getattr(p, n)) for n in ("a", "b", "y", "x", "core")}
        every = slice(None)
        if name == "a":
            dst = self.mine(i, at["a"])
            src = self.shard.at[i, self.own]
        else:
            if name == "b":
                dst = f.at[i, self.own, :, at["b"], p.y, p.core]
            elif name == "y":
                dst = f.at[i, self.own, :, :, at["y"], p.core]
            elif name == "x":
                dst = f.at[i, 2 * at["x"], :, :, :, p.core]
            else:
                dst = f.at[i, :, :, :, :, at["core"]]
            src = dst
        send, recv = self.sems[name]
        return remote(src, dst, send.at[i], recv.at[i], p.over(name))

    def start(self, i):
        self.keep(i).start()
        self.copy("a", i).start()

    def b_step(self, i):
        self.keep(i).wait()
        self.copy("a", i, True).wait_recv()
        self.copy("b", i).start()

    def y_step(self, i):
        self.copy("b", i, True).wait_recv()
        self.copy("y", i).start()

    def x_step(self, i):
        self.copy("y", i, True).wait_recv()
        self.copy("x", i).start()

    def core_step(self, i):
        self.copy("x", i, True).wait_recv()
        self.copy("core", i).start()

    def arrive(self, i):
        self.copy("core", i, True).wait_recv()

    def turn(self, t):
        for k in range(2):
            ahead = AHEAD + 2 * t + k
            when(ahead < self.pieces, lambda ahead=ahead: self.start(ahead))
        for lag, step in zip(GATHER_LAGS, (self.b_step, self.y_step, self.x_step, self.core_step)):
            when((t >= lag) & (t < self.pieces + lag), lambda lag=lag, step=step: step(t - lag))

    def sent(self, i):
        for name in ("a", "b", "y", "x", "core"):
            self.copy(name, i).wait_send()


class GatherVector:
    def __init__(self, place, shard, full, sems):
        self.p, self.shard, self.full = place, shard, full
        self.sems = {name: (sems[2 * k], sems[2 * k + 1]) for k, name in enumerate(("a", "b", "y", "core"))}
        self.kept = sems[8]

    def keep(self):
        p = self.p
        return pltpu.make_async_copy(self.shard, self.full.at[p.a, p.b, p.y, p.core], self.kept)

    def copy(self, name, incoming=False):
        p = self.p
        at = {n: (1 - getattr(p, n) if incoming and n == name else getattr(p, n)) for n in ("a", "b", "y", "core")}
        every = slice(None)
        first = ("a", "b", "y", "core").index(name)
        dst = self.full.at[tuple(at[n] if n == name or n == "core" or k > first else every for k, n in enumerate(("a", "b", "y", "core")))]
        src = self.shard if name == "a" else dst
        send, recv = self.sems[name]
        return remote(src, dst, send, recv, p.over(name))

    def start(self):
        self.keep().start()
        self.copy("a").start()

    def step(self, name, then):
        if name == "a":
            self.keep().wait()
        self.copy(name, True).wait_recv()
        self.copy(then).start()

    def arrive(self):
        self.copy("core", True).wait_recv()

    def sent(self):
        for name in ("a", "b", "y", "core"):
            self.copy(name).wait_send()


def tile(ref, i, t):
    rows = 16 * ref.shape[-2]
    return ref[i, t].reshape(rows, LANES)


def columns(ref, *pieces):
    return jnp.concatenate([tile(ref, i, t) for i in pieces for t in range(3)], 1)


def doc_bias(seg_row, bias_ref, r):
    segf = seg_row.astype(f32)
    seq = segf.shape[1]
    rep = jnp.broadcast_to(segf, (LANES, seq)).T
    for j in range(seq // LANES):
        sl = slice(j * LANES, (j + 1) * LANES)
        bias_ref[r, :, sl] = jnp.where(rep == segf[:, sl], 0.0, NEG)


def stage_kernel(heads, x_hbm, seg_ref, e_hbm, aw_hbm, dw_hbm, vp_ref,
                 qkv_o, c_o, lse_o, w_o, out_o, y1_o, g_o, gp_o, dz_o, dh2_o, n1_o, r1_o, dv_o, vrow,
                 full, vfull, shard, vshard, square, xb, eb, cb, n1b, y1b, acc, gp, gb, dzb, bias, lsea, binr, r1b,
                 in_sem, out_sem, w_sem, two_sem, *sems):
    place = Place()
    rows, seq = seg_ref.shape
    tokens, width = x_hbm.shape
    pairs = heads // 2
    pieces = shard.shape[0]
    chunks = gb.shape[0]
    own_rows = aw_hbm.shape[1]
    blk = 256
    big = 512
    g = Gather(place, shard, full, sems[:11], pieces)
    gv = GatherVector(place, vshard, vfull, sems[11:])

    loads = [pltpu.make_async_copy(aw_hbm.at[k], gp.at[0, pl.ds(k * own_rows, own_rows)], in_sem.at[k]) for k in range(4)]
    for k in range(2):
        for j in range(chunks):
            loads.append(pltpu.make_async_copy(
                dw_hbm.at[k, :, pl.ds(j * width, width)], gp.at[1 + k, pl.ds(j * own_rows, own_rows)], in_sem.at[4 + k * chunks + j]))
    n = len(loads)
    x_load = pltpu.make_async_copy(x_hbm, xb, in_sem.at[n])
    e_load = pltpu.make_async_copy(e_hbm, eb, in_sem.at[n + 1])
    for c in loads:
        c.start()
    place.greet(place.near)
    x_load.start()
    e_load.start()
    square[...] = jnp.zeros_like(square)
    lsea[...] = jnp.zeros_like(lsea)
    square[: vp_ref.shape[0], :own_rows] = vp_ref[...]
    vshard[...] = square[...].T[:own_rows].astype(bf16)

    def own_tile(k, j, t):
        return gp[k, j * own_rows : (j + 1) * own_rows, t * LANES : (t + 1) * LANES].astype(bf16)

    for c in loads[:3]:
        c.wait()
    for p in range(pairs):
        for t in range(3):
            shard[p, t] = own_tile(0, t, p)
    place.met(place.near)
    gv.start()
    for i in range(AHEAD):
        g.start(i)
    for c in loads[3:]:
        c.wait()
    for t in range(6):
        shard[pairs + t // 3, t % 3] = own_tile(0, 3, t)
        for j in range(chunks):
            for k in range(2):
                shard[pairs + 2 + 4 * j + 2 * k + t // 3, t % 3] = own_tile(1 + k, j, t)
    for r in range(rows):
        doc_bias(seg_ref[r : r + 1, :], bias, r)
    gv.step("a", "b")
    fill = GATHER_LAGS[-1] + 1
    for t in range(fill):
        g.turn(t)
        if t == 1:
            gv.step("b", "y")
        if t == 4:
            gv.step("y", "core")
    gv.arrive()
    vec = vfull[...].reshape(16 * own_rows, LANES).astype(f32).T
    vrow[...] = vec[: vrow.shape[0]]
    for j in range(chunks):
        binr[j] = vrow[8 + j : 9 + j, :]
    x_load.wait()

    first = lax.broadcasted_iota(jnp.int32, (LANES, LANES), 1) < HD
    lane = lax.broadcasted_iota(jnp.int32, (LANES, LANES), 1)
    ones = jnp.ones((seq, LANES), bf16)

    def qkv_at(p):
        return gb.at[p // 2, :, pl.ds(pl.multiple_of(lax.rem(p, 2) * PIECE, LANES), PIECE)]

    def qkv_out(p):
        return pltpu.make_async_copy(qkv_at(p), qkv_o.at[p], out_sem.at[p])

    def w_out(i):
        return pltpu.make_async_copy(full.at[i], w_o.at[i], w_sem.at[i])

    def pair(p):
        g.arrive(p)
        w_out(p).start()
        head = pl.ds(pl.multiple_of(p * LANES, LANES), LANES)
        w = columns(full, p)
        b = jnp.concatenate([vrow[4:5, head], jnp.zeros((1, LANES), f32), vrow[5:6, head]], 1)
        col = pl.multiple_of(lax.rem(p, 2) * PIECE, LANES)
        gb[p // 2, :, pl.ds(col, PIECE)] = (dot(xb[...], w) + b).astype(bf16)
        qkv_out(p).start()

        def row(r):
            tok = pl.ds(pl.multiple_of(r * seq, seq), seq)
            q2 = gb[p // 2, tok, pl.ds(col, LANES)]
            k2 = gb[p // 2, tok, pl.ds(col + LANES, LANES)]
            v2 = jnp.concatenate([gb[p // 2, tok, pl.ds(col + 2 * LANES, LANES)], ones], 1)
            for c in range(seq // LANES):
                lo, hi = key_range(c, seq, LANES)
                cut = slice(c * LANES, (c + 1) * LANES)
                outs = []
                la = lsea[r, cut, :]
                for h in range(2):
                    qm = jnp.where(first if h == 0 else ~first, q2[cut], jnp.zeros_like(q2[cut]))
                    s = dot_nt(qm, k2[lo:hi]) + bias[r, cut, lo:hi]
                    m = jnp.max(s, 1, keepdims=True)
                    o = dot(jnp.exp2((s - m) * SCALE2).astype(bf16), v2[lo:hi])
                    l = o[:, LANES:]
                    outs.append(o[:, :LANES] / l)
                    la = jnp.where(lane == 2 * p + h, m * SCALE2 + jnp.log(l) * LOG2E, la)
                lsea[r, cut, :] = la
                cb[pl.ds(pl.multiple_of(r * seq + c * LANES, LANES), LANES), head] = jnp.where(first, outs[0], outs[1]).astype(bf16)
            g.turn(fill + 2 * p + r)

        loop(rows, row)

    loop(pairs, pair)
    done = fill + 2 * pairs
    for r in range(rows):
        lse_o[r] = lsea[r].T[: lse_o.shape[1]]
    c_out = pltpu.make_async_copy(cb, c_o, out_sem.at[pairs])
    c_out.start()
    g1, s1, g2, s2, bo, bd = (vrow[j : j + 1, :] for j in (0, 1, 2, 3, 6, 7))

    def block(i):
        return pl.ds(pl.multiple_of(i * blk, blk), blk)

    for i in (pairs, pairs + 1):
        g.arrive(i)
        w_out(i).start()

    def norm_one(i):
        at = block(i)
        h1 = xb[at, :].astype(f32) + (dot(cb[at, :], columns(full, pairs, pairs + 1)) + bo)
        cen = h1 - jnp.mean(h1, 1, keepdims=True)
        r1 = lax.rsqrt(jnp.mean(cen * cen, 1, keepdims=True) + EPS)
        n1 = cen * r1
        y1 = n1 * g1 + s1
        n1b[at, :] = n1
        r1b[at, :] = jnp.broadcast_to(r1, (blk, LANES))
        y1b[at, :] = y1.astype(bf16)
        acc[at, :] = y1 + bd
        when(lax.rem(i, 2) == 1, lambda: g.turn(done + i // 2))

    loop(tokens // blk, norm_one)
    done += 2
    y1_out = pltpu.make_async_copy(y1b, y1_o, out_sem.at[pairs + 2])
    y1_out.start()
    n1_out = pltpu.make_async_copy(n1b, n1_o, out_sem.at[pairs + 1])
    n1_out.start()
    r1_out = pltpu.make_async_copy(r1b, r1_o, out_sem.at[pairs + 5 + chunks])
    r1_out.start()
    loop(pairs, lambda p: qkv_out(p).wait())

    def up(j):
        return columns(full, pairs + 2 + 4 * j, pairs + 3 + 4 * j)

    def down(j):
        return columns(full, pairs + 4 + 4 * j, pairs + 5 + 4 * j)

    def g_out(j):
        return pltpu.make_async_copy(gb.at[j], g_o.at[j], out_sem.at[pairs + 7 + j])

    def gp_out(j):
        return pltpu.make_async_copy(gp.at[j], gp_o.at[j], out_sem.at[pairs + 7 + chunks + j])

    def ff_chunk(j):
        def ready(k):
            for t in (k, k + 1):
                g.arrive(pairs + 2 + 4 * j + t)
                w_out(pairs + 2 + 4 * j + t).start()

        def up_block(i):
            at = pl.ds(pl.multiple_of(i * big, big), big)
            act, slope = gelu_parts(dot(y1b[at, :], up(j)) + binr[j])
            gb[j, at, :] = act.astype(bf16)
            gp[j, at, :] = slope
            g.turn(done + 4 * j + i)

        def down_block(i):
            at = pl.ds(pl.multiple_of(i * big, big), big)
            acc[at, :] += dot_nt(gb[j, at, :], down(j))
            g.turn(done + 4 * j + 2 + i)

        ready(0)
        loop(tokens // big, up_block)
        g_out(j).start()
        gp_out(j).start()
        ready(2)
        loop(tokens // big, down_block)

    loop(chunks, ff_chunk)
    e_load.wait()
    dv_o[...] = jnp.zeros_like(dv_o)

    def colsum(t):
        return jnp.sum(t, 0, keepdims=True)

    def norm_two(i):
        at = block(i)
        h2 = acc[at, :]
        cen = h2 - jnp.mean(h2, 1, keepdims=True)
        r2 = lax.rsqrt(jnp.mean(cen * cen, 1, keepdims=True) + EPS)
        n2 = cen * r2
        xb[at, :] = (n2 * g2 + s2).astype(bf16)
        e = eb[at, :].astype(f32)
        eg = e * g2
        dh2 = r2 * (eg - jnp.mean(eg, 1, keepdims=True) - n2 * jnp.mean(eg * n2, 1, keepdims=True))
        dz = dh2.astype(bf16)
        dzb[at, :] = dz
        acc[at, :] = dh2
        dv_o[2:3, :] += colsum(e * n2)
        dv_o[3:4, :] += colsum(e)
        dv_o[7:8, :] += colsum(dz.astype(f32))

    def norm_two_out(i):
        at = block(i)
        pairs_of = ((xb, out_o), (dzb, dz_o), (acc, dh2_o))
        return [pltpu.make_async_copy(src.at[at], dst.at[at], two_sem.at[k, i]) for k, (src, dst) in enumerate(pairs_of)]

    def norm_two_step(i):
        norm_two(i)
        for c in norm_two_out(i):
            c.start()

    loop(tokens // blk, norm_two_step)
    gv.sent()
    loop(pieces, g.sent)
    loop(pieces, lambda i: w_out(i).wait())
    for c in [c_out, y1_out, n1_out, r1_out]:
        c.wait()
    for i in range(tokens // blk):
        for c in norm_two_out(i):
            c.wait()
    loop(chunks, lambda j: g_out(j).wait())
    loop(chunks, lambda j: gp_out(j).wait())


def stage(x, seg, e, aw, dw, vp):
    rows, seq = seg.shape
    tokens, width = x.shape
    own_rows, ff = dw.shape[1:]
    heads, chunks = width // HD, ff // width
    pairs = heads // 2
    pieces = pairs + 2 + 4 * chunks
    sh = jax.ShapeDtypeStruct
    dma = pltpu.SemaphoreType.DMA
    v = pltpu.VMEM
    hbm = pl.BlockSpec(memory_space=pl.ANY)
    vmem = pl.BlockSpec(memory_space=pltpu.VMEM)
    tok = sh((tokens, width), bf16)
    wide = sh((chunks, tokens, width), bf16)
    long = sh((tokens, width), f32)
    block = (2, 2, 2, 2, own_rows, LANES)
    scratch = [
        v((pieces, 3) + block, bf16), v(block, bf16), v((pieces, 3, own_rows, LANES), bf16), v((own_rows, LANES), bf16),
        v((LANES, LANES), f32), v((tokens, width), bf16), v((tokens, width), bf16), v((tokens, width), bf16),
        v((tokens, width), f32), v((tokens, width), bf16), v((tokens, width), f32), v((chunks, tokens, width), f32),
        v((chunks, tokens, width), bf16), v((tokens, width), bf16), v((rows, seq, seq), f32), v((rows, seq, LANES), f32),
        v((chunks, 1, width), f32), v((tokens, LANES), f32),
        dma((6 + 2 * chunks,)), dma((pairs + 7 + 2 * chunks,)), dma((pieces,)), dma((3, tokens // 256)),
    ] + [dma((pieces,))] * 11 + [dma(())] * 9
    return pl.pallas_call(
        functools.partial(stage_kernel, heads),
        out_shape=(sh((pairs, tokens, PIECE), bf16), tok, sh((rows, 16, seq), f32), sh((pieces, 3) + block, bf16), tok, tok, wide,
                   sh((chunks, tokens, width), f32), tok, long, long, sh((tokens, LANES), f32), sh((8, width), f32), sh((16, width), f32)),
        in_specs=[hbm, vmem, hbm, hbm, hbm, vmem],
        out_specs=(hbm, hbm, vmem) + (hbm,) * 9 + (vmem, vmem),
        scratch_shapes=scratch,
        compiler_params=pltpu.CompilerParams(collective_id=0, has_side_effects=True, vmem_limit_bytes=BIG),
        name="stage",
    )(x, seg, e, aw, dw, vp)


class Reduce:
    def __init__(self, place, part, froms, done, out, sems, pieces, tiles=3):
        self.p, self.part, self.done, self.out, self.pieces, self.whole = place, part, done, out, pieces, tiles == 1
        self.names = ("core", "y", "p") if self.whole else ("core", "y", "p", "x", "early_y", "late_x")
        self.froms = dict(zip(("core", "y", "p", "z", "x", "early_y"), froms))
        self.zs, self.zr = sems[:2]
        self.sems = {name: (sems[2 + 2 * k], sems[3 + 2 * k]) for k, name in enumerate(self.names)}
        self.own = pl.ds(0, 1) if self.whole else pl.ds(place.x, 2)
        self.most = slice(None) if self.whole else pl.ds(0, 3)

    def copy(self, name, i):
        p, f, landing = self.p, self.part, self.froms
        if name == "core":
            src, dst = f.at[i, :, :, :, 1 - p.core], landing[name].at[i]
        elif name == "x":
            src, dst = f.at[i, 2 * (1 - p.x), self.most, :, p.core], landing[name].at[i, self.most]
        elif name == "late_x":
            src, dst = f.at[i, 2 * (1 - p.x), 3, p.y, p.core], landing["x"].at[i, 3, 0]
        elif name == "y":
            src, dst = f.at[i, self.own, self.most, 1 - p.y, p.core], landing[name].at[i, :, self.most]
        elif name == "early_y":
            src, dst = f.at[i, :, 3, 1 - p.y, p.core], landing[name].at[i]
        else:
            src, dst = self.done.at[i], landing[name].at[i]
        send, recv = self.sems[name]
        axis = {"p": "x", "early_y": "y", "late_x": "x"}.get(name, name)
        return remote(src, dst, send.at[i], recv.at[i], p.over(axis))

    def z_copy(self, i, k, incoming=False):
        p = self.p
        peer = p.z_peer(k)
        came = peer if incoming else p.z
        return remote(self.part.at[i, self.own, peer, p.y, p.core], self.froms["z"].at[i, came], self.zs.at[i, k], self.zr.at[i, came], p.over(k))

    def start(self, i):
        self.copy("core", i).start()

    def add(self, at, term):
        self.part[at] = self.part[at] + term

    def x_step(self, i):
        p = self.p
        self.copy("core", i).wait_recv()
        for t in range(1 if self.whole else 3):
            self.add((i, t, slice(None), slice(None), p.core), self.froms["core"][i, t])
        for name in ("y",) if self.whole else ("x", "early_y"):
            self.copy(name, i).start()

    def y_step(self, i):
        p = self.p
        self.copy("early_y", i).wait_recv()
        self.add((i, slice(None), 3, p.y, p.core), self.froms["early_y"][i])
        self.copy("late_x", i).start()
        self.copy("x", i).wait_recv()
        self.add((i, 2 * p.x, self.most, slice(None), p.core), self.froms["x"][i, :3])
        self.copy("y", i).start()

    def z_step(self, i):
        p = self.p
        self.copy("y", i).wait_recv()
        self.add((i, self.own, self.most, p.y, p.core), self.froms["y"][i, :, self.most])
        if not self.whole:
            self.copy("late_x", i).wait_recv()
            self.add((i, 2 * p.x, 3, p.y, p.core), self.froms["x"][i, 3, 0])
        for k in (2, 1, 3):
            self.z_copy(i, k).start()

    def p_step(self, i):
        p, f = self.p, self.part
        total = f[i, self.own, p.z, p.y, p.core].astype(f32)
        for k in (1, 2, 3):
            self.z_copy(i, k, True).wait_recv()
            total += self.froms["z"][i, p.z_peer(k)].astype(f32)
        self.done[i] = total.astype(bf16)
        self.copy("p", i).start()

    def finish(self, i):
        self.copy("p", i).wait_recv()
        a, b = self.done[i].astype(f32), self.froms["p"][i].astype(f32)
        if self.whole:
            self.out[i] = a[0] + b[0]
            return
        first = self.p.x == 0
        low, high = jnp.where(first, a, b), jnp.where(first, b, a)
        self.out[i] = jnp.concatenate([low[0], low[1] + high[0], high[1]], 1)

    def later(self, t):
        for lag, step in zip(REDUCE_LAGS, (self.y_step, self.z_step, self.p_step, self.finish)):
            when((t >= lag) & (t < self.pieces + lag), lambda lag=lag, step=step: step(t - lag))

    def turn(self, t):
        when(t < self.pieces, lambda: self.x_step(t))
        self.later(t)

    def sent(self, i):
        for name in self.names:
            self.copy(name, i).wait_send()
        for k in (1, 2, 3):
            self.z_copy(i, k).wait_send()


def back_kernel(heads, x_hbm, c_hbm, y1_hbm, dz_hbm, dh2_hbm, n1_hbm, r1_hbm, g_hbm, gp_hbm, qkv_hbm, w_hbm,
                seg_ref, lse_ref, dv_ref, vec_ref, gin_o, sum_o, vsum_o,
                part, fromc, fromy, fromp, fromz, fromx, frome, done, vpart, vfromc, vfromy, vfromp, vfromz, vdone, pool, wpool, gpool, acc, cb, dab, dcb, r1b, delta, vrow,
                ld, out_sem, *sems):
    place = Place()
    rows, seq = seg_ref.shape
    tokens, width = x_hbm.shape
    pairs = heads // 2
    chunks = g_hbm.shape[0]
    own_rows = part.shape[-2]
    pieces = part.shape[0]
    big = tokens
    r_ = Reduce(place, part, (fromc, fromy, fromp, fromz, fromx, frome), done, sum_o, sems[:14], pieces)
    rv = Reduce(place, vpart, (vfromc, vfromy, vfromp, vfromz), vdone, vsum_o, sems[14:], vpart.shape[0], 1)
    ff_pieces = 4 * chunks
    first_ff = pairs + 2
    du, dz, y1 = pool.at[2], pool.at[3], pool.at[4]
    x = y1

    def load(k, src, dst):
        return pltpu.make_async_copy(src, dst, ld.at[k])

    g_in = [load(j, g_hbm.at[j], pool.at[j % 2]) for j in range(chunks)]
    gp_in = [load(chunks + j, gp_hbm.at[j], gpool.at[j % 2]) for j in range(chunks)]
    w_in = [load(2 * chunks + j, w_hbm.at[pl.ds(first_ff + 4 * j, 4)], wpool.at[pl.ds(4 * (j % 2), 4)]) for j in range(chunks)]
    base = 3 * chunks
    dz_in, y1_in, acc_in, c_in, r1_in = (load(base + k, s, d) for k, (s, d) in enumerate(
        ((dz_hbm, dz), (y1_hbm, y1), (dh2_hbm, acc), (c_hbm, cb), (r1_hbm, r1b))))
    base += 5
    n1_in = load(base, n1_hbm, gpool.at[0])
    wo_in = load(base + 1, w_hbm.at[pl.ds(pairs, 2)], wpool.at[pl.ds(0, 2)])
    wq_in = load(base + 2, w_hbm.at[pl.ds(0, pairs)], wpool.at[pl.ds(2, pairs)])
    x_in = load(base + 3, x_hbm, x)
    base += 4

    def q_in(p):
        return load(base + p, qkv_hbm.at[p], pool.at[3, :, pl.ds(pl.multiple_of(lax.rem(p, 2) * PIECE, LANES), PIECE)])

    for c in (dz_in, g_in[0]):
        c.start()
    place.greet(place.reduce_peers)
    place.met(place.reduce_peers)
    vrow[...] = jnp.zeros_like(vrow)
    vrow[:8, :] = dv_ref[...]

    def colsum(t):
        return jnp.sum(t, 0, keepdims=True)

    half = width // 2

    def weight_grad(left, right, piece, count):
        d = dot_tn(left[...], right)
        for t in range(3 * count):
            part[piece + t // 3, t % 3] = d[:, t * LANES : (t + 1) * LANES].astype(bf16).reshape(4, 2, 2, own_rows, LANES)
        for k in range(count):
            r_.start(piece + k)

    dz_in.wait()
    for j in range(chunks):
        s = j % 2
        g_in[j].wait()
        if j == 0:
            for c in (gp_in[0], w_in[0], acc_in, y1_in, g_in[1], gp_in[1], w_in[1], c_in, r1_in):
                c.start()
        weight_grad(dz, pool[s], 4 * j, 2)
        r_.turn(3 * j)
        gp_in[j].wait()
        w_in[j].wait()
        if j == 0:
            y1_in.wait()
            acc_in.wait()

        def block(i, j=j, s=s):
            at = pl.ds(pl.multiple_of(i * big, big), big)
            d = (dot(dz[at, :], columns(wpool, 4 * s + 2, 4 * s + 3)) * gpool[s, at, :]).astype(bf16)
            du[at, :] = d
            acc[at, :] += dot_nt(d, columns(wpool, 4 * s, 4 * s + 1))
            vrow[8 + j : 9 + j, :] += colsum(d.astype(f32))

        loop(tokens // big, block)
        r_.turn(3 * j + 1)
        if j + 2 < chunks:
            g_in[j + 2].start()
            gp_in[j + 2].start()
            w_in[j + 2].start()
        if j == chunks - 2:
            n1_in.start()
            wo_in.start()
        weight_grad(y1, du[...], 4 * j + 2, 2)
        r_.turn(3 * j + 2)
    wq_in.start()
    x_in.start()
    q_in(0).start()
    q_in(1).start()
    for r in range(rows):
        segf = seg_ref[r : r + 1, :].astype(f32)
        rep = jnp.broadcast_to(segf, (LANES, seq)).T
        for k in range(seq // LANES):
            sl = slice(k * LANES, (k + 1) * LANES)
            gpool[1, r * seq : (r + 1) * seq, sl] = jnp.where(rep == segf[:, sl], 0.0, NEG)
    c_in.wait()
    r1_in.wait()
    n1_in.wait()
    wo_in.wait()
    g1 = vec_ref[0:1, :]
    sel_shape = (delta.shape[0], width)
    sel = jnp.where(lax.broadcasted_iota(jnp.int32, sel_shape, 0) == lax.broadcasted_iota(jnp.int32, sel_shape, 1) // HD, 1.0, 0.0).astype(bf16)

    def norm_one_back(i):
        at = pl.ds(pl.multiple_of(i * 256, 256), 256)
        dy1 = acc[at, :]
        n1 = gpool[0, at, :]
        dn = dy1 * g1
        r1 = r1b[at, :1]
        dh1 = r1 * (dn - jnp.mean(dn, 1, keepdims=True) - n1 * jnp.mean(dn * n1, 1, keepdims=True))
        acc[at, :] = dh1
        da = dh1.astype(bf16)
        dab[at, :] = da
        dc = dot_nt(da, columns(wpool, 0, 1)).astype(bf16)
        dcb[at, :] = dc
        prod = dc.astype(f32) * cb[at, :].astype(f32)
        hi = prod.astype(bf16)
        lo = (prod - hi.astype(f32)).astype(bf16)
        delta[:, at] = dot_nt(sel, hi) + dot_nt(sel, lo)
        vrow[0:1, :] += colsum(dy1 * n1)
        vrow[1:2, :] += colsum(dy1)
        vrow[6:7, :] += colsum(da.astype(f32))

    loop(tokens // 256, norm_one_back)
    r_.turn(3 * chunks)
    weight_grad(cb, dab[...], ff_pieces, 2)
    r_.turn(3 * chunks + 1)
    t0 = 3 * chunks + 2
    twice = ff_pieces + 2 - t0
    x_in.wait()
    first_seq = lax.broadcasted_iota(jnp.int32, (seq, LANES), 1) < HD

    def pair(p, last=False):
        head = pl.ds(pl.multiple_of(p * LANES, LANES), LANES)
        col = pl.multiple_of(lax.rem(p, 2) * PIECE, LANES)
        to = p // 2
        q_in(p).wait()

        def row(r):
            tok = pl.ds(pl.multiple_of(r * seq, seq), seq)
            q2 = pool[3, tok, pl.ds(col, LANES)]
            k2 = pool[3, tok, pl.ds(col + LANES, LANES)]
            v2 = pool[3, tok, pl.ds(col + 2 * LANES, LANES)]
            dc2 = dcb[tok, head]
            zero = jnp.zeros_like(k2)
            near = gpool[1, tok, :seq]
            grads = []
            for h in range(2):
                lse = lse_ref[r, pl.ds(2 * p + h, 1), :]
                dl = delta[pl.ds(2 * p + h, 1), tok]
                own = first_seq if h == 0 else ~first_seq
                pt = jnp.exp2((dot_nt(jnp.where(own, k2, zero), q2) + near) * SCALE2 - lse)
                ds = (pt * (dot_nt(jnp.where(own, v2, zero), dc2) - dl)).astype(bf16)
                dv = dot(pt.astype(bf16), dc2)
                grads.append((dot_tn(ds, k2) * 0.125, dot(ds, q2) * 0.125, dv))
            for k, (a, b) in enumerate(zip(*grads)):
                pool[to, tok, pl.ds(col + k * LANES, LANES)] = jnp.where(first_seq, a, b).astype(bf16)
            if last:
                r_.later(t0 + p + twice + 1 + r)
            else:
                when((r == 0) & (p < twice), lambda: r_.turn(t0 + 2 * p))
                when((r == 0) & (p == twice), lambda: r_.later(t0 + 2 * p))

        loop(rows, row)
        if not last:
            when(p + 2 < pairs, lambda: q_in(p + 2).start())
        d = pool[to, :, pl.ds(col, PIECE)]

        def biases():
            sums = colsum(d.astype(f32))
            vrow[4:5, head] = sums[:, :LANES]
            vrow[5:6, head] = sums[:, 2 * LANES :]

        if last:
            def product(a):
                w = dot_tn(x[:, pl.ds(pl.multiple_of(a * half, LANES), half)], d)
                for t in range(3):
                    vpart[t, 0, pl.ds(2 * a, 2)] = w[:, t * LANES : (t + 1) * LANES].astype(bf16).reshape(2, 2, 2, own_rows, LANES)

            loop(2, product)
            for t in range(3):
                rv.start(t)
            biases()
            vpart[3, 0] = vrow[...].T.astype(bf16).reshape(4, 2, 2, own_rows, LANES)
            rv.start(3)
        else:
            weight_grad(x, d, ff_pieces + 2 + p, 1)
            biases()
            late = p >= twice
            done = t0 + p + jnp.minimum(p + 1, twice)
            r_.x_step(done)
            r_.later(jnp.where(late, done + 1, done))

    loop(pairs - 1, pair)
    pair(pairs - 1, True)
    t0 += pairs + twice + rows
    singles = vpart.shape[0]
    wq_in.wait()
    blocks = tokens // 256

    def gin_block(i):
        at = pl.ds(pl.multiple_of(i * 256, 256), 256)
        d = jnp.concatenate([pool[k, at, :] for k in range(pairs // 2)], 1)
        dcb[at, :] = (acc[at, :] + dot_nt(d, columns(wpool, *range(2, 2 + pairs)))).astype(bf16)
        when(i == 0, lambda: loop(singles, rv.x_step))
        when(i < 2, lambda: r_.turn(t0 + i))
        when(i == 2, lambda: loop(singles, rv.z_step))
        when(i == 3, lambda: r_.turn(t0 + 2))

    loop(blocks, gin_block)
    gin_out = pltpu.make_async_copy(dcb, gin_o, out_sem)
    gin_out.start()
    t0 += 3
    rest = pieces + REDUCE_LAGS[-1] - t0

    def rest_turn(i):
        r_.turn(t0 + i)
        when(i == 0, lambda: loop(singles, rv.p_step))

    loop(rest, rest_turn)
    loop(singles, rv.finish)
    loop(pieces, r_.sent)
    loop(singles, rv.sent)
    gin_out.wait()


def back(x, c, y1, dz, dh2, n1, r1, g, gp, qkv, w, seg, lse, dv, vec):
    rows, seq = seg.shape
    tokens, width = x.shape
    chunks = g.shape[0]
    own_rows = w.shape[-2]
    heads = width // HD
    pairs = heads // 2
    pieces = 4 * chunks + 2 + pairs - 1
    sh = jax.ShapeDtypeStruct
    dma = pltpu.SemaphoreType.DMA
    v = pltpu.VMEM
    hbm = pl.BlockSpec(memory_space=pl.ANY)
    vmem = pl.BlockSpec(memory_space=pltpu.VMEM)
    tail = (own_rows, LANES)
    tok = v((tokens, width), bf16)
    scratch = [
        v((pieces, 3, 4, 2, 2) + tail, bf16), v((pieces, 3, 4, 2) + tail, bf16), v((pieces, 2, 4) + tail, bf16), v((pieces, 2) + tail, bf16),
        v((pieces, 4, 2) + tail, bf16), v((pieces, 4, 2) + tail, bf16), v((pieces, 3) + tail, bf16), v((pieces, 2) + tail, bf16),
        v((4, 1, 4, 2, 2) + tail, bf16), v((4, 1, 4, 2) + tail, bf16), v((4, 1, 4) + tail, bf16), v((4, 1) + tail, bf16),
        v((4, 4, 1) + tail, bf16), v((4, 1) + tail, bf16), v((5, tokens, width), bf16), v((8,) + w.shape[1:], bf16), v((2, tokens, width), f32),
        v((tokens, width), f32), tok, tok, tok, v((tokens, LANES), f32), v((16, tokens), f32),
        v((LANES, width), f32),
        dma((3 * chunks + 9 + pairs,)), dma(())] + [dma((pieces, 4))] * 2 + [dma((pieces,))] * 12 + [dma((4, 4))] * 2 + [dma((4,))] * 6
    return pl.pallas_call(
        functools.partial(back_kernel, heads),
        out_shape=(sh((tokens, width), bf16), sh((pieces, own_rows, PIECE), f32), sh((4, own_rows, LANES), f32)),
        in_specs=[hbm] * 11 + [vmem] * 4,
        out_specs=(hbm, vmem, vmem),
        scratch_shapes=scratch,
        compiler_params=pltpu.CompilerParams(collective_id=1, has_side_effects=True, vmem_limit_bytes=63 * 2**20),
        name="back",
    )(x, c, y1, dz, dh2, n1, r1, g, gp, qkv, w, seg, lse, dv, vec)


def update_kernel(rates, sum_ref, vsum_ref, gin_hbm, out_hbm, am, aw, aa, dm, dw, da, vm, vw, va,
                  gin_o, out_o, am_o, aw_o, aa_o, dm_o, dw_o, da_o, vm_o, vw_o, va_o, square, tok, att, den, ld, st):
    matrix, vector, replicas = rates
    moves = [(dm, den.at[0], dm_o), (dw, den.at[1], dw_o), (da, den.at[2], da_o), (am, att.at[0], am_o), (aw, att.at[1], aw_o),
             (aa, att.at[2], aa_o), (gin_hbm, tok.at[0], gin_o), (out_hbm, tok.at[1], out_o)]
    loads = [pltpu.make_async_copy(s, d, ld.at[k]) for k, (s, d, _) in enumerate(moves)]
    stores = [pltpu.make_async_copy(d, o, st.at[k]) for k, (_, d, o) in enumerate(moves)]
    for c in loads:
        c.start()

    def advance(grad, rate, moment, weight, average):
        grad = grad / replicas
        moment = momentum_decay * moment + grad
        weight = weight - rate * (grad + momentum_decay * moment)
        return moment, weight, average_decay * average + (1.0 - average_decay) * weight

    def advance_in(grad, ref, index):
        news = advance(grad, matrix, *(ref[(k,) + index] for k in range(3)))
        for k in range(3):
            ref[(k,) + index] = news[k]

    rows, own = vm.shape
    square[...] = jnp.zeros_like(square)
    square[:own, :] = vsum_ref[3]
    vm_o[...], vw_o[...], va_o[...] = advance(square[...].T[:rows, :own], vector, vm[...], vw[...], va[...])
    every = slice(None)
    pairs = att.shape[3] // LANES
    ff_pieces = sum_ref.shape[0] - 1 - pairs
    for c in loads[:3]:
        c.wait()
    for i in range(ff_pieces):
        col = i // 4 * 2 * PIECE + i % 2 * PIECE
        advance_in(sum_ref[i], den, (1 - i % 4 // 2, every, slice(col, col + PIECE)))
    for c in stores[:3]:
        c.start()
    for c in loads[3:6]:
        c.wait()
    for i in range(2):
        advance_in(sum_ref[ff_pieces + i], att, (3, every, slice(i * PIECE, (i + 1) * PIECE)))
    for p in range(pairs):
        for k in range(3):
            grad = vsum_ref[k] if p == pairs - 1 else sum_ref[ff_pieces + 2 + p, :, k * LANES : (k + 1) * LANES]
            advance_in(grad, att, (k, every, slice(p * LANES, (p + 1) * LANES)))
    for c in loads[6:]:
        c.wait()
    for c in stores[3:]:
        c.start()
    for c in stores:
        c.wait()


def update(rates, sums, vsums, gin, out, states):
    am, dm = states[0], states[3]
    sh = jax.ShapeDtypeStruct
    v = pltpu.VMEM
    hbm = pl.BlockSpec(memory_space=pl.ANY)
    vmem = pl.BlockSpec(memory_space=pltpu.VMEM)
    places = [hbm] * 8 + [vmem] * 3
    return pl.pallas_call(
        functools.partial(update_kernel, rates),
        out_shape=(sh(gin.shape, bf16), sh(out.shape, bf16)) + tuple(sh(s.shape, f32) for s in states),
        in_specs=[vmem, vmem] + places,
        out_specs=tuple(places),
        scratch_shapes=[v((LANES, LANES), f32), v((2,) + gin.shape, bf16), v((3,) + am.shape, f32), v((3,) + dm.shape, f32),
                        pltpu.SemaphoreType.DMA((8,)), pltpu.SemaphoreType.DMA((8,))],
        compiler_params=pltpu.CompilerParams(vmem_limit_bytes=BIG),
        name="update",
    )(sums, vsums, gin, out, *states)


def pack_columns(attention, dense, vectors):
    count = vectors.shape[0]
    vector_cols = jnp.pad(vectors.T, ((0, 0), (0, 128 - count)))
    first = jnp.concatenate([attention[0], attention[1], attention[2], vector_cols], 1)
    second = jnp.concatenate([attention[3], dense[0], dense[1]], 1)
    return first, second


def advance(gradient, moment, weight, average, step_rate):
    moment_new = momentum_decay * moment + gradient
    weight_new = weight - step_rate * (gradient + momentum_decay * moment_new)
    average_new = average_decay * average + (1.0 - average_decay) * weight_new
    return (moment_new, weight_new, average_new)


def plain_body(
    hidden_in,
    segment_ids,
    cotangent,
    attention_weights,
    attention_momentum,
    attention_average,
    dense_weights,
    dense_momentum,
    dense_average,
    vector_params,
    vector_momentum,
    vector_average,
):
    row_count, length, width = hidden_in.shape
    ff = dense_weights.shape[-1]
    vector_rows = vector_params.shape[0]
    x = hidden_in.reshape(-1, width)
    e = cotangent.reshape(-1, width)
    first, second = pack_columns(attention_weights, dense_weights, vector_params)
    first_full = lax.all_gather(first.astype(bf16), "wide", axis=0, tiled=True)
    second_full = lax.all_gather(second.astype(bf16), "wide", axis=0, tiled=True)
    vec = first_full[:, 3 * width : 3 * width + vector_rows].astype(f32).T
    bias_qkv = jnp.concatenate([vec[4:5], jnp.zeros((1, width), f32), vec[5:6]], 1)
    w_qkv = first_full[:, : 3 * width]
    wo, win, wd = (second_full[:, :width], second_full[:, width : width + ff], second_full[:, width + ff :])
    qkv, c, lse = attn_fwd(x, segment_ids, w_qkv, bias_qkv)
    out, y1, g, dz, du, da, dc, dh1, delta, dvec, dbin = mid(
        x, c, e, wo, win, wd, vec, vec[8:].reshape(1, ff)
    )
    grad_second = jnp.concatenate([wgrad(c, da), wgrad(y1, du), wgrad(dz, g)], 1)
    share_second = lax.psum_scatter(grad_second, "wide", scatter_dimension=0, tiled=True)
    dqkv, gin, dw, db = attn_bwd(segment_ids, qkv, dc, lse, delta, dh1, w_qkv, x)
    dvec = jnp.concatenate(
        [dvec[:4], db[:, :width], db[:, 2 * width :], dvec[6:8], dbin.reshape(-1, width)], 0
    )
    grad_first = jnp.concatenate(
        [dw, jnp.pad(dvec.T, ((0, 0), (0, 128 - vector_rows))).astype(bf16)], 1
    )
    share_first = lax.psum_scatter(grad_first, "wide", scatter_dimension=0, tiled=True)
    replicas = lax.axis_size("narrow")
    tokens_all = row_count * length * lax.axis_size("wide") * replicas
    grad_scale = math.sqrt(tokens_all) / replicas
    t1 = lax.psum(share_first, "narrow").astype(f32) / replicas
    t2 = lax.psum(share_second, "narrow").astype(f32) / replicas
    cut = lambda t, j: t[:, j * width : (j + 1) * width]
    attention_grad = jnp.stack([cut(t1, 0), cut(t1, 1), cut(t1, 2), cut(t2, 0)])
    dense_grad = jnp.stack([t2[:, width : width + ff], t2[:, width + ff :]])
    vector_grad = t1[:, 3 * width : 3 * width + vector_rows].T
    attention_new = advance(attention_grad, attention_momentum, attention_weights, attention_average, matrix_rate / grad_scale)
    dense_new = advance(dense_grad, dense_momentum, dense_weights, dense_average, matrix_rate / grad_scale)
    vector_new = advance(vector_grad, vector_momentum, vector_params, vector_average, vector_rate / grad_scale)
    return (out.reshape(hidden_in.shape), gin.reshape(hidden_in.shape)) + attention_new + dense_new + vector_new


def body(
    hidden_in,
    segment_ids,
    cotangent,
    attention_weights,
    attention_momentum,
    attention_average,
    dense_weights,
    dense_momentum,
    dense_average,
    vector_params,
    vector_momentum,
    vector_average,
):
    row_count, length, width = hidden_in.shape
    x = hidden_in.reshape(-1, width)
    e = cotangent.reshape(-1, width)
    replicas = lax.axis_size("narrow")
    tokens_all = row_count * length * lax.axis_size("wide") * replicas
    grad_scale = math.sqrt(tokens_all) / replicas
    rates = (matrix_rate / grad_scale, vector_rate / grad_scale, replicas)
    qkv, c, lse, w, out, y1, g, gp, dz, dh2, n1, r1, dv, vec = stage(
        x, segment_ids, e, attention_weights, dense_weights, vector_params
    )
    states = (
        attention_momentum, attention_weights, attention_average,
        dense_momentum, dense_weights, dense_average,
        vector_momentum, vector_params, vector_average,
    )
    gin, sums, vsums = back(x, c, y1, dz, dh2, n1, r1, g, gp, qkv, w, segment_ids, lse, dv, vec)
    news = update(rates, sums, vsums, gin, out, states)
    return (news[1].reshape(hidden_in.shape), news[0].reshape(hidden_in.shape)) + tuple(news[2:])


def solution(mesh):
    token = P(("wide", "narrow"), None, None)
    matrix = P(None, "wide", None)
    vector = P(None, "wide")
    in_specs = (token, P(("wide", "narrow"), None), token) + (matrix,) * 6 + (vector,) * 3
    out_specs = (token, token) + (matrix,) * 6 + (vector,) * 3
    ours = mesh.shape["wide"] == 16 and mesh.shape["narrow"] == 2
    return jax.shard_map(body if ours else plain_body, mesh=mesh, in_specs=in_specs, out_specs=out_specs, check_vma=False)
```

```python
import functools, math
import jax, jax.numpy as jnp
from jax import lax
from jax.sharding import PartitionSpec as P
from jax.experimental import pallas as pl
from jax.experimental.pallas import tpu as pltpu

HD = 64
LOG2E = 1.4426950408889634
SCALE2 = 0.125 * LOG2E
NEG = -1e30
EPS = 1e-12
momentum_decay = 0.5
average_decay = 0.5
matrix_rate = 0.03
vector_rate = 0.3
f32, bf16 = jnp.float32, jnp.bfloat16
BIG = 60 * 2**20

def dot(a, b):
    return lax.dot_general(a, b, (((1,), (0,)), ((), ())), preferred_element_type=f32)
def dot_nt(a, b):
    return lax.dot_general(a, b, (((1,), (1,)), ((), ())), preferred_element_type=f32)
def dot_tn(a, b):
    return lax.dot_general(a, b, (((0,), (0,)), ((), ())), preferred_element_type=f32)

def key_range(c, seq, blk):
    lo = max(0, c * blk - seq // 2 + 1) // blk * blk
    hi = min(seq, -(-((c + 1) * blk - 1 + seq // 2) // blk) * blk)
    return lo, hi

def fill_bias(seg_ref, bias_ref):
    segf = seg_ref[0].astype(f32)
    seq = segf.shape[1]
    rep = jnp.broadcast_to(segf, (128, seq)).T
    for j in range(seq // 128):
        bias_ref[:, j * 128:(j + 1) * 128] = jnp.where(rep == segf[:, j * 128:(j + 1) * 128], 0.0, NEG)

def fwd_kernel(blk, x_ref, seg_ref, w_ref, b_ref, qkv_ref, c_ref, lse_ref, bias_ref, lsea_ref):
    seq, width = x_ref.shape
    x = x_ref[...]
    for j in range(3):
        sl = slice(j * width, (j + 1) * width)
        qkv_ref[:, sl] = (dot(x, w_ref[:, sl]) + b_ref[:, sl]).astype(bf16)
    fill_bias(seg_ref, bias_ref)
    lane = lax.broadcasted_iota(jnp.int32, (blk, 128), 1)
    first = lane < HD
    ones = jnp.ones((seq, 128), bf16)
    def pair(p, _):
        col = pl.multiple_of(p * 128, 128)
        q2 = qkv_ref[:, pl.ds(col, 128)]
        k2 = qkv_ref[:, pl.ds(col + width, 128)]
        v2 = jnp.concatenate([qkv_ref[:, pl.ds(col + 2 * width, 128)], ones], 1)
        for c in range(seq // blk):
            lo, hi = key_range(c, seq, blk)
            rows = slice(c * blk, (c + 1) * blk)
            qc = q2[rows]
            outs = []
            la = lsea_ref[rows, :]
            for h in range(2):
                qm = jnp.where(first if h == 0 else ~first, qc, jnp.zeros_like(qc))
                s = dot_nt(qm, k2[lo:hi]) + bias_ref[rows, lo:hi]
                m = jnp.max(s, 1, keepdims=True)
                e = jnp.exp2((s - m) * SCALE2)
                o = dot(e.astype(bf16), v2[lo:hi])
                l = o[:, 128:]
                outs.append(o[:, :128] / l)
                la = jnp.where(lane == 2 * p + h, m * SCALE2 + jnp.log(l) * LOG2E, la)
            lsea_ref[rows, :] = la
            c_ref[rows, pl.ds(col, 128)] = jnp.where(first, outs[0], outs[1]).astype(bf16)
        return 0
    lax.fori_loop(0, width // 128, pair, 0)
    lse_ref[0] = lsea_ref[...].T[:lse_ref.shape[1]]

def attn_fwd(x, seg, w, b, blk=128):
    rows, seq = seg.shape
    width = x.shape[1]
    return pl.pallas_call(
        functools.partial(fwd_kernel, blk), grid=(rows,),
        out_shape=(jax.ShapeDtypeStruct((rows * seq, 3 * width), bf16), jax.ShapeDtypeStruct((rows * seq, width), bf16),
                   jax.ShapeDtypeStruct((rows, 16, seq), f32)),
        in_specs=[pl.BlockSpec((seq, width), lambda r: (r, 0)), pl.BlockSpec((1, 1, seq), lambda r: (r, 0, 0)),
                  pl.BlockSpec((width, 3 * width), lambda r: (0, 0)), pl.BlockSpec((1, 3 * width), lambda r: (0, 0))],
        out_specs=(pl.BlockSpec((seq, 3 * width), lambda r: (r, 0)), pl.BlockSpec((seq, width), lambda r: (r, 0)),
                   pl.BlockSpec((1, 16, seq), lambda r: (r, 0, 0))),
        scratch_shapes=[pltpu.VMEM((seq, seq), f32), pltpu.VMEM((seq, 128), f32)],
        compiler_params=pltpu.CompilerParams(vmem_limit_bytes=BIG),
        name="attn_fwd",
    )(x, seg.reshape(rows, 1, seq), w, b)

def bwd_kernel(blk, seg_ref, qkv_ref, dc_ref, lse_ref, delta_ref, dh1_ref, w_ref, x_ref, dqkv_ref, gin_ref, dw_ref, db_ref, bias_ref, ds_ref, acc_ref):
    r = pl.program_id(0)
    seq = dc_ref.shape[0]
    width = dc_ref.shape[1]
    fill_bias(seg_ref, bias_ref)
    ds_ref[...] = jnp.zeros_like(ds_ref)
    lane = lax.broadcasted_iota(jnp.int32, (blk, 128), 1)
    first = lane < HD
    lane_s = lax.broadcasted_iota(jnp.int32, (seq, 128), 1)
    def pair(p, _):
        col = pl.multiple_of(p * 128, 128)
        q2 = qkv_ref[:, pl.ds(col, 128)]
        k2 = qkv_ref[:, pl.ds(col + width, 128)]
        v2 = qkv_ref[:, pl.ds(col + 2 * width, 128)]
        dc2 = dc_ref[:, pl.ds(col, 128)]
        dqs = []
        for h in range(2):
            lse = lse_ref[0, pl.ds(2 * p + h, 1), :]
            dl = delta_ref[pl.ds(2 * p + h, 1), :]
            mine = first if h == 0 else ~first
            for c in range(seq // blk):
                lo, hi = key_range(c, seq, blk)
                rows = slice(c * blk, (c + 1) * blk)
                kc, vc = k2[rows], v2[rows]
                km = jnp.where(mine, kc, jnp.zeros_like(kc))
                vm = jnp.where(mine, vc, jnp.zeros_like(vc))
                st = dot_nt(km, q2[lo:hi])
                pt = jnp.exp2((st + bias_ref[rows, lo:hi]) * SCALE2 - lse[:, lo:hi])
                dp = dot_nt(vm, dc2[lo:hi])
                ds = (pt * (dp - dl[:, lo:hi])).astype(bf16)
                ds_ref[h, rows, lo:hi] = ds
                dv = dot(pt.astype(bf16), dc2[lo:hi])
                dk = dot(ds, q2[lo:hi]) * 0.125
                if h == 0:
                    dqkv_ref[rows, pl.ds(col + 2 * width, 128)] = dv.astype(bf16)
                    dqkv_ref[rows, pl.ds(col + width, 128)] = dk.astype(bf16)
                else:
                    ov = dqkv_ref[rows, pl.ds(col + 2 * width, 128)]
                    ok = dqkv_ref[rows, pl.ds(col + width, 128)]
                    dqkv_ref[rows, pl.ds(col + 2 * width, 128)] = jnp.where(first, ov, dv.astype(bf16))
                    dqkv_ref[rows, pl.ds(col + width, 128)] = jnp.where(first, ok, dk.astype(bf16))
            dqs.append(dot_tn(ds_ref[h], k2) * 0.125)
        dqkv_ref[:, pl.ds(col, 128)] = jnp.where(lane_s < HD, dqs[0], dqs[1]).astype(bf16)
        return 0
    lax.fori_loop(0, width // 128, pair, 0)
    dqkv = dqkv_ref[...]
    gin_ref[...] = (dh1_ref[...] + dot_nt(dqkv, w_ref[...])).astype(bf16)
    x = x_ref[...]
    for j in range(3):
        sl = slice(j * width, (j + 1) * width)
        d = dot_tn(x, dqkv[:, sl])
        s = jnp.sum(dqkv[:, sl].astype(f32), 0, keepdims=True)
        @pl.when(r == 0)
        def _():
            acc_ref[:, sl] = d
            db_ref[:, sl] = s
        @pl.when(r == pl.num_programs(0) - 1)
        def _():
            dw_ref[:, sl] = (acc_ref[:, sl] + d).astype(bf16)
            db_ref[:, sl] += s

def attn_bwd(seg, qkv, dc, lse, delta, dh1, w, x, blk=128):
    rows, seq = seg.shape
    width = dc.shape[1]
    assert rows == 2
    return pl.pallas_call(
        functools.partial(bwd_kernel, blk), grid=(rows,),
        out_shape=(jax.ShapeDtypeStruct((rows * seq, 3 * width), bf16), jax.ShapeDtypeStruct((rows * seq, width), bf16),
                   jax.ShapeDtypeStruct((width, 3 * width), bf16), jax.ShapeDtypeStruct((1, 3 * width), f32)),
        in_specs=[pl.BlockSpec((1, 1, seq), lambda r: (r, 0, 0)), pl.BlockSpec((seq, 3 * width), lambda r: (r, 0)),
                  pl.BlockSpec((seq, width), lambda r: (r, 0)), pl.BlockSpec((1, 16, seq), lambda r: (r, 0, 0)),
                  pl.BlockSpec((16, seq), lambda r: (0, r)), pl.BlockSpec((seq, width), lambda r: (r, 0)),
                  pl.BlockSpec((width, 3 * width), lambda r: (0, 0)), pl.BlockSpec((seq, width), lambda r: (r, 0))],
        out_specs=(pl.BlockSpec((seq, 3 * width), lambda r: (r, 0)), pl.BlockSpec((seq, width), lambda r: (r, 0)),
                   pl.BlockSpec((width, 3 * width), lambda r: (0, 0)), pl.BlockSpec((1, 3 * width), lambda r: (0, 0))),
        scratch_shapes=[pltpu.VMEM((seq, seq), f32), pltpu.VMEM((2, seq, seq), bf16), pltpu.VMEM((width, 3 * width), f32)],
        compiler_params=pltpu.CompilerParams(vmem_limit_bytes=BIG),
        name="attn_bwd",
    )(seg.reshape(rows, 1, seq), qkv, dc, lse, delta, dh1, w, x)

RSQRT_2PI = 1.0 / math.sqrt(2 * math.pi)
def gelu_parts(u):
    phi_cdf = 0.5 + 0.5 * lax.erf(u * math.sqrt(0.5))
    dens = jnp.exp2(u * u * (-0.5 * LOG2E)) * RSQRT_2PI
    return u * phi_cdf, phi_cdf + u * dens

def mid_kernel(chunk, x_ref, c_ref, e_ref, wo_ref, win_ref, wd_ref, v_ref, bin_ref,
               out_ref, y1_ref, g_ref, dz_ref, du_ref, da_ref, dc_ref, dh1_ref, delta_ref, dv_ref, dbin_ref, gp_ref):
    i = pl.program_id(0)
    blk, width = x_ref.shape
    ff = win_ref.shape[1]
    @pl.when(i == 0)
    def _():
        dv_ref[...] = jnp.zeros_like(dv_ref)
        dbin_ref[...] = jnp.zeros_like(dbin_ref)
    g1, s1, g2, s2, bo, bd = (v_ref[j:j + 1, :] for j in (0, 1, 2, 3, 6, 7))
    cb = c_ref[...]
    h1 = x_ref[...].astype(f32) + (dot(cb, wo_ref[...]) + bo)
    cen = h1 - jnp.mean(h1, 1, keepdims=True)
    r1 = lax.rsqrt(jnp.mean(cen * cen, 1, keepdims=True) + EPS)
    n1 = cen * r1
    y1 = n1 * g1 + s1
    y1l = y1.astype(bf16)
    y1_ref[...] = y1l
    z = jnp.zeros((blk, width), f32)
    for j in range(ff // chunk):
        sl = slice(j * chunk, (j + 1) * chunk)
        u = dot(y1l, win_ref[:, sl]) + bin_ref[:, sl]
        g, gp = gelu_parts(u)
        gl = g.astype(bf16)
        g_ref[:, sl] = gl
        gp_ref[:, sl] = gp
        z += dot_nt(gl, wd_ref[:, sl])
    h2 = y1 + (z + bd)
    cen = h2 - jnp.mean(h2, 1, keepdims=True)
    r2 = lax.rsqrt(jnp.mean(cen * cen, 1, keepdims=True) + EPS)
    n2 = cen * r2
    out_ref[...] = (n2 * g2 + s2).astype(bf16)
    e = e_ref[...].astype(f32)
    eg = e * g2
    dh2 = r2 * (eg - jnp.mean(eg, 1, keepdims=True) - n2 * jnp.mean(eg * n2, 1, keepdims=True))
    dz = dh2.astype(bf16)
    dz_ref[...] = dz
    dy1 = dh2
    for j in range(ff // chunk):
        sl = slice(j * chunk, (j + 1) * chunk)
        du = (dot(dz, wd_ref[:, sl]) * gp_ref[:, sl]).astype(bf16)
        du_ref[:, sl] = du
        dbin_ref[:, sl] += jnp.sum(du.astype(f32), 0, keepdims=True)
        dy1 += dot_nt(du, win_ref[:, sl])
    dn = dy1 * g1
    dh1 = r1 * (dn - jnp.mean(dn, 1, keepdims=True) - n1 * jnp.mean(dn * n1, 1, keepdims=True))
    dh1_ref[...] = dh1
    da = dh1.astype(bf16)
    da_ref[...] = da
    dc = dot_nt(da, wo_ref[...]).astype(bf16)
    dc_ref[...] = dc
    prod = dc.astype(f32) * cb.astype(f32)
    hi = prod.astype(bf16)
    lo = (prod - hi.astype(f32)).astype(bf16)
    sel = jnp.where(lax.broadcasted_iota(jnp.int32, (16, width), 0) == lax.broadcasted_iota(jnp.int32, (16, width), 1) // HD, 1.0, 0.0).astype(bf16)
    delta_ref[...] = dot_nt(sel, hi) + dot_nt(sel, lo)
    parts = [dy1 * n1, dy1, e * n2, e, da.astype(f32), dz.astype(f32)]
    for j, t in zip((0, 1, 2, 3, 6, 7), parts):
        dv_ref[j:j + 1, :] += jnp.sum(t, 0, keepdims=True)

def mid(x, c, e, wo, win, wd, vec, bin_, blk=256, chunk=768):
    n, width = x.shape
    ff = win.shape[1]
    tok = lambda w: pl.BlockSpec((blk, w), lambda i: (i, 0))
    full = lambda a: pl.BlockSpec(a.shape, lambda i: (0, 0), pipeline_mode=pl.Buffered(1))
    sh = jax.ShapeDtypeStruct
    return pl.pallas_call(
        functools.partial(mid_kernel, chunk), grid=(n // blk,),
        out_shape=(sh((n, width), bf16), sh((n, width), bf16), sh((n, ff), bf16), sh((n, width), bf16), sh((n, ff), bf16),
                   sh((n, width), bf16), sh((n, width), bf16), sh((n, width), f32), sh((16, n), f32), sh((8, width), f32), sh((1, ff), f32)),
        in_specs=[tok(width), tok(width), tok(width), full(wo), full(win), full(wd), full(vec), full(bin_)],
        out_specs=(tok(width), tok(width), tok(ff), tok(width), tok(ff), tok(width), tok(width), tok(width),
                   pl.BlockSpec((16, blk), lambda i: (0, i)), pl.BlockSpec((8, width), lambda i: (0, 0)), pl.BlockSpec((1, ff), lambda i: (0, 0))),
        scratch_shapes=[pltpu.VMEM((blk, ff), f32)],
        compiler_params=pltpu.CompilerParams(vmem_limit_bytes=BIG),
        name="middle",
    )(x, c, e, wo, win, wd, vec, bin_)

def wgrad_kernel(a_ref, b_ref, o_ref):
    o_ref[...] = dot_tn(a_ref[...], b_ref[...]).astype(bf16)

def wgrad(a, b, blk=768):
    n, m = a.shape
    k = b.shape[1]
    return pl.pallas_call(wgrad_kernel, grid=(k // blk,), out_shape=jax.ShapeDtypeStruct((m, k), bf16),
        in_specs=[pl.BlockSpec((n, m), lambda j: (0, 0)), pl.BlockSpec((n, blk), lambda j: (0, j))],
        out_specs=pl.BlockSpec((m, blk), lambda j: (0, j)),
        compiler_params=pltpu.CompilerParams(vmem_limit_bytes=BIG), name="wgrad")(a, b)


LANES = 128
PIECE = 3 * LANES
GATHER_LAGS = (0, 2, 4, 6)
REDUCE_LAGS = (2, 4, 6, 8)
AHEAD = 3
MESH = pl.DeviceIdType.MESH


class Place:
    def __init__(self):
        self.w = lax.axis_index("wide")
        self.x = lax.axis_index("narrow")
        self.core = lax.rem(self.w, 2)
        self.y = lax.rem(self.w // 2, 2)
        self.b = lax.rem(self.w // 4, 2)
        self.a = self.w // 8
        self.z = self.w // 4

    def z_peer(self, k):
        return lax.rem(self.z + k, 4)

    def over(self, name):
        if name == "x":
            return (self.w, 1 - self.x)
        if name in (1, 2, 3):
            return (4 * self.z_peer(name) + lax.rem(self.w, 4), self.x)
        step = {"a": 8, "b": 4, "y": 2, "core": 1}[name]
        return (self.w + step * (1 - 2 * getattr(self, name)), self.x)

    near = ("a", "b", "y", "x", "core")
    reduce_peers = (1, 2, 3, "y", "x", "core")

    def greet(self, names):
        for name in names:
            pl.semaphore_signal(pltpu.get_barrier_semaphore(), inc=1, device_id=self.over(name), device_id_type=MESH)

    def met(self, names):
        pl.semaphore_wait(pltpu.get_barrier_semaphore(), len(names))


def remote(src, dst, send, recv, device):
    return pltpu.make_async_remote_copy(src_ref=src, dst_ref=dst, send_sem=send, recv_sem=recv, device_id=device, device_id_type=MESH)


def when(condition, step):
    @pl.when(condition)
    def _():
        step()


def loop(count, step):
    lax.fori_loop(0, count, lambda i, _: (step(i), 0)[1], 0)


class Gather:
    def __init__(self, place, shard, full, sems, pieces):
        self.p, self.shard, self.full, self.pieces = place, shard, full, pieces
        self.sems = {name: (sems[2 * k], sems[2 * k + 1]) for k, name in enumerate(("a", "b", "y", "x", "core"))}
        self.kept = sems[10]
        self.own = pl.ds(place.x, 2)

    def mine(self, i, a):
        return self.full.at[i, self.own, a, self.p.b, self.p.y, self.p.core]

    def keep(self, i):
        return pltpu.make_async_copy(self.shard.at[i, self.own], self.mine(i, self.p.a), self.kept.at[i])

    def copy(self, name, i, incoming=False):
        p, f = self.p, self.full
        at = {n: (1 - getattr(p, n) if incoming and n == name else getattr(p, n)) for n in ("a", "b", "y", "x", "core")}
        every = slice(None)
        if name == "a":
            dst = self.mine(i, at["a"])
            src = self.shard.at[i, self.own]
        else:
            if name == "b":
                dst = f.at[i, self.own, :, at["b"], p.y, p.core]
            elif name == "y":
                dst = f.at[i, self.own, :, :, at["y"], p.core]
            elif name == "x":
                dst = f.at[i, 2 * at["x"], :, :, :, p.core]
            else:
                dst = f.at[i, :, :, :, :, at["core"]]
            src = dst
        send, recv = self.sems[name]
        return remote(src, dst, send.at[i], recv.at[i], p.over(name))

    def start(self, i):
        self.keep(i).start()
        self.copy("a", i).start()

    def b_step(self, i):
        self.keep(i).wait()
        self.copy("a", i, True).wait_recv()
        self.copy("b", i).start()

    def y_step(self, i):
        self.copy("b", i, True).wait_recv()
        self.copy("y", i).start()

    def x_step(self, i):
        self.copy("y", i, True).wait_recv()
        self.copy("x", i).start()

    def core_step(self, i):
        self.copy("x", i, True).wait_recv()
        self.copy("core", i).start()

    def arrive(self, i):
        self.copy("core", i, True).wait_recv()

    def turn(self, t):
        for k in range(2):
            ahead = AHEAD + 2 * t + k
            when(ahead < self.pieces, lambda ahead=ahead: self.start(ahead))
        for lag, step in zip(GATHER_LAGS, (self.b_step, self.y_step, self.x_step, self.core_step)):
            when((t >= lag) & (t < self.pieces + lag), lambda lag=lag, step=step: step(t - lag))

    def sent(self, i):
        for name in ("a", "b", "y", "x", "core"):
            self.copy(name, i).wait_send()


class GatherVector:
    def __init__(self, place, shard, full, sems):
        self.p, self.shard, self.full = place, shard, full
        self.sems = {name: (sems[2 * k], sems[2 * k + 1]) for k, name in enumerate(("a", "b", "y", "core"))}
        self.kept = sems[8]

    def keep(self):
        p = self.p
        return pltpu.make_async_copy(self.shard, self.full.at[p.a, p.b, p.y, p.core], self.kept)

    def copy(self, name, incoming=False):
        p = self.p
        at = {n: (1 - getattr(p, n) if incoming and n == name else getattr(p, n)) for n in ("a", "b", "y", "core")}
        every = slice(None)
        first = ("a", "b", "y", "core").index(name)
        dst = self.full.at[tuple(at[n] if n == name or n == "core" or k > first else every for k, n in enumerate(("a", "b", "y", "core")))]
        src = self.shard if name == "a" else dst
        send, recv = self.sems[name]
        return remote(src, dst, send, recv, p.over(name))

    def start(self):
        self.keep().start()
        self.copy("a").start()

    def step(self, name, then):
        if name == "a":
            self.keep().wait()
        self.copy(name, True).wait_recv()
        self.copy(then).start()

    def arrive(self):
        self.copy("core", True).wait_recv()

    def sent(self):
        for name in ("a", "b", "y", "core"):
            self.copy(name).wait_send()


def tile(ref, i, t):
    rows = 16 * ref.shape[-2]
    return ref[i, t].reshape(rows, LANES)


def columns(ref, *pieces):
    return jnp.concatenate([tile(ref, i, t) for i in pieces for t in range(3)], 1)


def doc_bias(seg_row, bias_ref, r):
    segf = seg_row.astype(f32)
    seq = segf.shape[1]
    rep = jnp.broadcast_to(segf, (LANES, seq)).T
    for j in range(seq // LANES):
        sl = slice(j * LANES, (j + 1) * LANES)
        bias_ref[r, :, sl] = jnp.where(rep == segf[:, sl], 0.0, NEG)


def stage_kernel(heads, x_hbm, seg_ref, e_hbm, aw_hbm, dw_hbm, vp_ref,
                 qkv_o, c_o, lse_o, w_o, out_o, y1_o, g_o, gp_o, dz_o, dh2_o, n1_o, r1_o, dv_o, vrow,
                 full, vfull, shard, vshard, square, xb, eb, cb, n1b, y1b, acc, gp, gb, dzb, bias, lsea, binr, r1b,
                 in_sem, out_sem, w_sem, two_sem, *sems):
    place = Place()
    rows, seq = seg_ref.shape
    tokens, width = x_hbm.shape
    pairs = heads // 2
    pieces = shard.shape[0]
    chunks = gb.shape[0]
    own_rows = aw_hbm.shape[1]
    blk = 256
    big = 512
    g = Gather(place, shard, full, sems[:11], pieces)
    gv = GatherVector(place, vshard, vfull, sems[11:])

    loads = [pltpu.make_async_copy(aw_hbm.at[k], gp.at[0, pl.ds(k * own_rows, own_rows)], in_sem.at[k]) for k in range(4)]
    for k in range(2):
        for j in range(chunks):
            loads.append(pltpu.make_async_copy(
                dw_hbm.at[k, :, pl.ds(j * width, width)], gp.at[1 + k, pl.ds(j * own_rows, own_rows)], in_sem.at[4 + k * chunks + j]))
    n = len(loads)
    x_load = pltpu.make_async_copy(x_hbm, xb, in_sem.at[n])
    e_load = pltpu.make_async_copy(e_hbm, eb, in_sem.at[n + 1])
    for c in loads:
        c.start()
    place.greet(place.near)
    x_load.start()
    e_load.start()
    square[...] = jnp.zeros_like(square)
    lsea[...] = jnp.zeros_like(lsea)
    square[: vp_ref.shape[0], :own_rows] = vp_ref[...]
    vshard[...] = square[...].T[:own_rows].astype(bf16)

    def own_tile(k, j, t):
        return gp[k, j * own_rows : (j + 1) * own_rows, t * LANES : (t + 1) * LANES].astype(bf16)

    for c in loads[:3]:
        c.wait()
    for p in range(pairs):
        for t in range(3):
            shard[p, t] = own_tile(0, t, p)
    place.met(place.near)
    gv.start()
    for i in range(AHEAD):
        g.start(i)
    for c in loads[3:]:
        c.wait()
    for t in range(6):
        shard[pairs + t // 3, t % 3] = own_tile(0, 3, t)
        for j in range(chunks):
            for k in range(2):
                shard[pairs + 2 + 4 * j + 2 * k + t // 3, t % 3] = own_tile(1 + k, j, t)
    for r in range(rows):
        doc_bias(seg_ref[r : r + 1, :], bias, r)
    gv.step("a", "b")
    fill = GATHER_LAGS[-1] + 1
    for t in range(fill):
        g.turn(t)
        if t == 1:
            gv.step("b", "y")
        if t == 4:
            gv.step("y", "core")
    gv.arrive()
    vec = vfull[...].reshape(16 * own_rows, LANES).astype(f32).T
    vrow[...] = vec[: vrow.shape[0]]
    for j in range(chunks):
        binr[j] = vrow[8 + j : 9 + j, :]
    x_load.wait()

    first = lax.broadcasted_iota(jnp.int32, (LANES, LANES), 1) < HD
    lane = lax.broadcasted_iota(jnp.int32, (LANES, LANES), 1)
    ones = jnp.ones((seq, LANES), bf16)

    def qkv_at(p):
        return gb.at[p // 2, :, pl.ds(pl.multiple_of(lax.rem(p, 2) * PIECE, LANES), PIECE)]

    def qkv_out(p):
        return pltpu.make_async_copy(qkv_at(p), qkv_o.at[p], out_sem.at[p])

    def w_out(i):
        return pltpu.make_async_copy(full.at[i], w_o.at[i], w_sem.at[i])

    def pair(p):
        g.arrive(p)
        w_out(p).start()
        head = pl.ds(pl.multiple_of(p * LANES, LANES), LANES)
        w = columns(full, p)
        b = jnp.concatenate([vrow[4:5, head], jnp.zeros((1, LANES), f32), vrow[5:6, head]], 1)
        col = pl.multiple_of(lax.rem(p, 2) * PIECE, LANES)
        gb[p // 2, :, pl.ds(col, PIECE)] = (dot(xb[...], w) + b).astype(bf16)
        qkv_out(p).start()

        def row(r):
            tok = pl.ds(pl.multiple_of(r * seq, seq), seq)
            q2 = gb[p // 2, tok, pl.ds(col, LANES)]
            k2 = gb[p // 2, tok, pl.ds(col + LANES, LANES)]
            v2 = jnp.concatenate([gb[p // 2, tok, pl.ds(col + 2 * LANES, LANES)], ones], 1)
            for c in range(seq // LANES):
                lo, hi = key_range(c, seq, LANES)
                cut = slice(c * LANES, (c + 1) * LANES)
                outs = []
                la = lsea[r, cut, :]
                for h in range(2):
                    qm = jnp.where(first if h == 0 else ~first, q2[cut], jnp.zeros_like(q2[cut]))
                    s = dot_nt(qm, k2[lo:hi]) + bias[r, cut, lo:hi]
                    m = jnp.max(s, 1, keepdims=True)
                    o = dot(jnp.exp2((s - m) * SCALE2).astype(bf16), v2[lo:hi])
                    l = o[:, LANES:]
                    outs.append(o[:, :LANES] / l)
                    la = jnp.where(lane == 2 * p + h, m * SCALE2 + jnp.log(l) * LOG2E, la)
                lsea[r, cut, :] = la
                cb[pl.ds(pl.multiple_of(r * seq + c * LANES, LANES), LANES), head] = jnp.where(first, outs[0], outs[1]).astype(bf16)
            g.turn(fill + 2 * p + r)

        loop(rows, row)

    loop(pairs, pair)
    done = fill + 2 * pairs
    for r in range(rows):
        lse_o[r] = lsea[r].T[: lse_o.shape[1]]
    c_out = pltpu.make_async_copy(cb, c_o, out_sem.at[pairs])
    c_out.start()
    g1, s1, g2, s2, bo, bd = (vrow[j : j + 1, :] for j in (0, 1, 2, 3, 6, 7))

    def block(i):
        return pl.ds(pl.multiple_of(i * blk, blk), blk)

    for i in (pairs, pairs + 1):
        g.arrive(i)
        w_out(i).start()

    def norm_one(i):
        at = block(i)
        h1 = xb[at, :].astype(f32) + (dot(cb[at, :], columns(full, pairs, pairs + 1)) + bo)
        cen = h1 - jnp.mean(h1, 1, keepdims=True)
        r1 = lax.rsqrt(jnp.mean(cen * cen, 1, keepdims=True) + EPS)
        n1 = cen * r1
        y1 = n1 * g1 + s1
        n1b[at, :] = n1
        r1b[at, :] = jnp.broadcast_to(r1, (blk, LANES))
        y1b[at, :] = y1.astype(bf16)
        acc[at, :] = y1 + bd
        when(lax.rem(i, 2) == 1, lambda: g.turn(done + i // 2))

    loop(tokens // blk, norm_one)
    done += 2
    y1_out = pltpu.make_async_copy(y1b, y1_o, out_sem.at[pairs + 2])
    y1_out.start()
    n1_out = pltpu.make_async_copy(n1b, n1_o, out_sem.at[pairs + 1])
    n1_out.start()
    r1_out = pltpu.make_async_copy(r1b, r1_o, out_sem.at[pairs + 5 + chunks])
    r1_out.start()
    loop(pairs, lambda p: qkv_out(p).wait())

    def up(j):
        return columns(full, pairs + 2 + 4 * j, pairs + 3 + 4 * j)

    def down(j):
        return columns(full, pairs + 4 + 4 * j, pairs + 5 + 4 * j)

    def g_out(j):
        return pltpu.make_async_copy(gb.at[j], g_o.at[j], out_sem.at[pairs + 7 + j])

    def gp_out(j):
        return pltpu.make_async_copy(gp.at[j], gp_o.at[j], out_sem.at[pairs + 7 + chunks + j])

    def ff_chunk(j):
        def ready(k):
            for t in (k, k + 1):
                g.arrive(pairs + 2 + 4 * j + t)
                w_out(pairs + 2 + 4 * j + t).start()

        def up_block(i):
            at = pl.ds(pl.multiple_of(i * big, big), big)
            act, slope = gelu_parts(dot(y1b[at, :], up(j)) + binr[j])
            gb[j, at, :] = act.astype(bf16)
            gp[j, at, :] = slope
            g.turn(done + 4 * j + i)

        def down_block(i):
            at = pl.ds(pl.multiple_of(i * big, big), big)
            acc[at, :] += dot_nt(gb[j, at, :], down(j))
            g.turn(done + 4 * j + 2 + i)

        ready(0)
        loop(tokens // big, up_block)
        g_out(j).start()
        gp_out(j).start()
        ready(2)
        loop(tokens // big, down_block)

    loop(chunks, ff_chunk)
    e_load.wait()
    dv_o[...] = jnp.zeros_like(dv_o)

    def colsum(t):
        return jnp.sum(t, 0, keepdims=True)

    def norm_two(i):
        at = block(i)
        h2 = acc[at, :]
        cen = h2 - jnp.mean(h2, 1, keepdims=True)
        r2 = lax.rsqrt(jnp.mean(cen * cen, 1, keepdims=True) + EPS)
        n2 = cen * r2
        xb[at, :] = (n2 * g2 + s2).astype(bf16)
        e = eb[at, :].astype(f32)
        eg = e * g2
        dh2 = r2 * (eg - jnp.mean(eg, 1, keepdims=True) - n2 * jnp.mean(eg * n2, 1, keepdims=True))
        dz = dh2.astype(bf16)
        dzb[at, :] = dz
        acc[at, :] = dh2
        dv_o[2:3, :] += colsum(e * n2)
        dv_o[3:4, :] += colsum(e)
        dv_o[7:8, :] += colsum(dz.astype(f32))

    def norm_two_out(i):
        at = block(i)
        pairs_of = ((xb, out_o), (dzb, dz_o), (acc, dh2_o))
        return [pltpu.make_async_copy(src.at[at], dst.at[at], two_sem.at[k, i]) for k, (src, dst) in enumerate(pairs_of)]

    def norm_two_step(i):
        norm_two(i)
        for c in norm_two_out(i):
            c.start()

    loop(tokens // blk, norm_two_step)
    gv.sent()
    loop(pieces, g.sent)
    loop(pieces, lambda i: w_out(i).wait())
    for c in [c_out, y1_out, n1_out, r1_out]:
        c.wait()
    for i in range(tokens // blk):
        for c in norm_two_out(i):
            c.wait()
    loop(chunks, lambda j: g_out(j).wait())
    loop(chunks, lambda j: gp_out(j).wait())


def stage(x, seg, e, aw, dw, vp):
    rows, seq = seg.shape
    tokens, width = x.shape
    own_rows, ff = dw.shape[1:]
    heads, chunks = width // HD, ff // width
    pairs = heads // 2
    pieces = pairs + 2 + 4 * chunks
    sh = jax.ShapeDtypeStruct
    dma = pltpu.SemaphoreType.DMA
    v = pltpu.VMEM
    hbm = pl.BlockSpec(memory_space=pl.ANY)
    vmem = pl.BlockSpec(memory_space=pltpu.VMEM)
    tok = sh((tokens, width), bf16)
    wide = sh((chunks, tokens, width), bf16)
    long = sh((tokens, width), f32)
    block = (2, 2, 2, 2, own_rows, LANES)
    scratch = [
        v((pieces, 3) + block, bf16), v(block, bf16), v((pieces, 3, own_rows, LANES), bf16), v((own_rows, LANES), bf16),
        v((LANES, LANES), f32), v((tokens, width), bf16), v((tokens, width), bf16), v((tokens, width), bf16),
        v((tokens, width), f32), v((tokens, width), bf16), v((tokens, width), f32), v((chunks, tokens, width), f32),
        v((chunks, tokens, width), bf16), v((tokens, width), bf16), v((rows, seq, seq), f32), v((rows, seq, LANES), f32),
        v((chunks, 1, width), f32), v((tokens, LANES), f32),
        dma((6 + 2 * chunks,)), dma((pairs + 7 + 2 * chunks,)), dma((pieces,)), dma((3, tokens // 256)),
    ] + [dma((pieces,))] * 11 + [dma(())] * 9
    return pl.pallas_call(
        functools.partial(stage_kernel, heads),
        out_shape=(sh((pairs, tokens, PIECE), bf16), tok, sh((rows, 16, seq), f32), sh((pieces, 3) + block, bf16), tok, tok, wide,
                   sh((chunks, tokens, width), f32), tok, long, long, sh((tokens, LANES), f32), sh((8, width), f32), sh((16, width), f32)),
        in_specs=[hbm, vmem, hbm, hbm, hbm, vmem],
        out_specs=(hbm, hbm, vmem) + (hbm,) * 9 + (vmem, vmem),
        scratch_shapes=scratch,
        compiler_params=pltpu.CompilerParams(collective_id=0, has_side_effects=True, vmem_limit_bytes=BIG),
        name="stage",
    )(x, seg, e, aw, dw, vp)


class Reduce:
    def __init__(self, place, part, froms, done, out, sems, pieces, tiles=3):
        self.p, self.part, self.done, self.out, self.pieces, self.whole = place, part, done, out, pieces, tiles == 1
        self.names = ("core", "y", "p") if self.whole else ("core", "y", "p", "x", "early_y", "late_x")
        self.froms = dict(zip(("core", "y", "p", "z", "x", "early_y"), froms))
        self.zs, self.zr = sems[:2]
        self.sems = {name: (sems[2 + 2 * k], sems[3 + 2 * k]) for k, name in enumerate(self.names)}
        self.own = pl.ds(0, 1) if self.whole else pl.ds(place.x, 2)
        self.most = slice(None) if self.whole else pl.ds(0, 3)

    def copy(self, name, i):
        p, f, landing = self.p, self.part, self.froms
        if name == "core":
            src, dst = f.at[i, :, :, :, 1 - p.core], landing[name].at[i]
        elif name == "x":
            src, dst = f.at[i, 2 * (1 - p.x), self.most, :, p.core], landing[name].at[i, self.most]
        elif name == "late_x":
            src, dst = f.at[i, 2 * (1 - p.x), 3, p.y, p.core], landing["x"].at[i, 3, 0]
        elif name == "y":
            src, dst = f.at[i, self.own, self.most, 1 - p.y, p.core], landing[name].at[i, :, self.most]
        elif name == "early_y":
            src, dst = f.at[i, :, 3, 1 - p.y, p.core], landing[name].at[i]
        else:
            src, dst = self.done.at[i], landing[name].at[i]
        send, recv = self.sems[name]
        axis = {"p": "x", "early_y": "y", "late_x": "x"}.get(name, name)
        return remote(src, dst, send.at[i], recv.at[i], p.over(axis))

    def z_copy(self, i, k, incoming=False):
        p = self.p
        peer = p.z_peer(k)
        came = peer if incoming else p.z
        return remote(self.part.at[i, self.own, peer, p.y, p.core], self.froms["z"].at[i, came], self.zs.at[i, k], self.zr.at[i, came], p.over(k))

    def start(self, i):
        self.copy("core", i).start()

    def add(self, at, term):
        self.part[at] = self.part[at] + term

    def x_step(self, i):
        p = self.p
        self.copy("core", i).wait_recv()
        for t in range(1 if self.whole else 3):
            self.add((i, t, slice(None), slice(None), p.core), self.froms["core"][i, t])
        for name in ("y",) if self.whole else ("x", "early_y"):
            self.copy(name, i).start()

    def y_step(self, i):
        p = self.p
        self.copy("early_y", i).wait_recv()
        self.add((i, slice(None), 3, p.y, p.core), self.froms["early_y"][i])
        self.copy("late_x", i).start()
        self.copy("x", i).wait_recv()
        self.add((i, 2 * p.x, self.most, slice(None), p.core), self.froms["x"][i, :3])
        self.copy("y", i).start()

    def z_step(self, i):
        p = self.p
        self.copy("y", i).wait_recv()
        self.add((i, self.own, self.most, p.y, p.core), self.froms["y"][i, :, self.most])
        if not self.whole:
            self.copy("late_x", i).wait_recv()
            self.add((i, 2 * p.x, 3, p.y, p.core), self.froms["x"][i, 3, 0])
        for k in (2, 1, 3):
            self.z_copy(i, k).start()

    def p_step(self, i):
        p, f = self.p, self.part
        total = f[i, self.own, p.z, p.y, p.core].astype(f32)
        for k in (1, 2, 3):
            self.z_copy(i, k, True).wait_recv()
            total += self.froms["z"][i, p.z_peer(k)].astype(f32)
        self.done[i] = total.astype(bf16)
        self.copy("p", i).start()

    def finish(self, i):
        self.copy("p", i).wait_recv()
        a, b = self.done[i].astype(f32), self.froms["p"][i].astype(f32)
        if self.whole:
            self.out[i] = a[0] + b[0]
            return
        first = self.p.x == 0
        low, high = jnp.where(first, a, b), jnp.where(first, b, a)
        self.out[i] = jnp.concatenate([low[0], low[1] + high[0], high[1]], 1)

    def later(self, t):
        for lag, step in zip(REDUCE_LAGS, (self.y_step, self.z_step, self.p_step, self.finish)):
            when((t >= lag) & (t < self.pieces + lag), lambda lag=lag, step=step: step(t - lag))

    def turn(self, t):
        when(t < self.pieces, lambda: self.x_step(t))
        self.later(t)

    def sent(self, i):
        for name in self.names:
            self.copy(name, i).wait_send()
        for k in (1, 2, 3):
            self.z_copy(i, k).wait_send()


def back_kernel(heads, x_hbm, c_hbm, y1_hbm, dz_hbm, dh2_hbm, n1_hbm, r1_hbm, g_hbm, gp_hbm, qkv_hbm, w_hbm,
                seg_ref, lse_ref, dv_ref, vec_ref, gin_o, sum_o, vsum_o,
                part, fromc, fromy, fromp, fromz, fromx, frome, done, vpart, vfromc, vfromy, vfromp, vfromz, vdone, pool, wpool, gpool, acc, cb, dab, dcb, r1b, delta, vrow,
                ld, out_sem, *sems):
    place = Place()
    rows, seq = seg_ref.shape
    tokens, width = x_hbm.shape
    pairs = heads // 2
    chunks = g_hbm.shape[0]
    own_rows = part.shape[-2]
    pieces = part.shape[0]
    big = 512
    r_ = Reduce(place, part, (fromc, fromy, fromp, fromz, fromx, frome), done, sum_o, sems[:14], pieces)
    rv = Reduce(place, vpart, (vfromc, vfromy, vfromp, vfromz), vdone, vsum_o, sems[14:], vpart.shape[0], 1)
    ff_pieces = 4 * chunks
    first_ff = pairs + 2
    du, dz, y1 = pool.at[2], pool.at[3], pool.at[4]
    x = y1

    def load(k, src, dst):
        return pltpu.make_async_copy(src, dst, ld.at[k])

    g_in = [load(j, g_hbm.at[j], pool.at[j % 2]) for j in range(chunks)]
    gp_in = [load(chunks + j, gp_hbm.at[j], gpool.at[j % 2]) for j in range(chunks)]
    w_in = [load(2 * chunks + j, w_hbm.at[pl.ds(first_ff + 4 * j, 4)], wpool.at[pl.ds(4 * (j % 2), 4)]) for j in range(chunks)]
    base = 3 * chunks
    dz_in, y1_in, acc_in, c_in, r1_in = (load(base + k, s, d) for k, (s, d) in enumerate(
        ((dz_hbm, dz), (y1_hbm, y1), (dh2_hbm, acc), (c_hbm, cb), (r1_hbm, r1b))))
    base += 5
    n1_in = load(base, n1_hbm, gpool.at[0])
    wo_in = load(base + 1, w_hbm.at[pl.ds(pairs, 2)], wpool.at[pl.ds(0, 2)])
    wq_in = load(base + 2, w_hbm.at[pl.ds(0, pairs)], wpool.at[pl.ds(2, pairs)])
    x_in = load(base + 3, x_hbm, x)
    base += 4

    def q_in(p):
        return load(base + p, qkv_hbm.at[p], pool.at[3, :, pl.ds(pl.multiple_of(lax.rem(p, 2) * PIECE, LANES), PIECE)])

    for c in (dz_in, g_in[0]):
        c.start()
    place.greet(place.reduce_peers)
    place.met(place.reduce_peers)
    vrow[...] = jnp.zeros_like(vrow)
    vrow[:8, :] = dv_ref[...]

    def colsum(t):
        return jnp.sum(t, 0, keepdims=True)

    half = width // 2

    def weight_grad(left, right, piece, count):
        d = dot_tn(left[...], right)
        for t in range(3 * count):
            part[piece + t // 3, t % 3] = d[:, t * LANES : (t + 1) * LANES].astype(bf16).reshape(4, 2, 2, own_rows, LANES)
        for k in range(count):
            r_.start(piece + k)

    dz_in.wait()
    for j in range(chunks):
        s = j % 2
        g_in[j].wait()
        if j == 0:
            for c in (gp_in[0], w_in[0], acc_in, y1_in, g_in[1], gp_in[1], w_in[1], c_in, r1_in):
                c.start()
        weight_grad(dz, pool[s], 4 * j, 2)
        r_.turn(3 * j)
        gp_in[j].wait()
        w_in[j].wait()
        if j == 0:
            y1_in.wait()
            acc_in.wait()

        def block(i, j=j, s=s):
            at = pl.ds(pl.multiple_of(i * big, big), big)
            d = (dot(dz[at, :], columns(wpool, 4 * s + 2, 4 * s + 3)) * gpool[s, at, :]).astype(bf16)
            du[at, :] = d
            acc[at, :] += dot_nt(d, columns(wpool, 4 * s, 4 * s + 1))
            vrow[8 + j : 9 + j, :] += colsum(d.astype(f32))

        loop(tokens // big, block)
        r_.turn(3 * j + 1)
        if j + 2 < chunks:
            g_in[j + 2].start()
            gp_in[j + 2].start()
            w_in[j + 2].start()
        if j == chunks - 2:
            n1_in.start()
            wo_in.start()
        weight_grad(y1, du[...], 4 * j + 2, 2)
        r_.turn(3 * j + 2)
    wq_in.start()
    x_in.start()
    q_in(0).start()
    q_in(1).start()
    for r in range(rows):
        segf = seg_ref[r : r + 1, :].astype(f32)
        rep = jnp.broadcast_to(segf, (LANES, seq)).T
        for k in range(seq // LANES):
            sl = slice(k * LANES, (k + 1) * LANES)
            gpool[1, r * seq : (r + 1) * seq, sl] = jnp.where(rep == segf[:, sl], 0.0, NEG)
    c_in.wait()
    r1_in.wait()
    n1_in.wait()
    wo_in.wait()
    g1 = vec_ref[0:1, :]
    sel_shape = (delta.shape[0], width)
    sel = jnp.where(lax.broadcasted_iota(jnp.int32, sel_shape, 0) == lax.broadcasted_iota(jnp.int32, sel_shape, 1) // HD, 1.0, 0.0).astype(bf16)

    def norm_one_back(i):
        at = pl.ds(pl.multiple_of(i * 256, 256), 256)
        dy1 = acc[at, :]
        n1 = gpool[0, at, :]
        dn = dy1 * g1
        r1 = r1b[at, :1]
        dh1 = r1 * (dn - jnp.mean(dn, 1, keepdims=True) - n1 * jnp.mean(dn * n1, 1, keepdims=True))
        acc[at, :] = dh1
        da = dh1.astype(bf16)
        dab[at, :] = da
        dc = dot_nt(da, columns(wpool, 0, 1)).astype(bf16)
        dcb[at, :] = dc
        prod = dc.astype(f32) * cb[at, :].astype(f32)
        hi = prod.astype(bf16)
        lo = (prod - hi.astype(f32)).astype(bf16)
        delta[:, at] = dot_nt(sel, hi) + dot_nt(sel, lo)
        vrow[0:1, :] += colsum(dy1 * n1)
        vrow[1:2, :] += colsum(dy1)
        vrow[6:7, :] += colsum(da.astype(f32))

    loop(tokens // 256, norm_one_back)
    r_.turn(3 * chunks)
    weight_grad(cb, dab[...], ff_pieces, 2)
    r_.turn(3 * chunks + 1)
    t0 = 3 * chunks + 2
    twice = ff_pieces + 2 - t0
    x_in.wait()
    first_seq = lax.broadcasted_iota(jnp.int32, (seq, LANES), 1) < HD

    def pair(p, last=False):
        head = pl.ds(pl.multiple_of(p * LANES, LANES), LANES)
        col = pl.multiple_of(lax.rem(p, 2) * PIECE, LANES)
        to = p // 2
        q_in(p).wait()

        def row(r):
            tok = pl.ds(pl.multiple_of(r * seq, seq), seq)
            q2 = pool[3, tok, pl.ds(col, LANES)]
            k2 = pool[3, tok, pl.ds(col + LANES, LANES)]
            v2 = pool[3, tok, pl.ds(col + 2 * LANES, LANES)]
            dc2 = dcb[tok, head]
            zero = jnp.zeros_like(k2)
            near = gpool[1, tok, :seq]
            grads = []
            for h in range(2):
                lse = lse_ref[r, pl.ds(2 * p + h, 1), :]
                dl = delta[pl.ds(2 * p + h, 1), tok]
                own = first_seq if h == 0 else ~first_seq
                pt = jnp.exp2((dot_nt(jnp.where(own, k2, zero), q2) + near) * SCALE2 - lse)
                ds = (pt * (dot_nt(jnp.where(own, v2, zero), dc2) - dl)).astype(bf16)
                dv = dot(pt.astype(bf16), dc2)
                grads.append((dot_tn(ds, k2) * 0.125, dot(ds, q2) * 0.125, dv))
            for k, (a, b) in enumerate(zip(*grads)):
                pool[to, tok, pl.ds(col + k * LANES, LANES)] = jnp.where(first_seq, a, b).astype(bf16)
            if last:
                r_.later(t0 + p + twice + 1 + r)
            else:
                when((r == 0) & (p < twice), lambda: r_.turn(t0 + 2 * p))
                when((r == 0) & (p == twice), lambda: r_.later(t0 + 2 * p))

        loop(rows, row)
        if not last:
            when(p + 2 < pairs, lambda: q_in(p + 2).start())
        d = pool[to, :, pl.ds(col, PIECE)]

        def biases():
            sums = colsum(d.astype(f32))
            vrow[4:5, head] = sums[:, :LANES]
            vrow[5:6, head] = sums[:, 2 * LANES :]

        if last:
            def product(a):
                w = dot_tn(x[:, pl.ds(pl.multiple_of(a * half, LANES), half)], d)
                for t in range(3):
                    vpart[t, 0, pl.ds(2 * a, 2)] = w[:, t * LANES : (t + 1) * LANES].astype(bf16).reshape(2, 2, 2, own_rows, LANES)

            loop(2, product)
            for t in range(3):
                rv.start(t)
            biases()
            vpart[3, 0] = vrow[...].T.astype(bf16).reshape(4, 2, 2, own_rows, LANES)
            rv.start(3)
        else:
            weight_grad(x, d, ff_pieces + 2 + p, 1)
            biases()
            late = p >= twice
            done = t0 + p + jnp.minimum(p + 1, twice)
            r_.x_step(done)
            r_.later(jnp.where(late, done + 1, done))

    loop(pairs - 1, pair)
    pair(pairs - 1, True)
    t0 += pairs + twice + rows
    singles = vpart.shape[0]
    wq_in.wait()
    blocks = tokens // 256

    def gin_block(i):
        at = pl.ds(pl.multiple_of(i * 256, 256), 256)
        d = jnp.concatenate([pool[k, at, :] for k in range(pairs // 2)], 1)
        dcb[at, :] = (acc[at, :] + dot_nt(d, columns(wpool, *range(2, 2 + pairs)))).astype(bf16)
        when(i == 0, lambda: loop(singles, rv.x_step))
        when(i < 2, lambda: r_.turn(t0 + i))
        when(i == 2, lambda: loop(singles, rv.z_step))
        when(i == 3, lambda: r_.turn(t0 + 2))

    loop(blocks, gin_block)
    gin_out = pltpu.make_async_copy(dcb, gin_o, out_sem)
    gin_out.start()
    t0 += 3
    rest = pieces + REDUCE_LAGS[-1] - t0

    def rest_turn(i):
        r_.turn(t0 + i)
        when(i == 0, lambda: loop(singles, rv.p_step))

    loop(rest, rest_turn)
    loop(singles, rv.finish)
    loop(pieces, r_.sent)
    loop(singles, rv.sent)
    gin_out.wait()


def back(x, c, y1, dz, dh2, n1, r1, g, gp, qkv, w, seg, lse, dv, vec):
    rows, seq = seg.shape
    tokens, width = x.shape
    chunks = g.shape[0]
    own_rows = w.shape[-2]
    heads = width // HD
    pairs = heads // 2
    pieces = 4 * chunks + 2 + pairs - 1
    sh = jax.ShapeDtypeStruct
    dma = pltpu.SemaphoreType.DMA
    v = pltpu.VMEM
    hbm = pl.BlockSpec(memory_space=pl.ANY)
    vmem = pl.BlockSpec(memory_space=pltpu.VMEM)
    tail = (own_rows, LANES)
    tok = v((tokens, width), bf16)
    scratch = [
        v((pieces, 3, 4, 2, 2) + tail, bf16), v((pieces, 3, 4, 2) + tail, bf16), v((pieces, 2, 4) + tail, bf16), v((pieces, 2) + tail, bf16),
        v((pieces, 4, 2) + tail, bf16), v((pieces, 4, 2) + tail, bf16), v((pieces, 3) + tail, bf16), v((pieces, 2) + tail, bf16),
        v((4, 1, 4, 2, 2) + tail, bf16), v((4, 1, 4, 2) + tail, bf16), v((4, 1, 4) + tail, bf16), v((4, 1) + tail, bf16),
        v((4, 4, 1) + tail, bf16), v((4, 1) + tail, bf16), v((5, tokens, width), bf16), v((8,) + w.shape[1:], bf16), v((2, tokens, width), f32),
        v((tokens, width), f32), tok, tok, tok, v((tokens, LANES), f32), v((16, tokens), f32),
        v((LANES, width), f32),
        dma((3 * chunks + 9 + pairs,)), dma(())] + [dma((pieces, 4))] * 2 + [dma((pieces,))] * 12 + [dma((4, 4))] * 2 + [dma((4,))] * 6
    return pl.pallas_call(
        functools.partial(back_kernel, heads),
        out_shape=(sh((tokens, width), bf16), sh((pieces, own_rows, PIECE), f32), sh((4, own_rows, LANES), f32)),
        in_specs=[hbm] * 11 + [vmem] * 4,
        out_specs=(hbm, vmem, vmem),
        scratch_shapes=scratch,
        compiler_params=pltpu.CompilerParams(collective_id=1, has_side_effects=True, vmem_limit_bytes=63 * 2**20),
        name="back",
    )(x, c, y1, dz, dh2, n1, r1, g, gp, qkv, w, seg, lse, dv, vec)


def update_kernel(rates, sum_ref, vsum_ref, gin_hbm, out_hbm, am, aw, aa, dm, dw, da, vm, vw, va,
                  gin_o, out_o, am_o, aw_o, aa_o, dm_o, dw_o, da_o, vm_o, vw_o, va_o, square, tok, att, den, ld, st):
    matrix, vector, replicas = rates
    moves = [(dm, den.at[0], dm_o), (dw, den.at[1], dw_o), (da, den.at[2], da_o), (am, att.at[0], am_o), (aw, att.at[1], aw_o),
             (aa, att.at[2], aa_o), (gin_hbm, tok.at[0], gin_o), (out_hbm, tok.at[1], out_o)]
    loads = [pltpu.make_async_copy(s, d, ld.at[k]) for k, (s, d, _) in enumerate(moves)]
    stores = [pltpu.make_async_copy(d, o, st.at[k]) for k, (_, d, o) in enumerate(moves)]
    for c in loads:
        c.start()

    def advance(grad, rate, moment, weight, average):
        grad = grad / replicas
        moment = momentum_decay * moment + grad
        weight = weight - rate * (grad + momentum_decay * moment)
        return moment, weight, average_decay * average + (1.0 - average_decay) * weight

    def advance_in(grad, ref, index):
        news = advance(grad, matrix, *(ref[(k,) + index] for k in range(3)))
        for k in range(3):
            ref[(k,) + index] = news[k]

    rows, own = vm.shape
    square[...] = jnp.zeros_like(square)
    square[:own, :] = vsum_ref[3]
    vm_o[...], vw_o[...], va_o[...] = advance(square[...].T[:rows, :own], vector, vm[...], vw[...], va[...])
    every = slice(None)
    pairs = att.shape[3] // LANES
    ff_pieces = sum_ref.shape[0] - 1 - pairs
    for c in loads[:3]:
        c.wait()
    for i in range(ff_pieces):
        col = i // 4 * 2 * PIECE + i % 2 * PIECE
        advance_in(sum_ref[i], den, (1 - i % 4 // 2, every, slice(col, col + PIECE)))
    for c in stores[:3]:
        c.start()
    for c in loads[3:6]:
        c.wait()
    for i in range(2):
        advance_in(sum_ref[ff_pieces + i], att, (3, every, slice(i * PIECE, (i + 1) * PIECE)))
    for p in range(pairs):
        for k in range(3):
            grad = vsum_ref[k] if p == pairs - 1 else sum_ref[ff_pieces + 2 + p, :, k * LANES : (k + 1) * LANES]
            advance_in(grad, att, (k, every, slice(p * LANES, (p + 1) * LANES)))
    for c in loads[6:]:
        c.wait()
    for c in stores[3:]:
        c.start()
    for c in stores:
        c.wait()


def update(rates, sums, vsums, gin, out, states):
    am, dm = states[0], states[3]
    sh = jax.ShapeDtypeStruct
    v = pltpu.VMEM
    hbm = pl.BlockSpec(memory_space=pl.ANY)
    vmem = pl.BlockSpec(memory_space=pltpu.VMEM)
    places = [hbm] * 8 + [vmem] * 3
    return pl.pallas_call(
        functools.partial(update_kernel, rates),
        out_shape=(sh(gin.shape, bf16), sh(out.shape, bf16)) + tuple(sh(s.shape, f32) for s in states),
        in_specs=[vmem, vmem] + places,
        out_specs=tuple(places),
        scratch_shapes=[v((LANES, LANES), f32), v((2,) + gin.shape, bf16), v((3,) + am.shape, f32), v((3,) + dm.shape, f32),
                        pltpu.SemaphoreType.DMA((8,)), pltpu.SemaphoreType.DMA((8,))],
        compiler_params=pltpu.CompilerParams(vmem_limit_bytes=BIG),
        name="update",
    )(sums, vsums, gin, out, *states)


def pack_columns(attention, dense, vectors):
    count = vectors.shape[0]
    vector_cols = jnp.pad(vectors.T, ((0, 0), (0, 128 - count)))
    first = jnp.concatenate([attention[0], attention[1], attention[2], vector_cols], 1)
    second = jnp.concatenate([attention[3], dense[0], dense[1]], 1)
    return first, second


def advance(gradient, moment, weight, average, step_rate):
    moment_new = momentum_decay * moment + gradient
    weight_new = weight - step_rate * (gradient + momentum_decay * moment_new)
    average_new = average_decay * average + (1.0 - average_decay) * weight_new
    return (moment_new, weight_new, average_new)


def plain_body(
    hidden_in,
    segment_ids,
    cotangent,
    attention_weights,
    attention_momentum,
    attention_average,
    dense_weights,
    dense_momentum,
    dense_average,
    vector_params,
    vector_momentum,
    vector_average,
):
    row_count, length, width = hidden_in.shape
    ff = dense_weights.shape[-1]
    vector_rows = vector_params.shape[0]
    x = hidden_in.reshape(-1, width)
    e = cotangent.reshape(-1, width)
    first, second = pack_columns(attention_weights, dense_weights, vector_params)
    first_full = lax.all_gather(first.astype(bf16), "wide", axis=0, tiled=True)
    second_full = lax.all_gather(second.astype(bf16), "wide", axis=0, tiled=True)
    vec = first_full[:, 3 * width : 3 * width + vector_rows].astype(f32).T
    bias_qkv = jnp.concatenate([vec[4:5], jnp.zeros((1, width), f32), vec[5:6]], 1)
    w_qkv = first_full[:, : 3 * width]
    wo, win, wd = (second_full[:, :width], second_full[:, width : width + ff], second_full[:, width + ff :])
    qkv, c, lse = attn_fwd(x, segment_ids, w_qkv, bias_qkv)
    out, y1, g, dz, du, da, dc, dh1, delta, dvec, dbin = mid(
        x, c, e, wo, win, wd, vec, vec[8:].reshape(1, ff)
    )
    grad_second = jnp.concatenate([wgrad(c, da), wgrad(y1, du), wgrad(dz, g)], 1)
    share_second = lax.psum_scatter(grad_second, "wide", scatter_dimension=0, tiled=True)
    dqkv, gin, dw, db = attn_bwd(segment_ids, qkv, dc, lse, delta, dh1, w_qkv, x)
    dvec = jnp.concatenate(
        [dvec[:4], db[:, :width], db[:, 2 * width :], dvec[6:8], dbin.reshape(-1, width)], 0
    )
    grad_first = jnp.concatenate(
        [dw, jnp.pad(dvec.T, ((0, 0), (0, 128 - vector_rows))).astype(bf16)], 1
    )
    share_first = lax.psum_scatter(grad_first, "wide", scatter_dimension=0, tiled=True)
    replicas = lax.axis_size("narrow")
    tokens_all = row_count * length * lax.axis_size("wide") * replicas
    grad_scale = math.sqrt(tokens_all) / replicas
    t1 = lax.psum(share_first, "narrow").astype(f32) / replicas
    t2 = lax.psum(share_second, "narrow").astype(f32) / replicas
    cut = lambda t, j: t[:, j * width : (j + 1) * width]
    attention_grad = jnp.stack([cut(t1, 0), cut(t1, 1), cut(t1, 2), cut(t2, 0)])
    dense_grad = jnp.stack([t2[:, width : width + ff], t2[:, width + ff :]])
    vector_grad = t1[:, 3 * width : 3 * width + vector_rows].T
    attention_new = advance(attention_grad, attention_momentum, attention_weights, attention_average, matrix_rate / grad_scale)
    dense_new = advance(dense_grad, dense_momentum, dense_weights, dense_average, matrix_rate / grad_scale)
    vector_new = advance(vector_grad, vector_momentum, vector_params, vector_average, vector_rate / grad_scale)
    return (out.reshape(hidden_in.shape), gin.reshape(hidden_in.shape)) + attention_new + dense_new + vector_new


def body(
    hidden_in,
    segment_ids,
    cotangent,
    attention_weights,
    attention_momentum,
    attention_average,
    dense_weights,
    dense_momentum,
    dense_average,
    vector_params,
    vector_momentum,
    vector_average,
):
    row_count, length, width = hidden_in.shape
    x = hidden_in.reshape(-1, width)
    e = cotangent.reshape(-1, width)
    replicas = lax.axis_size("narrow")
    tokens_all = row_count * length * lax.axis_size("wide") * replicas
    grad_scale = math.sqrt(tokens_all) / replicas
    rates = (matrix_rate / grad_scale, vector_rate / grad_scale, replicas)
    qkv, c, lse, w, out, y1, g, gp, dz, dh2, n1, r1, dv, vec = stage(
        x, segment_ids, e, attention_weights, dense_weights, vector_params
    )
    states = (
        attention_momentum, attention_weights, attention_average,
        dense_momentum, dense_weights, dense_average,
        vector_momentum, vector_params, vector_average,
    )
    gin, sums, vsums = back(x, c, y1, dz, dh2, n1, r1, g, gp, qkv, w, segment_ids, lse, dv, vec)
    news = update(rates, sums, vsums, gin, out, states)
    return (news[1].reshape(hidden_in.shape), news[0].reshape(hidden_in.shape)) + tuple(news[2:])


def solution(mesh):
    token = P(("wide", "narrow"), None, None)
    matrix = P(None, "wide", None)
    vector = P(None, "wide")
    in_specs = (token, P(("wide", "narrow"), None), token) + (matrix,) * 6 + (vector,) * 3
    out_specs = (token, token) + (matrix,) * 6 + (vector,) * 3
    ours = mesh.shape["wide"] == 16 and mesh.shape["narrow"] == 2
    return jax.shard_map(body if ours else plain_body, mesh=mesh, in_specs=in_specs, out_specs=out_specs, check_vma=False)
```

```python
import functools, math
import jax, jax.numpy as jnp
from jax import lax
from jax.sharding import PartitionSpec as P
from jax.experimental import pallas as pl
from jax.experimental.pallas import tpu as pltpu

HD = 64
LOG2E = 1.4426950408889634
SCALE2 = 0.125 * LOG2E
NEG = -1e30
EPS = 1e-12
momentum_decay = 0.5
average_decay = 0.5
matrix_rate = 0.03
vector_rate = 0.3
f32, bf16 = jnp.float32, jnp.bfloat16
BIG = 60 * 2**20

def dot(a, b):
    return lax.dot_general(a, b, (((1,), (0,)), ((), ())), preferred_element_type=f32)
def dot_nt(a, b):
    return lax.dot_general(a, b, (((1,), (1,)), ((), ())), preferred_element_type=f32)
def dot_tn(a, b):
    return lax.dot_general(a, b, (((0,), (0,)), ((), ())), preferred_element_type=f32)

def key_range(c, seq, blk):
    lo = max(0, c * blk - seq // 2 + 1) // blk * blk
    hi = min(seq, -(-((c + 1) * blk - 1 + seq // 2) // blk) * blk)
    return lo, hi

def fill_bias(seg_ref, bias_ref):
    segf = seg_ref[0].astype(f32)
    seq = segf.shape[1]
    rep = jnp.broadcast_to(segf, (128, seq)).T
    for j in range(seq // 128):
        bias_ref[:, j * 128:(j + 1) * 128] = jnp.where(rep == segf[:, j * 128:(j + 1) * 128], 0.0, NEG)

def fwd_kernel(blk, x_ref, seg_ref, w_ref, b_ref, qkv_ref, c_ref, lse_ref, bias_ref, lsea_ref):
    seq, width = x_ref.shape
    x = x_ref[...]
    for j in range(3):
        sl = slice(j * width, (j + 1) * width)
        qkv_ref[:, sl] = (dot(x, w_ref[:, sl]) + b_ref[:, sl]).astype(bf16)
    fill_bias(seg_ref, bias_ref)
    lane = lax.broadcasted_iota(jnp.int32, (blk, 128), 1)
    first = lane < HD
    ones = jnp.ones((seq, 128), bf16)
    def pair(p, _):
        col = pl.multiple_of(p * 128, 128)
        q2 = qkv_ref[:, pl.ds(col, 128)]
        k2 = qkv_ref[:, pl.ds(col + width, 128)]
        v2 = jnp.concatenate([qkv_ref[:, pl.ds(col + 2 * width, 128)], ones], 1)
        for c in range(seq // blk):
            lo, hi = key_range(c, seq, blk)
            rows = slice(c * blk, (c + 1) * blk)
            qc = q2[rows]
            outs = []
            la = lsea_ref[rows, :]
            for h in range(2):
                qm = jnp.where(first if h == 0 else ~first, qc, jnp.zeros_like(qc))
                s = dot_nt(qm, k2[lo:hi]) + bias_ref[rows, lo:hi]
                m = jnp.max(s, 1, keepdims=True)
                e = jnp.exp2((s - m) * SCALE2)
                o = dot(e.astype(bf16), v2[lo:hi])
                l = o[:, 128:]
                outs.append(o[:, :128] / l)
                la = jnp.where(lane == 2 * p + h, m * SCALE2 + jnp.log(l) * LOG2E, la)
            lsea_ref[rows, :] = la
            c_ref[rows, pl.ds(col, 128)] = jnp.where(first, outs[0], outs[1]).astype(bf16)
        return 0
    lax.fori_loop(0, width // 128, pair, 0)
    lse_ref[0] = lsea_ref[...].T[:lse_ref.shape[1]]

def attn_fwd(x, seg, w, b, blk=128):
    rows, seq = seg.shape
    width = x.shape[1]
    return pl.pallas_call(
        functools.partial(fwd_kernel, blk), grid=(rows,),
        out_shape=(jax.ShapeDtypeStruct((rows * seq, 3 * width), bf16), jax.ShapeDtypeStruct((rows * seq, width), bf16),
                   jax.ShapeDtypeStruct((rows, 16, seq), f32)),
        in_specs=[pl.BlockSpec((seq, width), lambda r: (r, 0)), pl.BlockSpec((1, 1, seq), lambda r: (r, 0, 0)),
                  pl.BlockSpec((width, 3 * width), lambda r: (0, 0)), pl.BlockSpec((1, 3 * width), lambda r: (0, 0))],
        out_specs=(pl.BlockSpec((seq, 3 * width), lambda r: (r, 0)), pl.BlockSpec((seq, width), lambda r: (r, 0)),
                   pl.BlockSpec((1, 16, seq), lambda r: (r, 0, 0))),
        scratch_shapes=[pltpu.VMEM((seq, seq), f32), pltpu.VMEM((seq, 128), f32)],
        compiler_params=pltpu.CompilerParams(vmem_limit_bytes=BIG),
        name="attn_fwd",
    )(x, seg.reshape(rows, 1, seq), w, b)

def bwd_kernel(blk, seg_ref, qkv_ref, dc_ref, lse_ref, delta_ref, dh1_ref, w_ref, x_ref, dqkv_ref, gin_ref, dw_ref, db_ref, bias_ref, ds_ref, acc_ref):
    r = pl.program_id(0)
    seq = dc_ref.shape[0]
    width = dc_ref.shape[1]
    fill_bias(seg_ref, bias_ref)
    ds_ref[...] = jnp.zeros_like(ds_ref)
    lane = lax.broadcasted_iota(jnp.int32, (blk, 128), 1)
    first = lane < HD
    lane_s = lax.broadcasted_iota(jnp.int32, (seq, 128), 1)
    def pair(p, _):
        col = pl.multiple_of(p * 128, 128)
        q2 = qkv_ref[:, pl.ds(col, 128)]
        k2 = qkv_ref[:, pl.ds(col + width, 128)]
        v2 = qkv_ref[:, pl.ds(col + 2 * width, 128)]
        dc2 = dc_ref[:, pl.ds(col, 128)]
        dqs = []
        for h in range(2):
            lse = lse_ref[0, pl.ds(2 * p + h, 1), :]
            dl = delta_ref[pl.ds(2 * p + h, 1), :]
            mine = first if h == 0 else ~first
            for c in range(seq // blk):
                lo, hi = key_range(c, seq, blk)
                rows = slice(c * blk, (c + 1) * blk)
                kc, vc = k2[rows], v2[rows]
                km = jnp.where(mine, kc, jnp.zeros_like(kc))
                vm = jnp.where(mine, vc, jnp.zeros_like(vc))
                st = dot_nt(km, q2[lo:hi])
                pt = jnp.exp2((st + bias_ref[rows, lo:hi]) * SCALE2 - lse[:, lo:hi])
                dp = dot_nt(vm, dc2[lo:hi])
                ds = (pt * (dp - dl[:, lo:hi])).astype(bf16)
                ds_ref[h, rows, lo:hi] = ds
                dv = dot(pt.astype(bf16), dc2[lo:hi])
                dk = dot(ds, q2[lo:hi]) * 0.125
                if h == 0:
                    dqkv_ref[rows, pl.ds(col + 2 * width, 128)] = dv.astype(bf16)
                    dqkv_ref[rows, pl.ds(col + width, 128)] = dk.astype(bf16)
                else:
                    ov = dqkv_ref[rows, pl.ds(col + 2 * width, 128)]
                    ok = dqkv_ref[rows, pl.ds(col + width, 128)]
                    dqkv_ref[rows, pl.ds(col + 2 * width, 128)] = jnp.where(first, ov, dv.astype(bf16))
                    dqkv_ref[rows, pl.ds(col + width, 128)] = jnp.where(first, ok, dk.astype(bf16))
            dqs.append(dot_tn(ds_ref[h], k2) * 0.125)
        dqkv_ref[:, pl.ds(col, 128)] = jnp.where(lane_s < HD, dqs[0], dqs[1]).astype(bf16)
        return 0
    lax.fori_loop(0, width // 128, pair, 0)
    dqkv = dqkv_ref[...]
    gin_ref[...] = (dh1_ref[...] + dot_nt(dqkv, w_ref[...])).astype(bf16)
    x = x_ref[...]
    for j in range(3):
        sl = slice(j * width, (j + 1) * width)
        d = dot_tn(x, dqkv[:, sl])
        s = jnp.sum(dqkv[:, sl].astype(f32), 0, keepdims=True)
        @pl.when(r == 0)
        def _():
            acc_ref[:, sl] = d
            db_ref[:, sl] = s
        @pl.when(r == pl.num_programs(0) - 1)
        def _():
            dw_ref[:, sl] = (acc_ref[:, sl] + d).astype(bf16)
            db_ref[:, sl] += s

def attn_bwd(seg, qkv, dc, lse, delta, dh1, w, x, blk=128):
    rows, seq = seg.shape
    width = dc.shape[1]
    assert rows == 2
    return pl.pallas_call(
        functools.partial(bwd_kernel, blk), grid=(rows,),
        out_shape=(jax.ShapeDtypeStruct((rows * seq, 3 * width), bf16), jax.ShapeDtypeStruct((rows * seq, width), bf16),
                   jax.ShapeDtypeStruct((width, 3 * width), bf16), jax.ShapeDtypeStruct((1, 3 * width), f32)),
        in_specs=[pl.BlockSpec((1, 1, seq), lambda r: (r, 0, 0)), pl.BlockSpec((seq, 3 * width), lambda r: (r, 0)),
                  pl.BlockSpec((seq, width), lambda r: (r, 0)), pl.BlockSpec((1, 16, seq), lambda r: (r, 0, 0)),
                  pl.BlockSpec((16, seq), lambda r: (0, r)), pl.BlockSpec((seq, width), lambda r: (r, 0)),
                  pl.BlockSpec((width, 3 * width), lambda r: (0, 0)), pl.BlockSpec((seq, width), lambda r: (r, 0))],
        out_specs=(pl.BlockSpec((seq, 3 * width), lambda r: (r, 0)), pl.BlockSpec((seq, width), lambda r: (r, 0)),
                   pl.BlockSpec((width, 3 * width), lambda r: (0, 0)), pl.BlockSpec((1, 3 * width), lambda r: (0, 0))),
        scratch_shapes=[pltpu.VMEM((seq, seq), f32), pltpu.VMEM((2, seq, seq), bf16), pltpu.VMEM((width, 3 * width), f32)],
        compiler_params=pltpu.CompilerParams(vmem_limit_bytes=BIG),
        name="attn_bwd",
    )(seg.reshape(rows, 1, seq), qkv, dc, lse, delta, dh1, w, x)

RSQRT_2PI = 1.0 / math.sqrt(2 * math.pi)
def gelu_parts(u):
    phi_cdf = 0.5 + 0.5 * lax.erf(u * math.sqrt(0.5))
    dens = jnp.exp2(u * u * (-0.5 * LOG2E)) * RSQRT_2PI
    return u * phi_cdf, phi_cdf + u * dens

def mid_kernel(chunk, x_ref, c_ref, e_ref, wo_ref, win_ref, wd_ref, v_ref, bin_ref,
               out_ref, y1_ref, g_ref, dz_ref, du_ref, da_ref, dc_ref, dh1_ref, delta_ref, dv_ref, dbin_ref, gp_ref):
    i = pl.program_id(0)
    blk, width = x_ref.shape
    ff = win_ref.shape[1]
    @pl.when(i == 0)
    def _():
        dv_ref[...] = jnp.zeros_like(dv_ref)
        dbin_ref[...] = jnp.zeros_like(dbin_ref)
    g1, s1, g2, s2, bo, bd = (v_ref[j:j + 1, :] for j in (0, 1, 2, 3, 6, 7))
    cb = c_ref[...]
    h1 = x_ref[...].astype(f32) + (dot(cb, wo_ref[...]) + bo)
    cen = h1 - jnp.mean(h1, 1, keepdims=True)
    r1 = lax.rsqrt(jnp.mean(cen * cen, 1, keepdims=True) + EPS)
    n1 = cen * r1
    y1 = n1 * g1 + s1
    y1l = y1.astype(bf16)
    y1_ref[...] = y1l
    z = jnp.zeros((blk, width), f32)
    for j in range(ff // chunk):
        sl = slice(j * chunk, (j + 1) * chunk)
        u = dot(y1l, win_ref[:, sl]) + bin_ref[:, sl]
        g, gp = gelu_parts(u)
        gl = g.astype(bf16)
        g_ref[:, sl] = gl
        gp_ref[:, sl] = gp
        z += dot_nt(gl, wd_ref[:, sl])
    h2 = y1 + (z + bd)
    cen = h2 - jnp.mean(h2, 1, keepdims=True)
    r2 = lax.rsqrt(jnp.mean(cen * cen, 1, keepdims=True) + EPS)
    n2 = cen * r2
    out_ref[...] = (n2 * g2 + s2).astype(bf16)
    e = e_ref[...].astype(f32)
    eg = e * g2
    dh2 = r2 * (eg - jnp.mean(eg, 1, keepdims=True) - n2 * jnp.mean(eg * n2, 1, keepdims=True))
    dz = dh2.astype(bf16)
    dz_ref[...] = dz
    dy1 = dh2
    for j in range(ff // chunk):
        sl = slice(j * chunk, (j + 1) * chunk)
        du = (dot(dz, wd_ref[:, sl]) * gp_ref[:, sl]).astype(bf16)
        du_ref[:, sl] = du
        dbin_ref[:, sl] += jnp.sum(du.astype(f32), 0, keepdims=True)
        dy1 += dot_nt(du, win_ref[:, sl])
    dn = dy1 * g1
    dh1 = r1 * (dn - jnp.mean(dn, 1, keepdims=True) - n1 * jnp.mean(dn * n1, 1, keepdims=True))
    dh1_ref[...] = dh1
    da = dh1.astype(bf16)
    da_ref[...] = da
    dc = dot_nt(da, wo_ref[...]).astype(bf16)
    dc_ref[...] = dc
    prod = dc.astype(f32) * cb.astype(f32)
    hi = prod.astype(bf16)
    lo = (prod - hi.astype(f32)).astype(bf16)
    sel = jnp.where(lax.broadcasted_iota(jnp.int32, (16, width), 0) == lax.broadcasted_iota(jnp.int32, (16, width), 1) // HD, 1.0, 0.0).astype(bf16)
    delta_ref[...] = dot_nt(sel, hi) + dot_nt(sel, lo)
    parts = [dy1 * n1, dy1, e * n2, e, da.astype(f32), dz.astype(f32)]
    for j, t in zip((0, 1, 2, 3, 6, 7), parts):
        dv_ref[j:j + 1, :] += jnp.sum(t, 0, keepdims=True)

def mid(x, c, e, wo, win, wd, vec, bin_, blk=256, chunk=768):
    n, width = x.shape
    ff = win.shape[1]
    tok = lambda w: pl.BlockSpec((blk, w), lambda i: (i, 0))
    full = lambda a: pl.BlockSpec(a.shape, lambda i: (0, 0), pipeline_mode=pl.Buffered(1))
    sh = jax.ShapeDtypeStruct
    return pl.pallas_call(
        functools.partial(mid_kernel, chunk), grid=(n // blk,),
        out_shape=(sh((n, width), bf16), sh((n, width), bf16), sh((n, ff), bf16), sh((n, width), bf16), sh((n, ff), bf16),
                   sh((n, width), bf16), sh((n, width), bf16), sh((n, width), f32), sh((16, n), f32), sh((8, width), f32), sh((1, ff), f32)),
        in_specs=[tok(width), tok(width), tok(width), full(wo), full(win), full(wd), full(vec), full(bin_)],
        out_specs=(tok(width), tok(width), tok(ff), tok(width), tok(ff), tok(width), tok(width), tok(width),
                   pl.BlockSpec((16, blk), lambda i: (0, i)), pl.BlockSpec((8, width), lambda i: (0, 0)), pl.BlockSpec((1, ff), lambda i: (0, 0))),
        scratch_shapes=[pltpu.VMEM((blk, ff), f32)],
        compiler_params=pltpu.CompilerParams(vmem_limit_bytes=BIG),
        name="middle",
    )(x, c, e, wo, win, wd, vec, bin_)

def wgrad_kernel(a_ref, b_ref, o_ref):
    o_ref[...] = dot_tn(a_ref[...], b_ref[...]).astype(bf16)

def wgrad(a, b, blk=768):
    n, m = a.shape
    k = b.shape[1]
    return pl.pallas_call(wgrad_kernel, grid=(k // blk,), out_shape=jax.ShapeDtypeStruct((m, k), bf16),
        in_specs=[pl.BlockSpec((n, m), lambda j: (0, 0)), pl.BlockSpec((n, blk), lambda j: (0, j))],
        out_specs=pl.BlockSpec((m, blk), lambda j: (0, j)),
        compiler_params=pltpu.CompilerParams(vmem_limit_bytes=BIG), name="wgrad")(a, b)


LANES = 128
PIECE = 3 * LANES
GATHER_LAGS = (0, 2, 4, 6)
REDUCE_LAGS = (2, 4, 6, 8)
AHEAD = 3
MESH = pl.DeviceIdType.MESH


class Place:
    def __init__(self):
        self.w = lax.axis_index("wide")
        self.x = lax.axis_index("narrow")
        self.core = lax.rem(self.w, 2)
        self.y = lax.rem(self.w // 2, 2)
        self.b = lax.rem(self.w // 4, 2)
        self.a = self.w // 8
        self.z = self.w // 4

    def z_peer(self, k):
        return lax.rem(self.z + k, 4)

    def over(self, name):
        if name == "x":
            return (self.w, 1 - self.x)
        if name in (1, 2, 3):
            return (4 * self.z_peer(name) + lax.rem(self.w, 4), self.x)
        step = {"a": 8, "b": 4, "y": 2, "core": 1}[name]
        return (self.w + step * (1 - 2 * getattr(self, name)), self.x)

    near = ("a", "b", "y", "x", "core")
    reduce_peers = (1, 2, 3, "y", "x", "core")

    def greet(self, names):
        for name in names:
            pl.semaphore_signal(pltpu.get_barrier_semaphore(), inc=1, device_id=self.over(name), device_id_type=MESH)

    def met(self, names):
        pl.semaphore_wait(pltpu.get_barrier_semaphore(), len(names))


def remote(src, dst, send, recv, device):
    return pltpu.make_async_remote_copy(src_ref=src, dst_ref=dst, send_sem=send, recv_sem=recv, device_id=device, device_id_type=MESH)


def when(condition, step):
    @pl.when(condition)
    def _():
        step()


def loop(count, step):
    lax.fori_loop(0, count, lambda i, _: (step(i), 0)[1], 0)


class Gather:
    def __init__(self, place, shard, full, sems, pieces):
        self.p, self.shard, self.full, self.pieces = place, shard, full, pieces
        self.sems = {name: (sems[2 * k], sems[2 * k + 1]) for k, name in enumerate(("a", "b", "y", "x", "core"))}
        self.kept = sems[10]
        self.own = pl.ds(place.x, 2)

    def mine(self, i, a):
        return self.full.at[i, self.own, a, self.p.b, self.p.y, self.p.core]

    def keep(self, i):
        return pltpu.make_async_copy(self.shard.at[i, self.own], self.mine(i, self.p.a), self.kept.at[i])

    def copy(self, name, i, incoming=False):
        p, f = self.p, self.full
        at = {n: (1 - getattr(p, n) if incoming and n == name else getattr(p, n)) for n in ("a", "b", "y", "x", "core")}
        every = slice(None)
        if name == "a":
            dst = self.mine(i, at["a"])
            src = self.shard.at[i, self.own]
        else:
            if name == "b":
                dst = f.at[i, self.own, :, at["b"], p.y, p.core]
            elif name == "y":
                dst = f.at[i, self.own, :, :, at["y"], p.core]
            elif name == "x":
                dst = f.at[i, 2 * at["x"], :, :, :, p.core]
            else:
                dst = f.at[i, :, :, :, :, at["core"]]
            src = dst
        send, recv = self.sems[name]
        return remote(src, dst, send.at[i], recv.at[i], p.over(name))

    def start(self, i):
        self.keep(i).start()
        self.copy("a", i).start()

    def b_step(self, i):
        self.keep(i).wait()
        self.copy("a", i, True).wait_recv()
        self.copy("b", i).start()

    def y_step(self, i):
        self.copy("b", i, True).wait_recv()
        self.copy("y", i).start()

    def x_step(self, i):
        self.copy("y", i, True).wait_recv()
        self.copy("x", i).start()

    def core_step(self, i):
        self.copy("x", i, True).wait_recv()
        self.copy("core", i).start()

    def arrive(self, i):
        self.copy("core", i, True).wait_recv()

    def turn(self, t):
        for k in range(2):
            ahead = AHEAD + 2 * t + k
            when(ahead < self.pieces, lambda ahead=ahead: self.start(ahead))
        for lag, step in zip(GATHER_LAGS, (self.b_step, self.y_step, self.x_step, self.core_step)):
            when((t >= lag) & (t < self.pieces + lag), lambda lag=lag, step=step: step(t - lag))

    def sent(self, i):
        for name in ("a", "b", "y", "x", "core"):
            self.copy(name, i).wait_send()


class GatherVector:
    def __init__(self, place, shard, full, sems):
        self.p, self.shard, self.full = place, shard, full
        self.sems = {name: (sems[2 * k], sems[2 * k + 1]) for k, name in enumerate(("a", "b", "y", "core"))}
        self.kept = sems[8]

    def keep(self):
        p = self.p
        return pltpu.make_async_copy(self.shard, self.full.at[p.a, p.b, p.y, p.core], self.kept)

    def copy(self, name, incoming=False):
        p = self.p
        at = {n: (1 - getattr(p, n) if incoming and n == name else getattr(p, n)) for n in ("a", "b", "y", "core")}
        every = slice(None)
        first = ("a", "b", "y", "core").index(name)
        dst = self.full.at[tuple(at[n] if n == name or n == "core" or k > first else every for k, n in enumerate(("a", "b", "y", "core")))]
        src = self.shard if name == "a" else dst
        send, recv = self.sems[name]
        return remote(src, dst, send, recv, p.over(name))

    def start(self):
        self.keep().start()
        self.copy("a").start()

    def step(self, name, then):
        if name == "a":
            self.keep().wait()
        self.copy(name, True).wait_recv()
        self.copy(then).start()

    def arrive(self):
        self.copy("core", True).wait_recv()

    def sent(self):
        for name in ("a", "b", "y", "core"):
            self.copy(name).wait_send()


def tile(ref, i, t):
    rows = 16 * ref.shape[-2]
    return ref[i, t].reshape(rows, LANES)


def columns(ref, *pieces):
    return jnp.concatenate([tile(ref, i, t) for i in pieces for t in range(3)], 1)


def doc_bias(seg_row, bias_ref, r):
    segf = seg_row.astype(f32)
    seq = segf.shape[1]
    rep = jnp.broadcast_to(segf, (LANES, seq)).T
    for j in range(seq // LANES):
        sl = slice(j * LANES, (j + 1) * LANES)
        bias_ref[r, :, sl] = jnp.where(rep == segf[:, sl], 0.0, NEG)


def stage_kernel(heads, x_hbm, seg_ref, e_hbm, aw_hbm, dw_hbm, vp_ref,
                 qkv_o, c_o, lse_o, w_o, out_o, y1_o, g_o, gp_o, dz_o, dh2_o, n1_o, r1_o, dv_o, vrow,
                 full, vfull, shard, vshard, square, xb, eb, cb, n1b, y1b, acc, gp, gb, dzb, bias, lsea, binr, r1b,
                 in_sem, out_sem, w_sem, two_sem, *sems):
    place = Place()
    rows, seq = seg_ref.shape
    tokens, width = x_hbm.shape
    pairs = heads // 2
    pieces = shard.shape[0]
    chunks = gb.shape[0]
    own_rows = aw_hbm.shape[1]
    blk = 256
    big = 512
    g = Gather(place, shard, full, sems[:11], pieces)
    gv = GatherVector(place, vshard, vfull, sems[11:])

    loads = [pltpu.make_async_copy(aw_hbm.at[k], gp.at[0, pl.ds(k * own_rows, own_rows)], in_sem.at[k]) for k in range(4)]
    for k in range(2):
        for j in range(chunks):
            loads.append(pltpu.make_async_copy(
                dw_hbm.at[k, :, pl.ds(j * width, width)], gp.at[1 + k, pl.ds(j * own_rows, own_rows)], in_sem.at[4 + k * chunks + j]))
    n = len(loads)
    x_load = pltpu.make_async_copy(x_hbm, xb, in_sem.at[n])
    e_load = pltpu.make_async_copy(e_hbm, eb, in_sem.at[n + 1])
    for c in loads:
        c.start()
    place.greet(place.near)
    x_load.start()
    e_load.start()
    square[...] = jnp.zeros_like(square)
    lsea[...] = jnp.zeros_like(lsea)
    square[: vp_ref.shape[0], :own_rows] = vp_ref[...]
    vshard[...] = square[...].T[:own_rows].astype(bf16)

    def own_tile(k, j, t):
        return gp[k, j * own_rows : (j + 1) * own_rows, t * LANES : (t + 1) * LANES].astype(bf16)

    for c in loads[:3]:
        c.wait()
    for p in range(pairs):
        for t in range(3):
            shard[p, t] = own_tile(0, t, p)
    place.met(place.near)
    gv.start()
    for i in range(AHEAD):
        g.start(i)
    for c in loads[3:]:
        c.wait()
    for t in range(6):
        shard[pairs + t // 3, t % 3] = own_tile(0, 3, t)
        for j in range(chunks):
            for k in range(2):
                shard[pairs + 2 + 4 * j + 2 * k + t // 3, t % 3] = own_tile(1 + k, j, t)
    for r in range(rows):
        doc_bias(seg_ref[r : r + 1, :], bias, r)
    gv.step("a", "b")
    fill = GATHER_LAGS[-1] + 1
    for t in range(fill):
        g.turn(t)
        if t == 1:
            gv.step("b", "y")
        if t == 4:
            gv.step("y", "core")
    gv.arrive()
    vec = vfull[...].reshape(16 * own_rows, LANES).astype(f32).T
    vrow[...] = vec[: vrow.shape[0]]
    for j in range(chunks):
        binr[j] = vrow[8 + j : 9 + j, :]
    x_load.wait()

    first = lax.broadcasted_iota(jnp.int32, (LANES, LANES), 1) < HD
    lane = lax.broadcasted_iota(jnp.int32, (LANES, LANES), 1)
    ones = jnp.ones((seq, LANES), bf16)

    def qkv_at(p):
        return gb.at[p // 2, :, pl.ds(pl.multiple_of(lax.rem(p, 2) * PIECE, LANES), PIECE)]

    def qkv_out(p):
        return pltpu.make_async_copy(qkv_at(p), qkv_o.at[p], out_sem.at[p])

    def w_out(i):
        return pltpu.make_async_copy(full.at[i], w_o.at[i], w_sem.at[i])

    def pair(p):
        g.arrive(p)
        w_out(p).start()
        head = pl.ds(pl.multiple_of(p * LANES, LANES), LANES)
        w = columns(full, p)
        b = jnp.concatenate([vrow[4:5, head], jnp.zeros((1, LANES), f32), vrow[5:6, head]], 1)
        col = pl.multiple_of(lax.rem(p, 2) * PIECE, LANES)
        gb[p // 2, :, pl.ds(col, PIECE)] = (dot(xb[...], w) + b).astype(bf16)
        qkv_out(p).start()

        def row(r):
            tok = pl.ds(pl.multiple_of(r * seq, seq), seq)
            q2 = gb[p // 2, tok, pl.ds(col, LANES)]
            k2 = gb[p // 2, tok, pl.ds(col + LANES, LANES)]
            v2 = jnp.concatenate([gb[p // 2, tok, pl.ds(col + 2 * LANES, LANES)], ones], 1)
            for c in range(seq // LANES):
                lo, hi = key_range(c, seq, LANES)
                cut = slice(c * LANES, (c + 1) * LANES)
                outs = []
                la = lsea[r, cut, :]
                for h in range(2):
                    qm = jnp.where(first if h == 0 else ~first, q2[cut], jnp.zeros_like(q2[cut]))
                    s = dot_nt(qm, k2[lo:hi]) + bias[r, cut, lo:hi]
                    m = jnp.max(s, 1, keepdims=True)
                    o = dot(jnp.exp2((s - m) * SCALE2).astype(bf16), v2[lo:hi])
                    l = o[:, LANES:]
                    outs.append(o[:, :LANES] / l)
                    la = jnp.where(lane == 2 * p + h, m * SCALE2 + jnp.log(l) * LOG2E, la)
                lsea[r, cut, :] = la
                cb[pl.ds(pl.multiple_of(r * seq + c * LANES, LANES), LANES), head] = jnp.where(first, outs[0], outs[1]).astype(bf16)
            g.turn(fill + 2 * p + r)

        loop(rows, row)

    loop(pairs, pair)
    done = fill + 2 * pairs
    for r in range(rows):
        lse_o[r] = lsea[r].T[: lse_o.shape[1]]
    c_out = pltpu.make_async_copy(cb, c_o, out_sem.at[pairs])
    c_out.start()
    g1, s1, g2, s2, bo, bd = (vrow[j : j + 1, :] for j in (0, 1, 2, 3, 6, 7))

    def block(i):
        return pl.ds(pl.multiple_of(i * blk, blk), blk)

    for i in (pairs, pairs + 1):
        g.arrive(i)
        w_out(i).start()

    def norm_one(i):
        at = block(i)
        h1 = xb[at, :].astype(f32) + (dot(cb[at, :], columns(full, pairs, pairs + 1)) + bo)
        cen = h1 - jnp.mean(h1, 1, keepdims=True)
        r1 = lax.rsqrt(jnp.mean(cen * cen, 1, keepdims=True) + EPS)
        n1 = cen * r1
        y1 = n1 * g1 + s1
        n1b[at, :] = n1
        r1b[at, :] = jnp.broadcast_to(r1, (blk, LANES))
        y1b[at, :] = y1.astype(bf16)
        acc[at, :] = y1 + bd
        when(lax.rem(i, 2) == 1, lambda: g.turn(done + i // 2))

    loop(tokens // blk, norm_one)
    done += 2
    y1_out = pltpu.make_async_copy(y1b, y1_o, out_sem.at[pairs + 2])
    y1_out.start()
    n1_out = pltpu.make_async_copy(n1b, n1_o, out_sem.at[pairs + 1])
    n1_out.start()
    r1_out = pltpu.make_async_copy(r1b, r1_o, out_sem.at[pairs + 5 + chunks])
    r1_out.start()
    loop(pairs, lambda p: qkv_out(p).wait())

    def up(j):
        return columns(full, pairs + 2 + 4 * j, pairs + 3 + 4 * j)

    def down(j):
        return columns(full, pairs + 4 + 4 * j, pairs + 5 + 4 * j)

    def g_out(j):
        return pltpu.make_async_copy(gb.at[j], g_o.at[j], out_sem.at[pairs + 7 + j])

    def gp_out(j):
        return pltpu.make_async_copy(gp.at[j], gp_o.at[j], out_sem.at[pairs + 7 + chunks + j])

    def ff_chunk(j):
        def ready(k):
            for t in (k, k + 1):
                g.arrive(pairs + 2 + 4 * j + t)
                w_out(pairs + 2 + 4 * j + t).start()

        def up_block(i):
            at = pl.ds(pl.multiple_of(i * big, big), big)
            act, slope = gelu_parts(dot(y1b[at, :], up(j)) + binr[j])
            gb[j, at, :] = act.astype(bf16)
            gp[j, at, :] = slope
            g.turn(done + 4 * j + i)

        def down_block(i):
            at = pl.ds(pl.multiple_of(i * big, big), big)
            acc[at, :] += dot_nt(gb[j, at, :], down(j))
            g.turn(done + 4 * j + 2 + i)

        ready(0)
        loop(tokens // big, up_block)
        g_out(j).start()
        gp_out(j).start()
        ready(2)
        loop(tokens // big, down_block)

    loop(chunks, ff_chunk)
    e_load.wait()
    dv_o[...] = jnp.zeros_like(dv_o)

    def colsum(t):
        return jnp.sum(t, 0, keepdims=True)

    def norm_two(i):
        at = block(i)
        h2 = acc[at, :]
        cen = h2 - jnp.mean(h2, 1, keepdims=True)
        r2 = lax.rsqrt(jnp.mean(cen * cen, 1, keepdims=True) + EPS)
        n2 = cen * r2
        xb[at, :] = (n2 * g2 + s2).astype(bf16)
        e = eb[at, :].astype(f32)
        eg = e * g2
        dh2 = r2 * (eg - jnp.mean(eg, 1, keepdims=True) - n2 * jnp.mean(eg * n2, 1, keepdims=True))
        dz = dh2.astype(bf16)
        dzb[at, :] = dz
        acc[at, :] = dh2
        dv_o[2:3, :] += colsum(e * n2)
        dv_o[3:4, :] += colsum(e)
        dv_o[7:8, :] += colsum(dz.astype(f32))

    def norm_two_out(i):
        at = block(i)
        pairs_of = ((xb, out_o), (dzb, dz_o), (acc, dh2_o))
        return [pltpu.make_async_copy(src.at[at], dst.at[at], two_sem.at[k, i]) for k, (src, dst) in enumerate(pairs_of)]

    def norm_two_step(i):
        norm_two(i)
        for c in norm_two_out(i):
            c.start()

    loop(tokens // blk, norm_two_step)
    gv.sent()
    loop(pieces, g.sent)
    loop(pieces, lambda i: w_out(i).wait())
    for c in [c_out, y1_out, n1_out, r1_out]:
        c.wait()
    for i in range(tokens // blk):
        for c in norm_two_out(i):
            c.wait()
    loop(chunks, lambda j: g_out(j).wait())
    loop(chunks, lambda j: gp_out(j).wait())


def stage(x, seg, e, aw, dw, vp):
    rows, seq = seg.shape
    tokens, width = x.shape
    own_rows, ff = dw.shape[1:]
    heads, chunks = width // HD, ff // width
    pairs = heads // 2
    pieces = pairs + 2 + 4 * chunks
    sh = jax.ShapeDtypeStruct
    dma = pltpu.SemaphoreType.DMA
    v = pltpu.VMEM
    hbm = pl.BlockSpec(memory_space=pl.ANY)
    vmem = pl.BlockSpec(memory_space=pltpu.VMEM)
    tok = sh((tokens, width), bf16)
    wide = sh((chunks, tokens, width), bf16)
    long = sh((tokens, width), f32)
    block = (2, 2, 2, 2, own_rows, LANES)
    scratch = [
        v((pieces, 3) + block, bf16), v(block, bf16), v((pieces, 3, own_rows, LANES), bf16), v((own_rows, LANES), bf16),
        v((LANES, LANES), f32), v((tokens, width), bf16), v((tokens, width), bf16), v((tokens, width), bf16),
        v((tokens, width), f32), v((tokens, width), bf16), v((tokens, width), f32), v((chunks, tokens, width), f32),
        v((chunks, tokens, width), bf16), v((tokens, width), bf16), v((rows, seq, seq), f32), v((rows, seq, LANES), f32),
        v((chunks, 1, width), f32), v((tokens, LANES), f32),
        dma((6 + 2 * chunks,)), dma((pairs + 7 + 2 * chunks,)), dma((pieces,)), dma((3, tokens // 256)),
    ] + [dma((pieces,))] * 11 + [dma(())] * 9
    return pl.pallas_call(
        functools.partial(stage_kernel, heads),
        out_shape=(sh((pairs, tokens, PIECE), bf16), tok, sh((rows, 16, seq), f32), sh((pieces, 3) + block, bf16), tok, tok, wide,
                   sh((chunks, tokens, width), f32), tok, long, long, sh((tokens, LANES), f32), sh((8, width), f32), sh((16, width), f32)),
        in_specs=[hbm, vmem, hbm, hbm, hbm, vmem],
        out_specs=(hbm, hbm, vmem) + (hbm,) * 9 + (vmem, vmem),
        scratch_shapes=scratch,
        compiler_params=pltpu.CompilerParams(collective_id=0, has_side_effects=True, vmem_limit_bytes=BIG),
        name="stage",
    )(x, seg, e, aw, dw, vp)


class Reduce:
    def __init__(self, place, part, froms, done, out, sems, pieces, tiles=3):
        self.p, self.part, self.done, self.out, self.pieces, self.whole = place, part, done, out, pieces, tiles == 1
        self.names = ("core", "y", "p") if self.whole else ("core", "y", "p", "x", "early_y", "late_x")
        self.froms = dict(zip(("core", "y", "p", "z", "x", "early_y"), froms))
        self.zs, self.zr = sems[:2]
        self.sems = {name: (sems[2 + 2 * k], sems[3 + 2 * k]) for k, name in enumerate(self.names)}
        self.own = pl.ds(0, 1) if self.whole else pl.ds(place.x, 2)
        self.most = slice(None) if self.whole else pl.ds(0, 3)

    def copy(self, name, i):
        p, f, landing = self.p, self.part, self.froms
        if name == "core":
            src, dst = f.at[i, :, :, :, 1 - p.core], landing[name].at[i]
        elif name == "x":
            src, dst = f.at[i, 2 * (1 - p.x), self.most, :, p.core], landing[name].at[i, self.most]
        elif name == "late_x":
            src, dst = f.at[i, 2 * (1 - p.x), 3, p.y, p.core], landing["x"].at[i, 3, 0]
        elif name == "y":
            src, dst = f.at[i, self.own, self.most, 1 - p.y, p.core], landing[name].at[i, :, self.most]
        elif name == "early_y":
            src, dst = f.at[i, :, 3, 1 - p.y, p.core], landing[name].at[i]
        else:
            src, dst = self.done.at[i], landing[name].at[i]
        send, recv = self.sems[name]
        axis = {"p": "x", "early_y": "y", "late_x": "x"}.get(name, name)
        return remote(src, dst, send.at[i], recv.at[i], p.over(axis))

    def z_copy(self, i, k, incoming=False):
        p = self.p
        peer = p.z_peer(k)
        came = peer if incoming else p.z
        return remote(self.part.at[i, self.own, peer, p.y, p.core], self.froms["z"].at[i, came], self.zs.at[i, k], self.zr.at[i, came], p.over(k))

    def start(self, i):
        self.copy("core", i).start()

    def add(self, at, term):
        self.part[at] = self.part[at] + term

    def x_step(self, i):
        p = self.p
        self.copy("core", i).wait_recv()
        for t in range(1 if self.whole else 3):
            self.add((i, t, slice(None), slice(None), p.core), self.froms["core"][i, t])
        for name in ("y",) if self.whole else ("x", "early_y"):
            self.copy(name, i).start()

    def y_step(self, i):
        p = self.p
        self.copy("early_y", i).wait_recv()
        self.add((i, slice(None), 3, p.y, p.core), self.froms["early_y"][i])
        self.copy("late_x", i).start()
        self.copy("x", i).wait_recv()
        self.add((i, 2 * p.x, self.most, slice(None), p.core), self.froms["x"][i, :3])
        self.copy("y", i).start()

    def z_step(self, i):
        p = self.p
        self.copy("y", i).wait_recv()
        self.add((i, self.own, self.most, p.y, p.core), self.froms["y"][i, :, self.most])
        if not self.whole:
            self.copy("late_x", i).wait_recv()
            self.add((i, 2 * p.x, 3, p.y, p.core), self.froms["x"][i, 3, 0])
        for k in (2, 1, 3):
            self.z_copy(i, k).start()

    def p_step(self, i):
        p, f = self.p, self.part
        total = f[i, self.own, p.z, p.y, p.core].astype(f32)
        for k in (1, 2, 3):
            self.z_copy(i, k, True).wait_recv()
            total += self.froms["z"][i, p.z_peer(k)].astype(f32)
        self.done[i] = total.astype(bf16)
        self.copy("p", i).start()

    def finish(self, i):
        self.copy("p", i).wait_recv()
        a, b = self.done[i].astype(f32), self.froms["p"][i].astype(f32)
        if self.whole:
            self.out[i] = a[0] + b[0]
            return
        first = self.p.x == 0
        low, high = jnp.where(first, a, b), jnp.where(first, b, a)
        self.out[i] = jnp.concatenate([low[0], low[1] + high[0], high[1]], 1)

    def later(self, t):
        for lag, step in zip(REDUCE_LAGS, (self.y_step, self.z_step, self.p_step, self.finish)):
            when((t >= lag) & (t < self.pieces + lag), lambda lag=lag, step=step: step(t - lag))

    def turn(self, t):
        when(t < self.pieces, lambda: self.x_step(t))
        self.later(t)

    def sent(self, i):
        for name in self.names:
            self.copy(name, i).wait_send()
        for k in (1, 2, 3):
            self.z_copy(i, k).wait_send()


def back_kernel(heads, x_hbm, c_hbm, y1_hbm, dz_hbm, dh2_hbm, n1_hbm, r1_hbm, g_hbm, gp_hbm, qkv_hbm, w_hbm,
                seg_ref, lse_ref, dv_ref, vec_ref, gin_o, sum_o, vsum_o,
                part, fromc, fromy, fromp, fromz, fromx, frome, done, vpart, vfromc, vfromy, vfromp, vfromz, vdone, pool, wpool, gpool, acc, cb, dab, dcb, r1b, delta, vrow,
                ld, out_sem, *sems):
    place = Place()
    rows, seq = seg_ref.shape
    tokens, width = x_hbm.shape
    pairs = heads // 2
    chunks = g_hbm.shape[0]
    own_rows = part.shape[-2]
    pieces = part.shape[0]
    r_ = Reduce(place, part, (fromc, fromy, fromp, fromz, fromx, frome), done, sum_o, sems[:14], pieces)
    rv = Reduce(place, vpart, (vfromc, vfromy, vfromp, vfromz), vdone, vsum_o, sems[14:], vpart.shape[0], 1)
    ff_pieces = 4 * chunks
    first_ff = pairs + 2
    du, dz, y1 = pool.at[2], pool.at[3], pool.at[4]
    x = y1

    def load(k, src, dst):
        return pltpu.make_async_copy(src, dst, ld.at[k])

    def g_in(j):
        return load(j, g_hbm.at[j], pool.at[lax.rem(j, 2)])

    def gp_in(j):
        return load(chunks + j, gp_hbm.at[j], gpool.at[lax.rem(j, 2)])

    def w_in(j):
        return load(2 * chunks + j, w_hbm.at[pl.ds(first_ff + 4 * j, 4)], wpool.at[pl.ds(4 * lax.rem(j, 2), 4)])

    base = 3 * chunks
    dz_in, y1_in, acc_in, c_in, r1_in = (load(base + k, s, d) for k, (s, d) in enumerate(
        ((dz_hbm, dz), (y1_hbm, y1), (dh2_hbm, acc), (c_hbm, cb), (r1_hbm, r1b))))
    base += 5
    n1_in = load(base, n1_hbm, gpool.at[0])
    wo_in = load(base + 1, w_hbm.at[pl.ds(pairs, 2)], wpool.at[pl.ds(0, 2)])
    wq_in = load(base + 2, w_hbm.at[pl.ds(0, pairs)], wpool.at[pl.ds(2, pairs)])
    x_in = load(base + 3, x_hbm, x)
    base += 4

    def q_in(p):
        return load(base + p, qkv_hbm.at[p], pool.at[3, :, pl.ds(pl.multiple_of(lax.rem(p, 2) * PIECE, LANES), PIECE)])

    for c in (dz_in, g_in(0)):
        c.start()
    place.greet(place.reduce_peers)
    place.met(place.reduce_peers)
    vrow[...] = jnp.zeros_like(vrow)
    vrow[:8, :] = dv_ref[...]

    def colsum(t):
        return jnp.sum(t, 0, keepdims=True)

    half = width // 2

    def weight_grad(left, right, piece, count):
        d = dot_tn(left[...], right)
        for t in range(3 * count):
            part[piece + t // 3, t % 3] = d[:, t * LANES : (t + 1) * LANES].astype(bf16).reshape(4, 2, 2, own_rows, LANES)
        for k in range(count):
            r_.start(piece + k)

    dz_in.wait()

    def chunk(j):
        s = lax.rem(j, 2)
        g_in(j).wait()

        def rest_of_loads():
            for c in (gp_in(0), w_in(0), acc_in, y1_in, g_in(1), gp_in(1), w_in(1), c_in, r1_in):
                c.start()

        when(j == 0, rest_of_loads)
        weight_grad(dz, pool[s], 4 * j, 2)
        r_.turn(3 * j)
        gp_in(j).wait()
        w_in(j).wait()

        def first_waits():
            y1_in.wait()
            acc_in.wait()

        when(j == 0, first_waits)

        def block(i):
            at = pl.ds(pl.multiple_of(i * 512, 512), 512)
            d = (dot(dz[at, :], columns(wpool, 4 * s + 2, 4 * s + 3)) * gpool[s, at, :]).astype(bf16)
            du[at, :] = d
            acc[at, :] += dot_nt(d, columns(wpool, 4 * s, 4 * s + 1))
            vrow[pl.ds(8 + j, 1), :] += colsum(d.astype(f32))

        loop(tokens // 512, block)
        r_.turn(3 * j + 1)

        def ahead():
            for c in (g_in(j + 2), gp_in(j + 2), w_in(j + 2)):
                c.start()

        when(j + 2 < chunks, ahead)

        def norm_loads():
            n1_in.start()
            wo_in.start()

        when(j == chunks - 2, norm_loads)
        weight_grad(y1, du[...], 4 * j + 2, 2)
        r_.turn(3 * j + 2)

    loop(chunks, chunk)
    wq_in.start()
    x_in.start()
    q_in(0).start()
    q_in(1).start()
    for r in range(rows):
        segf = seg_ref[r : r + 1, :].astype(f32)
        rep = jnp.broadcast_to(segf, (LANES, seq)).T
        for k in range(seq // LANES):
            sl = slice(k * LANES, (k + 1) * LANES)
            gpool[1, r * seq : (r + 1) * seq, sl] = jnp.where(rep == segf[:, sl], 0.0, NEG)
    c_in.wait()
    r1_in.wait()
    n1_in.wait()
    wo_in.wait()
    g1 = vec_ref[0:1, :]
    sel_shape = (delta.shape[0], width)
    sel = jnp.where(lax.broadcasted_iota(jnp.int32, sel_shape, 0) == lax.broadcasted_iota(jnp.int32, sel_shape, 1) // HD, 1.0, 0.0).astype(bf16)

    def norm_one_back(i):
        at = pl.ds(pl.multiple_of(i * 256, 256), 256)
        dy1 = acc[at, :]
        n1 = gpool[0, at, :]
        dn = dy1 * g1
        r1 = r1b[at, :1]
        dh1 = r1 * (dn - jnp.mean(dn, 1, keepdims=True) - n1 * jnp.mean(dn * n1, 1, keepdims=True))
        acc[at, :] = dh1
        da = dh1.astype(bf16)
        dab[at, :] = da
        dc = dot_nt(da, columns(wpool, 0, 1)).astype(bf16)
        dcb[at, :] = dc
        prod = dc.astype(f32) * cb[at, :].astype(f32)
        hi = prod.astype(bf16)
        lo = (prod - hi.astype(f32)).astype(bf16)
        delta[:, at] = dot_nt(sel, hi) + dot_nt(sel, lo)
        vrow[0:1, :] += colsum(dy1 * n1)
        vrow[1:2, :] += colsum(dy1)
        vrow[6:7, :] += colsum(da.astype(f32))

    loop(tokens // 256, norm_one_back)
    r_.turn(3 * chunks)
    weight_grad(cb, dab[...], ff_pieces, 2)
    r_.turn(3 * chunks + 1)
    t0 = 3 * chunks + 2
    twice = ff_pieces + 2 - t0
    x_in.wait()
    first_seq = lax.broadcasted_iota(jnp.int32, (seq, LANES), 1) < HD

    def pair(p, last=False):
        head = pl.ds(pl.multiple_of(p * LANES, LANES), LANES)
        col = pl.multiple_of(lax.rem(p, 2) * PIECE, LANES)
        to = p // 2
        q_in(p).wait()

        def row(r):
            tok = pl.ds(pl.multiple_of(r * seq, seq), seq)
            q2 = pool[3, tok, pl.ds(col, LANES)]
            k2 = pool[3, tok, pl.ds(col + LANES, LANES)]
            v2 = pool[3, tok, pl.ds(col + 2 * LANES, LANES)]
            dc2 = dcb[tok, head]
            zero = jnp.zeros_like(k2)
            near = gpool[1, tok, :seq]
            grads = []
            for h in range(2):
                lse = lse_ref[r, pl.ds(2 * p + h, 1), :]
                dl = delta[pl.ds(2 * p + h, 1), tok]
                own = first_seq if h == 0 else ~first_seq
                pt = jnp.exp2((dot_nt(jnp.where(own, k2, zero), q2) + near) * SCALE2 - lse)
                ds = (pt * (dot_nt(jnp.where(own, v2, zero), dc2) - dl)).astype(bf16)
                dv = dot(pt.astype(bf16), dc2)
                grads.append((dot_tn(ds, k2) * 0.125, dot(ds, q2) * 0.125, dv))
            for k, (a, b) in enumerate(zip(*grads)):
                pool[to, tok, pl.ds(col + k * LANES, LANES)] = jnp.where(first_seq, a, b).astype(bf16)
            if last:
                r_.later(t0 + p + twice + 1 + r)
            else:
                when((r == 0) & (p < twice), lambda: r_.turn(t0 + 2 * p))
                when((r == 0) & (p == twice), lambda: r_.later(t0 + 2 * p))

        loop(rows, row)
        if not last:
            when(p + 2 < pairs, lambda: q_in(p + 2).start())
        d = pool[to, :, pl.ds(col, PIECE)]

        def biases():
            sums = colsum(d.astype(f32))
            vrow[4:5, head] = sums[:, :LANES]
            vrow[5:6, head] = sums[:, 2 * LANES :]

        if last:
            def product(a):
                w = dot_tn(x[:, pl.ds(pl.multiple_of(a * half, LANES), half)], d)
                for t in range(3):
                    vpart[t, 0, pl.ds(2 * a, 2)] = w[:, t * LANES : (t + 1) * LANES].astype(bf16).reshape(2, 2, 2, own_rows, LANES)

            loop(2, product)
            for t in range(3):
                rv.start(t)
            biases()
            vpart[3, 0] = vrow[...].T.astype(bf16).reshape(4, 2, 2, own_rows, LANES)
            rv.start(3)
        else:
            weight_grad(x, d, ff_pieces + 2 + p, 1)
            biases()
            late = p >= twice
            done = t0 + p + jnp.minimum(p + 1, twice)
            r_.x_step(done)
            r_.later(jnp.where(late, done + 1, done))

    loop(pairs - 1, pair)
    pair(pairs - 1, True)
    t0 += pairs + twice + rows
    singles = vpart.shape[0]
    wq_in.wait()
    blocks = tokens // 256

    def gin_block(i):
        at = pl.ds(pl.multiple_of(i * 256, 256), 256)
        d = jnp.concatenate([pool[k, at, :] for k in range(pairs // 2)], 1)
        dcb[at, :] = (acc[at, :] + dot_nt(d, columns(wpool, *range(2, 2 + pairs)))).astype(bf16)
        when(i == 0, lambda: loop(singles, rv.x_step))
        when(i < 2, lambda: r_.turn(t0 + i))
        when(i == 2, lambda: loop(singles, rv.z_step))
        when(i == 3, lambda: r_.turn(t0 + 2))

    loop(blocks, gin_block)
    gin_out = pltpu.make_async_copy(dcb, gin_o, out_sem)
    gin_out.start()
    t0 += 3
    rest = pieces + REDUCE_LAGS[-1] - t0

    def rest_turn(i):
        r_.turn(t0 + i)
        when(i == 0, lambda: loop(singles, rv.p_step))

    loop(rest, rest_turn)
    loop(singles, rv.finish)
    loop(pieces, r_.sent)
    loop(singles, rv.sent)
    gin_out.wait()


def back(x, c, y1, dz, dh2, n1, r1, g, gp, qkv, w, seg, lse, dv, vec):
    rows, seq = seg.shape
    tokens, width = x.shape
    chunks = g.shape[0]
    own_rows = w.shape[-2]
    heads = width // HD
    pairs = heads // 2
    pieces = 4 * chunks + 2 + pairs - 1
    sh = jax.ShapeDtypeStruct
    dma = pltpu.SemaphoreType.DMA
    v = pltpu.VMEM
    hbm = pl.BlockSpec(memory_space=pl.ANY)
    vmem = pl.BlockSpec(memory_space=pltpu.VMEM)
    tail = (own_rows, LANES)
    tok = v((tokens, width), bf16)
    scratch = [
        v((pieces, 3, 4, 2, 2) + tail, bf16), v((pieces, 3, 4, 2) + tail, bf16), v((pieces, 2, 4) + tail, bf16), v((pieces, 2) + tail, bf16),
        v((pieces, 4, 2) + tail, bf16), v((pieces, 4, 2) + tail, bf16), v((pieces, 3) + tail, bf16), v((pieces, 2) + tail, bf16),
        v((4, 1, 4, 2, 2) + tail, bf16), v((4, 1, 4, 2) + tail, bf16), v((4, 1, 4) + tail, bf16), v((4, 1) + tail, bf16),
        v((4, 4, 1) + tail, bf16), v((4, 1) + tail, bf16), v((5, tokens, width), bf16), v((8,) + w.shape[1:], bf16), v((2, tokens, width), f32),
        v((tokens, width), f32), tok, tok, tok, v((tokens, LANES), f32), v((16, tokens), f32),
        v((LANES, width), f32),
        dma((3 * chunks + 9 + pairs,)), dma(())] + [dma((pieces, 4))] * 2 + [dma((pieces,))] * 12 + [dma((4, 4))] * 2 + [dma((4,))] * 6
    return pl.pallas_call(
        functools.partial(back_kernel, heads),
        out_shape=(sh((tokens, width), bf16), sh((pieces, own_rows, PIECE), f32), sh((4, own_rows, LANES), f32)),
        in_specs=[hbm] * 11 + [vmem] * 4,
        out_specs=(hbm, vmem, vmem),
        scratch_shapes=scratch,
        compiler_params=pltpu.CompilerParams(collective_id=1, has_side_effects=True, vmem_limit_bytes=63 * 2**20),
        name="back",
    )(x, c, y1, dz, dh2, n1, r1, g, gp, qkv, w, seg, lse, dv, vec)


def update_kernel(rates, sum_ref, vsum_ref, gin_hbm, out_hbm, am, aw, aa, dm, dw, da, vm, vw, va,
                  gin_o, out_o, am_o, aw_o, aa_o, dm_o, dw_o, da_o, vm_o, vw_o, va_o, square, tok, att, den, ld, st):
    matrix, vector, replicas = rates
    moves = [(dm, den.at[0], dm_o), (dw, den.at[1], dw_o), (da, den.at[2], da_o), (am, att.at[0], am_o), (aw, att.at[1], aw_o),
             (aa, att.at[2], aa_o), (gin_hbm, tok.at[0], gin_o), (out_hbm, tok.at[1], out_o)]
    loads = [pltpu.make_async_copy(s, d, ld.at[k]) for k, (s, d, _) in enumerate(moves)]
    stores = [pltpu.make_async_copy(d, o, st.at[k]) for k, (_, d, o) in enumerate(moves)]
    for c in loads:
        c.start()

    def advance(grad, rate, moment, weight, average):
        grad = grad / replicas
        moment = momentum_decay * moment + grad
        weight = weight - rate * (grad + momentum_decay * moment)
        return moment, weight, average_decay * average + (1.0 - average_decay) * weight

    def advance_in(grad, ref, index):
        news = advance(grad, matrix, *(ref[(k,) + index] for k in range(3)))
        for k in range(3):
            ref[(k,) + index] = news[k]

    rows, own = vm.shape
    square[...] = jnp.zeros_like(square)
    square[:own, :] = vsum_ref[3]
    vm_o[...], vw_o[...], va_o[...] = advance(square[...].T[:rows, :own], vector, vm[...], vw[...], va[...])
    every = slice(None)
    pairs = att.shape[3] // LANES
    ff_pieces = sum_ref.shape[0] - 1 - pairs
    for c in loads[:3]:
        c.wait()
    for i in range(ff_pieces):
        col = i // 4 * 2 * PIECE + i % 2 * PIECE
        advance_in(sum_ref[i], den, (1 - i % 4 // 2, every, slice(col, col + PIECE)))
    for c in stores[:3]:
        c.start()
    for c in loads[3:6]:
        c.wait()
    for i in range(2):
        advance_in(sum_ref[ff_pieces + i], att, (3, every, slice(i * PIECE, (i + 1) * PIECE)))
    for p in range(pairs):
        for k in range(3):
            grad = vsum_ref[k] if p == pairs - 1 else sum_ref[ff_pieces + 2 + p, :, k * LANES : (k + 1) * LANES]
            advance_in(grad, att, (k, every, slice(p * LANES, (p + 1) * LANES)))
    for c in loads[6:]:
        c.wait()
    for c in stores[3:]:
        c.start()
    for c in stores:
        c.wait()


def update(rates, sums, vsums, gin, out, states):
    am, dm = states[0], states[3]
    sh = jax.ShapeDtypeStruct
    v = pltpu.VMEM
    hbm = pl.BlockSpec(memory_space=pl.ANY)
    vmem = pl.BlockSpec(memory_space=pltpu.VMEM)
    places = [hbm] * 8 + [vmem] * 3
    return pl.pallas_call(
        functools.partial(update_kernel, rates),
        out_shape=(sh(gin.shape, bf16), sh(out.shape, bf16)) + tuple(sh(s.shape, f32) for s in states),
        in_specs=[vmem, vmem] + places,
        out_specs=tuple(places),
        scratch_shapes=[v((LANES, LANES), f32), v((2,) + gin.shape, bf16), v((3,) + am.shape, f32), v((3,) + dm.shape, f32),
                        pltpu.SemaphoreType.DMA((8,)), pltpu.SemaphoreType.DMA((8,))],
        compiler_params=pltpu.CompilerParams(vmem_limit_bytes=BIG),
        name="update",
    )(sums, vsums, gin, out, *states)


def pack_columns(attention, dense, vectors):
    count = vectors.shape[0]
    vector_cols = jnp.pad(vectors.T, ((0, 0), (0, 128 - count)))
    first = jnp.concatenate([attention[0], attention[1], attention[2], vector_cols], 1)
    second = jnp.concatenate([attention[3], dense[0], dense[1]], 1)
    return first, second


def advance(gradient, moment, weight, average, step_rate):
    moment_new = momentum_decay * moment + gradient
    weight_new = weight - step_rate * (gradient + momentum_decay * moment_new)
    average_new = average_decay * average + (1.0 - average_decay) * weight_new
    return (moment_new, weight_new, average_new)


def plain_body(
    hidden_in,
    segment_ids,
    cotangent,
    attention_weights,
    attention_momentum,
    attention_average,
    dense_weights,
    dense_momentum,
    dense_average,
    vector_params,
    vector_momentum,
    vector_average,
):
    row_count, length, width = hidden_in.shape
    ff = dense_weights.shape[-1]
    vector_rows = vector_params.shape[0]
    x = hidden_in.reshape(-1, width)
    e = cotangent.reshape(-1, width)
    first, second = pack_columns(attention_weights, dense_weights, vector_params)
    first_full = lax.all_gather(first.astype(bf16), "wide", axis=0, tiled=True)
    second_full = lax.all_gather(second.astype(bf16), "wide", axis=0, tiled=True)
    vec = first_full[:, 3 * width : 3 * width + vector_rows].astype(f32).T
    bias_qkv = jnp.concatenate([vec[4:5], jnp.zeros((1, width), f32), vec[5:6]], 1)
    w_qkv = first_full[:, : 3 * width]
    wo, win, wd = (second_full[:, :width], second_full[:, width : width + ff], second_full[:, width + ff :])
    qkv, c, lse = attn_fwd(x, segment_ids, w_qkv, bias_qkv)
    out, y1, g, dz, du, da, dc, dh1, delta, dvec, dbin = mid(
        x, c, e, wo, win, wd, vec, vec[8:].reshape(1, ff)
    )
    grad_second = jnp.concatenate([wgrad(c, da), wgrad(y1, du), wgrad(dz, g)], 1)
    share_second = lax.psum_scatter(grad_second, "wide", scatter_dimension=0, tiled=True)
    dqkv, gin, dw, db = attn_bwd(segment_ids, qkv, dc, lse, delta, dh1, w_qkv, x)
    dvec = jnp.concatenate(
        [dvec[:4], db[:, :width], db[:, 2 * width :], dvec[6:8], dbin.reshape(-1, width)], 0
    )
    grad_first = jnp.concatenate(
        [dw, jnp.pad(dvec.T, ((0, 0), (0, 128 - vector_rows))).astype(bf16)], 1
    )
    share_first = lax.psum_scatter(grad_first, "wide", scatter_dimension=0, tiled=True)
    replicas = lax.axis_size("narrow")
    tokens_all = row_count * length * lax.axis_size("wide") * replicas
    grad_scale = math.sqrt(tokens_all) / replicas
    t1 = lax.psum(share_first, "narrow").astype(f32) / replicas
    t2 = lax.psum(share_second, "narrow").astype(f32) / replicas
    cut = lambda t, j: t[:, j * width : (j + 1) * width]
    attention_grad = jnp.stack([cut(t1, 0), cut(t1, 1), cut(t1, 2), cut(t2, 0)])
    dense_grad = jnp.stack([t2[:, width : width + ff], t2[:, width + ff :]])
    vector_grad = t1[:, 3 * width : 3 * width + vector_rows].T
    attention_new = advance(attention_grad, attention_momentum, attention_weights, attention_average, matrix_rate / grad_scale)
    dense_new = advance(dense_grad, dense_momentum, dense_weights, dense_average, matrix_rate / grad_scale)
    vector_new = advance(vector_grad, vector_momentum, vector_params, vector_average, vector_rate / grad_scale)
    return (out.reshape(hidden_in.shape), gin.reshape(hidden_in.shape)) + attention_new + dense_new + vector_new


def body(
    hidden_in,
    segment_ids,
    cotangent,
    attention_weights,
    attention_momentum,
    attention_average,
    dense_weights,
    dense_momentum,
    dense_average,
    vector_params,
    vector_momentum,
    vector_average,
):
    row_count, length, width = hidden_in.shape
    x = hidden_in.reshape(-1, width)
    e = cotangent.reshape(-1, width)
    replicas = lax.axis_size("narrow")
    tokens_all = row_count * length * lax.axis_size("wide") * replicas
    grad_scale = math.sqrt(tokens_all) / replicas
    rates = (matrix_rate / grad_scale, vector_rate / grad_scale, replicas)
    qkv, c, lse, w, out, y1, g, gp, dz, dh2, n1, r1, dv, vec = stage(
        x, segment_ids, e, attention_weights, dense_weights, vector_params
    )
    states = (
        attention_momentum, attention_weights, attention_average,
        dense_momentum, dense_weights, dense_average,
        vector_momentum, vector_params, vector_average,
    )
    gin, sums, vsums = back(x, c, y1, dz, dh2, n1, r1, g, gp, qkv, w, segment_ids, lse, dv, vec)
    news = update(rates, sums, vsums, gin, out, states)
    return (news[1].reshape(hidden_in.shape), news[0].reshape(hidden_in.shape)) + tuple(news[2:])


def solution(mesh):
    token = P(("wide", "narrow"), None, None)
    matrix = P(None, "wide", None)
    vector = P(None, "wide")
    in_specs = (token, P(("wide", "narrow"), None), token) + (matrix,) * 6 + (vector,) * 3
    out_specs = (token, token) + (matrix,) * 6 + (vector,) * 3
    ours = mesh.shape["wide"] == 16 and mesh.shape["narrow"] == 2
    return jax.shard_map(body if ours else plain_body, mesh=mesh, in_specs=in_specs, out_specs=out_specs, check_vma=False)
```
